32 devices in a mesh: head: 8 (over z, core), blk: 4 (over y, x).
Axes of the slice: x: 2, y: 2, z: 4, core: 2. Of those that a mesh axis runs over, the one named last changes fastest.
Arguments:
- tokens: bfloat16 [4096, 1024], P(('head', 'blk')), may hold values from -6 to 6
- gain_attn: bfloat16 [2, 1024], P(None, ('head', 'blk')), may hold values from 0.5 to 1.5
- w_query: bfloat16 [2, 1024, 1024], P(None, ('head', 'blk')), may hold values from -0.1875 to 0.1875
- w_key: bfloat16 [2, 1024, 1024], P(None, ('head', 'blk')), may hold values from -0.1875 to 0.1875
- w_value: bfloat16 [2, 1024, 1024], P(None, ('head', 'blk')), may hold values from -0.1875 to 0.1875
- w_out: bfloat16 [2, 1024, 1024], P(None, ('head', 'blk')), may hold values from -1 to 1
- gain_ffn: bfloat16 [2, 1024], P(None, ('head', 'blk')), may hold values from 0.5 to 1.5
- w_gate: bfloat16 [2, 1024, 4096], P(None, ('head', 'blk')), may hold values from -0.1875 to 0.1875
- w_up: bfloat16 [2, 1024, 4096], P(None, ('head', 'blk')), may hold values from -0.1875 to 0.1875
- w_down: bfloat16 [2, 4096, 1024], P(None, ('head', 'blk')), may hold values from -0.09375 to 0.09375
- doc_ids: int32 [4096], replicated, may hold values from 0 to 15, never falling along the last dimension, each value on 1 to 1024 neighbouring positions
- cotangent: bfloat16 [4096, 1024], P(('head', 'blk')), may hold values from -6 to 6
Outputs:
- output: bfloat16 [4096, 1024], P(('head', 'blk'))
- grad_tokens: float32 [4096, 1024], P(('head', 'blk'))
- grad_gain_attn: float32 [2, 1024], P(None, ('head', 'blk'))
- grad_query: float32 [2, 1024, 1024], P(None, ('head', 'blk'))
- grad_key: float32 [2, 1024, 1024], P(None, ('head', 'blk'))
- grad_value: float32 [2, 1024, 1024], P(None, ('head', 'blk'))
- grad_out: float32 [2, 1024, 1024], P(None, ('head', 'blk'))
- grad_gain_ffn: float32 [2, 1024], P(None, ('head', 'blk'))
- grad_gate: float32 [2, 1024, 4096], P(None, ('head', 'blk'))
- grad_up: float32 [2, 1024, 4096], P(None, ('head', 'blk'))
- grad_down: float32 [2, 4096, 1024], P(None, ('head', 'blk'))
The draws below stay inside these ranges and needn't reach their ends.
Inputs may be any that keep to these rules, and one draw needn't show every extreme that they name: `doc_ids`: never falling along the stream; each document holds 1 to 1024 tokens and one holds exactly 1024.
All inputs are finite; a program needn't handle non-finite values.
Results may differ from the reference program's by a relative error of at most 0.029.
Values may be sent and summed in bfloat16 or wider, within the bound.
A program may use at most 320 MiB of HBM per device.

```python
import math
import jax
import jax.numpy as jnp
import numpy as np
from jax import lax

D = 1024
HEADS = 16
HD = 64
FF = 4096
LAYERS = 2
TOKENS = 4096
DOC_MAX = 1024
DOCS = 16


def shard_levels(stream_key, extent, pieces, low, high):
    def one(dim, blocks):
        draws = jax.random.uniform(jax.random.fold_in(jax.random.fold_in(stream_key, 6), dim), (blocks,), jnp.float32, low / len(pieces), high / len(pieces))
        return jnp.repeat(jnp.exp(draws), extent[dim] // blocks).reshape((-1,) + (1,) * (len(extent) - dim - 1))

    gain = one(*pieces[0])
    for cut in pieces[1:]:
        gain = gain * one(*cut)
    return gain


def length_profile(amount, total, most, lean):
    portions = [(1 << 20) // math.isqrt(grade ** lean) + 1 for grade in range(2, amount + 1)]
    spare, holding = total - most - (amount - 1), [1] * (amount - 1)
    while spare > 0:
        free = [i for i in range(amount - 1) if holding[i] < most]
        pool, left = sum([portions[i] for i in free]), spare
        for i in free:
            extra = min(most - holding[i], max(1, left * portions[i] // pool), spare)
            holding[i] = holding[i] + extra
            spare = spare - extra
    return np.array([most] + holding)


def uneven(stream_key, number_of, total, limit, slope):
    if number_of == 2:
        one = jax.random.randint(stream_key, (), max(1, total - limit), min(limit, total - 1) + 1)
        return jnp.stack([one, total - one])
    lengths = jnp.asarray(length_profile(number_of, total, limit, slope), jnp.int32)
    pairs = (number_of - 1) // 2
    giver, receiver = lengths[1:1 + 2 * pairs:2], lengths[2:2 + 2 * pairs:2]
    slack = jnp.minimum(giver - 1, limit - receiver)
    shifted = jax.random.randint(jax.random.fold_in(stream_key, 1), (pairs,), 0, 1 << 20) % (slack + 1)
    lengths = lengths.at[1:1 + 2 * pairs:2].set(giver - shifted).at[2:2 + 2 * pairs:2].set(receiver + shifted)
    return lengths[jax.random.permutation(jax.random.fold_in(stream_key, 2), number_of)]


def scatter_about(rng, dims, scale, limit, cuts=(), held_as=jnp.bfloat16):
    values = scale * jax.random.normal(rng, dims, jnp.float32)
    if cuts:
        values = values * shard_levels(rng, dims, cuts, -0.22, 0.18)
    return jnp.clip(values, -limit, limit).astype(held_as)


def setup_inputs(seed: int = 0) -> dict:
    arg_keys = jax.random.split(jax.random.key(seed), 13)
    tokens = scatter_about(arg_keys[0], (TOKENS, D), 1.0, 6.0, ((0, 32),))
    gain_attn = jnp.clip(1.0 + 0.1 * jax.random.normal(arg_keys[1], (LAYERS, D), jnp.float32), 0.5, 1.5).astype(jnp.bfloat16)
    w_query = scatter_about(arg_keys[2], (LAYERS, D, D), D ** -0.5, 0.1875, ((1, 32),))
    w_key = scatter_about(arg_keys[3], (LAYERS, D, D), D ** -0.5, 0.1875, ((1, 32),))
    w_value = scatter_about(arg_keys[4], (LAYERS, D, D), D ** -0.5, 0.1875, ((1, 32),))
    w_out = scatter_about(arg_keys[5], (LAYERS, D, D), (D // 32) ** -0.5, 1.0, ((1, 32),))
    gain_ffn = jnp.clip(1.0 + 0.1 * jax.random.normal(arg_keys[6], (LAYERS, D), jnp.float32), 0.5, 1.5).astype(jnp.bfloat16)
    w_gate = scatter_about(arg_keys[7], (LAYERS, D, FF), D ** -0.5, 0.1875, ((1, 32),))
    w_up = scatter_about(arg_keys[8], (LAYERS, D, FF), D ** -0.5, 0.1875, ((1, 32),))
    w_down = scatter_about(arg_keys[9], (LAYERS, FF, D), FF ** -0.5, 0.09375, ((1, 32),))
    doc_ids = jnp.searchsorted(jnp.cumsum(uneven(arg_keys[10], DOCS, TOKENS, DOC_MAX, 1)), jnp.arange(TOKENS), side="right").astype(jnp.int32)
    cotangent = scatter_about(arg_keys[11], (TOKENS, D), 1.0, 6.0, ((0, 32),))
    return {"tokens": tokens, "gain_attn": gain_attn, "w_query": w_query, "w_key": w_key, "w_value": w_value, "w_out": w_out, "gain_ffn": gain_ffn, "w_gate": w_gate, "w_up": w_up, "w_down": w_down, "doc_ids": doc_ids, "cotangent": cotangent}


@jax.custom_vjp
def low(v):
    return lax.optimization_barrier(v.astype(jnp.bfloat16)).astype(jnp.float32)

@jax.custom_vjp
def low_back(v):
    return v

def low_keep(v):
    return (low(v), None)

def low_pass(kept, grad):
    return (grad,)

def back_keep(v):
    return (v, None)

def back_low(kept, grad):
    return (low(grad),)
low.defvjp(low_keep, low_pass)
low_back.defvjp(back_keep, back_low)

def matmul_high(left, right):
    return jnp.dot(left, right, precision=lax.Precision.HIGHEST, preferred_element_type=jnp.float32)

def rms_scale(values):
    return values * lax.rsqrt(lax.optimization_barrier(jnp.mean(values * values, axis=-1, keepdims=True)) + 1e-05)

def attention(queries, keys, values, positions, documents):
    score_scale = HD ** (-0.5)
    block_rows = math.gcd(TOKENS, 512)
    block_count = TOKENS // block_rows

    def one_block(inputs):
        query_block, query_pos, query_doc = inputs
        raw_scores = jnp.einsum('qhd,khd->hqk', query_block, keys, precision=lax.Precision.HIGHEST) * score_scale
        raw_scores = low_back(raw_scores)
        allowed = (query_doc[:, None] == documents[None, :]) & (positions[None, :] <= query_pos[:, None])
        scores = jnp.where(allowed[None], raw_scores, -1e+30)
        weights = low(jax.nn.softmax(scores, axis=-1))
        return jnp.einsum('hqk,khd->qhd', weights, values, precision=lax.Precision.HIGHEST)
    result = lax.map(jax.checkpoint(one_block), (queries.reshape(block_count, block_rows, HEADS, HD), positions.reshape(block_count, block_rows), documents.reshape(block_count, block_rows)))
    return result.reshape(TOKENS, HEADS * HD)

def one_layer(stream, attn_gain, query_weight, key_weight, value_weight, out_weight, ffn_gain, gate_weight, up_weight, down_weight, positions, documents):
    normed = low(rms_scale(stream) * attn_gain)
    queries = low_back(low(matmul_high(normed, query_weight)))
    keys = low_back(low(matmul_high(normed, key_weight)))
    values = low_back(low(matmul_high(normed, value_weight)))
    attended = attention(queries.reshape(TOKENS, HEADS, HD), keys.reshape(TOKENS, HEADS, HD), values.reshape(TOKENS, HEADS, HD), positions, documents)
    mixed = low_back(low(attended))
    middle = stream + low_back(matmul_high(mixed, out_weight))
    normed_ffn = low(rms_scale(middle) * ffn_gain)
    gate_proj = low_back(matmul_high(normed_ffn, gate_weight))
    up_proj = low_back(matmul_high(normed_ffn, up_weight))
    hidden = low(jax.nn.silu(gate_proj) * up_proj)
    return middle + low_back(matmul_high(hidden, down_weight))

def reference(tokens, gain_attn, w_query, w_key, w_value, w_out, gain_ffn, w_gate, w_up, w_down, doc_ids, cotangent):
    positions = jnp.arange(TOKENS, dtype=jnp.int32)
    params = (gain_attn.astype(jnp.float32), w_query.astype(jnp.float32), w_key.astype(jnp.float32), w_value.astype(jnp.float32), w_out.astype(jnp.float32), gain_ffn.astype(jnp.float32), w_gate.astype(jnp.float32), w_up.astype(jnp.float32), w_down.astype(jnp.float32))

    def forward(stream, weights):
        for layer_index in range(LAYERS):
            stream = one_layer(stream, weights[0][layer_index], weights[1][layer_index], weights[2][layer_index], weights[3][layer_index], weights[4][layer_index], weights[5][layer_index], weights[6][layer_index], weights[7][layer_index], weights[8][layer_index], positions, doc_ids)
        return stream
    final, pullback = jax.vjp(forward, tokens.astype(jnp.float32), params)
    grad_input, grad_params = pullback(cotangent.astype(jnp.float32))
    return (final.astype(jnp.bfloat16), grad_input, grad_params[0], grad_params[1], grad_params[2], grad_params[3], grad_params[4], grad_params[5], grad_params[6], grad_params[7], grad_params[8])
```

```python
import functools

import jax
import jax.numpy as jnp
from jax import lax
from jax.experimental import pallas as pl
from jax.experimental.pallas import tpu as pltpu
from jax.sharding import PartitionSpec as P

D = 1024
HD = 64
HEADS = D // HD
LAYERS = 2
EPSILON = 1e-05
MASKED = -1e30
MESH = pl.DeviceIdType.MESH
F32 = jnp.float32
BF16 = jnp.bfloat16
ANY = pl.BlockSpec(memory_space=pl.ANY)


def greet_blk(count):
    me = lax.axis_index("blk")
    barrier = pltpu.get_barrier_semaphore()
    for step in range(1, count):
        pl.semaphore_signal(
            barrier,
            inc=1,
            device_id={"blk": lax.rem(me + step, count)},
            device_id_type=MESH,
        )
    pl.semaphore_wait(barrier, count - 1)
    return me


def plane_gather_kernel(count, x_ref, o_ref, send_sem, recv_sem, local_sem):
    me = greet_blk(count)
    copies = []
    for step in range(1, count):
        copy = pltpu.make_async_remote_copy(
            src_ref=x_ref,
            dst_ref=o_ref.at[me],
            send_sem=send_sem.at[step - 1],
            recv_sem=recv_sem.at[step - 1],
            device_id={"blk": lax.rem(me + step, count)},
            device_id_type=MESH,
        )
        copy.start()
        copies.append(copy)
    own = pltpu.make_async_copy(x_ref, o_ref.at[me], local_sem)
    own.start()
    own.wait()
    for copy in copies:
        copy.wait()


def plane_swap_kernel(count, x_ref, o_ref, send_sem, recv_sem, local_sem):
    me = greet_blk(count)
    copies = []
    for step in range(1, count):
        peer = lax.rem(me + step, count)
        copy = pltpu.make_async_remote_copy(
            src_ref=x_ref.at[peer],
            dst_ref=o_ref.at[me],
            send_sem=send_sem.at[step - 1],
            recv_sem=recv_sem.at[step - 1],
            device_id={"blk": peer},
            device_id_type=MESH,
        )
        copy.start()
        copies.append(copy)
    own = pltpu.make_async_copy(x_ref.at[me], o_ref.at[me], local_sem)
    own.start()
    own.wait()
    for copy in copies:
        copy.wait()


def plane_call(kernel, x, out_shape, collective_id, name):
    count = lax.axis_size("blk")
    return pl.pallas_call(
        functools.partial(kernel, count),
        out_shape=jax.ShapeDtypeStruct(out_shape, x.dtype),
        in_specs=[ANY],
        out_specs=ANY,
        scratch_shapes=[
            pltpu.SemaphoreType.DMA((count - 1,)),
            pltpu.SemaphoreType.DMA((count - 1,)),
            pltpu.SemaphoreType.DMA,
        ],
        compiler_params=pltpu.CompilerParams(collective_id=collective_id, has_side_effects=True),
        cost_estimate=pl.CostEstimate(flops=0, bytes_accessed=20_000_000, transcendentals=0),
        name=name,
    )(x)


def plane_gather(x, collective_id, name):
    return plane_call(
        plane_gather_kernel, x, (lax.axis_size("blk"),) + x.shape, collective_id, name
    )


def plane_swap(x, collective_id, name):
    return plane_call(plane_swap_kernel, x, x.shape, collective_id, name)


def halo_kernel(count, reach, x_ref, o_ref, send_sem, recv_sem, local_sem):
    me = lax.axis_index("head")
    barrier = pltpu.get_barrier_semaphore()
    for k in range(1, reach + 1):

        @pl.when(me - k >= 0)
        def _(k=k):
            pl.semaphore_signal(barrier, inc=1, device_id={"head": me - k}, device_id_type=MESH)

    for k in range(1, reach + 1):

        @pl.when((me + k == count - 1) if k < reach else (me + k < count))
        def _(k=k):
            pl.semaphore_wait(barrier, k)

    def copy_to(k):
        return pltpu.make_async_remote_copy(
            src_ref=x_ref,
            dst_ref=o_ref.at[reach - k],
            send_sem=send_sem.at[k - 1],
            recv_sem=recv_sem.at[k - 1],
            device_id={"head": me + k},
            device_id_type=MESH,
        )

    for k in range(1, reach + 1):

        @pl.when(me + k < count)
        def _(k=k):
            copy_to(k).start()

    own = pltpu.make_async_copy(x_ref, o_ref.at[reach], local_sem)
    own.start()
    own.wait()
    for k in range(1, reach + 1):

        @pl.when(me + k < count)
        def _(k=k):
            copy_to(k).wait_send()

        @pl.when(me - k >= 0)
        def _(k=k):
            copy_to(k).wait_recv()


def halo_forward(x, reach, collective_id, name):
    count = lax.axis_size("head")
    return pl.pallas_call(
        functools.partial(halo_kernel, count, reach),
        out_shape=jax.ShapeDtypeStruct((reach + 1,) + x.shape, x.dtype),
        in_specs=[ANY],
        out_specs=ANY,
        scratch_shapes=[
            pltpu.SemaphoreType.DMA((reach,)),
            pltpu.SemaphoreType.DMA((reach,)),
            pltpu.SemaphoreType.DMA,
        ],
        compiler_params=pltpu.CompilerParams(collective_id=collective_id, has_side_effects=True),
        cost_estimate=pl.CostEstimate(flops=0, bytes_accessed=20_000_000, transcendentals=0),
        name=name,
    )(x)


def halo_back_kernel(count, reach, x_ref, o_ref, send_sem, recv_sem, local_sem):
    me = lax.axis_index("head")
    barrier = pltpu.get_barrier_semaphore()
    for k in range(1, reach + 1):

        @pl.when(me + k < count)
        def _(k=k):
            pl.semaphore_signal(barrier, inc=1, device_id={"head": me + k}, device_id_type=MESH)

    for k in range(1, reach + 1):

        @pl.when((me == k) if k < reach else (me >= k))
        def _(k=k):
            pl.semaphore_wait(barrier, k)

    def copy_to(k):
        return pltpu.make_async_remote_copy(
            src_ref=x_ref.at[reach - k],
            dst_ref=o_ref.at[k],
            send_sem=send_sem.at[k - 1],
            recv_sem=recv_sem.at[k - 1],
            device_id={"head": me - k},
            device_id_type=MESH,
        )

    for k in range(1, reach + 1):

        @pl.when(me - k >= 0)
        def _(k=k):
            copy_to(k).start()

    own = pltpu.make_async_copy(x_ref.at[reach], o_ref.at[0], local_sem)
    own.start()
    own.wait()
    for k in range(1, reach + 1):

        @pl.when(me - k >= 0)
        def _(k=k):
            copy_to(k).wait_send()

        @pl.when(me + k < count)
        def _(k=k):
            copy_to(k).wait_recv()


def halo_back(x, collective_id, name):
    count = lax.axis_size("head")
    reach = x.shape[0] - 1
    return pl.pallas_call(
        functools.partial(halo_back_kernel, count, reach),
        out_shape=jax.ShapeDtypeStruct(x.shape, x.dtype),
        in_specs=[ANY],
        out_specs=ANY,
        scratch_shapes=[
            pltpu.SemaphoreType.DMA((reach,)),
            pltpu.SemaphoreType.DMA((reach,)),
            pltpu.SemaphoreType.DMA,
        ],
        compiler_params=pltpu.CompilerParams(collective_id=collective_id, has_side_effects=True),
        cost_estimate=pl.CostEstimate(flops=0, bytes_accessed=20_000_000, transcendentals=0),
        name=name,
    )(x)


def dot_nt(left, right):
    return lax.dot_general(left, right, (((1,), (1,)), ((), ())), preferred_element_type=F32)


def dot_nn(left, right):
    return lax.dot_general(left, right, (((1,), (0,)), ((), ())), preferred_element_type=F32)


def dot_tn(left, right):
    return lax.dot_general(left, right, (((0,), (0,)), ((), ())), preferred_element_type=F32)


def head_masks(rows):
    lane = lax.broadcasted_iota(jnp.int32, (rows, 2 * HD), 1)
    return (lane < HD, lane >= HD)


def attend_kernel(tile, chunk, lead, low_ref, q_ref, k_ref, v_ref, start_ref, o_ref, mixed_ref, log_ref):
    index = pl.program_id(1)
    queries = q_ref[...] * jnp.asarray(HD ** (-0.5), BF16)
    masks = head_masks(tile)
    halves = [jnp.where(mask, queries, jnp.zeros_like(queries)) for mask in masks]
    first = start_ref[...]
    last = lead + index * tile + lax.broadcasted_iota(jnp.int32, (tile, 1), 0)

    def step(block, state):
        offset = pl.multiple_of(block * chunk, chunk)
        keys = k_ref[pl.ds(offset, chunk), :]
        values = v_ref[pl.ds(offset, chunk), :]
        place = offset + lax.broadcasted_iota(jnp.int32, (tile, chunk), 1)
        allowed = (place >= first) & (place <= last)
        out = []
        for half, (top, total, accum) in zip(halves, state):
            scores = jnp.where(allowed, dot_nt(half, keys), MASKED)
            new_top = jnp.maximum(top, jnp.max(scores, axis=1, keepdims=True))
            factor = jnp.exp(top - new_top)
            weights = jnp.where(allowed, jnp.exp(scores - new_top), 0.0)
            total = total * factor + jnp.sum(weights, axis=1, keepdims=True)
            accum = accum * factor + dot_nn(weights.astype(BF16), values)
            out.append((new_top, total, accum))
        return tuple(out)

    start = (
        jnp.full((tile, 1), MASKED, F32),
        jnp.zeros((tile, 1), F32),
        jnp.zeros((tile, 2 * HD), F32),
    )
    stop = (lead + (index + 1) * tile + chunk - 1) // chunk
    state = lax.fori_loop(low_ref[index], stop, step, (start, start))
    attended = [accum / total for _, total, accum in state]
    logs = [top + jnp.log(total) for top, total, _ in state]
    result = jnp.where(masks[0], attended[0], attended[1])
    o_ref[...] = result
    mixed_ref[...] = result.astype(BF16)
    log_ref[...] = jnp.where(masks[0], logs[0], logs[1])


def attend(queries, keys_values, first_place, low, tile, chunk):
    rows, cols = queries.shape
    span = keys_values.shape[0]
    pairs = cols // (2 * HD)
    tiles = rows // tile
    query_spec = pl.BlockSpec((tile, 2 * HD), lambda p, i, low: (i, p))
    return pl.pallas_call(
        functools.partial(attend_kernel, tile, chunk, span - rows),
        grid_spec=pltpu.PrefetchScalarGridSpec(
            num_scalar_prefetch=1,
            grid=(pairs, tiles),
            in_specs=[
                query_spec,
                pl.BlockSpec((span, 2 * HD), lambda p, i, low: (0, p)),
                pl.BlockSpec((span, 2 * HD), lambda p, i, low: (0, p + pairs)),
                pl.BlockSpec((tile, 1), lambda p, i, low: (i, 0)),
            ],
            out_specs=[query_spec, query_spec, query_spec],
        ),
        out_shape=[
            jax.ShapeDtypeStruct((rows, cols), F32),
            jax.ShapeDtypeStruct((rows, cols), BF16),
            jax.ShapeDtypeStruct((rows, cols), F32),
        ],
        cost_estimate=pl.CostEstimate(
            flops=rows * span * cols * 4, bytes_accessed=30_000_000, transcendentals=rows * span
        ),
        name="attend",
    )(low, queries, keys_values, keys_values, first_place)


def attend_back_kernel(
    tile,
    chunk,
    lead,
    low_ref,
    q_ref,
    k_ref,
    v_ref,
    g_ref,
    o_ref,
    log_ref,
    start_ref,
    dq_ref,
    dk_ref,
    dv_ref,
    dk_sum,
    dv_sum,
):
    tiles = q_ref.shape[0] // tile
    dk_sum[...] = jnp.zeros_like(dk_sum)
    dv_sum[...] = jnp.zeros_like(dv_sum)
    masks = head_masks(tile)

    def tile_step(index, carry):
        row = pl.multiple_of(index * tile, tile)
        here = pl.ds(row, tile)
        queries = q_ref[here, :] * jnp.asarray(HD ** (-0.5), BF16)
        grads = g_ref[here, :]
        product = grads.astype(F32) * o_ref[here, :]
        logs = log_ref[here, :]
        first = start_ref[here, :]
        last = lead + row + lax.broadcasted_iota(jnp.int32, (tile, 1), 0)
        zero = jnp.zeros_like(queries)
        parts = []
        for which, mask in enumerate(masks):
            parts.append(
                (
                    jnp.where(mask, queries, zero),
                    jnp.where(mask, grads, zero),
                    jnp.sum(jnp.where(mask, product, 0.0), axis=1, keepdims=True),
                    logs[:, which * HD : which * HD + 1],
                )
            )

        def step(block, totals):
            offset = pl.multiple_of(block * chunk, chunk)
            there = pl.ds(offset, chunk)
            keys = k_ref[there, :]
            values = v_ref[there, :]
            place = offset + lax.broadcasted_iota(jnp.int32, (tile, chunk), 1)
            allowed = (place >= first) & (place <= last)
            out = []
            key_part = None
            value_part = None
            for (half, grad, delta, log_total), total in zip(parts, totals):
                probs = jnp.where(allowed, jnp.exp(dot_nt(half, keys) - log_total), 0.0)
                score = (probs * (dot_nt(grad, values) - delta)).astype(BF16)
                out.append(total + dot_nn(score, keys))
                key_now = dot_tn(score, half)
                value_now = dot_tn(probs.astype(BF16), grad)
                key_part = key_now if key_part is None else key_part + key_now
                value_part = value_now if value_part is None else value_part + value_now
            dk_sum[there, :] += key_part
            dv_sum[there, :] += value_part
            return tuple(out)

        stop = (lead + row + tile + chunk - 1) // chunk
        empty = jnp.zeros((tile, 2 * HD), F32)
        totals = lax.fori_loop(low_ref[index], stop, step, (empty, empty))
        total = jnp.where(masks[0], totals[0], totals[1]) * (HD ** (-0.5))
        dq_ref[here, :] = total.astype(BF16)
        return carry

    lax.fori_loop(0, tiles, tile_step, 0)
    dk_ref[...] = dk_sum[...].astype(BF16)
    dv_ref[...] = dv_sum[...].astype(BF16)


def attend_back(queries, keys_values, grads, attended, logs, first_place, low, tile, chunk):
    rows, cols = queries.shape
    span = keys_values.shape[0]
    pairs = cols // (2 * HD)
    query_spec = pl.BlockSpec((rows, 2 * HD), lambda p, low: (0, p))
    key_spec = pl.BlockSpec((span, 2 * HD), lambda p, low: (0, p))
    return pl.pallas_call(
        functools.partial(attend_back_kernel, tile, chunk, span - rows),
        grid_spec=pltpu.PrefetchScalarGridSpec(
            num_scalar_prefetch=1,
            grid=(pairs,),
            in_specs=[
                query_spec,
                key_spec,
                pl.BlockSpec((span, 2 * HD), lambda p, low: (0, p + pairs)),
                query_spec,
                query_spec,
                query_spec,
                pl.BlockSpec((rows, 1), lambda p, low: (0, 0)),
            ],
            out_specs=[query_spec, key_spec, key_spec],
            scratch_shapes=[
                pltpu.VMEM((span, 2 * HD), F32),
                pltpu.VMEM((span, 2 * HD), F32),
            ],
        ),
        out_shape=[
            jax.ShapeDtypeStruct((rows, cols), BF16),
            jax.ShapeDtypeStruct((span, cols), BF16),
            jax.ShapeDtypeStruct((span, cols), BF16),
        ],
        cost_estimate=pl.CostEstimate(
            flops=rows * span * cols * 10, bytes_accessed=60_000_000, transcendentals=rows * span
        ),
        name="attend_back",
    )(low, queries, keys_values, keys_values, grads, attended, logs, first_place)


def inverse_rms(values):
    return lax.rsqrt(jnp.mean(values * values, axis=-1, keepdims=True) + EPSILON)


def rms_back(values, upstream):
    inverse = inverse_rms(values)
    inner_mean = jnp.mean(upstream * values, axis=-1, keepdims=True)
    return inverse * upstream - values * (inverse * inverse * inverse) * inner_mean


def matmul(left, right):
    return jnp.dot(left, right, preferred_element_type=F32)


def contract_rows(left, right):
    return jnp.einsum("td,te->de", left, right, preferred_element_type=F32)


def contract_cols(left, right):
    return jnp.einsum("te,de->td", left, right, preferred_element_type=F32)


def local(
    tokens,
    gain_attn,
    w_query,
    w_key,
    w_value,
    w_out,
    gain_ffn,
    w_gate,
    w_up,
    w_down,
    doc_ids,
    cotangent,
):
    planes = lax.axis_size("head")
    peers = lax.axis_size("blk")
    plane = lax.axis_index("head")
    tok = tokens.shape[0]
    group = tok * peers
    stream_rows = group * planes
    doc_max = stream_rows // 4
    reach = min(planes - 1, (doc_max - 1 + group - 1) // group)
    own_rows = w_query.shape[1]
    cols = D // peers
    strip = w_down.shape[1]
    hidden_cols = strip * planes
    tile = 256
    chunk = 256
    lead = reach * group

    places = jnp.arange(stream_rows, dtype=jnp.int32)
    opens = jnp.concatenate([jnp.ones((1,), jnp.bool_), doc_ids[1:] != doc_ids[:-1]])
    starts = lax.cummax(jnp.where(opens, places, 0))
    first_place = lax.dynamic_slice_in_dim(starts, plane * group, group, 0) - (
        plane * group - lead
    )
    low = first_place[::tile] // chunk
    first_place = first_place[:, None]

    attn_rows = gain_attn.astype(F32)[:, :, None]
    ffn_rows = gain_ffn.astype(F32)[:, :, None]

    def for_peers(weight, gain):
        scaled = (weight.astype(F32) * gain).astype(BF16)
        return scaled.reshape(LAYERS, own_rows, peers, cols).transpose(2, 0, 1, 3)

    def for_peers_ffn(weight, gain):
        scaled = (weight.astype(F32) * gain).astype(BF16)
        scaled = scaled.reshape(LAYERS, own_rows, planes, peers, strip).transpose(3, 0, 1, 2, 4)
        return scaled.reshape(peers, LAYERS, own_rows, hidden_cols)

    packed = jnp.concatenate(
        [
            for_peers(w_query, attn_rows),
            for_peers(w_key, attn_rows),
            for_peers(w_value, attn_rows),
            for_peers_ffn(w_gate, ffn_rows),
            for_peers_ffn(w_up, ffn_rows),
        ],
        axis=3,
    )
    swapped = plane_swap(packed, 1, "weights_swap")
    full = []
    for layer in range(LAYERS):
        mine = swapped[:, layer].reshape(peers * own_rows, 3 * cols + 2 * hidden_cols)
        attn_full = lax.all_gather(mine[:, : 3 * cols], "head", axis=0, tiled=True)
        out_full = lax.all_gather(w_out[layer], ("head", "blk"), axis=0, tiled=True)
        ffn_full = lax.all_gather(mine[:, 3 * cols :], "head", axis=0, tiled=True)
        down_full = lax.all_gather(w_down[layer], "head", axis=0, tiled=True)
        full.append((attn_full, out_full, ffn_full, down_full))

    stream = tokens.astype(F32)
    saved = []
    for layer in range(LAYERS):
        attn_full, out_full, ffn_full, down_full = full[layer]
        scaled = (stream * inverse_rms(stream)).astype(BF16)
        scaled_group = plane_gather(scaled, 2, "normed_gather").reshape(group, D)
        projected = matmul(scaled_group, attn_full).astype(BF16)
        queries = projected[:, :cols]
        keys_values = halo_forward(projected[:, cols:], reach, 3, "halo").reshape(
            (reach + 1) * group, 2 * cols
        )
        attended, mixed_heads, logs = attend(queries, keys_values, first_place, low, tile, chunk)
        mixed = plane_swap(mixed_heads.reshape(peers, tok, cols), 4, "mixed_swap")
        mixed = mixed.transpose(1, 0, 2).reshape(tok, D)
        middle = stream + matmul(mixed, out_full)
        scaled_ffn = (middle * inverse_rms(middle)).astype(BF16)
        scaled_ffn_group = plane_gather(scaled_ffn, 2, "normed_gather").reshape(group, D)
        gate_up = matmul(scaled_ffn_group, ffn_full)
        gate_proj = gate_up[:, :hidden_cols]
        up_proj = gate_up[:, hidden_cols:]
        hidden = (jax.nn.silu(gate_proj) * up_proj).astype(BF16)
        part = matmul(hidden, down_full).astype(BF16)
        parts = plane_swap(part.reshape(peers, tok, D), 5, "sum_swap")
        next_stream = middle + jnp.sum(parts.astype(F32), axis=0)
        saved.append(
            (
                stream,
                scaled_group,
                queries,
                keys_values,
                attended,
                logs,
                mixed,
                middle,
                scaled_ffn_group,
                gate_proj,
                up_proj,
                hidden,
            )
        )
        stream = next_stream
    output = stream.astype(BF16)

    grad = cotangent.astype(F32)
    grads = [None] * LAYERS
    for layer in reversed(range(LAYERS)):
        attn_full, out_full, ffn_full, down_full = full[layer]
        (
            stream_in,
            scaled_group,
            queries,
            keys_values,
            attended,
            logs,
            mixed,
            middle,
            scaled_ffn_group,
            gate_proj,
            up_proj,
            hidden,
        ) = saved[layer]
        down_in = plane_gather(grad.astype(BF16), 2, "normed_gather").reshape(group, D)
        grad_hidden = contract_cols(down_in, down_full)
        sigmoid_gate = jax.nn.sigmoid(gate_proj)
        gate_in = (
            grad_hidden * up_proj * (sigmoid_gate * (1.0 + gate_proj * (1.0 - sigmoid_gate)))
        ).astype(BF16)
        up_in = (grad_hidden * (gate_proj * sigmoid_gate)).astype(BF16)
        gate_up_in = jnp.concatenate([gate_in, up_in], axis=1)
        part = contract_cols(gate_up_in, ffn_full).astype(BF16)
        parts = plane_swap(part.reshape(peers, tok, D), 5, "sum_swap")
        grad_scaled = jnp.sum(parts.astype(F32), axis=0)
        grad_middle = grad + rms_back(middle, grad_scaled)
        proj_in = grad_middle.astype(BF16)
        mixed_grad = contract_cols(proj_in, out_full).astype(BF16)
        mixed_grad = mixed_grad.reshape(tok, peers, cols).transpose(1, 0, 2)
        mixed_grad = plane_swap(mixed_grad, 4, "mixed_swap").reshape(group, cols)

        raw_down = lax.psum_scatter(
            contract_rows(hidden, down_in).astype(BF16), "head", scatter_dimension=0, tiled=True
        )
        raw_ffn = lax.psum_scatter(
            contract_rows(scaled_ffn_group, gate_up_in).astype(BF16),
            "head",
            scatter_dimension=0,
            tiled=True,
        )
        raw_out = lax.psum_scatter(
            contract_rows(mixed, proj_in).astype(BF16),
            ("head", "blk"),
            scatter_dimension=0,
            tiled=True,
        )

        query_in, key_back, value_back = attend_back(
            queries, keys_values, mixed_grad, attended, logs, first_place, low, tile, chunk
        )
        back = jnp.concatenate([key_back, value_back], axis=1).reshape(
            reach + 1, group, 2 * cols
        )
        back = halo_back(back, 6, "halo_back").astype(F32)
        key_value_in = back[0]
        for k in range(1, reach + 1):
            key_value_in = key_value_in + jnp.where(plane + k < planes, back[k], 0.0)
        qkv_in = jnp.concatenate([query_in, key_value_in.astype(BF16)], axis=1)
        raw_attn = lax.psum_scatter(
            contract_rows(scaled_group, qkv_in).astype(BF16),
            "head",
            scatter_dimension=0,
            tiled=True,
        )
        part = contract_cols(qkv_in, attn_full).astype(BF16)
        parts = plane_swap(part.reshape(peers, tok, D), 5, "sum_swap")
        grad_scaled = jnp.sum(parts.astype(F32), axis=0)
        grad = grad_middle + rms_back(stream_in, grad_scaled)
        grads[layer] = (raw_attn, raw_ffn, raw_out, raw_down)

    raw = jnp.stack([jnp.concatenate([g[0], g[1]], axis=1) for g in grads])
    raw = raw.reshape(LAYERS, peers, own_rows, 3 * cols + 2 * hidden_cols).transpose(1, 0, 2, 3)
    raw = plane_swap(raw, 1, "weights_swap").astype(F32)

    def attn_rows_of(which):
        piece = raw[:, :, :, which * cols : (which + 1) * cols]
        return piece.transpose(1, 2, 0, 3).reshape(LAYERS, own_rows, D)

    def ffn_rows_of(which):
        begin = 3 * cols + which * hidden_cols
        piece = raw[:, :, :, begin : begin + hidden_cols]
        piece = piece.reshape(peers, LAYERS, own_rows, planes, strip).transpose(1, 2, 3, 0, 4)
        return piece.reshape(LAYERS, own_rows, peers * hidden_cols)

    raw_query, raw_key, raw_value = (attn_rows_of(which) for which in range(3))
    raw_gate, raw_up = (ffn_rows_of(which) for which in range(2))

    def gain_grad(*pairs):
        return sum(jnp.sum(weight.astype(F32) * raw_part, axis=2) for weight, raw_part in pairs)

    grad_gain_attn = gain_grad((w_query, raw_query), (w_key, raw_key), (w_value, raw_value))
    grad_gain_ffn = gain_grad((w_gate, raw_gate), (w_up, raw_up))
    return (
        output,
        grad,
        grad_gain_attn,
        raw_query * attn_rows,
        raw_key * attn_rows,
        raw_value * attn_rows,
        jnp.stack([g[2] for g in grads]).astype(F32),
        grad_gain_ffn,
        raw_gate * ffn_rows,
        raw_up * ffn_rows,
        jnp.stack([g[3] for g in grads]).astype(F32),
    )


def solution(mesh):
    rows = P(("head", "blk"), None)
    vector = P(None, ("head", "blk"))
    matrix = P(None, ("head", "blk"), None)
    return jax.shard_map(
        local,
        mesh=mesh,
        in_specs=(
            rows,
            vector,
            matrix,
            matrix,
            matrix,
            matrix,
            vector,
            matrix,
            matrix,
            matrix,
            P(),
            rows,
        ),
        out_specs=(
            rows,
            rows,
            vector,
            matrix,
            matrix,
            matrix,
            matrix,
            vector,
            matrix,
            matrix,
            matrix,
        ),
        check_vma=False,
    )
```

```python
import functools
import math
import types

import jax
import jax.numpy as jnp
from jax import lax
from jax.experimental import pallas as pl
from jax.experimental.pallas import tpu as pltpu
from jax.sharding import PartitionSpec as P

D = 1024
HD = 64
HEADS = D // HD
LAYERS = 2
EPSILON = 1e-05
MASKED = -1e30
MESH = pl.DeviceIdType.MESH
F32 = jnp.float32
BF16 = jnp.bfloat16
ANY = pl.BlockSpec(memory_space=pl.ANY)


def greet_blk(count):
    me = lax.axis_index("blk")
    barrier = pltpu.get_barrier_semaphore()
    for step in range(1, count):
        pl.semaphore_signal(
            barrier,
            inc=1,
            device_id={"blk": lax.rem(me + step, count)},
            device_id_type=MESH,
        )
    pl.semaphore_wait(barrier, count - 1)
    return me


def plane_gather_kernel(count, x_ref, o_ref, send_sem, recv_sem, local_sem):
    me = greet_blk(count)
    copies = []
    for step in range(1, count):
        copy = pltpu.make_async_remote_copy(
            src_ref=x_ref,
            dst_ref=o_ref.at[me],
            send_sem=send_sem.at[step - 1],
            recv_sem=recv_sem.at[step - 1],
            device_id={"blk": lax.rem(me + step, count)},
            device_id_type=MESH,
        )
        copy.start()
        copies.append(copy)
    own = pltpu.make_async_copy(x_ref, o_ref.at[me], local_sem)
    own.start()
    own.wait()
    for copy in copies:
        copy.wait()


def plane_swap_kernel(count, x_ref, o_ref, send_sem, recv_sem, local_sem):
    me = greet_blk(count)
    copies = []
    for step in range(1, count):
        peer = lax.rem(me + step, count)
        copy = pltpu.make_async_remote_copy(
            src_ref=x_ref.at[peer],
            dst_ref=o_ref.at[me],
            send_sem=send_sem.at[step - 1],
            recv_sem=recv_sem.at[step - 1],
            device_id={"blk": peer},
            device_id_type=MESH,
        )
        copy.start()
        copies.append(copy)
    own = pltpu.make_async_copy(x_ref.at[me], o_ref.at[me], local_sem)
    own.start()
    own.wait()
    for copy in copies:
        copy.wait()


def plane_call(kernel, x, out_shape, collective_id, name):
    count = lax.axis_size("blk")
    return pl.pallas_call(
        functools.partial(kernel, count),
        out_shape=jax.ShapeDtypeStruct(out_shape, x.dtype),
        in_specs=[ANY],
        out_specs=ANY,
        scratch_shapes=[
            pltpu.SemaphoreType.DMA((count - 1,)),
            pltpu.SemaphoreType.DMA((count - 1,)),
            pltpu.SemaphoreType.DMA,
        ],
        compiler_params=pltpu.CompilerParams(collective_id=collective_id, has_side_effects=True),
        cost_estimate=pl.CostEstimate(flops=0, bytes_accessed=20_000_000, transcendentals=0),
        name=name,
    )(x)


def plane_gather(x, collective_id, name):
    return plane_call(
        plane_gather_kernel, x, (lax.axis_size("blk"),) + x.shape, collective_id, name
    )


def plane_swap(x, collective_id, name):
    return plane_call(plane_swap_kernel, x, x.shape, collective_id, name)


def halo_kernel(count, reach, x_ref, o_ref, send_sem, recv_sem, local_sem):
    me = lax.axis_index("head")
    barrier = pltpu.get_barrier_semaphore()
    for k in range(1, reach + 1):

        @pl.when(me - k >= 0)
        def _(k=k):
            pl.semaphore_signal(barrier, inc=1, device_id={"head": me - k}, device_id_type=MESH)

    for k in range(1, reach + 1):

        @pl.when((me + k == count - 1) if k < reach else (me + k < count))
        def _(k=k):
            pl.semaphore_wait(barrier, k)

    def copy_to(k):
        return pltpu.make_async_remote_copy(
            src_ref=x_ref,
            dst_ref=o_ref.at[reach - k],
            send_sem=send_sem.at[k - 1],
            recv_sem=recv_sem.at[k - 1],
            device_id={"head": me + k},
            device_id_type=MESH,
        )

    for k in range(1, reach + 1):

        @pl.when(me + k < count)
        def _(k=k):
            copy_to(k).start()

    own = pltpu.make_async_copy(x_ref, o_ref.at[reach], local_sem)
    own.start()
    own.wait()
    for k in range(1, reach + 1):

        @pl.when(me + k < count)
        def _(k=k):
            copy_to(k).wait_send()

        @pl.when(me - k >= 0)
        def _(k=k):
            copy_to(k).wait_recv()


def halo_forward(x, reach, collective_id, name):
    count = lax.axis_size("head")
    return pl.pallas_call(
        functools.partial(halo_kernel, count, reach),
        out_shape=jax.ShapeDtypeStruct((reach + 1,) + x.shape, x.dtype),
        in_specs=[ANY],
        out_specs=ANY,
        scratch_shapes=[
            pltpu.SemaphoreType.DMA((reach,)),
            pltpu.SemaphoreType.DMA((reach,)),
            pltpu.SemaphoreType.DMA,
        ],
        compiler_params=pltpu.CompilerParams(collective_id=collective_id, has_side_effects=True),
        cost_estimate=pl.CostEstimate(flops=0, bytes_accessed=20_000_000, transcendentals=0),
        name=name,
    )(x)


def halo_back_kernel(count, reach, x_ref, o_ref, send_sem, recv_sem, local_sem):
    me = lax.axis_index("head")
    barrier = pltpu.get_barrier_semaphore()
    for k in range(1, reach + 1):

        @pl.when(me + k < count)
        def _(k=k):
            pl.semaphore_signal(barrier, inc=1, device_id={"head": me + k}, device_id_type=MESH)

    for k in range(1, reach + 1):

        @pl.when((me == k) if k < reach else (me >= k))
        def _(k=k):
            pl.semaphore_wait(barrier, k)

    def copy_to(k):
        return pltpu.make_async_remote_copy(
            src_ref=x_ref.at[reach - k],
            dst_ref=o_ref.at[k],
            send_sem=send_sem.at[k - 1],
            recv_sem=recv_sem.at[k - 1],
            device_id={"head": me - k},
            device_id_type=MESH,
        )

    for k in range(1, reach + 1):

        @pl.when(me - k >= 0)
        def _(k=k):
            copy_to(k).start()

    own = pltpu.make_async_copy(x_ref.at[reach], o_ref.at[0], local_sem)
    own.start()
    own.wait()
    for k in range(1, reach + 1):

        @pl.when(me - k >= 0)
        def _(k=k):
            copy_to(k).wait_send()

        @pl.when(me + k < count)
        def _(k=k):
            copy_to(k).wait_recv()


def halo_back(x, collective_id, name):
    count = lax.axis_size("head")
    reach = x.shape[0] - 1
    return pl.pallas_call(
        functools.partial(halo_back_kernel, count, reach),
        out_shape=jax.ShapeDtypeStruct(x.shape, x.dtype),
        in_specs=[ANY],
        out_specs=ANY,
        scratch_shapes=[
            pltpu.SemaphoreType.DMA((reach,)),
            pltpu.SemaphoreType.DMA((reach,)),
            pltpu.SemaphoreType.DMA,
        ],
        compiler_params=pltpu.CompilerParams(collective_id=collective_id, has_side_effects=True),
        cost_estimate=pl.CostEstimate(flops=0, bytes_accessed=20_000_000, transcendentals=0),
        name=name,
    )(x)


def launch(body, name, inputs, outputs, scratch, collective_id, flops=0):
    names = list(inputs) + list(outputs)
    flat = []
    for value in scratch.values():
        flat.extend(value if isinstance(value, list) else [value])

    def kernel(*refs):
        named = dict(zip(names, refs))
        rest = list(refs[len(names) :])
        for name, value in scratch.items():
            if isinstance(value, list):
                named[name], rest = rest[: len(value)], rest[len(value) :]
            else:
                named[name], rest = rest[0], rest[1:]
        body(types.SimpleNamespace(**named))

    results = pl.pallas_call(
        kernel,
        out_shape=[jax.ShapeDtypeStruct(shape, dtype) for shape, dtype, _ in outputs.values()],
        in_specs=[spec for _, spec in inputs.values()],
        out_specs=[spec for _, _, spec in outputs.values()],
        scratch_shapes=flat,
        compiler_params=pltpu.CompilerParams(
            collective_id=collective_id, has_side_effects=True, vmem_limit_bytes=56 << 20
        ),
        cost_estimate=pl.CostEstimate(
            flops=flops, bytes_accessed=200_000_000, transcendentals=0
        ),
        name=name,
    )(*[array for array, _ in inputs.values()])
    return dict(zip(outputs, results))


VMEM = pl.BlockSpec(memory_space=pltpu.VMEM)


def dma(*shape):
    return pltpu.SemaphoreType.DMA(shape)


def remote(src, dst, send_sem, recv_sem, **place):
    return pltpu.make_async_remote_copy(
        src_ref=src,
        dst_ref=dst,
        send_sem=send_sem,
        recv_sem=recv_sem,
        device_id=place,
        device_id_type=MESH,
    )


class Place:
    def __init__(self):
        self.peers = lax.axis_size("blk")
        self.planes = lax.axis_size("head")
        self.depth = self.planes // 2
        self.peer = lax.axis_index("blk")
        self.plane = lax.axis_index("head")
        self.z = lax.div(self.plane, 2)
        self.core = lax.rem(self.plane, 2)
        self.sibling = self.plane + 1 - 2 * self.core

    def peer_after(self, step):
        return lax.rem(self.peer + step, self.peers)

    def peer_before(self, step):
        return lax.rem(self.peer + self.peers - step, self.peers)

    def z_after(self, step):
        return lax.rem(self.z + step, self.depth)

    def z_before(self, step):
        return lax.rem(self.z + self.depth - step, self.depth)

    def greet(self):
        barrier = pltpu.get_barrier_semaphore()
        for step in range(1, self.peers):
            pl.semaphore_signal(
                barrier, inc=1, device_id={"blk": self.peer_after(step)}, device_id_type=MESH
            )
        for step in range(1, self.depth):
            pl.semaphore_signal(
                barrier,
                inc=1,
                device_id={"head": 2 * self.z_after(step) + self.core},
                device_id_type=MESH,
            )
        pl.semaphore_signal(barrier, inc=1, device_id={"head": self.sibling}, device_id_type=MESH)
        pl.semaphore_wait(barrier, self.peers - 1 + self.depth - 1 + 1)


class PlaneGather:
    def __init__(self, place, src, dst, send, recv):
        self.place, self.src, self.dst, self.send, self.recv = place, src, dst, send, recv

    def start(self):
        for step in range(1, self.place.peers):
            remote(
                self.src,
                self.dst.at[self.place.peer],
                self.send.at[step - 1],
                self.recv.at[step - 1],
                blk=self.place.peer_after(step),
            ).start()

    def await_step(self, step):
        @pl.when(step > 0)
        def _():
            index = jnp.maximum(step - 1, 0)
            source = self.place.peer_before(step)
            remote(
                self.src,
                self.dst.at[source],
                self.send.at[index],
                self.recv.at[index],
                blk=source,
            ).wait_recv()

    def finish(self):
        for step in range(1, self.place.peers):
            remote(
                self.src,
                self.dst.at[self.place.peer],
                self.send.at[step - 1],
                self.recv.at[step - 1],
                blk=self.place.peer_after(step),
            ).wait_send()


class PlaneSum:
    def __init__(self, place, src, dst, send, recv):
        self.place, self.src, self.dst, self.send, self.recv = place, src, dst, send, recv

    def copy_to(self, peer):
        index = jnp.maximum(
            lax.rem(self.place.peer + self.place.peers - peer, self.place.peers) - 1, 0
        )
        return remote(
            self.src.at[peer],
            self.dst.at[self.place.peer],
            self.send.at[index],
            self.recv.at[index],
            blk=peer,
        )

    def send_to(self, peer):
        @pl.when(peer != self.place.peer)
        def _():
            self.copy_to(peer).start()

    def total(self):
        total = self.src[self.place.peer].astype(F32)
        for step in range(1, self.place.peers):
            source = self.place.peer_after(step)
            remote(
                self.src.at[source],
                self.dst.at[source],
                self.send.at[step - 1],
                self.recv.at[step - 1],
                blk=source,
            ).wait_recv()
            total = total + self.dst[source].astype(F32)
        return total

    def finish(self):
        for step in range(1, self.place.peers):
            self.copy_to(self.place.peer_before(step)).wait_send()


class HeadGather:
    def __init__(self, place, src, full, sems):
        self.place, self.src, self.full = place, src, full
        self.z_send, self.z_recv, self.s_send, self.s_recv, self.local = sems

    @staticmethod
    def sems(depth):
        return [dma(depth - 1), dma(depth - 1), dma(depth), dma(depth), dma()]

    def slot(self, z, core):
        rows = self.src.shape[0]
        return self.full.at[pl.ds(pl.multiple_of((2 * z + core) * rows, rows), rows)]

    def z_copy(self, step):
        return remote(
            self.src,
            self.slot(self.place.z, self.place.core),
            self.z_send.at[step - 1],
            self.z_recv.at[step - 1],
            head=2 * self.place.z_after(step) + self.place.core,
        )

    def s_copy(self, step, core):
        z = self.place.z_before(step)
        where = self.slot(z, core)
        return remote(
            self.src if step == 0 else where,
            where,
            self.s_send.at[step],
            self.s_recv.at[step],
            head=self.place.sibling,
        )

    def own_copy(self):
        return pltpu.make_async_copy(
            self.src, self.slot(self.place.z, self.place.core), self.local
        )

    def start(self):
        for step in range(1, self.place.depth):
            self.z_copy(step).start()
        self.s_copy(0, self.place.core).start()
        self.own_copy().start()

    def forward(self):
        for step in range(1, self.place.depth):
            where = self.slot(self.place.z_before(step), self.place.core)
            remote(
                self.src,
                where,
                self.z_send.at[step - 1],
                self.z_recv.at[step - 1],
                head=self.place.sibling,
            ).wait_recv()
            self.s_copy(step, self.place.core).start()

    def arrive(self):
        self.own_copy().wait()
        for step in range(self.place.depth):
            self.s_copy(step, 1 - self.place.core).wait_recv()

    def finish(self):
        for step in range(1, self.place.depth):
            self.z_copy(step).wait_send()
        for step in range(self.place.depth):
            self.s_copy(step, self.place.core).wait_send()


class OutGather:
    def __init__(self, place, src, mine, full, sems):
        self.place, self.src, self.mine, self.full = place, src, mine, full
        (
            self.p_send,
            self.p_recv,
            self.z_send,
            self.z_recv,
            self.s_send,
            self.s_recv,
            self.local,
        ) = sems

    @staticmethod
    def sems(peers, depth):
        return [dma(peers - 1), dma(peers - 1), dma(depth - 1), dma(), dma(), dma(), dma()]

    def piece(self, peer):
        rows = self.src.shape[0]
        return self.mine.at[pl.ds(pl.multiple_of(peer * rows, rows), rows)]

    def half(self, core):
        rows = self.mine.shape[0]
        return self.full.at[pl.ds(pl.multiple_of(core * rows, rows), rows)]

    def home(self):
        return self.place.peer == self.place.z

    def step_to_home(self):
        return lax.rem(self.place.z + self.place.peers - self.place.peer, self.place.peers)

    def p_copy(self):
        index = jnp.maximum(self.step_to_home() - 1, 0)
        return remote(
            self.src,
            self.piece(self.place.peer),
            self.p_send.at[index],
            self.p_recv.at[index],
            blk=self.place.z,
        )

    def own_copy(self):
        return pltpu.make_async_copy(self.src, self.piece(self.place.peer), self.local)

    def start(self):
        @pl.when(self.home())
        def _():
            self.own_copy().start()

        @pl.when(jnp.logical_not(self.home()))
        def _():
            self.p_copy().start()

    def z_copy(self, step):
        return remote(
            self.mine,
            self.half(self.place.core),
            self.z_send.at[step - 1],
            self.z_recv,
            head=2 * self.place.z_after(step) + self.place.core,
        )

    def s_copy(self, core):
        return remote(
            self.half(core), self.half(core), self.s_send, self.s_recv, head=self.place.sibling
        )

    def spread(self):
        @pl.when(self.home())
        def _():
            self.own_copy().wait()
            for step in range(1, self.place.peers):
                source = self.place.peer_before(step)
                remote(
                    self.src,
                    self.piece(source),
                    self.p_send.at[step - 1],
                    self.p_recv.at[step - 1],
                    blk=source,
                ).wait_recv()
            for step in range(1, self.place.depth):
                self.z_copy(step).start()
            pltpu.make_async_copy(self.mine, self.half(self.place.core), self.local).start()

    def forward(self):
        @pl.when(self.home())
        def _():
            pltpu.make_async_copy(self.mine, self.half(self.place.core), self.local).wait()

        @pl.when(jnp.logical_not(self.home()))
        def _():
            remote(
                self.mine,
                self.half(self.place.core),
                self.z_send.at[0],
                self.z_recv,
                head=self.place.sibling,
            ).wait_recv()

        self.s_copy(self.place.core).start()

    def arrive(self):
        self.s_copy(1 - self.place.core).wait_recv()

    def finish(self):
        @pl.when(self.home())
        def _():
            for step in range(1, self.place.depth):
                self.z_copy(step).wait_send()

        @pl.when(jnp.logical_not(self.home()))
        def _():
            self.p_copy().wait_send()

        self.s_copy(self.place.core).wait_send()


class WeightSwap:
    def __init__(self, place, src, layer, mine, sems):
        self.place, self.src, self.layer, self.mine = place, src, layer, mine
        self.send, self.recv, self.local = sems

    @staticmethod
    def sems(peers):
        return [dma(peers - 1), dma(peers - 1), dma()]

    def piece(self, peer):
        rows = self.src.shape[2]
        return self.mine.at[pl.ds(pl.multiple_of(peer * rows, rows), rows)]

    def copy(self, step):
        target = self.place.peer_after(step)
        return remote(
            self.src.at[target, self.layer],
            self.piece(self.place.peer),
            self.send.at[step - 1],
            self.recv.at[step - 1],
            blk=target,
        )

    def own_copy(self):
        return pltpu.make_async_copy(
            self.src.at[self.place.peer, self.layer], self.piece(self.place.peer), self.local
        )

    def start(self):
        for step in range(1, self.place.peers):
            self.copy(step).start()
        self.own_copy().start()

    def arrive(self):
        self.own_copy().wait()
        for step in range(1, self.place.peers):
            source = self.place.peer_before(step)
            remote(
                self.src.at[source, self.layer],
                self.piece(source),
                self.send.at[step - 1],
                self.recv.at[step - 1],
                blk=source,
            ).wait_recv()

    def finish(self):
        for step in range(1, self.place.peers):
            self.copy(step).wait_send()


class Halo:
    def __init__(self, place, keys, reach, sems):
        self.place, self.keys, self.reach = place, keys, reach
        self.rows = keys.shape[0] // (reach + 1)
        self.z_send, self.z_recv, self.s_send, self.s_recv = sems

    def block(self, offset):
        return self.keys.at[pl.ds((self.reach - offset) * self.rows, self.rows)]

    @staticmethod
    def sems(reach):
        return [dma(reach // 2), dma(reach // 2), dma(reach // 2), dma(reach // 2)]

    def z_copy(self, hop):
        return remote(
            self.block(0),
            self.block(2 * hop),
            self.z_send.at[hop - 1],
            self.z_recv.at[hop - 1],
            head=self.place.plane + 2 * hop,
        )

    def sends(self, hop):
        return self.place.z + hop < self.place.depth

    def receives(self, hop):
        return self.place.z - hop >= 0

    def start(self):
        for hop in range(1, self.reach // 2 + 1):

            @pl.when(self.sends(hop))
            def _(hop=hop):
                self.z_copy(hop).start()


    def hand(self, i):
        def copy(offset):
            return remote(
                self.block(offset),
                self.block(2 * i - 1),
                self.s_send.at[i - 1],
                self.s_recv.at[i - 1],
                head=self.place.sibling,
            )

        return copy

    def hand_ready(self, i):
        return (
            (self.place.core == 1) & self.receives(i),
            (self.place.core == 0) & self.receives(i - 1),
        )

    def relay(self):
        for i in range(1, self.reach // 2 + 1):
            from_one, from_zero = self.hand_ready(i)
            if i == 1:

                @pl.when(from_zero)
                def _(i=i):
                    self.hand(i)(2 * i - 2).start()

            @pl.when(self.receives(i))
            def _(i=i):
                remote(
                    self.block(0),
                    self.block(2 * i),
                    self.z_send.at[i - 1],
                    self.z_recv.at[i - 1],
                    head=self.place.sibling,
                ).wait_recv()

            @pl.when(from_one)
            def _(i=i):
                self.hand(i)(2 * i).start()

            if i < self.reach // 2:

                @pl.when(self.hand_ready(i + 1)[1])
                def _(i=i):
                    self.hand(i + 1)(2 * i).start()

    def arrive(self):
        for i in range(1, self.reach // 2 + 1):

            @pl.when(self.place.z - i + self.place.core >= 0)
            def _(i=i):
                self.hand(i)(0).wait_recv()

    def finish(self):
        for hop in range(1, self.reach // 2 + 1):

            @pl.when(self.sends(hop))
            def _(hop=hop):
                self.z_copy(hop).wait_send()

            from_one, from_zero = self.hand_ready(hop)

            @pl.when(from_one)
            def _(hop=hop):
                self.hand(hop)(2 * hop).wait_send()

            @pl.when(from_zero)
            def _(hop=hop):
                self.hand(hop)(2 * hop - 2).wait_send()


def columns(total, most=256):
    width = math.gcd(total, most)
    return total // width, width


def by_columns(total, step, most=256):
    count, width = columns(total, most)

    def body(index, carry):
        step(pl.ds(pl.multiple_of(index * width, width), width))
        return carry

    lax.fori_loop(0, count, body, 0)


def attend_tile(sizes, place, tile_index, q_ref, keys_ref, first_ref, mixed_ref, attended_ref, log_ref):
    tile, chunk, cols, group, lead = sizes.tile, sizes.chunk, sizes.cols, sizes.group, sizes.lead
    row = pl.multiple_of(tile_index * tile, tile)
    rows = pl.ds(row, tile)
    first = first_ref[:, rows]
    last = lead + row + lax.broadcasted_iota(jnp.int32, (1, tile), 1)
    lane = lax.broadcasted_iota(jnp.int32, (tile, 2 * HD), 1)
    lowest = jnp.maximum(lead + row - (sizes.doc_max - 1), lead - place.plane * group)
    begin = lax.div(jnp.maximum(lowest, 0), chunk)
    end = lax.div(lead + row + tile + chunk - 1, chunk)
    for pair in range(cols // (2 * HD)):
        lanes = slice(pair * 2 * HD, (pair + 1) * 2 * HD)
        value_lanes = slice(cols + pair * 2 * HD, cols + (pair + 1) * 2 * HD)
        queries = q_ref[rows, lanes] * jnp.asarray(HD ** (-0.5), BF16)
        zero = jnp.zeros_like(queries)
        halves = [jnp.where(lane < HD, queries, zero), jnp.where(lane >= HD, queries, zero)]

        def step(block, state, lanes=lanes, value_lanes=value_lanes, halves=halves):
            offset = pl.multiple_of(block * chunk, chunk)
            keys = keys_ref[pl.ds(offset, chunk), lanes]
            values = keys_ref[pl.ds(offset, chunk), value_lanes]
            spot = offset + lax.broadcasted_iota(jnp.int32, (chunk, tile), 0)
            allowed = (spot >= first) & (spot <= last)
            out = []
            for half, (top, total, accum) in zip(halves, state):
                scores = jnp.where(allowed, dot_nt(keys, half), MASKED)
                new_top = jnp.maximum(top, jnp.max(scores, axis=0, keepdims=True))
                factor = jnp.exp(top - new_top)
                weights = jnp.exp(scores - new_top)
                total = total * factor + jnp.sum(weights, axis=0, keepdims=True)
                accum = accum * factor + dot_tn(values, weights.astype(BF16))
                out.append((new_top, total, accum))
            return tuple(out)

        start = (
            jnp.full((1, tile), MASKED, F32),
            jnp.zeros((1, tile), F32),
            jnp.zeros((2 * HD, tile), F32),
        )
        state = lax.fori_loop(begin, end, step, (start, start))
        parts = []
        for which, (top, total, accum) in enumerate(state):
            log_ref[2 * pair + which : 2 * pair + which + 1, rows] = top + jnp.log(total)
            parts.append(accum[which * HD : (which + 1) * HD] / total)
        attended = jnp.transpose(jnp.concatenate(parts, axis=0))
        attended_ref[rows, lanes] = attended
        mixed_ref[rows, lanes] = attended.astype(BF16)


def forward_body(sizes, layer, refs):
    place = Place()
    tok, cols, group, hidden = sizes.tok, sizes.cols, sizes.group, sizes.hidden
    tile = sizes.tile
    place.greet()
    loads = refs.load_sem
    gathers = []
    swaps = []
    if layer == 0:
        swap_q = [
            WeightSwap(place, refs.pack_q, l, refs.mine_q.at[l], getattr(refs, f"swap_q{l}"))
            for l in range(LAYERS)
        ]
        swap_g = [
            WeightSwap(place, refs.pack_g, l, refs.mine_g.at[l], getattr(refs, f"swap_g{l}"))
            for l in range(LAYERS)
        ]
        out_w = [
            OutGather(
                place,
                refs.w_out.at[l],
                refs.mine_o.at[l],
                getattr(refs, f"out_full{l}"),
                getattr(refs, f"out_sem{l}"),
            )
            for l in range(LAYERS)
        ]
        gather_q = [
            HeadGather(
                place, refs.mine_q.at[l], getattr(refs, f"q_full{l}"), getattr(refs, f"gq_sem{l}")
            )
            for l in range(LAYERS)
        ]
        gather_g = HeadGather(place, refs.mine_g.at[0], refs.g_full, refs.gg_sem)
        swap_q[0].start()
    else:
        gather_g = HeadGather(place, refs.mine_g.at[layer], refs.g_full, refs.gg_sem)
    gather_d = HeadGather(place, refs.w_down.at[layer], refs.d_full, refs.gd_sem)

    stream = refs.stream[...]
    scaled = (stream * inverse_rms(stream)).astype(BF16)
    refs.scaled[place.peer] = scaled
    ag1 = PlaneGather(place, refs.scaled.at[place.peer], refs.scaled, refs.ag1_s, refs.ag1_r)
    ag1.start()
    if layer == 0:
        out_w[0].start()
        swap_g[0].start()
        swap_q[1].start()
        out_w[1].start()
        swap_g[1].start()
        swap_q[0].arrive()
        gather_q[0].start()
        out_w[0].spread()
        swap_g[0].arrive()
        gather_g.start()
        gather_d.start()
        gather_q[0].forward()
        gather_q[0].arrive()
    else:
        gather_g.start()
        gather_d.start()
    q_load = pltpu.make_async_copy(refs.q_full0 if layer == 0 else refs.q_full, refs.wq, loads.at[0])
    q_load.start()
    q_load.wait()

    def project(step, carry):
        ag1.await_step(step)
        peer = place.peer_before(step)
        rows = pl.ds(pl.multiple_of(peer * tok, tok), tok)
        x = refs.scaled[peer]

        for part in range(3):

            def block(where, part=part):
                offset = where.start
                weight = refs.wq[:, pl.ds(pl.multiple_of(part * cols + offset, where.size), where.size)]
                value = dot_nn(x, weight).astype(BF16)
                if part == 0:
                    refs.queries[rows, where] = value
                else:
                    there = pl.ds(pl.multiple_of((part - 1) * cols + offset, where.size), where.size)
                    refs.keys[pl.ds(pl.multiple_of(sizes.lead + peer * tok, tok), tok), there] = value

            by_columns(cols, block)
        return carry

    lax.fori_loop(0, place.peers, project, 0)
    halo = Halo(place, refs.keys, sizes.reach, refs.halo_sem)
    halo.start()
    halo.relay()
    halo.arrive()

    if layer == 0:
        out_w[0].forward()
        out_w[0].arrive()
    o_load = pltpu.make_async_copy(
        refs.out_full0 if layer == 0 else refs.o_full, refs.wo, loads.at[1]
    )
    o_load.start()
    o_load.wait()

    sum1 = PlaneSum(place, refs.part1, refs.sum1, refs.rs1_s, refs.rs1_r)

    def attend_step(index, carry):
        attend_tile(
            sizes,
            place,
            index,
            refs.queries,
            refs.keys,
            refs.first,
            refs.mixed,
            refs.attended,
            refs.logs,
        )
        for k in range(tile // tok):
            peer = index * (tile // tok) + k
            x = refs.mixed[pl.ds(pl.multiple_of(peer * tok, tok), tok), :]

            def block(where, x=x, peer=peer):
                refs.part1[peer, :, where] = dot_nn(x, refs.wo[:, where]).astype(BF16)

            by_columns(D, block)
            sum1.send_to(peer)
        return carry

    lax.fori_loop(0, group // tile, attend_step, 0)

    gather_g.forward()
    gather_d.forward()
    gather_g.arrive()
    gather_d.arrive()
    g_load = pltpu.make_async_copy(refs.g_full, refs.wg, loads.at[2])
    d_load = pltpu.make_async_copy(refs.d_full, refs.wd, loads.at[3])
    g_load.start()
    d_load.start()
    if layer == 0:
        swap_q[1].arrive()
        gather_q[1].start()
        out_w[1].spread()
        swap_g[1].arrive()

    middle = stream + sum1.total()
    refs.middle[...] = middle
    refs.scaled_ffn[place.peer] = (middle * inverse_rms(middle)).astype(BF16)
    ag2 = PlaneGather(
        place, refs.scaled_ffn.at[place.peer], refs.scaled_ffn, refs.ag2_s, refs.ag2_r
    )
    ag2.start()
    g_load.wait()
    d_load.wait()
    sum2 = PlaneSum(place, refs.part2, refs.sum2, refs.rs2_s, refs.rs2_r)

    def feed(step, carry):
        ag2.await_step(step)
        peer = place.peer_before(step)
        rows = pl.ds(pl.multiple_of(peer * tok, tok), tok)
        x = refs.scaled_ffn[peer]

        def block(where):
            there = pl.ds(pl.multiple_of(hidden + where.start, where.size), where.size)
            gate = dot_nn(x, refs.wg[:, where])
            up = dot_nn(x, refs.wg[:, there])
            refs.gate_up[rows, where] = gate
            refs.gate_up[rows, there] = up
            refs.hidden[rows, where] = (gate / (1.0 + jnp.exp(-gate)) * up).astype(BF16)

        by_columns(hidden, block)
        low = refs.hidden[rows, :]

        def down(where):
            refs.part2[peer, :, where] = dot_nn(low, refs.wd[:, where]).astype(BF16)

        by_columns(D, down)
        sum2.send_to(peer)
        return carry

    lax.fori_loop(0, place.peers, feed, 0)
    if layer == 0:
        gather_q[1].forward()
        out_w[1].forward()
    refs.next[...] = middle + sum2.total()
    if layer == 0:
        gather_q[1].arrive()
        out_w[1].arrive()
        for item in swap_q + swap_g + gather_q + out_w:
            item.finish()
    for item in (ag1, ag2, sum1, sum2, gather_g, gather_d, halo):
        item.finish()


def forward_layer(sizes, layer, stream, first_row, weights, collective_id):
    peers, planes, depth = sizes.peers, sizes.planes, sizes.planes // 2
    tok, cols, group, hidden, reach = sizes.tok, sizes.cols, sizes.group, sizes.hidden, sizes.reach
    inputs = {"stream": (stream, VMEM), "first": (first_row, VMEM), "w_down": (weights["w_down"], ANY)}
    outputs = {
        "next": ((tok, D), F32, VMEM),
        "middle": ((tok, D), F32, VMEM),
        "scaled": ((peers, tok, D), BF16, VMEM),
        "scaled_ffn": ((peers, tok, D), BF16, VMEM),
        "queries": ((group, cols), BF16, VMEM),
        "keys": (((reach + 1) * group, 2 * cols), BF16, VMEM),
        "mixed": ((group, cols), BF16, VMEM),
        "attended": ((group, cols), F32, VMEM),
        "logs": ((cols // HD, group), F32, VMEM),
        "gate_up": ((group, 2 * hidden), F32, VMEM),
        "hidden": ((group, hidden), BF16, VMEM),
        "g_full": ((D, 2 * hidden), BF16, ANY),
        "d_full": ((hidden, D), BF16, ANY),
    }
    scratch = {
        "wq": pltpu.VMEM((D, 3 * cols), BF16),
        "wo": pltpu.VMEM((cols, D), BF16),
        "wg": pltpu.VMEM((D, 2 * hidden), BF16),
        "wd": pltpu.VMEM((hidden, D), BF16),
        "part1": pltpu.VMEM((peers, tok, D), BF16),
        "sum1": pltpu.VMEM((peers, tok, D), BF16),
        "part2": pltpu.VMEM((peers, tok, D), BF16),
        "sum2": pltpu.VMEM((peers, tok, D), BF16),
        "load_sem": dma(4),
        "halo_sem": Halo.sems(reach),
        "gg_sem": HeadGather.sems(depth),
        "gd_sem": HeadGather.sems(depth),
    }
    for name in ("ag1_s", "ag1_r", "ag2_s", "ag2_r", "rs1_s", "rs1_r", "rs2_s", "rs2_r"):
        scratch[name] = dma(peers - 1)
    if layer == 0:
        rows = peers * sizes.own_rows
        inputs["pack_q"] = (weights["pack_q"], ANY)
        inputs["pack_g"] = (weights["pack_g"], ANY)
        inputs["w_out"] = (weights["w_out"], ANY)
        outputs["mine_q"] = ((LAYERS, rows, 3 * cols), BF16, ANY)
        outputs["mine_g"] = ((LAYERS, rows, 2 * hidden), BF16, ANY)
        outputs["mine_o"] = ((LAYERS, rows, D), BF16, ANY)
        for l in range(LAYERS):
            outputs[f"q_full{l}"] = ((D, 3 * cols), BF16, ANY)
            outputs[f"out_full{l}"] = ((cols, D), BF16, ANY)
            scratch[f"swap_q{l}"] = WeightSwap.sems(peers)
            scratch[f"swap_g{l}"] = WeightSwap.sems(peers)
            scratch[f"out_sem{l}"] = OutGather.sems(peers, depth)
            scratch[f"gq_sem{l}"] = HeadGather.sems(depth)
    else:
        inputs["mine_g"] = (weights["mine_g"], ANY)
        inputs["q_full"] = (weights["q_full"], ANY)
        inputs["o_full"] = (weights["o_full"], ANY)
    return launch(
        functools.partial(forward_body, sizes, layer),
        f"forward{layer}",
        inputs,
        outputs,
        scratch,
        collective_id,
        flops=group * D * (4 * cols + 3 * hidden) * 2,
    )


def dot_nt(left, right):
    return lax.dot_general(left, right, (((1,), (1,)), ((), ())), preferred_element_type=F32)


def dot_nn(left, right):
    return lax.dot_general(left, right, (((1,), (0,)), ((), ())), preferred_element_type=F32)


def dot_tn(left, right):
    return lax.dot_general(left, right, (((0,), (0,)), ((), ())), preferred_element_type=F32)


def head_masks(rows):
    lane = lax.broadcasted_iota(jnp.int32, (rows, 2 * HD), 1)
    return (lane < HD, lane >= HD)


def attend_kernel(tile, chunk, lead, low_ref, q_ref, k_ref, v_ref, start_ref, o_ref, mixed_ref, log_ref):
    index = pl.program_id(1)
    queries = q_ref[...] * jnp.asarray(HD ** (-0.5), BF16)
    masks = head_masks(tile)
    halves = [jnp.where(mask, queries, jnp.zeros_like(queries)) for mask in masks]
    first = start_ref[...]
    last = lead + index * tile + lax.broadcasted_iota(jnp.int32, (tile, 1), 0)

    def step(block, state):
        offset = pl.multiple_of(block * chunk, chunk)
        keys = k_ref[pl.ds(offset, chunk), :]
        values = v_ref[pl.ds(offset, chunk), :]
        place = offset + lax.broadcasted_iota(jnp.int32, (tile, chunk), 1)
        allowed = (place >= first) & (place <= last)
        out = []
        for half, (top, total, accum) in zip(halves, state):
            scores = jnp.where(allowed, dot_nt(half, keys), MASKED)
            new_top = jnp.maximum(top, jnp.max(scores, axis=1, keepdims=True))
            factor = jnp.exp(top - new_top)
            weights = jnp.where(allowed, jnp.exp(scores - new_top), 0.0)
            total = total * factor + jnp.sum(weights, axis=1, keepdims=True)
            accum = accum * factor + dot_nn(weights.astype(BF16), values)
            out.append((new_top, total, accum))
        return tuple(out)

    start = (
        jnp.full((tile, 1), MASKED, F32),
        jnp.zeros((tile, 1), F32),
        jnp.zeros((tile, 2 * HD), F32),
    )
    stop = (lead + (index + 1) * tile + chunk - 1) // chunk
    state = lax.fori_loop(low_ref[index], stop, step, (start, start))
    attended = [accum / total for _, total, accum in state]
    logs = [top + jnp.log(total) for top, total, _ in state]
    result = jnp.where(masks[0], attended[0], attended[1])
    o_ref[...] = result
    mixed_ref[...] = result.astype(BF16)
    log_ref[...] = jnp.where(masks[0], logs[0], logs[1])


def attend(queries, keys_values, first_place, low, tile, chunk):
    rows, cols = queries.shape
    span = keys_values.shape[0]
    pairs = cols // (2 * HD)
    tiles = rows // tile
    query_spec = pl.BlockSpec((tile, 2 * HD), lambda p, i, low: (i, p))
    return pl.pallas_call(
        functools.partial(attend_kernel, tile, chunk, span - rows),
        grid_spec=pltpu.PrefetchScalarGridSpec(
            num_scalar_prefetch=1,
            grid=(pairs, tiles),
            in_specs=[
                query_spec,
                pl.BlockSpec((span, 2 * HD), lambda p, i, low: (0, p)),
                pl.BlockSpec((span, 2 * HD), lambda p, i, low: (0, p + pairs)),
                pl.BlockSpec((tile, 1), lambda p, i, low: (i, 0)),
            ],
            out_specs=[query_spec, query_spec, query_spec],
        ),
        out_shape=[
            jax.ShapeDtypeStruct((rows, cols), F32),
            jax.ShapeDtypeStruct((rows, cols), BF16),
            jax.ShapeDtypeStruct((rows, cols), F32),
        ],
        cost_estimate=pl.CostEstimate(
            flops=rows * span * cols * 4, bytes_accessed=30_000_000, transcendentals=rows * span
        ),
        name="attend",
    )(low, queries, keys_values, keys_values, first_place)


def attend_back_kernel(
    tile,
    chunk,
    lead,
    low_ref,
    q_ref,
    k_ref,
    v_ref,
    g_ref,
    o_ref,
    log_ref,
    start_ref,
    dq_ref,
    dk_ref,
    dv_ref,
    dk_sum,
    dv_sum,
):
    tiles = q_ref.shape[0] // tile
    dk_sum[...] = jnp.zeros_like(dk_sum)
    dv_sum[...] = jnp.zeros_like(dv_sum)
    masks = head_masks(tile)

    def tile_step(index, carry):
        row = pl.multiple_of(index * tile, tile)
        here = pl.ds(row, tile)
        queries = q_ref[here, :] * jnp.asarray(HD ** (-0.5), BF16)
        grads = g_ref[here, :]
        product = grads.astype(F32) * o_ref[here, :]
        logs = log_ref[here, :]
        first = start_ref[here, :]
        last = lead + row + lax.broadcasted_iota(jnp.int32, (tile, 1), 0)
        zero = jnp.zeros_like(queries)
        parts = []
        for which, mask in enumerate(masks):
            parts.append(
                (
                    jnp.where(mask, queries, zero),
                    jnp.where(mask, grads, zero),
                    jnp.sum(jnp.where(mask, product, 0.0), axis=1, keepdims=True),
                    logs[:, which * HD : which * HD + 1],
                )
            )

        def step(block, totals):
            offset = pl.multiple_of(block * chunk, chunk)
            there = pl.ds(offset, chunk)
            keys = k_ref[there, :]
            values = v_ref[there, :]
            place = offset + lax.broadcasted_iota(jnp.int32, (tile, chunk), 1)
            allowed = (place >= first) & (place <= last)
            out = []
            key_part = None
            value_part = None
            for (half, grad, delta, log_total), total in zip(parts, totals):
                probs = jnp.where(allowed, jnp.exp(dot_nt(half, keys) - log_total), 0.0)
                score = (probs * (dot_nt(grad, values) - delta)).astype(BF16)
                out.append(total + dot_nn(score, keys))
                key_now = dot_tn(score, half)
                value_now = dot_tn(probs.astype(BF16), grad)
                key_part = key_now if key_part is None else key_part + key_now
                value_part = value_now if value_part is None else value_part + value_now
            dk_sum[there, :] += key_part
            dv_sum[there, :] += value_part
            return tuple(out)

        stop = (lead + row + tile + chunk - 1) // chunk
        empty = jnp.zeros((tile, 2 * HD), F32)
        totals = lax.fori_loop(low_ref[index], stop, step, (empty, empty))
        total = jnp.where(masks[0], totals[0], totals[1]) * (HD ** (-0.5))
        dq_ref[here, :] = total.astype(BF16)
        return carry

    lax.fori_loop(0, tiles, tile_step, 0)
    dk_ref[...] = dk_sum[...].astype(BF16)
    dv_ref[...] = dv_sum[...].astype(BF16)


def attend_back(queries, keys_values, grads, attended, logs, first_place, low, tile, chunk):
    rows, cols = queries.shape
    span = keys_values.shape[0]
    pairs = cols // (2 * HD)
    query_spec = pl.BlockSpec((rows, 2 * HD), lambda p, low: (0, p))
    key_spec = pl.BlockSpec((span, 2 * HD), lambda p, low: (0, p))
    return pl.pallas_call(
        functools.partial(attend_back_kernel, tile, chunk, span - rows),
        grid_spec=pltpu.PrefetchScalarGridSpec(
            num_scalar_prefetch=1,
            grid=(pairs,),
            in_specs=[
                query_spec,
                key_spec,
                pl.BlockSpec((span, 2 * HD), lambda p, low: (0, p + pairs)),
                query_spec,
                query_spec,
                query_spec,
                pl.BlockSpec((rows, 1), lambda p, low: (0, 0)),
            ],
            out_specs=[query_spec, key_spec, key_spec],
            scratch_shapes=[
                pltpu.VMEM((span, 2 * HD), F32),
                pltpu.VMEM((span, 2 * HD), F32),
            ],
        ),
        out_shape=[
            jax.ShapeDtypeStruct((rows, cols), BF16),
            jax.ShapeDtypeStruct((span, cols), BF16),
            jax.ShapeDtypeStruct((span, cols), BF16),
        ],
        cost_estimate=pl.CostEstimate(
            flops=rows * span * cols * 10, bytes_accessed=60_000_000, transcendentals=rows * span
        ),
        name="attend_back",
    )(low, queries, keys_values, keys_values, grads, attended, logs, first_place)


def inverse_rms(values):
    return lax.rsqrt(jnp.mean(values * values, axis=-1, keepdims=True) + EPSILON)


def rms_back(values, upstream):
    inverse = inverse_rms(values)
    inner_mean = jnp.mean(upstream * values, axis=-1, keepdims=True)
    return inverse * upstream - values * (inverse * inverse * inverse) * inner_mean


def matmul(left, right):
    return jnp.dot(left, right, preferred_element_type=F32)


def contract_rows(left, right):
    return jnp.einsum("td,te->de", left, right, preferred_element_type=F32)


def contract_cols(left, right):
    return jnp.einsum("te,de->td", left, right, preferred_element_type=F32)


def local(
    tokens,
    gain_attn,
    w_query,
    w_key,
    w_value,
    w_out,
    gain_ffn,
    w_gate,
    w_up,
    w_down,
    doc_ids,
    cotangent,
):
    planes = lax.axis_size("head")
    peers = lax.axis_size("blk")
    plane = lax.axis_index("head")
    tok = tokens.shape[0]
    group = tok * peers
    stream_rows = group * planes
    doc_max = stream_rows // 4
    reach = (doc_max - 1 + group - 1) // group
    reach = reach + reach % 2
    own_rows = w_query.shape[1]
    cols = D // peers
    strip = w_down.shape[1]
    hidden_cols = strip * planes
    tile = 256
    chunk = 256
    lead = reach * group

    places = jnp.arange(stream_rows, dtype=jnp.int32)
    opens = jnp.concatenate([jnp.ones((1,), jnp.bool_), doc_ids[1:] != doc_ids[:-1]])
    starts = lax.cummax(jnp.where(opens, places, 0))
    first_place = lax.dynamic_slice_in_dim(starts, plane * group, group, 0) - (
        plane * group - lead
    )
    low = first_place[::tile] // chunk
    first_place = first_place[:, None]

    attn_rows = gain_attn.astype(F32)[:, :, None]
    ffn_rows = gain_ffn.astype(F32)[:, :, None]

    def for_peers(weight, gain):
        scaled = (weight.astype(F32) * gain).astype(BF16)
        return scaled.reshape(LAYERS, own_rows, peers, cols).transpose(2, 0, 1, 3)

    def for_peers_ffn(weight, gain):
        scaled = (weight.astype(F32) * gain).astype(BF16)
        scaled = scaled.reshape(LAYERS, own_rows, planes, peers, strip).transpose(3, 0, 1, 2, 4)
        return scaled.reshape(peers, LAYERS, own_rows, hidden_cols)

    weights = {
        "pack_q": jnp.concatenate(
            [for_peers(w, attn_rows) for w in (w_query, w_key, w_value)], axis=3
        ),
        "pack_g": jnp.concatenate([for_peers_ffn(w, ffn_rows) for w in (w_gate, w_up)], axis=3),
        "w_out": w_out,
        "w_down": w_down,
    }
    sizes = types.SimpleNamespace(
        peers=peers,
        planes=planes,
        tok=tok,
        cols=cols,
        group=group,
        hidden=hidden_cols,
        reach=reach,
        own_rows=own_rows,
        tile=tile,
        chunk=chunk,
        lead=lead,
        doc_max=doc_max,
    )
    first_row = first_place.reshape(1, group)
    stream = tokens.astype(F32)
    saved = []
    full = []
    for layer in range(LAYERS):
        kept = forward_layer(sizes, layer, stream, first_row, weights, 10 + layer)
        if layer == 0:
            weights = weights | {
                "mine_g": kept["mine_g"],
                "q_full": kept["q_full1"],
                "o_full": kept["out_full1"],
            }
            full.append((kept["q_full0"], kept["out_full0"], kept["g_full"], kept["d_full"]))
        else:
            full.append((weights["q_full"], weights["o_full"], kept["g_full"], kept["d_full"]))
        saved.append(kept | {"stream": stream})
        stream = kept["next"]
    output = stream.astype(BF16)

    grad = cotangent.astype(F32)
    grads = [None] * LAYERS
    for layer in reversed(range(LAYERS)):
        attn_full, out_full, ffn_full, down_full = full[layer]
        kept = saved[layer]
        stream_in, middle = kept["stream"], kept["middle"]
        scaled_group = kept["scaled"].reshape(group, D)
        scaled_ffn_group = kept["scaled_ffn"].reshape(group, D)
        queries, keys_values, attended = kept["queries"], kept["keys"], kept["attended"]
        logs = jnp.repeat(kept["logs"].T, HD, axis=1)
        mixed = kept["mixed"]
        gate_proj = kept["gate_up"][:, :hidden_cols]
        up_proj = kept["gate_up"][:, hidden_cols:]
        hidden = kept["hidden"]
        down_in = plane_gather(grad.astype(BF16), 2, "normed_gather").reshape(group, D)
        grad_hidden = contract_cols(down_in, down_full)
        sigmoid_gate = jax.nn.sigmoid(gate_proj)
        gate_in = (
            grad_hidden * up_proj * (sigmoid_gate * (1.0 + gate_proj * (1.0 - sigmoid_gate)))
        ).astype(BF16)
        up_in = (grad_hidden * (gate_proj * sigmoid_gate)).astype(BF16)
        gate_up_in = jnp.concatenate([gate_in, up_in], axis=1)
        part = contract_cols(gate_up_in, ffn_full).astype(BF16)
        parts = plane_swap(part.reshape(peers, tok, D), 5, "sum_swap")
        grad_scaled = jnp.sum(parts.astype(F32), axis=0)
        grad_middle = grad + rms_back(middle, grad_scaled)
        proj_in = grad_middle.astype(BF16)
        proj_group = plane_gather(proj_in, 2, "normed_gather").reshape(group, D)
        mixed_grad = contract_cols(proj_group, out_full).astype(BF16)

        raw_down = lax.psum_scatter(
            contract_rows(hidden, down_in).astype(BF16), "head", scatter_dimension=0, tiled=True
        )
        raw_ffn = lax.psum_scatter(
            contract_rows(scaled_ffn_group, gate_up_in).astype(BF16),
            "head",
            scatter_dimension=0,
            tiled=True,
        )
        raw_out = lax.psum_scatter(
            lax.dynamic_update_slice(
                jnp.zeros((D, D), BF16),
                contract_rows(mixed, proj_group).astype(BF16),
                (lax.axis_index("blk") * cols, 0),
            ),
            ("head", "blk"),
            scatter_dimension=0,
            tiled=True,
        )

        query_in, key_back, value_back = attend_back(
            queries, keys_values, mixed_grad, attended, logs, first_place, low, tile, chunk
        )
        back = jnp.concatenate([key_back, value_back], axis=1).reshape(
            reach + 1, group, 2 * cols
        )
        back = halo_back(back, 6, "halo_back").astype(F32)
        key_value_in = back[0]
        for k in range(1, reach + 1):
            key_value_in = key_value_in + jnp.where(plane + k < planes, back[k], 0.0)
        qkv_in = jnp.concatenate([query_in, key_value_in.astype(BF16)], axis=1)
        raw_attn = lax.psum_scatter(
            contract_rows(scaled_group, qkv_in).astype(BF16),
            "head",
            scatter_dimension=0,
            tiled=True,
        )
        part = contract_cols(qkv_in, attn_full).astype(BF16)
        parts = plane_swap(part.reshape(peers, tok, D), 5, "sum_swap")
        grad_scaled = jnp.sum(parts.astype(F32), axis=0)
        grad = grad_middle + rms_back(stream_in, grad_scaled)
        grads[layer] = (raw_attn, raw_ffn, raw_out, raw_down)

    raw = jnp.stack([jnp.concatenate([g[0], g[1]], axis=1) for g in grads])
    raw = raw.reshape(LAYERS, peers, own_rows, 3 * cols + 2 * hidden_cols).transpose(1, 0, 2, 3)
    raw = plane_swap(raw, 1, "weights_swap").astype(F32)

    def attn_rows_of(which):
        piece = raw[:, :, :, which * cols : (which + 1) * cols]
        return piece.transpose(1, 2, 0, 3).reshape(LAYERS, own_rows, D)

    def ffn_rows_of(which):
        begin = 3 * cols + which * hidden_cols
        piece = raw[:, :, :, begin : begin + hidden_cols]
        piece = piece.reshape(peers, LAYERS, own_rows, planes, strip).transpose(1, 2, 3, 0, 4)
        return piece.reshape(LAYERS, own_rows, peers * hidden_cols)

    raw_query, raw_key, raw_value = (attn_rows_of(which) for which in range(3))
    raw_gate, raw_up = (ffn_rows_of(which) for which in range(2))

    def gain_grad(*pairs):
        return sum(jnp.sum(weight.astype(F32) * raw_part, axis=2) for weight, raw_part in pairs)

    grad_gain_attn = gain_grad((w_query, raw_query), (w_key, raw_key), (w_value, raw_value))
    grad_gain_ffn = gain_grad((w_gate, raw_gate), (w_up, raw_up))
    return (
        output,
        grad,
        grad_gain_attn,
        raw_query * attn_rows,
        raw_key * attn_rows,
        raw_value * attn_rows,
        jnp.stack([g[2] for g in grads]).astype(F32),
        grad_gain_ffn,
        raw_gate * ffn_rows,
        raw_up * ffn_rows,
        jnp.stack([g[3] for g in grads]).astype(F32),
    )


def solution(mesh):
    rows = P(("head", "blk"), None)
    vector = P(None, ("head", "blk"))
    matrix = P(None, ("head", "blk"), None)
    return jax.shard_map(
        local,
        mesh=mesh,
        in_specs=(
            rows,
            vector,
            matrix,
            matrix,
            matrix,
            matrix,
            vector,
            matrix,
            matrix,
            matrix,
            P(),
            rows,
        ),
        out_specs=(
            rows,
            rows,
            vector,
            matrix,
            matrix,
            matrix,
            matrix,
            vector,
            matrix,
            matrix,
            matrix,
        ),
        check_vma=False,
    )
```

```python
import functools
import math
import types

import jax
import jax.numpy as jnp
from jax import lax
from jax.experimental import pallas as pl
from jax.experimental.pallas import tpu as pltpu
from jax.sharding import PartitionSpec as P

D = 1024
HD = 64
HEADS = D // HD
LAYERS = 2
EPSILON = 1e-05
MASKED = -1e30
MESH = pl.DeviceIdType.MESH
F32 = jnp.float32
BF16 = jnp.bfloat16
ANY = pl.BlockSpec(memory_space=pl.ANY)


def greet_blk(count):
    me = lax.axis_index("blk")
    barrier = pltpu.get_barrier_semaphore()
    for step in range(1, count):
        pl.semaphore_signal(
            barrier,
            inc=1,
            device_id={"blk": lax.rem(me + step, count)},
            device_id_type=MESH,
        )
    pl.semaphore_wait(barrier, count - 1)
    return me


def plane_gather_kernel(count, x_ref, o_ref, send_sem, recv_sem, local_sem):
    me = greet_blk(count)
    copies = []
    for step in range(1, count):
        copy = pltpu.make_async_remote_copy(
            src_ref=x_ref,
            dst_ref=o_ref.at[me],
            send_sem=send_sem.at[step - 1],
            recv_sem=recv_sem.at[step - 1],
            device_id={"blk": lax.rem(me + step, count)},
            device_id_type=MESH,
        )
        copy.start()
        copies.append(copy)
    own = pltpu.make_async_copy(x_ref, o_ref.at[me], local_sem)
    own.start()
    own.wait()
    for copy in copies:
        copy.wait()


def plane_swap_kernel(count, x_ref, o_ref, send_sem, recv_sem, local_sem):
    me = greet_blk(count)
    copies = []
    for step in range(1, count):
        peer = lax.rem(me + step, count)
        copy = pltpu.make_async_remote_copy(
            src_ref=x_ref.at[peer],
            dst_ref=o_ref.at[me],
            send_sem=send_sem.at[step - 1],
            recv_sem=recv_sem.at[step - 1],
            device_id={"blk": peer},
            device_id_type=MESH,
        )
        copy.start()
        copies.append(copy)
    own = pltpu.make_async_copy(x_ref.at[me], o_ref.at[me], local_sem)
    own.start()
    own.wait()
    for copy in copies:
        copy.wait()


def plane_call(kernel, x, out_shape, collective_id, name):
    count = lax.axis_size("blk")
    return pl.pallas_call(
        functools.partial(kernel, count),
        out_shape=jax.ShapeDtypeStruct(out_shape, x.dtype),
        in_specs=[ANY],
        out_specs=ANY,
        scratch_shapes=[
            pltpu.SemaphoreType.DMA((count - 1,)),
            pltpu.SemaphoreType.DMA((count - 1,)),
            pltpu.SemaphoreType.DMA,
        ],
        compiler_params=pltpu.CompilerParams(collective_id=collective_id, has_side_effects=True),
        cost_estimate=pl.CostEstimate(flops=0, bytes_accessed=20_000_000, transcendentals=0),
        name=name,
    )(x)


def plane_gather(x, collective_id, name):
    return plane_call(
        plane_gather_kernel, x, (lax.axis_size("blk"),) + x.shape, collective_id, name
    )


def plane_swap(x, collective_id, name):
    return plane_call(plane_swap_kernel, x, x.shape, collective_id, name)


def launch(body, name, inputs, outputs, scratch, collective_id, flops=0):
    names = list(inputs) + list(outputs)
    flat = []
    for value in scratch.values():
        flat.extend(value if isinstance(value, list) else [value])

    def kernel(*refs):
        named = dict(zip(names, refs))
        rest = list(refs[len(names) :])
        for name, value in scratch.items():
            if isinstance(value, list):
                named[name], rest = rest[: len(value)], rest[len(value) :]
            else:
                named[name], rest = rest[0], rest[1:]
        body(types.SimpleNamespace(**named))

    results = pl.pallas_call(
        kernel,
        out_shape=[jax.ShapeDtypeStruct(shape, dtype) for shape, dtype, _ in outputs.values()],
        in_specs=[spec for _, spec in inputs.values()],
        out_specs=[spec for _, _, spec in outputs.values()],
        scratch_shapes=flat,
        compiler_params=pltpu.CompilerParams(
            collective_id=collective_id, has_side_effects=True, vmem_limit_bytes=60 << 20
        ),
        cost_estimate=pl.CostEstimate(
            flops=flops, bytes_accessed=200_000_000, transcendentals=0
        ),
        name=name,
    )(*[array for array, _ in inputs.values()])
    return dict(zip(outputs, results))


VMEM = pl.BlockSpec(memory_space=pltpu.VMEM)


def dma(*shape):
    return pltpu.SemaphoreType.DMA(shape)


def remote(src, dst, send_sem, recv_sem, **place):
    return pltpu.make_async_remote_copy(
        src_ref=src,
        dst_ref=dst,
        send_sem=send_sem,
        recv_sem=recv_sem,
        device_id=place,
        device_id_type=MESH,
    )


class Place:
    def __init__(self):
        self.peers = lax.axis_size("blk")
        self.planes = lax.axis_size("head")
        self.depth = self.planes // 2
        self.peer = lax.axis_index("blk")
        self.plane = lax.axis_index("head")
        self.z = lax.div(self.plane, 2)
        self.core = lax.rem(self.plane, 2)
        self.sibling = self.plane + 1 - 2 * self.core

    def peer_after(self, step):
        return lax.rem(self.peer + step, self.peers)

    def peer_before(self, step):
        return lax.rem(self.peer + self.peers - step, self.peers)

    def z_after(self, step):
        return lax.rem(self.z + step, self.depth)

    def z_before(self, step):
        return lax.rem(self.z + self.depth - step, self.depth)

    def greet(self):
        barrier = pltpu.get_barrier_semaphore()
        for step in range(1, self.peers):
            pl.semaphore_signal(
                barrier, inc=1, device_id={"blk": self.peer_after(step)}, device_id_type=MESH
            )
        for step in range(1, self.depth):
            pl.semaphore_signal(
                barrier,
                inc=1,
                device_id={"head": 2 * self.z_after(step) + self.core},
                device_id_type=MESH,
            )
        pl.semaphore_signal(barrier, inc=1, device_id={"head": self.sibling}, device_id_type=MESH)
        pl.semaphore_wait(barrier, self.peers - 1 + self.depth - 1 + 1)


class PlaneGather:
    def __init__(self, place, src, dst, send, recv):
        self.place, self.src, self.dst, self.send, self.recv = place, src, dst, send, recv

    def start(self):
        for step in range(1, self.place.peers):
            remote(
                self.src,
                self.dst.at[self.place.peer],
                self.send.at[step - 1],
                self.recv.at[step - 1],
                blk=self.place.peer_after(step),
            ).start()

    def await_step(self, step):
        @pl.when(step > 0)
        def _():
            index = jnp.maximum(step - 1, 0)
            source = self.place.peer_before(step)
            remote(
                self.src,
                self.dst.at[source],
                self.send.at[index],
                self.recv.at[index],
                blk=source,
            ).wait_recv()

    def finish(self):
        for step in range(1, self.place.peers):
            remote(
                self.src,
                self.dst.at[self.place.peer],
                self.send.at[step - 1],
                self.recv.at[step - 1],
                blk=self.place.peer_after(step),
            ).wait_send()


class PlaneSum:
    def __init__(self, place, src, dst, send, recv):
        self.place, self.src, self.dst, self.send, self.recv = place, src, dst, send, recv

    def copy_to(self, peer):
        index = jnp.maximum(
            lax.rem(self.place.peer + self.place.peers - peer, self.place.peers) - 1, 0
        )
        return remote(
            self.src.at[peer],
            self.dst.at[self.place.peer],
            self.send.at[index],
            self.recv.at[index],
            blk=peer,
        )

    def send_to(self, peer):
        @pl.when(peer != self.place.peer)
        def _():
            self.copy_to(peer).start()

    def total(self):
        total = self.src[self.place.peer].astype(F32)
        for step in range(1, self.place.peers):
            source = self.place.peer_after(step)
            remote(
                self.src.at[source],
                self.dst.at[source],
                self.send.at[step - 1],
                self.recv.at[step - 1],
                blk=source,
            ).wait_recv()
            total = total + self.dst[source].astype(F32)
        return total

    def finish(self):
        for step in range(1, self.place.peers):
            self.copy_to(self.place.peer_before(step)).wait_send()


class HeadGather:
    def __init__(self, place, src, full, sems):
        self.place, self.src, self.full = place, src, full
        self.z_send, self.z_recv, self.s_send, self.s_recv, self.local = sems

    @staticmethod
    def sems(depth):
        return [dma(depth - 1), dma(depth - 1), dma(depth), dma(depth), dma()]

    def slot(self, z, core):
        rows = self.src.shape[0]
        return self.full.at[pl.ds(pl.multiple_of((2 * z + core) * rows, rows), rows)]

    def z_copy(self, step):
        return remote(
            self.src,
            self.slot(self.place.z, self.place.core),
            self.z_send.at[step - 1],
            self.z_recv.at[step - 1],
            head=2 * self.place.z_after(step) + self.place.core,
        )

    def s_copy(self, step, core):
        z = self.place.z_before(step)
        where = self.slot(z, core)
        return remote(
            self.src if step == 0 else where,
            where,
            self.s_send.at[step],
            self.s_recv.at[step],
            head=self.place.sibling,
        )

    def own_copy(self):
        return pltpu.make_async_copy(
            self.src, self.slot(self.place.z, self.place.core), self.local
        )

    def start(self):
        for step in range(1, self.place.depth):
            self.z_copy(step).start()
        self.s_copy(0, self.place.core).start()
        self.own_copy().start()

    def forward(self):
        for step in range(1, self.place.depth):
            where = self.slot(self.place.z_before(step), self.place.core)
            remote(
                self.src,
                where,
                self.z_send.at[step - 1],
                self.z_recv.at[step - 1],
                head=self.place.sibling,
            ).wait_recv()
            self.s_copy(step, self.place.core).start()

    def arrive(self):
        self.own_copy().wait()
        for step in range(self.place.depth):
            self.s_copy(step, 1 - self.place.core).wait_recv()

    def finish(self):
        for step in range(1, self.place.depth):
            self.z_copy(step).wait_send()
        for step in range(self.place.depth):
            self.s_copy(step, self.place.core).wait_send()


class OutGather:
    def __init__(self, place, src, mine, full, sems):
        self.place, self.src, self.mine, self.full = place, src, mine, full
        (
            self.p_send,
            self.p_recv,
            self.z_send,
            self.z_recv,
            self.s_send,
            self.s_recv,
            self.local,
        ) = sems

    @staticmethod
    def sems(peers, depth):
        return [dma(peers - 1), dma(peers - 1), dma(depth - 1), dma(), dma(), dma(), dma()]

    def piece(self, peer):
        rows = self.src.shape[0]
        return self.mine.at[pl.ds(pl.multiple_of(peer * rows, rows), rows)]

    def half(self, core):
        rows = self.mine.shape[0]
        return self.full.at[pl.ds(pl.multiple_of(core * rows, rows), rows)]

    def home(self):
        return self.place.peer == self.place.z

    def step_to_home(self):
        return lax.rem(self.place.z + self.place.peers - self.place.peer, self.place.peers)

    def p_copy(self):
        index = jnp.maximum(self.step_to_home() - 1, 0)
        return remote(
            self.src,
            self.piece(self.place.peer),
            self.p_send.at[index],
            self.p_recv.at[index],
            blk=self.place.z,
        )

    def own_copy(self):
        return pltpu.make_async_copy(self.src, self.piece(self.place.peer), self.local)

    def start(self):
        @pl.when(self.home())
        def _():
            self.own_copy().start()

        @pl.when(jnp.logical_not(self.home()))
        def _():
            self.p_copy().start()

    def z_copy(self, step):
        return remote(
            self.mine,
            self.half(self.place.core),
            self.z_send.at[step - 1],
            self.z_recv,
            head=2 * self.place.z_after(step) + self.place.core,
        )

    def s_copy(self, core):
        return remote(
            self.half(core), self.half(core), self.s_send, self.s_recv, head=self.place.sibling
        )

    def spread(self):
        @pl.when(self.home())
        def _():
            self.own_copy().wait()
            for step in range(1, self.place.peers):
                source = self.place.peer_before(step)
                remote(
                    self.src,
                    self.piece(source),
                    self.p_send.at[step - 1],
                    self.p_recv.at[step - 1],
                    blk=source,
                ).wait_recv()
            for step in range(1, self.place.depth):
                self.z_copy(step).start()
            pltpu.make_async_copy(self.mine, self.half(self.place.core), self.local).start()

    def forward(self):
        @pl.when(self.home())
        def _():
            pltpu.make_async_copy(self.mine, self.half(self.place.core), self.local).wait()

        @pl.when(jnp.logical_not(self.home()))
        def _():
            remote(
                self.mine,
                self.half(self.place.core),
                self.z_send.at[0],
                self.z_recv,
                head=self.place.sibling,
            ).wait_recv()

        self.s_copy(self.place.core).start()

    def arrive(self):
        self.s_copy(1 - self.place.core).wait_recv()

    def finish(self):
        @pl.when(self.home())
        def _():
            for step in range(1, self.place.depth):
                self.z_copy(step).wait_send()

        @pl.when(jnp.logical_not(self.home()))
        def _():
            self.p_copy().wait_send()

        self.s_copy(self.place.core).wait_send()


class WeightSwap:
    def __init__(self, place, src, layer, mine, sems):
        self.place, self.src, self.layer, self.mine = place, src, layer, mine
        self.send, self.recv, self.local = sems

    @staticmethod
    def sems(peers):
        return [dma(peers - 1), dma(peers - 1), dma()]

    def piece(self, peer):
        rows = self.src.shape[2]
        return self.mine.at[pl.ds(pl.multiple_of(peer * rows, rows), rows)]

    def copy(self, step):
        target = self.place.peer_after(step)
        return remote(
            self.src.at[target, self.layer],
            self.piece(self.place.peer),
            self.send.at[step - 1],
            self.recv.at[step - 1],
            blk=target,
        )

    def own_copy(self):
        return pltpu.make_async_copy(
            self.src.at[self.place.peer, self.layer], self.piece(self.place.peer), self.local
        )

    def start(self):
        for step in range(1, self.place.peers):
            self.copy(step).start()
        self.own_copy().start()

    def arrive(self):
        self.own_copy().wait()
        for step in range(1, self.place.peers):
            source = self.place.peer_before(step)
            remote(
                self.src.at[source, self.layer],
                self.piece(source),
                self.send.at[step - 1],
                self.recv.at[step - 1],
                blk=source,
            ).wait_recv()

    def finish(self):
        for step in range(1, self.place.peers):
            self.copy(step).wait_send()


class Halo:
    def __init__(self, place, keys, reach, sems):
        self.place, self.keys, self.reach = place, keys, reach
        self.rows = keys.shape[0] // (reach + 1)
        self.z_send, self.z_recv, self.s_send, self.s_recv = sems

    def block(self, offset):
        return self.keys.at[pl.ds((self.reach - offset) * self.rows, self.rows)]

    @staticmethod
    def sems(reach):
        return [dma(reach // 2), dma(reach // 2), dma(reach // 2), dma(reach // 2)]

    def z_copy(self, hop):
        return remote(
            self.block(0),
            self.block(2 * hop),
            self.z_send.at[hop - 1],
            self.z_recv.at[hop - 1],
            head=self.place.plane + 2 * hop,
        )

    def sends(self, hop):
        return self.place.z + hop < self.place.depth

    def receives(self, hop):
        return self.place.z - hop >= 0

    def start(self):
        for hop in range(1, self.reach // 2 + 1):

            @pl.when(self.sends(hop))
            def _(hop=hop):
                self.z_copy(hop).start()


    def hand(self, i):
        def copy(offset):
            return remote(
                self.block(offset),
                self.block(2 * i - 1),
                self.s_send.at[i - 1],
                self.s_recv.at[i - 1],
                head=self.place.sibling,
            )

        return copy

    def hand_ready(self, i):
        return (
            (self.place.core == 1) & self.receives(i),
            (self.place.core == 0) & self.receives(i - 1),
        )

    def relay(self):
        for i in range(1, self.reach // 2 + 1):
            from_one, from_zero = self.hand_ready(i)
            if i == 1:

                @pl.when(from_zero)
                def _(i=i):
                    self.hand(i)(2 * i - 2).start()

            @pl.when(self.receives(i))
            def _(i=i):
                remote(
                    self.block(0),
                    self.block(2 * i),
                    self.z_send.at[i - 1],
                    self.z_recv.at[i - 1],
                    head=self.place.sibling,
                ).wait_recv()

            @pl.when(from_one)
            def _(i=i):
                self.hand(i)(2 * i).start()

            if i < self.reach // 2:

                @pl.when(self.hand_ready(i + 1)[1])
                def _(i=i):
                    self.hand(i + 1)(2 * i).start()

    def arrive(self):
        for i in range(1, self.reach // 2 + 1):

            @pl.when(self.place.z - i + self.place.core >= 0)
            def _(i=i):
                self.hand(i)(0).wait_recv()

    def finish(self):
        for hop in range(1, self.reach // 2 + 1):

            @pl.when(self.sends(hop))
            def _(hop=hop):
                self.z_copy(hop).wait_send()

            from_one, from_zero = self.hand_ready(hop)

            @pl.when(from_one)
            def _(hop=hop):
                self.hand(hop)(2 * hop).wait_send()

            @pl.when(from_zero)
            def _(hop=hop):
                self.hand(hop)(2 * hop - 2).wait_send()


def columns(total, most=256):
    width = math.gcd(total, most)
    return total // width, width


def by_columns(total, step, most=256):
    count, width = columns(total, most)

    def body(index, carry):
        step(pl.ds(pl.multiple_of(index * width, width), width))
        return carry

    lax.fori_loop(0, count, body, 0)


def attend_tile(sizes, place, tile_index, q_ref, keys_ref, first_ref, mixed_ref, attended_ref, log_ref):
    tile, chunk, cols, group, lead = sizes.tile, sizes.chunk, sizes.cols, sizes.group, sizes.lead
    row = pl.multiple_of(tile_index * tile, tile)
    rows = pl.ds(row, tile)
    first = first_ref[:, rows]
    last = lead + row + lax.broadcasted_iota(jnp.int32, (1, tile), 1)
    lane = lax.broadcasted_iota(jnp.int32, (tile, 2 * HD), 1)
    lowest = jnp.maximum(lead + row - (sizes.doc_max - 1), lead - place.plane * group)
    begin = lax.div(jnp.maximum(lowest, 0), chunk)
    end = lax.div(lead + row + tile + chunk - 1, chunk)
    for pair in range(cols // (2 * HD)):
        lanes = slice(pair * 2 * HD, (pair + 1) * 2 * HD)
        value_lanes = slice(cols + pair * 2 * HD, cols + (pair + 1) * 2 * HD)
        queries = q_ref[rows, lanes] * jnp.asarray(HD ** (-0.5), BF16)
        zero = jnp.zeros_like(queries)
        halves = [jnp.where(lane < HD, queries, zero), jnp.where(lane >= HD, queries, zero)]

        def step(block, state, lanes=lanes, value_lanes=value_lanes, halves=halves):
            offset = pl.multiple_of(block * chunk, chunk)
            keys = keys_ref[pl.ds(offset, chunk), lanes]
            values = keys_ref[pl.ds(offset, chunk), value_lanes]
            spot = offset + lax.broadcasted_iota(jnp.int32, (chunk, tile), 0)
            allowed = (spot >= first) & (spot <= last)
            out = []
            for half, (top, total, accum) in zip(halves, state):
                scores = jnp.where(allowed, dot_nt(keys, half), MASKED)
                new_top = jnp.maximum(top, jnp.max(scores, axis=0, keepdims=True))
                factor = jnp.exp(top - new_top)
                weights = jnp.exp(scores - new_top)
                total = total * factor + jnp.sum(weights, axis=0, keepdims=True)
                accum = accum * factor + dot_tn(values, weights.astype(BF16))
                out.append((new_top, total, accum))
            return tuple(out)

        start = (
            jnp.full((1, tile), MASKED, F32),
            jnp.zeros((1, tile), F32),
            jnp.zeros((2 * HD, tile), F32),
        )
        state = lax.fori_loop(begin, end, step, (start, start))
        parts = []
        for which, (top, total, accum) in enumerate(state):
            log_ref[2 * pair + which : 2 * pair + which + 1, rows] = top + jnp.log(total)
            parts.append(accum[which * HD : (which + 1) * HD] / total)
        attended = jnp.transpose(jnp.concatenate(parts, axis=0))
        attended_ref[rows, lanes] = attended
        mixed_ref[rows, lanes] = attended.astype(BF16)


def forward_body(sizes, layer, refs):
    place = Place()
    tok, cols, group, hidden = sizes.tok, sizes.cols, sizes.group, sizes.hidden
    tile = sizes.tile
    place.greet()
    loads = refs.load_sem
    gathers = []
    swaps = []
    if layer == 0:
        swap_q = [
            WeightSwap(place, refs.pack_q, l, refs.mine_q.at[l], getattr(refs, f"swap_q{l}"))
            for l in range(LAYERS)
        ]
        swap_g = [
            WeightSwap(place, refs.pack_g, l, refs.mine_g.at[l], getattr(refs, f"swap_g{l}"))
            for l in range(LAYERS)
        ]
        out_w = [
            OutGather(
                place,
                refs.w_out.at[l],
                refs.mine_o.at[l],
                getattr(refs, f"out_full{l}"),
                getattr(refs, f"out_sem{l}"),
            )
            for l in range(LAYERS)
        ]
        gather_q = [
            HeadGather(
                place, refs.mine_q.at[l], getattr(refs, f"q_full{l}"), getattr(refs, f"gq_sem{l}")
            )
            for l in range(LAYERS)
        ]
        gather_g = HeadGather(place, refs.mine_g.at[0], refs.g_full, refs.gg_sem)
        swap_q[0].start()
    else:
        gather_g = HeadGather(place, refs.mine_g.at[layer], refs.g_full, refs.gg_sem)
    gather_d = HeadGather(place, refs.w_down.at[layer], refs.d_full, refs.gd_sem)

    stream = refs.stream[...]
    scaled = (stream * inverse_rms(stream)).astype(BF16)
    refs.scaled[place.peer] = scaled
    ag1 = PlaneGather(place, refs.scaled.at[place.peer], refs.scaled, refs.ag1_s, refs.ag1_r)
    ag1.start()
    if layer == 0:
        out_w[0].start()
        swap_g[0].start()
        swap_q[1].start()
        out_w[1].start()
        swap_g[1].start()
        swap_q[0].arrive()
        gather_q[0].start()
        out_w[0].spread()
        swap_g[0].arrive()
        gather_g.start()
        gather_d.start()
        gather_q[0].forward()
        gather_q[0].arrive()
    else:
        gather_g.start()
        gather_d.start()
    q_load = pltpu.make_async_copy(refs.q_full0 if layer == 0 else refs.q_full, refs.wq, loads.at[0])
    q_load.start()
    q_load.wait()

    def project(step, carry):
        ag1.await_step(step)
        peer = place.peer_before(step)
        rows = pl.ds(pl.multiple_of(peer * tok, tok), tok)
        x = refs.scaled[peer]

        for part in range(3):

            def block(where, part=part):
                offset = where.start
                weight = refs.wq[:, pl.ds(pl.multiple_of(part * cols + offset, where.size), where.size)]
                value = dot_nn(x, weight).astype(BF16)
                if part == 0:
                    refs.queries[rows, where] = value
                else:
                    there = pl.ds(pl.multiple_of((part - 1) * cols + offset, where.size), where.size)
                    refs.keys[pl.ds(pl.multiple_of(sizes.lead + peer * tok, tok), tok), there] = value

            by_columns(cols, block)
        return carry

    lax.fori_loop(0, place.peers, project, 0)
    halo = Halo(place, refs.keys, sizes.reach, refs.halo_sem)
    halo.start()
    halo.relay()
    halo.arrive()

    if layer == 0:
        out_w[0].forward()
        out_w[0].arrive()
    o_load = pltpu.make_async_copy(
        refs.out_full0 if layer == 0 else refs.o_full, refs.wo, loads.at[1]
    )
    o_load.start()
    o_load.wait()

    sum1 = PlaneSum(place, refs.part1, refs.sum1, refs.rs1_s, refs.rs1_r)

    def attend_step(index, carry):
        attend_tile(
            sizes,
            place,
            index,
            refs.queries,
            refs.keys,
            refs.first,
            refs.mixed,
            refs.attended,
            refs.logs,
        )
        for k in range(tile // tok):
            peer = index * (tile // tok) + k
            x = refs.mixed[pl.ds(pl.multiple_of(peer * tok, tok), tok), :]

            def block(where, x=x, peer=peer):
                refs.part1[peer, :, where] = dot_nn(x, refs.wo[:, where]).astype(BF16)

            by_columns(D, block)
            sum1.send_to(peer)
        return carry

    lax.fori_loop(0, group // tile, attend_step, 0)

    gather_g.forward()
    gather_d.forward()
    gather_g.arrive()
    gather_d.arrive()
    g_load = pltpu.make_async_copy(refs.g_full, refs.wg, loads.at[2])
    d_load = pltpu.make_async_copy(refs.d_full, refs.wd, loads.at[3])
    g_load.start()
    d_load.start()
    if layer == 0:
        swap_q[1].arrive()
        gather_q[1].start()
        out_w[1].spread()
        swap_g[1].arrive()

    middle = stream + sum1.total()
    refs.middle[...] = middle
    refs.scaled_ffn[place.peer] = (middle * inverse_rms(middle)).astype(BF16)
    ag2 = PlaneGather(
        place, refs.scaled_ffn.at[place.peer], refs.scaled_ffn, refs.ag2_s, refs.ag2_r
    )
    ag2.start()
    g_load.wait()
    d_load.wait()
    sum2 = PlaneSum(place, refs.part2, refs.sum2, refs.rs2_s, refs.rs2_r)

    def feed(step, carry):
        ag2.await_step(step)
        peer = place.peer_before(step)
        rows = pl.ds(pl.multiple_of(peer * tok, tok), tok)
        x = refs.scaled_ffn[peer]

        def block(where):
            there = pl.ds(pl.multiple_of(hidden + where.start, where.size), where.size)
            gate = dot_nn(x, refs.wg[:, where])
            up = dot_nn(x, refs.wg[:, there])
            refs.gate_up[rows, where] = gate
            refs.gate_up[rows, there] = up
            refs.hidden[rows, where] = (gate / (1.0 + jnp.exp(-gate)) * up).astype(BF16)

        by_columns(hidden, block)
        low = refs.hidden[rows, :]

        def down(where):
            refs.part2[peer, :, where] = dot_nn(low, refs.wd[:, where]).astype(BF16)

        by_columns(D, down)
        sum2.send_to(peer)
        return carry

    lax.fori_loop(0, place.peers, feed, 0)
    if layer == 0:
        gather_q[1].forward()
        out_w[1].forward()
    refs.next[...] = middle + sum2.total()
    if layer == 0:
        gather_q[1].arrive()
        out_w[1].arrive()
        for item in swap_q + swap_g + gather_q + out_w:
            item.finish()
    for item in (ag1, ag2, sum1, sum2, gather_g, gather_d, halo):
        item.finish()


def forward_layer(sizes, layer, stream, first_row, weights, collective_id):
    peers, planes, depth = sizes.peers, sizes.planes, sizes.planes // 2
    tok, cols, group, hidden, reach = sizes.tok, sizes.cols, sizes.group, sizes.hidden, sizes.reach
    inputs = {"stream": (stream, VMEM), "first": (first_row, VMEM), "w_down": (weights["w_down"], VMEM)}
    outputs = {
        "next": ((tok, D), F32, VMEM),
        "middle": ((tok, D), F32, VMEM),
        "scaled": ((peers, tok, D), BF16, VMEM),
        "scaled_ffn": ((peers, tok, D), BF16, VMEM),
        "queries": ((group, cols), BF16, VMEM),
        "keys": (((reach + 1) * group, 2 * cols), BF16, VMEM),
        "mixed": ((group, cols), BF16, VMEM),
        "attended": ((group, cols), F32, VMEM),
        "logs": ((cols // HD, group), F32, VMEM),
        "gate_up": ((group, 2 * hidden), F32, VMEM),
        "hidden": ((group, hidden), BF16, VMEM),
        "g_full": ((D, 2 * hidden), BF16, ANY),
        "d_full": ((hidden, D), BF16, ANY),
    }
    scratch = {
        "wq": pltpu.VMEM((D, 3 * cols), BF16),
        "wo": pltpu.VMEM((cols, D), BF16),
        "wg": pltpu.VMEM((D, 2 * hidden), BF16),
        "wd": pltpu.VMEM((hidden, D), BF16),
        "part1": pltpu.VMEM((peers, tok, D), BF16),
        "sum1": pltpu.VMEM((peers, tok, D), BF16),
        "part2": pltpu.VMEM((peers, tok, D), BF16),
        "sum2": pltpu.VMEM((peers, tok, D), BF16),
        "load_sem": dma(4),
        "halo_sem": Halo.sems(reach),
        "gg_sem": HeadGather.sems(depth),
        "gd_sem": HeadGather.sems(depth),
    }
    for name in ("ag1_s", "ag1_r", "ag2_s", "ag2_r", "rs1_s", "rs1_r", "rs2_s", "rs2_r"):
        scratch[name] = dma(peers - 1)
    if layer == 0:
        rows = peers * sizes.own_rows
        inputs["pack_q"] = (weights["pack_q"], ANY)
        inputs["pack_g"] = (weights["pack_g"], ANY)
        inputs["w_out"] = (weights["w_out"], ANY)
        outputs["mine_q"] = ((LAYERS, rows, 3 * cols), BF16, VMEM)
        outputs["mine_g"] = ((LAYERS, rows, 2 * hidden), BF16, VMEM)
        outputs["mine_o"] = ((LAYERS, rows, D), BF16, VMEM)
        for l in range(LAYERS):
            outputs[f"q_full{l}"] = ((D, 3 * cols), BF16, ANY)
            outputs[f"out_full{l}"] = ((cols, D), BF16, ANY)
            scratch[f"swap_q{l}"] = WeightSwap.sems(peers)
            scratch[f"swap_g{l}"] = WeightSwap.sems(peers)
            scratch[f"out_sem{l}"] = OutGather.sems(peers, depth)
            scratch[f"gq_sem{l}"] = HeadGather.sems(depth)
    else:
        inputs["mine_g"] = (weights["mine_g"], VMEM)
        inputs["q_full"] = (weights["q_full"], ANY)
        inputs["o_full"] = (weights["o_full"], ANY)
    return launch(
        functools.partial(forward_body, sizes, layer),
        f"forward{layer}",
        inputs,
        outputs,
        scratch,
        collective_id,
        flops=group * D * (4 * cols + 3 * hidden) * 2,
    )


def dot_nt(left, right):
    return lax.dot_general(left, right, (((1,), (1,)), ((), ())), preferred_element_type=F32)


def dot_nn(left, right):
    return lax.dot_general(left, right, (((1,), (0,)), ((), ())), preferred_element_type=F32)


def dot_tn(left, right):
    return lax.dot_general(left, right, (((0,), (0,)), ((), ())), preferred_element_type=F32)


class HaloBack:
    def __init__(self, place, total, give, land, s_land, reach, sems):
        self.place, self.total, self.give, self.land, self.s_land = place, total, give, land, s_land
        self.reach = reach
        self.rows = total.shape[0] // (reach + 1)
        self.z_send, self.z_recv, self.s_send, self.s_recv = sems

    def block(self, ref, offset):
        return ref.at[pl.ds((self.reach - offset) * self.rows, self.rows)]

    def hand_copy(self, i):
        return remote(
            self.block(self.give, 2 * i - 1),
            self.s_land.at[i - 1],
            self.s_send.at[i - 1],
            self.s_recv.at[i - 1],
            head=self.place.sibling,
        )

    def hands(self, i):
        return self.place.z - i + self.place.core >= 0

    def handed(self, i):
        return self.place.z - i + 1 - self.place.core >= 0

    def low(self, offset):
        where = pl.ds((self.reach - offset) * self.rows, self.rows)
        self.give[where, :] = self.total[where, :].astype(BF16)

    def hand(self):
        for i in range(1, self.reach // 2 + 1):

            @pl.when(self.hands(i))
            def _(i=i):
                self.low(2 * i - 1)
                self.hand_copy(i).start()

    def add(self, i, offset):
        where = pl.ds((self.reach - offset) * self.rows, self.rows)
        self.total[where, :] = self.total[where, :] + self.s_land[i - 1].astype(F32)

    def z_copy(self, i):
        return remote(
            self.block(self.give, 2 * i),
            self.land.at[i - 1],
            self.z_send.at[i - 1],
            self.z_recv.at[i - 1],
            head=self.place.plane - 2 * i,
        )

    def sends(self, i):
        return self.place.z - i >= 0

    def receives(self, i):
        return self.place.z + i < self.place.depth

    def send(self):
        for i in range(1, self.reach // 2 + 1):

            @pl.when((self.place.core == 1) & self.handed(i))
            def _(i=i):
                self.hand_copy(i).wait_recv()
                self.add(i, 2 * i)

            if i > 1:

                @pl.when((self.place.core == 0) & self.handed(i))
                def _(i=i):
                    self.hand_copy(i).wait_recv()
                    self.add(i, 2 * i - 2)

        for i in range(1, self.reach // 2 + 1):

            @pl.when(self.sends(i))
            def _(i=i):
                self.low(2 * i)
                self.z_copy(i).start()

    def collect(self):
        @pl.when((self.place.core == 0) & self.handed(1))
        def _():
            self.hand_copy(1).wait_recv()
            self.add(1, 0)

        where = pl.ds(self.reach * self.rows, self.rows)
        for i in range(1, self.reach // 2 + 1):

            @pl.when(self.receives(i))
            def _(i=i):
                self.z_copy(i).wait_recv()
                self.total[where, :] = self.total[where, :] + self.land[i - 1].astype(F32)

    def finish(self):
        for i in range(1, self.reach // 2 + 1):

            @pl.when(self.hands(i))
            def _(i=i):
                self.hand_copy(i).wait_send()

            @pl.when(self.sends(i))
            def _(i=i):
                self.z_copy(i).wait_send()


class GradJob:
    def __init__(self, place, left, right, bufs, sems):
        self.place, self.left, self.right = place, left, right
        self.left_sib, self.right_sib, self.out, self.land = bufs
        self.s_send, self.s_recv, self.z_send, self.z_recv = sems
        self.width = self.out.shape[1]

    @staticmethod
    def sems(depth):
        return [dma(depth + 1), dma(depth + 1), dma(depth - 1), dma(depth - 1)]

    @staticmethod
    def bufs(group, depth, width, cols):
        return [
            pltpu.VMEM((group, depth * width), BF16),
            pltpu.VMEM((group, cols), BF16),
            pltpu.VMEM((depth, width, cols), BF16),
            pltpu.VMEM((depth - 1, width, cols), BF16),
        ]

    def lanes(self, z, core):
        return pl.ds(pl.multiple_of((2 * z + core) * self.width, self.width), self.width)

    def right_copy(self):
        return remote(
            self.right,
            self.right_sib,
            self.s_send.at[0],
            self.s_recv.at[0],
            head=self.place.sibling,
        )

    def left_copy(self, z):
        return remote(
            self.left.at[:, self.lanes(z, 1 - self.place.core)],
            self.left_sib.at[:, pl.ds(z * self.width, self.width)],
            self.s_send.at[z + 1],
            self.s_recv.at[z + 1],
            head=self.place.sibling,
        )

    def exchange(self):
        self.right_copy().start()
        for z in range(self.place.depth):
            self.left_copy(z).start()

    def z_copy(self, step):
        z = self.place.z_after(step)
        return remote(
            self.out.at[z],
            self.land.at[step - 1],
            self.z_send.at[step - 1],
            self.z_recv.at[step - 1],
            head=2 * z + self.place.core,
        )

    def compute(self):
        self.right_copy().wait_recv()
        for z in range(self.place.depth):
            self.left_copy(z).wait_recv()

        def block(index, carry):
            step = lax.rem(index + 1, self.place.depth)
            z = self.place.z_after(step)
            mine = jnp.transpose(self.left[:, self.lanes(z, self.place.core)].astype(F32))
            here = pl.ds(pl.multiple_of(z * self.width, self.width), self.width)
            theirs = jnp.transpose(self.left_sib[:, here].astype(F32))
            mine, theirs = mine.astype(BF16), theirs.astype(BF16)

            def tile(where):
                value = dot_nn(mine, self.right[:, where]) + dot_nn(theirs, self.right_sib[:, where])
                self.out[z, :, where] = value.astype(BF16)

            by_columns(self.out.shape[2], tile)

            @pl.when(step > 0)
            def _():
                self.z_copy(jnp.maximum(step, 1)).start()

            return carry

        lax.fori_loop(0, self.place.depth, block, 0)

    def total(self):
        total = self.out[self.place.z].astype(F32)
        for step in range(1, self.place.depth):
            self.z_copy(step).wait_recv()
            total = total + self.land[step - 1].astype(F32)
        return total

    def finish(self):
        self.right_copy().wait_send()
        for z in range(self.place.depth):
            self.left_copy(z).wait_send()
        for step in range(1, self.place.depth):
            self.z_copy(step).wait_send()


class OutGradJob:
    def __init__(self, place, left, right, bufs, sems):
        self.place, self.left, self.right = place, left, right
        self.left_sib, self.right_sib, self.out, self.land = bufs
        self.s_send, self.s_recv, self.z_send, self.z_recv = sems
        self.width = self.out.shape[0]

    @staticmethod
    def sems(depth):
        return [dma(2), dma(2), dma(), dma(depth - 1)]

    @staticmethod
    def bufs(group, depth, width, cols):
        return [
            pltpu.VMEM((group, width), BF16),
            pltpu.VMEM((group, cols), BF16),
            pltpu.VMEM((width, cols), BF16),
            pltpu.VMEM((depth - 1, width, cols), BF16),
        ]

    def lanes(self, core):
        return pl.ds(pl.multiple_of(core * self.width, self.width), self.width)

    def copies(self):
        return (
            remote(
                self.right,
                self.right_sib,
                self.s_send.at[0],
                self.s_recv.at[0],
                head=self.place.sibling,
            ),
            remote(
                self.left.at[:, self.lanes(1 - self.place.core)],
                self.left_sib,
                self.s_send.at[1],
                self.s_recv.at[1],
                head=self.place.sibling,
            ),
        )

    def exchange(self):
        for copy in self.copies():
            copy.start()

    def home(self):
        return self.place.peer == self.place.z

    def z_copy(self):
        step = lax.rem(self.place.peer + self.place.depth - self.place.z, self.place.depth)
        index = jnp.maximum(step - 1, 0)
        return remote(
            self.out,
            self.land.at[index],
            self.z_send,
            self.z_recv.at[index],
            head=2 * self.place.peer + self.place.core,
        )

    def compute(self):
        for copy in self.copies():
            copy.wait_recv()
        mine = jnp.transpose(self.left[:, self.lanes(self.place.core)].astype(F32)).astype(BF16)
        theirs = jnp.transpose(self.left_sib[...].astype(F32)).astype(BF16)

        def tile(where):
            value = dot_nn(mine, self.right[:, where]) + dot_nn(theirs, self.right_sib[:, where])
            self.out[:, where] = value.astype(BF16)

        by_columns(self.out.shape[1], tile)

        @pl.when(jnp.logical_not(self.home()))
        def _():
            self.z_copy().start()

    def store(self, ref):
        @pl.when(self.home())
        def _():
            total = self.out[...].astype(F32)
            for step in range(1, self.place.depth):
                remote(
                    self.out,
                    self.land.at[step - 1],
                    self.z_send,
                    self.z_recv.at[step - 1],
                    head=self.place.sibling,
                ).wait_recv()
                total = total + self.land[step - 1].astype(F32)
            ref[...] = total.astype(BF16)

        @pl.when(jnp.logical_not(self.home()))
        def _():
            ref[...] = jnp.zeros_like(ref)

    def finish(self):
        for copy in self.copies():
            copy.wait_send()

        @pl.when(jnp.logical_not(self.home()))
        def _():
            self.z_copy().wait_send()


def rms_back_of(values, upstream):
    inverse = inverse_rms(values)
    inner_mean = jnp.mean(upstream * values, axis=-1, keepdims=True)
    return inverse * upstream - values * (inverse * inverse * inverse) * inner_mean


def attend_back_chunk(sizes, place, block, refs):
    tile, chunk, cols, group, lead = sizes.tile, sizes.chunk, sizes.cols, sizes.group, sizes.lead
    offset = pl.multiple_of(block * chunk, chunk)
    there = pl.ds(offset, chunk)
    spot = offset + lax.broadcasted_iota(jnp.int32, (chunk, 1), 0)
    lane = lax.broadcasted_iota(jnp.int32, (tile, 2 * HD), 1)
    begin = lax.div(jnp.maximum(offset - lead, 0), tile)
    end = jnp.minimum(
        lax.div(jnp.maximum(offset + chunk + sizes.doc_max - 2 - lead + tile, 0), tile), group // tile
    )
    for pair in range(cols // (2 * HD)):
        lanes = slice(pair * 2 * HD, (pair + 1) * 2 * HD)
        value_lanes = slice(cols + pair * 2 * HD, cols + (pair + 1) * 2 * HD)
        keys = refs.keys[there, lanes]
        values = refs.keys[there, value_lanes]

        def step(index, state, pair=pair, lanes=lanes, keys=keys, values=values):
            key_sum, value_sum = state
            row = pl.multiple_of(index * tile, tile)
            rows = pl.ds(row, tile)
            last = lead + row + lax.broadcasted_iota(jnp.int32, (1, tile), 1)
            allowed = (spot >= refs.first[:, rows]) & (spot <= last)
            queries = refs.queries[rows, lanes] * jnp.asarray(HD ** (-0.5), BF16)
            grads = refs.mixed_grad[rows, lanes]
            zero = jnp.zeros_like(queries)
            back = []
            for which in range(2):
                mask = lane < HD if which == 0 else lane >= HD
                half = jnp.where(mask, queries, zero)
                grad = jnp.where(mask, grads, zero)
                head = slice(2 * pair + which, 2 * pair + which + 1)
                scores = dot_nt(keys, half)
                probs = jnp.where(allowed, jnp.exp(scores - refs.logs[head, rows]), 0.0)
                change = (probs * (dot_nt(values, grad) - refs.delta[head, rows])).astype(BF16)
                key_sum = key_sum + dot_nn(change, half)
                value_sum = value_sum + dot_nn(probs.astype(BF16), grad)
                back.append(dot_tn(change, keys))
            refs.dq[rows, lanes] += jnp.where(lane < HD, back[0], back[1])
            return key_sum, value_sum

        empty = jnp.zeros((chunk, 2 * HD), F32)
        key_sum, value_sum = lax.fori_loop(begin, end, step, (empty, empty))
        refs.dkv[there, lanes] = key_sum
        refs.dkv[there, value_lanes] = value_sum


def backward_body(sizes, layer, fused, refs):
    place = Place()
    tok, cols, group, hidden = sizes.tok, sizes.cols, sizes.group, sizes.hidden
    tile, chunk, lead, reach = sizes.tile, sizes.chunk, sizes.lead, sizes.reach
    place.greet()
    grad = refs.grad[...]
    refs.down_in[place.peer] = grad.astype(BF16)
    ag1 = PlaneGather(place, refs.down_in.at[place.peer], refs.down_in, refs.ag1_s, refs.ag1_r)
    ag1.start()
    loads = {
        name: pltpu.make_async_copy(src, dst, refs.load_sem.at[index])
        for index, (name, src, dst) in enumerate(
            (
                ("d", refs.d_full, refs.wd),
                ("gate_up", refs.gate_up_in, refs.gate_up),
                ("g", refs.g_full, refs.wg),
                ("o", refs.o_full, refs.wo),
                ("q", refs.q_full, refs.wq),
                ("hidden", refs.hidden_in, refs.hidden),
                ("scaled_ffn", refs.scaled_ffn_in, refs.scaled_ffn),
            )
        )
    }
    for copy in loads.values():
        copy.start()
    jobs = []
    if fused:
        loads["hidden"].wait()
        loads["scaled_ffn"].wait()
        job_d = GradJob(place, refs.hidden, refs.down_flat, refs.jd_buf, refs.jd_sem)
        job_g = GradJob(place, refs.scaled_ffn, refs.gate_up_grad, refs.jg_buf, refs.jg_sem)
        job_o = OutGradJob(place, refs.mixed, refs.proj_flat, refs.jo_buf, refs.jo_sem)
        jobs = [job_d, job_g, job_o]
        if layer == 0:
            job_q = GradJob(place, refs.old_scaled, refs.old_qkv, refs.jq_buf, refs.jq_sem)
            jobs.append(job_q)
            job_q.exchange()
    loads["d"].wait()
    loads["gate_up"].wait()
    loads["g"].wait()

    sum1 = PlaneSum(place, refs.part1, refs.sum1, refs.rs1_s, refs.rs1_r)

    def feed(step, carry):
        ag1.await_step(step)
        peer = place.peer_before(step)
        rows = pl.ds(pl.multiple_of(peer * tok, tok), tok)
        x = refs.down_in[peer]
        if fused:
            refs.down_flat[rows, :] = x

        def block(where):
            there = pl.ds(pl.multiple_of(hidden + where.start, where.size), where.size)
            grad_hidden = dot_nt(x, refs.wd[where, :])
            gate = refs.gate_up[rows, where]
            up = refs.gate_up[rows, there]
            sigmoid = 1.0 / (1.0 + jnp.exp(-gate))
            gate_grad = grad_hidden * up * (sigmoid * (1.0 + gate * (1.0 - sigmoid)))
            refs.gate_up_grad[rows, where] = gate_grad.astype(BF16)
            refs.gate_up_grad[rows, there] = (grad_hidden * (gate * sigmoid)).astype(BF16)

        by_columns(hidden, block)
        low = refs.gate_up_grad[rows, :]

        def back(where):
            refs.part1[peer, :, where] = dot_nt(low, refs.wg[where, :]).astype(BF16)

        by_columns(D, back)
        sum1.send_to(peer)
        return carry

    lax.fori_loop(0, place.peers, feed, 0)
    if fused:
        job_d.exchange()
        job_g.exchange()
        job_d.compute()
    middle = refs.middle[...]
    grad_middle = grad + rms_back_of(middle, sum1.total())
    refs.proj_in[place.peer] = grad_middle.astype(BF16)
    ag2 = PlaneGather(place, refs.proj_in.at[place.peer], refs.proj_in, refs.ag2_s, refs.ag2_r)
    ag2.start()
    if fused:
        job_g.compute()
    refs.dq[...] = jnp.zeros_like(refs.dq)
    loads["o"].wait()
    loads["q"].wait()

    def unmix(step, carry):
        ag2.await_step(step)
        peer = place.peer_before(step)
        rows = pl.ds(pl.multiple_of(peer * tok, tok), tok)
        x = refs.proj_in[peer]
        if fused:
            refs.proj_flat[rows, :] = x

        def block(where):
            refs.mixed_grad[rows, where] = dot_nt(x, refs.wo[where, :]).astype(BF16)

        by_columns(cols, block)
        return carry

    lax.fori_loop(0, place.peers, unmix, 0)
    if fused:
        job_o.exchange()

    def deltas(index, carry):
        rows = pl.ds(pl.multiple_of(index * tile, tile), tile)
        for pair in range(cols // (2 * HD)):
            lanes = slice(pair * 2 * HD, (pair + 1) * 2 * HD)
            product = jnp.transpose(
                refs.mixed_grad[rows, lanes].astype(F32) * refs.attended[rows, lanes]
            )
            for which in range(2):
                refs.delta[2 * pair + which : 2 * pair + which + 1, rows] = jnp.sum(
                    product[which * HD : (which + 1) * HD], axis=0, keepdims=True
                )
        return carry

    lax.fori_loop(0, group // tile, deltas, 0)

    halo = HaloBack(place, refs.dkv, refs.give, refs.land, refs.s_land, reach, refs.halo_sem)
    per_block = group // chunk

    def key_blocks(offset):
        @pl.when(place.plane >= offset)
        def _():
            def body(index, carry):
                attend_back_chunk(sizes, place, (reach - offset) * per_block + index, refs)
                return carry

            lax.fori_loop(0, per_block, body, 0)

    for offset in range(1, reach + 1, 2):
        key_blocks(offset)
    halo.hand()
    for offset in range(2, reach + 1, 2):
        key_blocks(offset)
    halo.send()
    key_blocks(0)
    if fused:
        job_o.compute()
        if layer == 0:
            job_q.compute()
    refs.qkv_grad[:, 0:cols] = (refs.dq[...] * (HD ** (-0.5))).astype(BF16)
    halo.collect()
    refs.qkv_grad[:, cols:] = refs.dkv[lead:, :].astype(BF16)

    sum2 = PlaneSum(place, refs.part2, refs.sum2, refs.rs2_s, refs.rs2_r)

    def unproject(step, carry):
        peer = place.peer_after(lax.rem(step + 1, place.peers))
        low = refs.qkv_grad[pl.ds(pl.multiple_of(peer * tok, tok), tok), :]

        def back(where):
            refs.part2[peer, :, where] = dot_nt(low, refs.wq[where, :]).astype(BF16)

        by_columns(D, back)
        sum2.send_to(peer)
        return carry

    lax.fori_loop(0, place.peers, unproject, 0)
    refs.next[...] = grad_middle + rms_back_of(refs.stream[...], sum2.total())
    if fused:
        refs.raw_down[...] = job_d.total()
        refs.raw_g[...] = job_g.total().astype(BF16)
        job_o.store(refs.raw_o)
        if layer == 0:
            refs.raw_q[...] = job_q.total().astype(BF16)
    else:
        loads["hidden"].wait()
        loads["scaled_ffn"].wait()
    for item in [ag1, ag2, sum1, sum2, halo] + jobs:
        item.finish()


def backward_layer(sizes, layer, fused, grad, first_row, kept, full, old, collective_id):
    peers, planes, depth = sizes.peers, sizes.planes, sizes.planes // 2
    tok, cols, group, hidden, reach = sizes.tok, sizes.cols, sizes.group, sizes.hidden, sizes.reach
    q_full, o_full, g_full, d_full = full
    inputs = {
        "grad": (grad, VMEM),
        "first": (first_row, VMEM),
        "middle": (kept["middle"], VMEM),
        "stream": (kept["stream"], VMEM),
        "queries": (kept["queries"], VMEM),
        "keys": (kept["keys"], VMEM),
        "attended": (kept["attended"], VMEM),
        "logs": (kept["logs"], VMEM),
        "mixed": (kept["mixed"], VMEM),
        "gate_up_in": (kept["gate_up"], ANY),
        "hidden_in": (kept["hidden"], ANY),
        "scaled_ffn_in": (kept["scaled_ffn"].reshape(group, D), ANY),
        "q_full": (q_full, ANY),
        "o_full": (o_full, ANY),
        "g_full": (g_full, ANY),
        "d_full": (d_full, ANY),
    }
    outputs = {
        "next": ((tok, D), F32, VMEM),
        "qkv_grad": ((group, 3 * cols), BF16, VMEM),
    }
    scratch = {
        "wq": pltpu.VMEM((D, 3 * cols), BF16),
        "wo": pltpu.VMEM((cols, D), BF16),
        "wg": pltpu.VMEM((D, 2 * hidden), BF16),
        "wd": pltpu.VMEM((hidden, D), BF16),
        "gate_up": pltpu.VMEM((group, 2 * hidden), F32),
        "hidden": pltpu.VMEM((group, hidden), BF16),
        "scaled_ffn": pltpu.VMEM((group, D), BF16),
        "mixed_grad": pltpu.VMEM((group, cols), BF16),
        "delta": pltpu.VMEM((cols // HD, group), F32),
        "dq": pltpu.VMEM((group, cols), F32),
        "dkv": pltpu.VMEM(((reach + 1) * group, 2 * cols), F32),
        "give": pltpu.VMEM(((reach + 1) * group, 2 * cols), BF16),
        "land": pltpu.VMEM((reach // 2, group, 2 * cols), BF16),
        "s_land": pltpu.VMEM((reach // 2, group, 2 * cols), BF16),
        "load_sem": dma(7),
        "halo_sem": Halo.sems(reach),
    }
    for name in ("part1", "sum1", "part2", "sum2"):
        scratch[name] = pltpu.VMEM((peers, tok, D), BF16)
    for name in ("ag1_s", "ag1_r", "ag2_s", "ag2_r", "rs1_s", "rs1_r", "rs2_s", "rs2_r"):
        scratch[name] = dma(peers - 1)
    space = pltpu.VMEM
    if fused:
        scratch["down_in"] = space((peers, tok, D), BF16)
        scratch["proj_in"] = space((peers, tok, D), BF16)
        scratch["down_flat"] = space((group, D), BF16)
        scratch["proj_flat"] = space((group, D), BF16)
        scratch["gate_up_grad"] = space((group, 2 * hidden), BF16)
        width = D // planes
        strip = hidden // planes
        scratch["jd_buf"] = GradJob.bufs(group, depth, strip, D)
        scratch["jg_buf"] = GradJob.bufs(group, depth, width, 2 * hidden)
        scratch["jo_buf"] = OutGradJob.bufs(group, depth, cols // 2, D)
        scratch["jd_sem"] = GradJob.sems(depth)
        scratch["jg_sem"] = GradJob.sems(depth)
        scratch["jo_sem"] = OutGradJob.sems(depth)
        outputs["raw_down"] = ((strip, D), F32, VMEM)
        outputs["raw_g"] = ((width, 2 * hidden), BF16, VMEM)
        outputs["raw_o"] = ((cols // 2, D), BF16, VMEM)
        if layer == 0:
            inputs["old_scaled"] = (old["scaled"].reshape(group, D), VMEM)
            inputs["old_qkv"] = (old["qkv_grad"], VMEM)
            scratch["jq_buf"] = GradJob.bufs(group, depth, width, 3 * cols)
            scratch["jq_sem"] = GradJob.sems(depth)
            outputs["raw_q"] = ((width, 3 * cols), BF16, VMEM)
    else:
        outputs["down_in"] = ((peers, tok, D), BF16, VMEM)
        outputs["proj_in"] = ((peers, tok, D), BF16, VMEM)
        outputs["gate_up_grad"] = ((group, 2 * hidden), BF16, VMEM)
    return launch(
        functools.partial(backward_body, sizes, layer, fused),
        f"backward{layer}",
        inputs,
        outputs,
        scratch,
        collective_id,
        flops=group * D * (4 * cols + 3 * hidden) * 4,
    )


def tail_body(sizes, refs):
    place = Place()
    place.greet()
    job = GradJob(place, refs.old_scaled, refs.old_qkv, refs.jq_buf, refs.jq_sem)
    job.exchange()
    swaps = []
    rows = sizes.own_rows
    for l in range(LAYERS):
        swaps.append(
            WeightSwap(
                place,
                getattr(refs, f"raw_g{l}"),
                0,
                getattr(refs, f"rows_g{l}"),
                getattr(refs, f"swap_g{l}"),
            )
        )
    swaps.append(WeightSwap(place, refs.raw_q1, 0, refs.rows_q1, refs.swap_q1))
    for swap in swaps:
        swap.start()
    outs = []

    def out_copy(l, peer, step):
        return remote(
            getattr(refs, f"raw_o{l}").at[pl.ds(pl.multiple_of(peer * rows, rows), rows)],
            getattr(refs, f"rows_o{l}"),
            getattr(refs, f"out_s{l}").at[step - 1],
            getattr(refs, f"out_r{l}"),
            blk=peer,
        )

    def own_out(l):
        return pltpu.make_async_copy(
            getattr(refs, f"raw_o{l}").at[pl.ds(pl.multiple_of(place.peer * rows, rows), rows)],
            getattr(refs, f"rows_o{l}"),
            getattr(refs, f"out_l{l}"),
        )

    home = place.peer == place.z

    @pl.when(home)
    def _():
        for l in range(LAYERS):
            for step in range(1, place.peers):
                out_copy(l, place.peer_after(step), step).start()
            own_out(l).start()

    job.compute()
    total = job.total().astype(BF16)
    for peer in range(sizes.peers):
        refs.pack_q0[peer, 0] = total[peer * rows : (peer + 1) * rows]
    last = WeightSwap(place, refs.pack_q0, 0, refs.rows_q0, refs.swap_q0)
    last.start()
    swaps.append(last)

    @pl.when(home)
    def _():
        for l in range(LAYERS):
            own_out(l).wait()

    @pl.when(jnp.logical_not(home))
    def _():
        for l in range(LAYERS):
            out_copy(l, place.z, 1).wait_recv()

    for swap in swaps:
        swap.arrive()
        swap.finish()

    @pl.when(home)
    def _():
        for l in range(LAYERS):
            for step in range(1, place.peers):
                out_copy(l, place.peer_after(step), step).wait_send()

    job.finish()


def tail(sizes, old, raws, collective_id):
    peers, planes, depth = sizes.peers, sizes.planes, sizes.planes // 2
    cols, group, hidden, rows = sizes.cols, sizes.group, sizes.hidden, sizes.own_rows
    inputs = {
        "old_scaled": (old["scaled"].reshape(group, D), VMEM),
        "old_qkv": (old["qkv_grad"], VMEM),
    }
    outputs = {}
    scratch = {
        "jq_buf": GradJob.bufs(group, depth, D // planes, 3 * cols),
        "jq_sem": GradJob.sems(depth),
        "pack_q0": pltpu.VMEM((peers, 1, rows, 3 * cols), BF16),
        "swap_q0": WeightSwap.sems(peers),
        "swap_q1": WeightSwap.sems(peers),
    }
    inputs["raw_q1"] = (raws[0]["raw_q"].reshape(peers, 1, rows, 3 * cols), VMEM)
    for l in range(LAYERS):
        inputs[f"raw_g{l}"] = (raws[l]["raw_g"].reshape(peers, 1, rows, 2 * hidden), VMEM)
        inputs[f"raw_o{l}"] = (raws[l]["raw_o"], VMEM)
        outputs[f"rows_g{l}"] = ((peers * rows, 2 * hidden), BF16, VMEM)
        outputs[f"rows_q{l}"] = ((peers * rows, 3 * cols), BF16, VMEM)
        outputs[f"rows_o{l}"] = ((rows, D), BF16, VMEM)
        scratch[f"swap_g{l}"] = WeightSwap.sems(peers)
        scratch[f"out_s{l}"] = dma(peers - 1)
        scratch[f"out_r{l}"] = dma()
        scratch[f"out_l{l}"] = dma()
    return launch(
        functools.partial(tail_body, sizes), "tail", inputs, outputs, scratch, collective_id
    )


def inverse_rms(values):
    return lax.rsqrt(jnp.mean(values * values, axis=-1, keepdims=True) + EPSILON)


def matmul(left, right):
    return jnp.dot(left, right, preferred_element_type=F32)


def contract_rows(left, right):
    return jnp.einsum("td,te->de", left, right, preferred_element_type=F32)


def contract_cols(left, right):
    return jnp.einsum("te,de->td", left, right, preferred_element_type=F32)


def local(
    tokens,
    gain_attn,
    w_query,
    w_key,
    w_value,
    w_out,
    gain_ffn,
    w_gate,
    w_up,
    w_down,
    doc_ids,
    cotangent,
):
    planes = lax.axis_size("head")
    peers = lax.axis_size("blk")
    plane = lax.axis_index("head")
    tok = tokens.shape[0]
    group = tok * peers
    stream_rows = group * planes
    doc_max = stream_rows // 4
    reach = (doc_max - 1 + group - 1) // group
    reach = reach + reach % 2
    own_rows = w_query.shape[1]
    cols = D // peers
    strip = w_down.shape[1]
    hidden_cols = strip * planes
    tile = 256
    chunk = 256
    lead = reach * group

    places = jnp.arange(stream_rows, dtype=jnp.int32)
    opens = jnp.concatenate([jnp.ones((1,), jnp.bool_), doc_ids[1:] != doc_ids[:-1]])
    starts = lax.cummax(jnp.where(opens, places, 0))
    first_place = lax.dynamic_slice_in_dim(starts, plane * group, group, 0) - (
        plane * group - lead
    )
    low = first_place[::tile] // chunk
    first_place = first_place[:, None]

    attn_rows = gain_attn.astype(F32)[:, :, None]
    ffn_rows = gain_ffn.astype(F32)[:, :, None]

    def for_peers(weight, gain):
        scaled = (weight.astype(F32) * gain).astype(BF16)
        return scaled.reshape(LAYERS, own_rows, peers, cols).transpose(2, 0, 1, 3)

    def for_peers_ffn(weight, gain):
        scaled = (weight.astype(F32) * gain).astype(BF16)
        scaled = scaled.reshape(LAYERS, own_rows, planes, peers, strip).transpose(3, 0, 1, 2, 4)
        return scaled.reshape(peers, LAYERS, own_rows, hidden_cols)

    weights = {
        "pack_q": jnp.concatenate(
            [for_peers(w, attn_rows) for w in (w_query, w_key, w_value)], axis=3
        ),
        "pack_g": jnp.concatenate([for_peers_ffn(w, ffn_rows) for w in (w_gate, w_up)], axis=3),
        "w_out": w_out,
        "w_down": w_down,
    }
    sizes = types.SimpleNamespace(
        peers=peers,
        planes=planes,
        tok=tok,
        cols=cols,
        group=group,
        hidden=hidden_cols,
        reach=reach,
        own_rows=own_rows,
        tile=tile,
        chunk=chunk,
        lead=lead,
        doc_max=doc_max,
    )
    first_row = first_place.reshape(1, group)
    stream = tokens.astype(F32)
    saved = []
    full = []
    for layer in range(LAYERS):
        kept = forward_layer(sizes, layer, stream, first_row, weights, 10 + layer)
        if layer == 0:
            weights = weights | {
                "mine_g": kept["mine_g"],
                "q_full": kept["q_full1"],
                "o_full": kept["out_full1"],
            }
            full.append((kept["q_full0"], kept["out_full0"], kept["g_full"], kept["d_full"]))
        else:
            full.append((weights["q_full"], weights["o_full"], kept["g_full"], kept["d_full"]))
        saved.append(kept | {"stream": stream})
        stream = kept["next"]
    output = stream.astype(BF16)

    grad = cotangent.astype(F32)
    fused = (D // planes) % 128 == 0 and strip % 128 == 0
    backs = [None] * LAYERS
    old = None
    for layer in reversed(range(LAYERS)):
        kept = saved[layer]
        back = backward_layer(
            sizes, layer, fused, grad, first_row, kept, full[layer], old, 12 + layer
        )
        grad = back["next"]
        old = {"scaled": kept["scaled"], "qkv_grad": back["qkv_grad"]}
        backs[layer] = back
    if fused:
        rows = tail(sizes, old, backs, 14)
        raw = jnp.stack(
            [jnp.concatenate([rows[f"rows_q{l}"], rows[f"rows_g{l}"]], axis=1) for l in range(LAYERS)]
        )
        raw = raw.reshape(LAYERS, peers, own_rows, 3 * cols + 2 * hidden_cols)
        raw = raw.transpose(1, 0, 2, 3).astype(F32)
        grad_out = jnp.stack([rows[f"rows_o{l}"] for l in range(LAYERS)]).astype(F32)
        grad_down = jnp.stack([back["raw_down"] for back in backs])
    else:
        raw, grad_out, grad_down = [], [], []
        for kept, back in zip(saved, backs):
            down_in = back["down_in"].reshape(group, D)
            proj_in = back["proj_in"].reshape(group, D)
            scatter = functools.partial(lax.psum_scatter, scatter_dimension=0, tiled=True)
            grad_down.append(
                scatter(contract_rows(kept["hidden"], down_in).astype(BF16), "head").astype(F32)
            )
            padded = lax.dynamic_update_slice(
                jnp.zeros((D, D), BF16),
                contract_rows(kept["mixed"], proj_in).astype(BF16),
                (lax.axis_index("blk") * cols, 0),
            )
            grad_out.append(scatter(padded, ("head", "blk")).astype(F32))
            pieces = [
                scatter(contract_rows(kept[name].reshape(group, D), right).astype(BF16), "head")
                for name, right in (
                    ("scaled", back["qkv_grad"]),
                    ("scaled_ffn", back["gate_up_grad"]),
                )
            ]
            raw.append(jnp.concatenate(pieces, axis=1))
        raw = jnp.stack(raw).reshape(LAYERS, peers, own_rows, 3 * cols + 2 * hidden_cols)
        raw = plane_swap(raw.transpose(1, 0, 2, 3), 1, "rows_swap").astype(F32)
        grad_out, grad_down = jnp.stack(grad_out), jnp.stack(grad_down)

    def attn_rows_of(which):
        piece = raw[:, :, :, which * cols : (which + 1) * cols]
        return piece.transpose(1, 2, 0, 3).reshape(LAYERS, own_rows, D)

    def ffn_rows_of(which):
        begin = 3 * cols + which * hidden_cols
        piece = raw[:, :, :, begin : begin + hidden_cols]
        piece = piece.reshape(peers, LAYERS, own_rows, planes, strip).transpose(1, 2, 3, 0, 4)
        return piece.reshape(LAYERS, own_rows, peers * hidden_cols)

    raw_query, raw_key, raw_value = (attn_rows_of(which) for which in range(3))
    raw_gate, raw_up = (ffn_rows_of(which) for which in range(2))

    def gain_grad(*pairs):
        return sum(jnp.sum(weight.astype(F32) * raw_part, axis=2) for weight, raw_part in pairs)

    grad_gain_attn = gain_grad((w_query, raw_query), (w_key, raw_key), (w_value, raw_value))
    grad_gain_ffn = gain_grad((w_gate, raw_gate), (w_up, raw_up))
    return (
        output,
        grad,
        grad_gain_attn,
        raw_query * attn_rows,
        raw_key * attn_rows,
        raw_value * attn_rows,
        grad_out,
        grad_gain_ffn,
        raw_gate * ffn_rows,
        raw_up * ffn_rows,
        grad_down,
    )


def solution(mesh):
    rows = P(("head", "blk"), None)
    vector = P(None, ("head", "blk"))
    matrix = P(None, ("head", "blk"), None)
    return jax.shard_map(
        local,
        mesh=mesh,
        in_specs=(
            rows,
            vector,
            matrix,
            matrix,
            matrix,
            matrix,
            vector,
            matrix,
            matrix,
            matrix,
            P(),
            rows,
        ),
        out_specs=(
            rows,
            rows,
            vector,
            matrix,
            matrix,
            matrix,
            matrix,
            vector,
            matrix,
            matrix,
            matrix,
        ),
        check_vma=False,
    )
```

```python
import functools
import math
import types

import jax
import jax.numpy as jnp
from jax import lax
from jax.experimental import pallas as pl
from jax.experimental.pallas import tpu as pltpu
from jax.sharding import PartitionSpec as P

D = 1024
HD = 64
HEADS = D // HD
LAYERS = 2
EPSILON = 1e-05
MASKED = -1e30
MESH = pl.DeviceIdType.MESH
F32 = jnp.float32
BF16 = jnp.bfloat16
ANY = pl.BlockSpec(memory_space=pl.ANY)


def greet_blk(count):
    me = lax.axis_index("blk")
    barrier = pltpu.get_barrier_semaphore()
    for step in range(1, count):
        pl.semaphore_signal(
            barrier,
            inc=1,
            device_id={"blk": lax.rem(me + step, count)},
            device_id_type=MESH,
        )
    pl.semaphore_wait(barrier, count - 1)
    return me


def plane_gather_kernel(count, x_ref, o_ref, send_sem, recv_sem, local_sem):
    me = greet_blk(count)
    copies = []
    for step in range(1, count):
        copy = pltpu.make_async_remote_copy(
            src_ref=x_ref,
            dst_ref=o_ref.at[me],
            send_sem=send_sem.at[step - 1],
            recv_sem=recv_sem.at[step - 1],
            device_id={"blk": lax.rem(me + step, count)},
            device_id_type=MESH,
        )
        copy.start()
        copies.append(copy)
    own = pltpu.make_async_copy(x_ref, o_ref.at[me], local_sem)
    own.start()
    own.wait()
    for copy in copies:
        copy.wait()


def plane_swap_kernel(count, x_ref, o_ref, send_sem, recv_sem, local_sem):
    me = greet_blk(count)
    copies = []
    for step in range(1, count):
        peer = lax.rem(me + step, count)
        copy = pltpu.make_async_remote_copy(
            src_ref=x_ref.at[peer],
            dst_ref=o_ref.at[me],
            send_sem=send_sem.at[step - 1],
            recv_sem=recv_sem.at[step - 1],
            device_id={"blk": peer},
            device_id_type=MESH,
        )
        copy.start()
        copies.append(copy)
    own = pltpu.make_async_copy(x_ref.at[me], o_ref.at[me], local_sem)
    own.start()
    own.wait()
    for copy in copies:
        copy.wait()


def plane_call(kernel, x, out_shape, collective_id, name):
    count = lax.axis_size("blk")
    return pl.pallas_call(
        functools.partial(kernel, count),
        out_shape=jax.ShapeDtypeStruct(out_shape, x.dtype),
        in_specs=[ANY],
        out_specs=ANY,
        scratch_shapes=[
            pltpu.SemaphoreType.DMA((count - 1,)),
            pltpu.SemaphoreType.DMA((count - 1,)),
            pltpu.SemaphoreType.DMA,
        ],
        compiler_params=pltpu.CompilerParams(collective_id=collective_id, has_side_effects=True),
        cost_estimate=pl.CostEstimate(flops=0, bytes_accessed=20_000_000, transcendentals=0),
        name=name,
    )(x)


def plane_gather(x, collective_id, name):
    return plane_call(
        plane_gather_kernel, x, (lax.axis_size("blk"),) + x.shape, collective_id, name
    )


def plane_swap(x, collective_id, name):
    return plane_call(plane_swap_kernel, x, x.shape, collective_id, name)


def launch(body, name, inputs, outputs, scratch, collective_id, flops=0):
    names = list(inputs) + list(outputs)
    flat = []
    for value in scratch.values():
        flat.extend(value if isinstance(value, list) else [value])

    def kernel(*refs):
        named = dict(zip(names, refs))
        rest = list(refs[len(names) :])
        for name, value in scratch.items():
            if isinstance(value, list):
                named[name], rest = rest[: len(value)], rest[len(value) :]
            else:
                named[name], rest = rest[0], rest[1:]
        body(types.SimpleNamespace(**named))

    results = pl.pallas_call(
        kernel,
        out_shape=[jax.ShapeDtypeStruct(shape, dtype) for shape, dtype, _ in outputs.values()],
        in_specs=[spec for _, spec in inputs.values()],
        out_specs=[spec for _, _, spec in outputs.values()],
        scratch_shapes=flat,
        compiler_params=pltpu.CompilerParams(
            collective_id=collective_id, has_side_effects=True, vmem_limit_bytes=60 << 20
        ),
        cost_estimate=pl.CostEstimate(
            flops=flops, bytes_accessed=200_000_000, transcendentals=0
        ),
        name=name,
    )(*[array for array, _ in inputs.values()])
    return dict(zip(outputs, results))


VMEM = pl.BlockSpec(memory_space=pltpu.VMEM)


def dma(*shape):
    return pltpu.SemaphoreType.DMA(shape)


def remote(src, dst, send_sem, recv_sem, **place):
    return pltpu.make_async_remote_copy(
        src_ref=src,
        dst_ref=dst,
        send_sem=send_sem,
        recv_sem=recv_sem,
        device_id=place,
        device_id_type=MESH,
    )


class Place:
    def __init__(self):
        self.peers = lax.axis_size("blk")
        self.planes = lax.axis_size("head")
        self.depth = self.planes // 2
        self.peer = lax.axis_index("blk")
        self.plane = lax.axis_index("head")
        self.z = lax.div(self.plane, 2)
        self.core = lax.rem(self.plane, 2)
        self.sibling = self.plane + 1 - 2 * self.core


    def moved(self, step, sign):
        half = self.peers // 2
        low, high = (step % 2, step // 2) if isinstance(step, int) else (lax.rem(step, 2), lax.div(step, 2))
        bit = lax.rem(lax.rem(self.peer, 2) + low, 2)
        return bit + 2 * lax.rem(lax.div(self.peer, 2) + sign * high + half, half)

    def peer_after(self, step):
        return self.moved(step, 1)

    def peer_before(self, step):
        return self.moved(step, -1)

    def steps_between(self, early, late):
        half = self.peers // 2
        bit = lax.rem(lax.rem(early, 2) + lax.rem(late, 2), 2)
        return bit + 2 * lax.rem(lax.div(late, 2) - lax.div(early, 2) + half, half)

    def z_after(self, step):
        return lax.rem(self.z + step, self.depth)

    def z_before(self, step):
        return lax.rem(self.z + self.depth - step, self.depth)

    def greet(self):
        barrier = pltpu.get_barrier_semaphore()
        for step in range(1, self.peers):
            pl.semaphore_signal(
                barrier, inc=1, device_id={"blk": self.peer_after(step)}, device_id_type=MESH
            )
        for step in range(1, self.depth):
            pl.semaphore_signal(
                barrier,
                inc=1,
                device_id={"head": 2 * self.z_after(step) + self.core},
                device_id_type=MESH,
            )
        pl.semaphore_signal(barrier, inc=1, device_id={"head": self.sibling}, device_id_type=MESH)
        pl.semaphore_wait(barrier, self.peers - 1 + self.depth - 1 + 1)


class PlaneGather:
    def __init__(self, place, flat, send, recv):
        self.place, self.flat, self.send, self.recv = place, flat, send, recv
        self.rows = flat.shape[0] // place.peers

    def slot(self, peer):
        return self.flat.at[pl.ds(pl.multiple_of(peer * self.rows, self.rows), self.rows)]

    def copy(self, step):
        own = self.slot(self.place.peer)
        return remote(
            own,
            own,
            self.send.at[step - 1],
            self.recv.at[step - 1],
            blk=self.place.peer_after(step),
        )

    def start(self):
        for step in range(1, self.place.peers):
            self.copy(step).start()

    def await_step(self, step):
        if step:
            source = self.place.peer_before(step)
            remote(
                self.slot(source),
                self.slot(source),
                self.send.at[step - 1],
                self.recv.at[step - 1],
                blk=source,
            ).wait_recv()

    def finish(self):
        for step in range(1, self.place.peers):
            self.copy(step).wait_send()


def peer_groups(peers):
    return [(0,), (1, 2)] + [(step,) for step in range(3, peers)] if peers > 2 else [(0,), (1,)]


class PlaneSum:
    def __init__(self, place, src, dst, send, recv):
        self.place, self.src, self.dst, self.send, self.recv = place, src, dst, send, recv

    def copy_to(self, peer):
        index = jnp.maximum(self.place.steps_between(peer, self.place.peer) - 1, 0)
        return remote(
            self.src.at[peer],
            self.dst.at[self.place.peer],
            self.send.at[index],
            self.recv.at[index],
            blk=peer,
        )

    def send_to(self, peer):
        @pl.when(peer != self.place.peer)
        def _():
            self.copy_to(peer).start()

    def total(self):
        total = self.src[self.place.peer].astype(F32)
        for step in range(1, self.place.peers):
            source = self.place.peer_after(step)
            remote(
                self.src.at[source],
                self.dst.at[source],
                self.send.at[step - 1],
                self.recv.at[step - 1],
                blk=source,
            ).wait_recv()
            total = total + self.dst[source].astype(F32)
        return total

    def finish(self):
        for step in range(1, self.place.peers):
            self.copy_to(self.place.peer_before(step)).wait_send()


class HeadGather:
    def __init__(self, place, src, full, sems):
        self.place, self.src, self.full = place, src, full
        self.z_send, self.z_recv, self.s_send, self.s_recv, self.local, self.r_send = sems
        self.line = place.depth == 4

    @staticmethod
    def sems(depth):
        return [dma(depth - 1), dma(depth - 1), dma(depth), dma(depth), dma(), dma()]

    def slot(self, z, core):
        rows = self.src.shape[0]
        return self.full.at[pl.ds(pl.multiple_of((2 * z + core) * rows, rows), rows)]

    def z_copy(self, step):
        return remote(
            self.src,
            self.slot(self.place.z, self.place.core),
            self.z_send.at[step - 1],
            self.z_recv.at[step - 1],
            head=2 * self.place.z_after(step) + self.place.core,
        )

    def near(self, step):
        z = self.place.z
        if not self.line or step == 2:
            return z >= 0
        return z < 3 if step == 1 else z > 0

    def relays(self, which):
        return self.place.z == (2 if which == 3 else 1)

    def relay_copy(self, which):
        where = self.slot(self.place.z_before(2), self.place.core)
        return remote(
            where,
            where,
            self.r_send,
            self.z_recv.at[which - 1],
            head=2 * (3 if which == 3 else 0) + self.place.core,
        )

    def s_copy(self, step, core):
        z = self.place.z_before(step)
        where = self.slot(z, core)
        return remote(
            self.src if step == 0 else where,
            where,
            self.s_send.at[step],
            self.s_recv.at[step],
            head=self.place.sibling,
        )

    def own_copy(self):
        return pltpu.make_async_copy(
            self.src, self.slot(self.place.z, self.place.core), self.local
        )

    def start(self):
        for step in sorted(range(1, self.place.depth), key=lambda k: k != 2):

            @pl.when(self.near(step))
            def _(step=step):
                self.z_copy(step).start()

        self.s_copy(0, self.place.core).start()
        self.own_copy().start()

    def await_z(self, step):
        where = self.slot(self.place.z_before(step), self.place.core)
        remote(
            self.src,
            where,
            self.z_send.at[step - 1],
            self.z_recv.at[step - 1],
            head=self.place.sibling,
        ).wait_recv()

    def relay(self):
        if self.line:
            self.await_z(2)
            for which in (1, 3):

                @pl.when(self.relays(which))
                def _(which=which):
                    self.relay_copy(which).start()

            self.s_copy(2, self.place.core).start()

    def forward(self):
        for step in range(1, self.place.depth):
            if not (self.line and step == 2):
                self.await_z(step)
                self.s_copy(step, self.place.core).start()

    def arrive(self):
        self.own_copy().wait()
        for step in range(self.place.depth):
            self.s_copy(step, 1 - self.place.core).wait_recv()

    def finish(self):
        for step in range(1, self.place.depth):

            @pl.when(self.near(step))
            def _(step=step):
                self.z_copy(step).wait_send()

        if self.line:
            for which in (1, 3):

                @pl.when(self.relays(which))
                def _(which=which):
                    self.relay_copy(which).wait_send()

        for step in range(self.place.depth):
            self.s_copy(step, self.place.core).wait_send()


class OutGather:
    def __init__(self, place, src, mine, full, sems):
        self.place, self.src, self.mine, self.full = place, src, mine, full
        (
            self.p_send,
            self.p_recv,
            self.z_send,
            self.z_recv,
            self.s_send,
            self.s_recv,
            self.local,
        ) = sems

    @staticmethod
    def sems(peers, depth):
        return [dma(peers - 1), dma(peers - 1), dma(depth - 1), dma(), dma(), dma(), dma()]

    def piece(self, peer):
        rows = self.src.shape[0]
        return self.mine.at[pl.ds(pl.multiple_of(peer * rows, rows), rows)]

    def half(self, core):
        rows = self.mine.shape[0]
        return self.full.at[pl.ds(pl.multiple_of(core * rows, rows), rows)]

    def home(self):
        return self.place.peer == self.place.z

    def step_to_home(self):
        return self.place.steps_between(self.place.peer, self.place.z)

    def p_copy(self):
        index = jnp.maximum(self.step_to_home() - 1, 0)
        return remote(
            self.src,
            self.piece(self.place.peer),
            self.p_send.at[index],
            self.p_recv.at[index],
            blk=self.place.z,
        )

    def own_copy(self):
        return pltpu.make_async_copy(self.src, self.piece(self.place.peer), self.local)

    def start(self):
        @pl.when(self.home())
        def _():
            self.own_copy().start()

        @pl.when(jnp.logical_not(self.home()))
        def _():
            self.p_copy().start()

    def z_copy(self, step):
        return remote(
            self.mine,
            self.half(self.place.core),
            self.z_send.at[step - 1],
            self.z_recv,
            head=2 * self.place.z_after(step) + self.place.core,
        )

    def s_copy(self, core):
        return remote(
            self.half(core), self.half(core), self.s_send, self.s_recv, head=self.place.sibling
        )

    def spread(self):
        @pl.when(self.home())
        def _():
            self.own_copy().wait()
            for step in range(1, self.place.peers):
                source = self.place.peer_before(step)
                remote(
                    self.src,
                    self.piece(source),
                    self.p_send.at[step - 1],
                    self.p_recv.at[step - 1],
                    blk=source,
                ).wait_recv()
            for step in range(1, self.place.depth):
                self.z_copy(step).start()
            pltpu.make_async_copy(self.mine, self.half(self.place.core), self.local).start()

    def forward(self):
        @pl.when(self.home())
        def _():
            pltpu.make_async_copy(self.mine, self.half(self.place.core), self.local).wait()

        @pl.when(jnp.logical_not(self.home()))
        def _():
            remote(
                self.mine,
                self.half(self.place.core),
                self.z_send.at[0],
                self.z_recv,
                head=self.place.sibling,
            ).wait_recv()

        self.s_copy(self.place.core).start()

    def arrive(self):
        self.s_copy(1 - self.place.core).wait_recv()

    def finish(self):
        @pl.when(self.home())
        def _():
            for step in range(1, self.place.depth):
                self.z_copy(step).wait_send()

        @pl.when(jnp.logical_not(self.home()))
        def _():
            self.p_copy().wait_send()

        self.s_copy(self.place.core).wait_send()


class WeightSwap:
    def __init__(self, place, src, layer, mine, sems):
        self.place, self.src, self.layer, self.mine = place, src, layer, mine
        self.send, self.recv, self.local = sems

    @staticmethod
    def sems(peers):
        return [dma(peers - 1), dma(peers - 1), dma()]

    def piece(self, peer):
        rows = self.src.shape[2]
        return self.mine.at[pl.ds(pl.multiple_of(peer * rows, rows), rows)]

    def copy(self, step):
        target = self.place.peer_after(step)
        return remote(
            self.src.at[target, self.layer],
            self.piece(self.place.peer),
            self.send.at[step - 1],
            self.recv.at[step - 1],
            blk=target,
        )

    def own_copy(self):
        return pltpu.make_async_copy(
            self.src.at[self.place.peer, self.layer], self.piece(self.place.peer), self.local
        )

    def start(self):
        for step in range(1, self.place.peers):
            self.copy(step).start()
        self.own_copy().start()

    def arrive(self):
        self.own_copy().wait()
        for step in range(1, self.place.peers):
            source = self.place.peer_before(step)
            remote(
                self.src.at[source, self.layer],
                self.piece(source),
                self.send.at[step - 1],
                self.recv.at[step - 1],
                blk=source,
            ).wait_recv()

    def finish(self):
        for step in range(1, self.place.peers):
            self.copy(step).wait_send()


class Halo:
    def __init__(self, place, keys, reach, sems):
        self.place, self.keys, self.reach = place, keys, reach
        self.rows = keys.shape[0] // (reach + 1)
        self.z_send, self.z_recv, self.s_send, self.s_recv = sems

    def block(self, offset):
        return self.keys.at[pl.ds((self.reach - offset) * self.rows, self.rows)]

    @staticmethod
    def sems(reach):
        return [dma(reach // 2), dma(reach // 2), dma(reach // 2), dma(reach // 2)]

    def z_copy(self, hop):
        return remote(
            self.block(0),
            self.block(2 * hop),
            self.z_send.at[hop - 1],
            self.z_recv.at[hop - 1],
            head=self.place.plane + 2 * hop,
        )

    def sends(self, hop):
        return self.place.z + hop < self.place.depth

    def receives(self, hop):
        return self.place.z - hop >= 0

    def start(self):
        for hop in range(1, self.reach // 2 + 1):

            @pl.when(self.sends(hop))
            def _(hop=hop):
                self.z_copy(hop).start()


    def hand(self, i):
        def copy(offset):
            return remote(
                self.block(offset),
                self.block(2 * i - 1),
                self.s_send.at[i - 1],
                self.s_recv.at[i - 1],
                head=self.place.sibling,
            )

        return copy

    def hand_ready(self, i):
        return (
            (self.place.core == 1) & self.receives(i),
            (self.place.core == 0) & self.receives(i - 1),
        )

    def relay(self):
        for i in range(1, self.reach // 2 + 1):
            from_one, from_zero = self.hand_ready(i)
            if i == 1:

                @pl.when(from_zero)
                def _(i=i):
                    self.hand(i)(2 * i - 2).start()

            @pl.when(self.receives(i))
            def _(i=i):
                remote(
                    self.block(0),
                    self.block(2 * i),
                    self.z_send.at[i - 1],
                    self.z_recv.at[i - 1],
                    head=self.place.sibling,
                ).wait_recv()

            @pl.when(from_one)
            def _(i=i):
                self.hand(i)(2 * i).start()

            if i < self.reach // 2:

                @pl.when(self.hand_ready(i + 1)[1])
                def _(i=i):
                    self.hand(i + 1)(2 * i).start()

    def arrive(self):
        for i in range(1, self.reach // 2 + 1):

            @pl.when(self.place.z - i + self.place.core >= 0)
            def _(i=i):
                self.hand(i)(0).wait_recv()

    def finish(self):
        for hop in range(1, self.reach // 2 + 1):

            @pl.when(self.sends(hop))
            def _(hop=hop):
                self.z_copy(hop).wait_send()

            from_one, from_zero = self.hand_ready(hop)

            @pl.when(from_one)
            def _(hop=hop):
                self.hand(hop)(2 * hop).wait_send()

            @pl.when(from_zero)
            def _(hop=hop):
                self.hand(hop)(2 * hop - 2).wait_send()


def columns(total, most=256):
    width = math.gcd(total, most)
    return total // width, width


def by_columns(total, step, most=256):
    count, width = columns(total, most)

    def body(index, carry):
        step(pl.ds(pl.multiple_of(index * width, width), width))
        return carry

    lax.fori_loop(0, count, body, 0)


def attend_tile(sizes, place, tile_index, q_ref, keys_ref, first_ref, mixed_ref, attended_ref, log_ref):
    tile, chunk, cols, group, lead = sizes.tile, sizes.chunk, sizes.cols, sizes.group, sizes.lead
    row = pl.multiple_of(tile_index * tile, tile)
    rows = pl.ds(row, tile)
    first = first_ref[:, rows]
    last = lead + row + lax.broadcasted_iota(jnp.int32, (1, tile), 1)
    lane = lax.broadcasted_iota(jnp.int32, (tile, 2 * HD), 1)
    lowest = jnp.maximum(lead + row - (sizes.doc_max - 1), lead - place.plane * group)
    begin = lax.div(jnp.maximum(lowest, 0), chunk)
    end = lax.div(lead + row + tile + chunk - 1, chunk)
    for pair in range(cols // (2 * HD)):
        lanes = slice(pair * 2 * HD, (pair + 1) * 2 * HD)
        value_lanes = slice(cols + pair * 2 * HD, cols + (pair + 1) * 2 * HD)
        queries = q_ref[rows, lanes] * jnp.asarray(HD ** (-0.5), BF16)
        zero = jnp.zeros_like(queries)
        halves = [jnp.where(lane < HD, queries, zero), jnp.where(lane >= HD, queries, zero)]

        def step(block, state, lanes=lanes, value_lanes=value_lanes, halves=halves):
            offset = pl.multiple_of(block * chunk, chunk)
            keys = keys_ref[pl.ds(offset, chunk), lanes]
            values = keys_ref[pl.ds(offset, chunk), value_lanes]
            spot = offset + lax.broadcasted_iota(jnp.int32, (chunk, tile), 0)
            allowed = (spot >= first) & (spot <= last)
            out = []
            for half, (top, total, accum) in zip(halves, state):
                scores = jnp.where(allowed, dot_nt(keys, half), MASKED)
                new_top = jnp.maximum(top, jnp.max(scores, axis=0, keepdims=True))
                factor = jnp.exp(top - new_top)
                weights = jnp.exp(scores - new_top)
                total = total * factor + jnp.sum(weights, axis=0, keepdims=True)
                accum = accum * factor + dot_tn(values, weights.astype(BF16))
                out.append((new_top, total, accum))
            return tuple(out)

        start = (
            jnp.full((1, tile), MASKED, F32),
            jnp.zeros((1, tile), F32),
            jnp.zeros((2 * HD, tile), F32),
        )
        state = lax.fori_loop(begin, end, step, (start, start))
        parts = []
        for which, (top, total, accum) in enumerate(state):
            log_ref[2 * pair + which : 2 * pair + which + 1, rows] = top + jnp.log(total)
            parts.append(accum[which * HD : (which + 1) * HD] / total)
        attended = jnp.transpose(jnp.concatenate(parts, axis=0))
        attended_ref[rows, lanes] = attended
        mixed_ref[rows, lanes] = attended.astype(BF16)


def forward_body(sizes, layer, refs):
    place = Place()
    tok, cols, group, hidden = sizes.tok, sizes.cols, sizes.group, sizes.hidden
    tile = sizes.tile
    place.greet()
    loads = refs.load_sem
    gathers = []
    swaps = []
    if layer == 0:
        swap_q = [
            WeightSwap(place, refs.pack_q, l, refs.mine_q.at[l], getattr(refs, f"swap_q{l}"))
            for l in range(LAYERS)
        ]
        swap_g = [
            WeightSwap(place, refs.pack_g, l, refs.mine_g.at[l], getattr(refs, f"swap_g{l}"))
            for l in range(LAYERS)
        ]
        out_w = [
            OutGather(
                place,
                refs.w_out.at[l],
                refs.mine_o.at[l],
                getattr(refs, f"out_full{l}"),
                getattr(refs, f"out_sem{l}"),
            )
            for l in range(LAYERS)
        ]
        gather_q = [
            HeadGather(
                place, refs.mine_q.at[l], getattr(refs, f"q_full{l}"), getattr(refs, f"gq_sem{l}")
            )
            for l in range(LAYERS)
        ]
        gather_g = HeadGather(place, refs.mine_g.at[0], refs.g_full, refs.gg_sem)
        swap_q[0].start()
    else:
        gather_g = HeadGather(place, refs.mine_g.at[layer], refs.g_full, refs.gg_sem)
    gather_d = HeadGather(place, refs.w_down.at[layer], refs.d_full, refs.gd_sem)

    stream = refs.stream[...]
    scaled = (stream * inverse_rms(stream)).astype(BF16)
    own_rows = pl.ds(pl.multiple_of(place.peer * tok, tok), tok)
    refs.scaled[own_rows, :] = scaled
    ag1 = PlaneGather(place, refs.scaled, refs.ag1_s, refs.ag1_r)
    ag1.start()
    if layer == 0:
        out_w[0].start()
        swap_g[0].start()
        swap_q[0].arrive()
        gather_q[0].start()
        out_w[0].spread()
        gather_d.start()
        gather_q[0].relay()
        gather_q[0].forward()
        gather_q[0].arrive()
    else:
        gather_d.start()
    q_load = pltpu.make_async_copy(refs.q_full0 if layer == 0 else refs.q_full, refs.wq, loads.at[0])
    q_load.start()
    q_load.wait()

    for steps in peer_groups(place.peers):
        peers = [place.peer_before(step) for step in steps]
        rows = [pl.ds(pl.multiple_of(peer * tok, tok), tok) for peer in peers]
        for step in steps:
            ag1.await_step(step)
        x = jnp.concatenate([refs.scaled[where, :] for where in rows], axis=0)
        for part in range(3):

            def block(where, part=part, x=x, peers=peers, rows=rows):
                weight = refs.wq[
                    :, pl.ds(pl.multiple_of(part * cols + where.start, where.size), where.size)
                ]
                value = dot_nn(x, weight).astype(BF16)
                there = pl.ds(
                    pl.multiple_of(max(part - 1, 0) * cols + where.start, where.size), where.size
                )
                for index, peer in enumerate(peers):
                    piece = value[index * tok : (index + 1) * tok]
                    if part == 0:
                        refs.queries[rows[index], there] = piece
                    else:
                        spot = pl.multiple_of(sizes.lead + peer * tok, tok)
                        refs.keys[pl.ds(spot, tok), there] = piece

            by_columns(cols, block)
    halo = Halo(place, refs.keys, sizes.reach, refs.halo_sem)
    gather_d.relay()
    halo.start()
    if layer == 0:
        swap_g[0].arrive()
        gather_g.start()
        swap_q[1].start()
        out_w[1].start()
        swap_g[1].start()
    else:
        gather_g.start()
    halo.relay()
    halo.arrive()

    if layer == 0:
        out_w[0].forward()
        out_w[0].arrive()
    o_load = pltpu.make_async_copy(
        refs.out_full0 if layer == 0 else refs.o_full, refs.wo, loads.at[1]
    )
    o_load.start()
    o_load.wait()

    sum1 = PlaneSum(place, refs.part1, refs.sum1, refs.rs1_s, refs.rs1_r)

    def attend_step(index, carry):
        attend_tile(
            sizes,
            place,
            index,
            refs.queries,
            refs.keys,
            refs.first,
            refs.mixed,
            refs.attended,
            refs.logs,
        )
        for k in range(tile // tok):
            peer = index * (tile // tok) + k
            x = refs.mixed[pl.ds(pl.multiple_of(peer * tok, tok), tok), :]

            def block(where, x=x, peer=peer):
                refs.part1[peer, :, where] = dot_nn(x, refs.wo[:, where]).astype(BF16)

            by_columns(D, block)
            sum1.send_to(peer)
        return carry

    lax.fori_loop(0, group // tile, attend_step, 0)

    gather_g.relay()
    gather_d.forward()
    gather_g.forward()
    gather_g.arrive()
    gather_d.arrive()
    g_load = pltpu.make_async_copy(refs.g_full, refs.wg, loads.at[2])
    d_load = pltpu.make_async_copy(refs.d_full, refs.wd, loads.at[3])
    g_load.start()
    d_load.start()
    if layer == 0:
        swap_q[1].arrive()
        gather_q[1].start()
        out_w[1].spread()
        swap_g[1].arrive()

    middle = stream + sum1.total()
    refs.middle[...] = middle
    refs.scaled_ffn[own_rows, :] = (middle * inverse_rms(middle)).astype(BF16)
    ag2 = PlaneGather(place, refs.scaled_ffn, refs.ag2_s, refs.ag2_r)
    ag2.start()
    g_load.wait()
    d_load.wait()
    sum2 = PlaneSum(place, refs.part2, refs.sum2, refs.rs2_s, refs.rs2_r)

    stores = []
    for steps in peer_groups(place.peers):
        peers = [place.peer_before(step) for step in steps]
        rows = [pl.ds(pl.multiple_of(peer * tok, tok), tok) for peer in peers]
        for step in steps:
            ag2.await_step(step)
        x = jnp.concatenate([refs.scaled_ffn[where, :] for where in rows], axis=0)

        def block(where, x=x, rows=rows):
            there = pl.ds(pl.multiple_of(hidden + where.start, where.size), where.size)
            gate = dot_nn(x, refs.wg[:, where])
            up = dot_nn(x, refs.wg[:, there])
            low = (gate / (1.0 + jnp.exp(-gate)) * up).astype(BF16)
            for index, row in enumerate(rows):
                piece = slice(index * tok, (index + 1) * tok)
                refs.gate_up[row, where] = gate[piece]
                refs.gate_up[row, there] = up[piece]
                refs.hidden[row, where] = low[piece]

        by_columns(hidden, block)
        low = jnp.concatenate([refs.hidden[where, :] for where in rows], axis=0)

        def down(where, low=low, peers=peers):
            value = dot_nn(low, refs.wd[:, where]).astype(BF16)
            for index, peer in enumerate(peers):
                refs.part2[peer, :, where] = value[index * tok : (index + 1) * tok]

        by_columns(D, down)
        for step, peer, row in zip(steps, peers, rows):
            sum2.send_to(peer)
            store = pltpu.make_async_copy(
                refs.gate_up.at[row], refs.gate_up_out.at[row], refs.store_sem.at[step]
            )
            store.start()
            stores.append(store)
    if layer == 0:
        gather_q[1].relay()
        gather_q[1].forward()
        out_w[1].forward()
    refs.next[...] = middle + sum2.total()
    if layer == 0:
        gather_q[1].arrive()
        out_w[1].arrive()
        for item in swap_q + swap_g + gather_q + out_w:
            item.finish()
    for store in stores:
        store.wait()
    for item in (ag1, ag2, sum1, sum2, gather_g, gather_d, halo):
        item.finish()


def forward_layer(sizes, layer, stream, first_row, weights, collective_id):
    peers, planes, depth = sizes.peers, sizes.planes, sizes.planes // 2
    tok, cols, group, hidden, reach = sizes.tok, sizes.cols, sizes.group, sizes.hidden, sizes.reach
    inputs = {"stream": (stream, VMEM), "first": (first_row, VMEM), "w_down": (weights["w_down"], VMEM)}
    outputs = {
        "next": ((tok, D), F32, VMEM),
        "middle": ((tok, D), F32, VMEM),
        "scaled": ((group, D), BF16, VMEM),
        "scaled_ffn": ((group, D), BF16, VMEM),
        "queries": ((group, cols), BF16, VMEM),
        "keys": (((reach + 1) * group, 2 * cols), BF16, VMEM),
        "mixed": ((group, cols), BF16, VMEM),
        "attended": ((group, cols), F32, VMEM),
        "logs": ((cols // HD, group), F32, VMEM),
        "gate_up_out": ((group, 2 * hidden), F32, ANY),
        "hidden": ((group, hidden), BF16, VMEM),
        "g_full": ((D, 2 * hidden), BF16, ANY),
        "d_full": ((hidden, D), BF16, ANY),
    }
    scratch = {
        "wq": pltpu.VMEM((D, 3 * cols), BF16),
        "wo": pltpu.VMEM((cols, D), BF16),
        "wg": pltpu.VMEM((D, 2 * hidden), BF16),
        "wd": pltpu.VMEM((hidden, D), BF16),
        "gate_up": pltpu.VMEM((group, 2 * hidden), F32),
        "store_sem": dma(peers),
        "part1": pltpu.VMEM((peers, tok, D), BF16),
        "sum1": pltpu.VMEM((peers, tok, D), BF16),
        "part2": pltpu.VMEM((peers, tok, D), BF16),
        "sum2": pltpu.VMEM((peers, tok, D), BF16),
        "load_sem": dma(4),
        "halo_sem": Halo.sems(reach),
        "gg_sem": HeadGather.sems(depth),
        "gd_sem": HeadGather.sems(depth),
    }
    for name in ("ag1_s", "ag1_r", "ag2_s", "ag2_r", "rs1_s", "rs1_r", "rs2_s", "rs2_r"):
        scratch[name] = dma(peers - 1)
    if layer == 0:
        rows = peers * sizes.own_rows
        inputs["pack_q"] = (weights["pack_q"], ANY)
        inputs["pack_g"] = (weights["pack_g"], ANY)
        inputs["w_out"] = (weights["w_out"], ANY)
        outputs["mine_q"] = ((LAYERS, rows, 3 * cols), BF16, VMEM)
        outputs["mine_g"] = ((LAYERS, rows, 2 * hidden), BF16, VMEM)
        outputs["mine_o"] = ((LAYERS, rows, D), BF16, VMEM)
        for l in range(LAYERS):
            outputs[f"q_full{l}"] = ((D, 3 * cols), BF16, ANY)
            outputs[f"out_full{l}"] = ((cols, D), BF16, ANY)
            scratch[f"swap_q{l}"] = WeightSwap.sems(peers)
            scratch[f"swap_g{l}"] = WeightSwap.sems(peers)
            scratch[f"out_sem{l}"] = OutGather.sems(peers, depth)
            scratch[f"gq_sem{l}"] = HeadGather.sems(depth)
    else:
        inputs["mine_g"] = (weights["mine_g"], VMEM)
        inputs["q_full"] = (weights["q_full"], ANY)
        inputs["o_full"] = (weights["o_full"], ANY)
    return launch(
        functools.partial(forward_body, sizes, layer),
        f"forward{layer}",
        inputs,
        outputs,
        scratch,
        collective_id,
        flops=group * D * (4 * cols + 3 * hidden) * 2,
    )


def dot_nt(left, right):
    return lax.dot_general(left, right, (((1,), (1,)), ((), ())), preferred_element_type=F32)


def dot_nn(left, right):
    return lax.dot_general(left, right, (((1,), (0,)), ((), ())), preferred_element_type=F32)


def dot_tn(left, right):
    return lax.dot_general(left, right, (((0,), (0,)), ((), ())), preferred_element_type=F32)


class HaloBack:
    def __init__(self, place, total, give, land, s_land, reach, sems):
        self.place, self.total, self.give, self.land, self.s_land = place, total, give, land, s_land
        self.reach = reach
        self.rows = total.shape[0] // (reach + 1)
        self.z_send, self.z_recv, self.s_send, self.s_recv = sems

    def block(self, ref, offset):
        return ref.at[pl.ds((self.reach - offset) * self.rows, self.rows)]

    def hand_copy(self, i):
        return remote(
            self.block(self.give, 2 * i - 1),
            self.s_land.at[i - 1],
            self.s_send.at[i - 1],
            self.s_recv.at[i - 1],
            head=self.place.sibling,
        )

    def hands(self, i):
        return self.place.z - i + self.place.core >= 0

    def handed(self, i):
        return self.place.z - i + 1 - self.place.core >= 0

    def low(self, offset):
        where = pl.ds((self.reach - offset) * self.rows, self.rows)
        self.give[where, :] = self.total[where, :].astype(BF16)

    def hand(self):
        for i in range(1, self.reach // 2 + 1):

            @pl.when(self.hands(i))
            def _(i=i):
                self.low(2 * i - 1)
                self.hand_copy(i).start()

    def add(self, i, offset):
        where = pl.ds((self.reach - offset) * self.rows, self.rows)
        self.total[where, :] = self.total[where, :] + self.s_land[i - 1].astype(F32)

    def z_copy(self, i):
        return remote(
            self.block(self.give, 2 * i),
            self.land.at[i - 1],
            self.z_send.at[i - 1],
            self.z_recv.at[i - 1],
            head=self.place.plane - 2 * i,
        )

    def sends(self, i):
        return self.place.z - i >= 0

    def receives(self, i):
        return self.place.z + i < self.place.depth

    def send(self):
        for i in range(1, self.reach // 2 + 1):

            @pl.when((self.place.core == 1) & self.handed(i))
            def _(i=i):
                self.hand_copy(i).wait_recv()
                self.add(i, 2 * i)

            if i > 1:

                @pl.when((self.place.core == 0) & self.handed(i))
                def _(i=i):
                    self.hand_copy(i).wait_recv()
                    self.add(i, 2 * i - 2)

        for i in range(1, self.reach // 2 + 1):

            @pl.when(self.sends(i))
            def _(i=i):
                self.low(2 * i)
                self.z_copy(i).start()

    def collect(self):
        @pl.when((self.place.core == 0) & self.handed(1))
        def _():
            self.hand_copy(1).wait_recv()
            self.add(1, 0)

        where = pl.ds(self.reach * self.rows, self.rows)
        for i in range(1, self.reach // 2 + 1):

            @pl.when(self.receives(i))
            def _(i=i):
                self.z_copy(i).wait_recv()
                self.total[where, :] = self.total[where, :] + self.land[i - 1].astype(F32)

    def finish(self):
        for i in range(1, self.reach // 2 + 1):

            @pl.when(self.hands(i))
            def _(i=i):
                self.hand_copy(i).wait_send()

            @pl.when(self.sends(i))
            def _(i=i):
                self.z_copy(i).wait_send()


class GradJob:
    def __init__(self, place, left, right, bufs, flips, sems):
        self.place, self.left, self.right = place, left, right
        self.left_sib, self.right_sib, self.out, self.land = bufs
        self.flipped, self.flipped_sib = flips
        self.s_send, self.s_recv, self.z_send, self.z_recv = sems
        self.width = self.out.shape[1]

    @staticmethod
    def sems(depth):
        return [dma(depth + 1), dma(depth + 1), dma(depth - 1), dma(depth - 1)]

    @staticmethod
    def bufs(group, depth, width, cols):
        return [
            pltpu.VMEM((group, depth * width), BF16),
            pltpu.VMEM((group, cols), BF16),
            pltpu.VMEM((depth, width, cols), BF16),
            pltpu.VMEM((depth - 1, width, cols), BF16),
        ]

    def lanes(self, z, core):
        return pl.ds(pl.multiple_of((2 * z + core) * self.width, self.width), self.width)

    def right_copy(self):
        return remote(
            self.right,
            self.right_sib,
            self.s_send.at[0],
            self.s_recv.at[0],
            head=self.place.sibling,
        )

    def left_copy(self, z):
        return remote(
            self.left.at[:, self.lanes(z, 1 - self.place.core)],
            self.left_sib.at[:, pl.ds(z * self.width, self.width)],
            self.s_send.at[z + 1],
            self.s_recv.at[z + 1],
            head=self.place.sibling,
        )

    def exchange(self):
        self.right_copy().start()
        for z in range(self.place.depth):
            self.left_copy(z).start()

    def z_copy(self, step):
        z = self.place.z_after(step)
        return remote(
            self.out.at[z],
            self.land.at[step - 1],
            self.z_send.at[step - 1],
            self.z_recv.at[step - 1],
            head=2 * z + self.place.core,
        )

    def send(self, step):
        self.z_copy(step).start()

    def compute(self, hold=0):
        for z in range(self.place.depth):
            mine = jnp.transpose(self.left[:, self.lanes(z, self.place.core)].astype(F32))
            self.flipped[z * self.width : (z + 1) * self.width, :] = mine.astype(BF16)
        for z in range(self.place.depth):
            self.left_copy(z).wait_recv()
            here = slice(z * self.width, (z + 1) * self.width)
            theirs = jnp.transpose(self.left_sib[:, here].astype(F32))
            self.flipped_sib[here, :] = theirs.astype(BF16)
        self.right_copy().wait_recv()

        def tile(where):
            value = dot_nn(self.flipped[...], self.right[:, where])
            value = value + dot_nn(self.flipped_sib[...], self.right_sib[:, where])
            value = value.astype(BF16)
            for z in range(self.place.depth):
                self.out[z, :, where] = value[z * self.width : (z + 1) * self.width]

        by_columns(self.out.shape[2], tile)
        for step in range(1, self.place.depth):
            if step != hold:
                self.z_copy(step).start()

    def total(self):
        total = self.out[self.place.z].astype(F32)
        for step in range(1, self.place.depth):
            self.z_copy(step).wait_recv()
            total = total + self.land[step - 1].astype(F32)
        return total

    def finish(self):
        self.right_copy().wait_send()
        for z in range(self.place.depth):
            self.left_copy(z).wait_send()
        for step in range(1, self.place.depth):
            self.z_copy(step).wait_send()


class OutGradJob:
    def __init__(self, place, left, right, bufs, sems):
        self.place, self.left, self.right = place, left, right
        self.left_sib, self.right_sib, self.out, self.land = bufs
        self.s_send, self.s_recv, self.z_send, self.z_recv = sems
        self.width = self.out.shape[0]

    @staticmethod
    def sems(depth):
        return [dma(2), dma(2), dma(), dma(depth - 1)]

    @staticmethod
    def bufs(group, depth, width, cols):
        return [
            pltpu.VMEM((group, width), BF16),
            pltpu.VMEM((group, cols), BF16),
            pltpu.VMEM((width, cols), BF16),
            pltpu.VMEM((depth - 1, width, cols), BF16),
        ]

    def lanes(self, core):
        return pl.ds(pl.multiple_of(core * self.width, self.width), self.width)

    def copies(self):
        return (
            remote(
                self.right,
                self.right_sib,
                self.s_send.at[0],
                self.s_recv.at[0],
                head=self.place.sibling,
            ),
            remote(
                self.left.at[:, self.lanes(1 - self.place.core)],
                self.left_sib,
                self.s_send.at[1],
                self.s_recv.at[1],
                head=self.place.sibling,
            ),
        )

    def exchange(self):
        for copy in self.copies():
            copy.start()

    def home(self):
        return self.place.peer == self.place.z

    def z_copy(self):
        step = lax.rem(self.place.peer + self.place.depth - self.place.z, self.place.depth)
        index = jnp.maximum(step - 1, 0)
        return remote(
            self.out,
            self.land.at[index],
            self.z_send,
            self.z_recv.at[index],
            head=2 * self.place.peer + self.place.core,
        )

    def compute(self):
        for copy in self.copies():
            copy.wait_recv()
        mine = jnp.transpose(self.left[:, self.lanes(self.place.core)].astype(F32)).astype(BF16)
        theirs = jnp.transpose(self.left_sib[...].astype(F32)).astype(BF16)

        def tile(where):
            value = dot_nn(mine, self.right[:, where]) + dot_nn(theirs, self.right_sib[:, where])
            self.out[:, where] = value.astype(BF16)

        by_columns(self.out.shape[1], tile)

        @pl.when(jnp.logical_not(self.home()))
        def _():
            self.z_copy().start()

    def store(self, ref):
        @pl.when(self.home())
        def _():
            total = self.out[...].astype(F32)
            for step in range(1, self.place.depth):
                remote(
                    self.out,
                    self.land.at[step - 1],
                    self.z_send,
                    self.z_recv.at[step - 1],
                    head=self.place.sibling,
                ).wait_recv()
                total = total + self.land[step - 1].astype(F32)
            ref[...] = total.astype(BF16)

        @pl.when(jnp.logical_not(self.home()))
        def _():
            ref[...] = jnp.zeros_like(ref)

    def finish(self):
        for copy in self.copies():
            copy.wait_send()

        @pl.when(jnp.logical_not(self.home()))
        def _():
            self.z_copy().wait_send()


def rms_back_of(values, upstream):
    inverse = inverse_rms(values)
    inner_mean = jnp.mean(upstream * values, axis=-1, keepdims=True)
    return inverse * upstream - values * (inverse * inverse * inverse) * inner_mean


def attend_back_chunk(sizes, place, block, refs):
    tile, chunk, cols, group, lead = sizes.tile, sizes.chunk, sizes.cols, sizes.group, sizes.lead
    offset = pl.multiple_of(block * chunk, chunk)
    there = pl.ds(offset, chunk)
    spot = offset + lax.broadcasted_iota(jnp.int32, (chunk, 1), 0)
    lane = lax.broadcasted_iota(jnp.int32, (tile, 2 * HD), 1)
    begin = lax.div(jnp.maximum(offset - lead, 0), tile)
    end = jnp.minimum(
        lax.div(jnp.maximum(offset + chunk + sizes.doc_max - 2 - lead + tile, 0), tile), group // tile
    )
    for pair in range(cols // (2 * HD)):
        lanes = slice(pair * 2 * HD, (pair + 1) * 2 * HD)
        value_lanes = slice(cols + pair * 2 * HD, cols + (pair + 1) * 2 * HD)
        keys = refs.keys[there, lanes]
        values = refs.keys[there, value_lanes]

        def step(index, state, pair=pair, lanes=lanes, keys=keys, values=values):
            key_sum, value_sum = state
            row = pl.multiple_of(index * tile, tile)
            rows = pl.ds(row, tile)
            last = lead + row + lax.broadcasted_iota(jnp.int32, (1, tile), 1)
            allowed = (spot >= refs.first[:, rows]) & (spot <= last)
            queries = refs.queries[rows, lanes] * jnp.asarray(HD ** (-0.5), BF16)
            grads = refs.mixed_grad[rows, lanes]
            zero = jnp.zeros_like(queries)
            back = []
            for which in range(2):
                mask = lane < HD if which == 0 else lane >= HD
                half = jnp.where(mask, queries, zero)
                grad = jnp.where(mask, grads, zero)
                head = slice(2 * pair + which, 2 * pair + which + 1)
                scores = dot_nt(keys, half)
                probs = jnp.where(allowed, jnp.exp(scores - refs.logs[head, rows]), 0.0)
                change = (probs * (dot_nt(values, grad) - refs.delta[head, rows])).astype(BF16)
                key_sum = key_sum + dot_nn(change, half)
                value_sum = value_sum + dot_nn(probs.astype(BF16), grad)
                back.append(dot_tn(change, keys))
            refs.dq[rows, lanes] += jnp.where(lane < HD, back[0], back[1])
            return key_sum, value_sum

        empty = jnp.zeros((chunk, 2 * HD), F32)
        key_sum, value_sum = lax.fori_loop(begin, end, step, (empty, empty))
        refs.dkv[there, lanes] = key_sum
        refs.dkv[there, value_lanes] = value_sum


def backward_body(sizes, layer, fused, refs):
    place = Place()
    tok, cols, group, hidden = sizes.tok, sizes.cols, sizes.group, sizes.hidden
    tile, chunk, lead, reach = sizes.tile, sizes.chunk, sizes.lead, sizes.reach
    place.greet()
    grad = refs.grad[...]
    own_rows = pl.ds(pl.multiple_of(place.peer * tok, tok), tok)
    refs.down_in[own_rows, :] = grad.astype(BF16)
    ag1 = PlaneGather(place, refs.down_in, refs.ag1_s, refs.ag1_r)
    ag1.start()
    loads = {
        name: pltpu.make_async_copy(src, dst, refs.load_sem.at[index])
        for index, (name, src, dst) in enumerate(
            (
                ("d", refs.d_full, refs.wd),
                ("gate_up", refs.gate_up_in, refs.gate_up),
                ("g", refs.g_full, refs.wg),
                ("o", refs.o_full, refs.wo),
                ("q", refs.q_full, refs.wq),
                ("hidden", refs.hidden_in, refs.hidden),
                ("scaled_ffn", refs.scaled_ffn_in, refs.scaled_ffn),
            )
        )
    }
    for copy in loads.values():
        copy.start()
    jobs = []
    if fused:
        loads["hidden"].wait()
        loads["scaled_ffn"].wait()
        job_d = GradJob(place, refs.hidden, refs.down_in, refs.jd_buf, refs.flips, refs.jd_sem)
        job_g = GradJob(place, refs.scaled_ffn, refs.gate_up_grad, refs.jg_buf, refs.flips, refs.jg_sem)
        job_o = OutGradJob(place, refs.mixed, refs.proj_in, refs.jo_buf, refs.jo_sem)
        jobs = [job_d, job_g, job_o]
        if layer == 0:
            job_q = GradJob(place, refs.old_scaled, refs.old_qkv, refs.jq_buf, refs.flips, refs.jq_sem)
            jobs.append(job_q)
            job_q.exchange()
    loads["d"].wait()
    loads["gate_up"].wait()
    loads["g"].wait()
    if fused and layer == 0:
        job_q.compute()

    sum1 = PlaneSum(place, refs.part1, refs.sum1, refs.rs1_s, refs.rs1_r)

    for steps in peer_groups(place.peers):
        peers = [place.peer_before(step) for step in steps]
        rows = [pl.ds(pl.multiple_of(peer * tok, tok), tok) for peer in peers]
        for step in steps:
            ag1.await_step(step)
        x = jnp.concatenate([refs.down_in[where, :] for where in rows], axis=0)

        def block(where, x=x, rows=rows):
            there = pl.ds(pl.multiple_of(hidden + where.start, where.size), where.size)
            grad_hidden = dot_nt(x, refs.wd[where, :])
            for index, row in enumerate(rows):
                piece = grad_hidden[index * tok : (index + 1) * tok]
                gate = refs.gate_up[row, where]
                up = refs.gate_up[row, there]
                sigmoid = 1.0 / (1.0 + jnp.exp(-gate))
                gate_grad = piece * up * (sigmoid * (1.0 + gate * (1.0 - sigmoid)))
                refs.gate_up_grad[row, where] = gate_grad.astype(BF16)
                refs.gate_up_grad[row, there] = (piece * (gate * sigmoid)).astype(BF16)

        by_columns(hidden, block)
        low = jnp.concatenate([refs.gate_up_grad[where, :] for where in rows], axis=0)

        def back(where, low=low, peers=peers):
            value = dot_nt(low, refs.wg[where, :]).astype(BF16)
            for index, peer in enumerate(peers):
                refs.part1[peer, :, where] = value[index * tok : (index + 1) * tok]

        by_columns(D, back)
        for peer in peers:
            sum1.send_to(peer)

    if fused:
        job_d.exchange()
        job_g.exchange()
        job_d.compute()
    middle = refs.middle[...]
    grad_middle = grad + rms_back_of(middle, sum1.total())
    refs.proj_in[own_rows, :] = grad_middle.astype(BF16)
    ag2 = PlaneGather(place, refs.proj_in, refs.ag2_s, refs.ag2_r)
    ag2.start()
    if fused:
        job_g.compute(hold=2)
    refs.dq[...] = jnp.zeros_like(refs.dq)
    loads["o"].wait()
    loads["q"].wait()

    for steps in peer_groups(place.peers):
        rows = [
            pl.ds(pl.multiple_of(place.peer_before(step) * tok, tok), tok) for step in steps
        ]
        for step in steps:
            ag2.await_step(step)
        x = jnp.concatenate([refs.proj_in[where, :] for where in rows], axis=0)

        def block(where, x=x, rows=rows):
            value = dot_nt(x, refs.wo[where, :]).astype(BF16)
            for index, row in enumerate(rows):
                refs.mixed_grad[row, where] = value[index * tok : (index + 1) * tok]

        by_columns(cols, block)
    if fused:
        job_o.exchange()

    def deltas(index, carry):
        rows = pl.ds(pl.multiple_of(index * tile, tile), tile)
        for pair in range(cols // (2 * HD)):
            lanes = slice(pair * 2 * HD, (pair + 1) * 2 * HD)
            product = jnp.transpose(
                refs.mixed_grad[rows, lanes].astype(F32) * refs.attended[rows, lanes]
            )
            for which in range(2):
                refs.delta[2 * pair + which : 2 * pair + which + 1, rows] = jnp.sum(
                    product[which * HD : (which + 1) * HD], axis=0, keepdims=True
                )
        return carry

    lax.fori_loop(0, group // tile, deltas, 0)

    halo = HaloBack(place, refs.dkv, refs.give, refs.land, refs.s_land, reach, refs.halo_sem)
    per_block = group // chunk

    def key_blocks(offset):
        @pl.when(place.plane >= offset)
        def _():
            def body(index, carry):
                attend_back_chunk(sizes, place, (reach - offset) * per_block + index, refs)
                return carry

            lax.fori_loop(0, per_block, body, 0)

    for offset in range(1, reach + 1, 2):
        key_blocks(offset)
    halo.hand()
    for offset in range(2, reach + 1, 2):
        key_blocks(offset)
    halo.send()
    key_blocks(0)
    if fused:
        job_o.compute()
    refs.qkv_grad[:, 0:cols] = (refs.dq[...] * (HD ** (-0.5))).astype(BF16)
    halo.collect()
    if fused:
        job_g.send(2)
    refs.qkv_grad[:, cols:] = refs.dkv[lead:, :].astype(BF16)

    sum2 = PlaneSum(place, refs.part2, refs.sum2, refs.rs2_s, refs.rs2_r)

    for steps in [g for g in peer_groups(place.peers)[1:]] + [(0,)]:
        peers = [place.peer_before(step) for step in steps]
        low = jnp.concatenate(
            [refs.qkv_grad[pl.ds(pl.multiple_of(peer * tok, tok), tok), :] for peer in peers], axis=0
        )

        def back(where, low=low, peers=peers):
            value = dot_nt(low, refs.wq[where, :]).astype(BF16)
            for index, peer in enumerate(peers):
                refs.part2[peer, :, where] = value[index * tok : (index + 1) * tok]

        by_columns(D, back)
        for peer in peers:
            sum2.send_to(peer)

    refs.next[...] = grad_middle + rms_back_of(refs.stream[...], sum2.total())
    if fused:
        refs.raw_down[...] = job_d.total()
        refs.raw_g[...] = job_g.total().astype(BF16)
        job_o.store(refs.raw_o)
        if layer == 0:
            refs.raw_q[...] = job_q.total().astype(BF16)
    else:
        loads["hidden"].wait()
        loads["scaled_ffn"].wait()
    for item in [ag1, ag2, sum1, sum2, halo] + jobs:
        item.finish()


def backward_layer(sizes, layer, fused, grad, first_row, kept, full, old, collective_id):
    peers, planes, depth = sizes.peers, sizes.planes, sizes.planes // 2
    tok, cols, group, hidden, reach = sizes.tok, sizes.cols, sizes.group, sizes.hidden, sizes.reach
    q_full, o_full, g_full, d_full = full
    inputs = {
        "grad": (grad, VMEM),
        "first": (first_row, VMEM),
        "middle": (kept["middle"], VMEM),
        "stream": (kept["stream"], VMEM),
        "queries": (kept["queries"], VMEM),
        "keys": (kept["keys"], VMEM),
        "attended": (kept["attended"], VMEM),
        "logs": (kept["logs"], VMEM),
        "mixed": (kept["mixed"], VMEM),
        "gate_up_in": (kept["gate_up_out"], ANY),
        "hidden_in": (kept["hidden"], ANY),
        "scaled_ffn_in": (kept["scaled_ffn"], ANY),
        "q_full": (q_full, ANY),
        "o_full": (o_full, ANY),
        "g_full": (g_full, ANY),
        "d_full": (d_full, ANY),
    }
    outputs = {
        "next": ((tok, D), F32, VMEM),
        "qkv_grad": ((group, 3 * cols), BF16, VMEM),
    }
    scratch = {
        "wq": pltpu.VMEM((D, 3 * cols), BF16),
        "wo": pltpu.VMEM((cols, D), BF16),
        "wg": pltpu.VMEM((D, 2 * hidden), BF16),
        "wd": pltpu.VMEM((hidden, D), BF16),
        "gate_up": pltpu.VMEM((group, 2 * hidden), F32),
        "hidden": pltpu.VMEM((group, hidden), BF16),
        "scaled_ffn": pltpu.VMEM((group, D), BF16),
        "mixed_grad": pltpu.VMEM((group, cols), BF16),
        "delta": pltpu.VMEM((cols // HD, group), F32),
        "dq": pltpu.VMEM((group, cols), F32),
        "dkv": pltpu.VMEM(((reach + 1) * group, 2 * cols), F32),
        "give": pltpu.VMEM(((reach + 1) * group, 2 * cols), BF16),
        "land": pltpu.VMEM((reach // 2, group, 2 * cols), BF16),
        "s_land": pltpu.VMEM((reach // 2, group, 2 * cols), BF16),
        "load_sem": dma(7),
        "halo_sem": Halo.sems(reach),
    }
    for name in ("part1", "sum1", "part2", "sum2"):
        scratch[name] = pltpu.VMEM((peers, tok, D), BF16)
    for name in ("ag1_s", "ag1_r", "ag2_s", "ag2_r", "rs1_s", "rs1_r", "rs2_s", "rs2_r"):
        scratch[name] = dma(peers - 1)
    space = pltpu.VMEM
    if fused:
        scratch["down_in"] = space((group, D), BF16)
        scratch["proj_in"] = space((group, D), BF16)
        scratch["gate_up_grad"] = space((group, 2 * hidden), BF16)
        width = D // planes
        strip = hidden // planes
        scratch["flips"] = [pltpu.VMEM((depth * width, group), BF16)] * 2
        scratch["jd_buf"] = GradJob.bufs(group, depth, strip, D)
        scratch["jg_buf"] = GradJob.bufs(group, depth, width, 2 * hidden)
        scratch["jo_buf"] = OutGradJob.bufs(group, depth, cols // 2, D)
        scratch["jd_sem"] = GradJob.sems(depth)
        scratch["jg_sem"] = GradJob.sems(depth)
        scratch["jo_sem"] = OutGradJob.sems(depth)
        outputs["raw_down"] = ((strip, D), F32, VMEM)
        outputs["raw_g"] = ((width, 2 * hidden), BF16, VMEM)
        outputs["raw_o"] = ((cols // 2, D), BF16, VMEM)
        if layer == 0:
            inputs["old_scaled"] = (old["scaled"], VMEM)
            inputs["old_qkv"] = (old["qkv_grad"], VMEM)
            scratch["jq_buf"] = GradJob.bufs(group, depth, width, 3 * cols)
            scratch["jq_sem"] = GradJob.sems(depth)
            outputs["raw_q"] = ((width, 3 * cols), BF16, VMEM)
    else:
        outputs["down_in"] = ((group, D), BF16, VMEM)
        outputs["proj_in"] = ((group, D), BF16, VMEM)
        outputs["gate_up_grad"] = ((group, 2 * hidden), BF16, VMEM)
    return launch(
        functools.partial(backward_body, sizes, layer, fused),
        f"backward{layer}",
        inputs,
        outputs,
        scratch,
        collective_id,
        flops=group * D * (4 * cols + 3 * hidden) * 4,
    )


def tail_body(sizes, refs):
    place = Place()
    place.greet()
    job = GradJob(place, refs.old_scaled, refs.old_qkv, refs.jq_buf, refs.flips, refs.jq_sem)
    job.exchange()
    swaps = []
    rows = sizes.own_rows
    for l in range(LAYERS):
        swaps.append(
            WeightSwap(
                place,
                getattr(refs, f"raw_g{l}"),
                0,
                getattr(refs, f"rows_g{l}"),
                getattr(refs, f"swap_g{l}"),
            )
        )
    swaps.append(WeightSwap(place, refs.raw_q1, 0, refs.rows_q1, refs.swap_q1))
    for swap in swaps:
        swap.start()
    outs = []

    def out_copy(l, peer, step):
        return remote(
            getattr(refs, f"raw_o{l}").at[pl.ds(pl.multiple_of(peer * rows, rows), rows)],
            getattr(refs, f"rows_o{l}"),
            getattr(refs, f"out_s{l}").at[step - 1],
            getattr(refs, f"out_r{l}"),
            blk=peer,
        )

    def own_out(l):
        return pltpu.make_async_copy(
            getattr(refs, f"raw_o{l}").at[pl.ds(pl.multiple_of(place.peer * rows, rows), rows)],
            getattr(refs, f"rows_o{l}"),
            getattr(refs, f"out_l{l}"),
        )

    home = place.peer == place.z

    @pl.when(home)
    def _():
        for l in range(LAYERS):
            for step in range(1, place.peers):
                out_copy(l, place.peer_after(step), step).start()
            own_out(l).start()

    job.compute()
    total = job.total().astype(BF16)
    for peer in range(sizes.peers):
        refs.pack_q0[peer, 0] = total[peer * rows : (peer + 1) * rows]
    last = WeightSwap(place, refs.pack_q0, 0, refs.rows_q0, refs.swap_q0)
    last.start()
    swaps.append(last)

    @pl.when(home)
    def _():
        for l in range(LAYERS):
            own_out(l).wait()

    @pl.when(jnp.logical_not(home))
    def _():
        for l in range(LAYERS):
            out_copy(l, place.z, 1).wait_recv()

    for swap in swaps:
        swap.arrive()
        swap.finish()

    @pl.when(home)
    def _():
        for l in range(LAYERS):
            for step in range(1, place.peers):
                out_copy(l, place.peer_after(step), step).wait_send()

    job.finish()


def tail(sizes, old, raws, collective_id):
    peers, planes, depth = sizes.peers, sizes.planes, sizes.planes // 2
    cols, group, hidden, rows = sizes.cols, sizes.group, sizes.hidden, sizes.own_rows
    inputs = {
        "old_scaled": (old["scaled"], VMEM),
        "old_qkv": (old["qkv_grad"], VMEM),
    }
    outputs = {}
    scratch = {
        "jq_buf": GradJob.bufs(group, depth, D // planes, 3 * cols),
        "flips": [pltpu.VMEM((depth * (D // planes), group), BF16)] * 2,
        "jq_sem": GradJob.sems(depth),
        "pack_q0": pltpu.VMEM((peers, 1, rows, 3 * cols), BF16),
        "swap_q0": WeightSwap.sems(peers),
        "swap_q1": WeightSwap.sems(peers),
    }
    inputs["raw_q1"] = (raws[0]["raw_q"].reshape(peers, 1, rows, 3 * cols), VMEM)
    for l in range(LAYERS):
        inputs[f"raw_g{l}"] = (raws[l]["raw_g"].reshape(peers, 1, rows, 2 * hidden), VMEM)
        inputs[f"raw_o{l}"] = (raws[l]["raw_o"], VMEM)
        outputs[f"rows_g{l}"] = ((peers * rows, 2 * hidden), BF16, VMEM)
        outputs[f"rows_q{l}"] = ((peers * rows, 3 * cols), BF16, VMEM)
        outputs[f"rows_o{l}"] = ((rows, D), BF16, VMEM)
        scratch[f"swap_g{l}"] = WeightSwap.sems(peers)
        scratch[f"out_s{l}"] = dma(peers - 1)
        scratch[f"out_r{l}"] = dma()
        scratch[f"out_l{l}"] = dma()
    return launch(
        functools.partial(tail_body, sizes), "tail", inputs, outputs, scratch, collective_id
    )


def inverse_rms(values):
    return lax.rsqrt(jnp.mean(values * values, axis=-1, keepdims=True) + EPSILON)


def matmul(left, right):
    return jnp.dot(left, right, preferred_element_type=F32)


def contract_rows(left, right):
    return jnp.einsum("td,te->de", left, right, preferred_element_type=F32)


def contract_cols(left, right):
    return jnp.einsum("te,de->td", left, right, preferred_element_type=F32)


def local(
    tokens,
    gain_attn,
    w_query,
    w_key,
    w_value,
    w_out,
    gain_ffn,
    w_gate,
    w_up,
    w_down,
    doc_ids,
    cotangent,
):
    planes = lax.axis_size("head")
    peers = lax.axis_size("blk")
    plane = lax.axis_index("head")
    tok = tokens.shape[0]
    group = tok * peers
    stream_rows = group * planes
    doc_max = stream_rows // 4
    reach = (doc_max - 1 + group - 1) // group
    reach = reach + reach % 2
    own_rows = w_query.shape[1]
    cols = D // peers
    strip = w_down.shape[1]
    hidden_cols = strip * planes
    tile = 256
    chunk = 256
    lead = reach * group

    places = jnp.arange(stream_rows, dtype=jnp.int32)
    opens = jnp.concatenate([jnp.ones((1,), jnp.bool_), doc_ids[1:] != doc_ids[:-1]])
    starts = lax.cummax(jnp.where(opens, places, 0))
    first_place = lax.dynamic_slice_in_dim(starts, plane * group, group, 0) - (
        plane * group - lead
    )
    low = first_place[::tile] // chunk
    first_place = first_place[:, None]

    attn_rows = gain_attn.astype(F32)[:, :, None]
    ffn_rows = gain_ffn.astype(F32)[:, :, None]

    def for_peers(weight, gain):
        scaled = (weight.astype(F32) * gain).astype(BF16)
        return scaled.reshape(LAYERS, own_rows, peers, cols).transpose(2, 0, 1, 3)

    def for_peers_ffn(weight, gain):
        scaled = (weight.astype(F32) * gain).astype(BF16)
        scaled = scaled.reshape(LAYERS, own_rows, planes, peers, strip).transpose(3, 0, 1, 2, 4)
        return scaled.reshape(peers, LAYERS, own_rows, hidden_cols)

    weights = {
        "pack_q": jnp.concatenate(
            [for_peers(w, attn_rows) for w in (w_query, w_key, w_value)], axis=3
        ),
        "pack_g": jnp.concatenate([for_peers_ffn(w, ffn_rows) for w in (w_gate, w_up)], axis=3),
        "w_out": w_out,
        "w_down": w_down,
    }
    sizes = types.SimpleNamespace(
        peers=peers,
        planes=planes,
        tok=tok,
        cols=cols,
        group=group,
        hidden=hidden_cols,
        reach=reach,
        own_rows=own_rows,
        tile=tile,
        chunk=chunk,
        lead=lead,
        doc_max=doc_max,
    )
    first_row = first_place.reshape(1, group)
    stream = tokens.astype(F32)
    saved = []
    full = []
    for layer in range(LAYERS):
        kept = forward_layer(sizes, layer, stream, first_row, weights, 10 + layer)
        if layer == 0:
            weights = weights | {
                "mine_g": kept["mine_g"],
                "q_full": kept["q_full1"],
                "o_full": kept["out_full1"],
            }
            full.append((kept["q_full0"], kept["out_full0"], kept["g_full"], kept["d_full"]))
        else:
            full.append((weights["q_full"], weights["o_full"], kept["g_full"], kept["d_full"]))
        saved.append(kept | {"stream": stream})
        stream = kept["next"]
    output = stream.astype(BF16)

    grad = cotangent.astype(F32)
    fused = (D // planes) % 128 == 0 and strip % 128 == 0
    backs = [None] * LAYERS
    old = None
    for layer in reversed(range(LAYERS)):
        kept = saved[layer]
        back = backward_layer(
            sizes, layer, fused, grad, first_row, kept, full[layer], old, 12 + layer
        )
        grad = back["next"]
        old = {"scaled": kept["scaled"], "qkv_grad": back["qkv_grad"]}
        backs[layer] = back
    if fused:
        rows = tail(sizes, old, backs, 14)
        raw = jnp.stack(
            [jnp.concatenate([rows[f"rows_q{l}"], rows[f"rows_g{l}"]], axis=1) for l in range(LAYERS)]
        )
        raw = raw.reshape(LAYERS, peers, own_rows, 3 * cols + 2 * hidden_cols)
        raw = raw.transpose(1, 0, 2, 3).astype(F32)
        grad_out = jnp.stack([rows[f"rows_o{l}"] for l in range(LAYERS)]).astype(F32)
        grad_down = jnp.stack([back["raw_down"] for back in backs])
    else:
        raw, grad_out, grad_down = [], [], []
        for kept, back in zip(saved, backs):
            down_in = back["down_in"]
            proj_in = back["proj_in"]
            scatter = functools.partial(lax.psum_scatter, scatter_dimension=0, tiled=True)
            grad_down.append(
                scatter(contract_rows(kept["hidden"], down_in).astype(BF16), "head").astype(F32)
            )
            padded = lax.dynamic_update_slice(
                jnp.zeros((D, D), BF16),
                contract_rows(kept["mixed"], proj_in).astype(BF16),
                (lax.axis_index("blk") * cols, 0),
            )
            grad_out.append(scatter(padded, ("head", "blk")).astype(F32))
            pieces = [
                scatter(contract_rows(kept[name], right).astype(BF16), "head")
                for name, right in (
                    ("scaled", back["qkv_grad"]),
                    ("scaled_ffn", back["gate_up_grad"]),
                )
            ]
            raw.append(jnp.concatenate(pieces, axis=1))
        raw = jnp.stack(raw).reshape(LAYERS, peers, own_rows, 3 * cols + 2 * hidden_cols)
        raw = plane_swap(raw.transpose(1, 0, 2, 3), 1, "rows_swap").astype(F32)
        grad_out, grad_down = jnp.stack(grad_out), jnp.stack(grad_down)

    def attn_rows_of(which):
        piece = raw[:, :, :, which * cols : (which + 1) * cols]
        return piece.transpose(1, 2, 0, 3).reshape(LAYERS, own_rows, D)

    def ffn_rows_of(which):
        begin = 3 * cols + which * hidden_cols
        piece = raw[:, :, :, begin : begin + hidden_cols]
        piece = piece.reshape(peers, LAYERS, own_rows, planes, strip).transpose(1, 2, 3, 0, 4)
        return piece.reshape(LAYERS, own_rows, peers * hidden_cols)

    raw_query, raw_key, raw_value = (attn_rows_of(which) for which in range(3))
    raw_gate, raw_up = (ffn_rows_of(which) for which in range(2))

    def gain_grad(*pairs):
        return sum(jnp.sum(weight.astype(F32) * raw_part, axis=2) for weight, raw_part in pairs)

    grad_gain_attn = gain_grad((w_query, raw_query), (w_key, raw_key), (w_value, raw_value))
    grad_gain_ffn = gain_grad((w_gate, raw_gate), (w_up, raw_up))
    return (
        output,
        grad,
        grad_gain_attn,
        raw_query * attn_rows,
        raw_key * attn_rows,
        raw_value * attn_rows,
        grad_out,
        grad_gain_ffn,
        raw_gate * ffn_rows,
        raw_up * ffn_rows,
        grad_down,
    )


def solution(mesh):
    rows = P(("head", "blk"), None)
    vector = P(None, ("head", "blk"))
    matrix = P(None, ("head", "blk"), None)
    return jax.shard_map(
        local,
        mesh=mesh,
        in_specs=(
            rows,
            vector,
            matrix,
            matrix,
            matrix,
            matrix,
            vector,
            matrix,
            matrix,
            matrix,
            P(),
            rows,
        ),
        out_specs=(
            rows,
            rows,
            vector,
            matrix,
            matrix,
            matrix,
            matrix,
            vector,
            matrix,
            matrix,
            matrix,
        ),
        check_vma=False,
    )
```

```python
import functools
import math
import types

import jax
import jax.numpy as jnp
from jax import lax
from jax.experimental import pallas as pl
from jax.experimental.pallas import tpu as pltpu
from jax.sharding import PartitionSpec as P

D = 1024
HD = 64
HEADS = D // HD
LAYERS = 2
EPSILON = 1e-05
MASKED = -1e30
MESH = pl.DeviceIdType.MESH
F32 = jnp.float32
BF16 = jnp.bfloat16
ANY = pl.BlockSpec(memory_space=pl.ANY)


def greet_blk(count):
    me = lax.axis_index("blk")
    barrier = pltpu.get_barrier_semaphore()
    for step in range(1, count):
        pl.semaphore_signal(
            barrier,
            inc=1,
            device_id={"blk": lax.rem(me + step, count)},
            device_id_type=MESH,
        )
    pl.semaphore_wait(barrier, count - 1)
    return me


def plane_gather_kernel(count, x_ref, o_ref, send_sem, recv_sem, local_sem):
    me = greet_blk(count)
    copies = []
    for step in range(1, count):
        copy = pltpu.make_async_remote_copy(
            src_ref=x_ref,
            dst_ref=o_ref.at[me],
            send_sem=send_sem.at[step - 1],
            recv_sem=recv_sem.at[step - 1],
            device_id={"blk": lax.rem(me + step, count)},
            device_id_type=MESH,
        )
        copy.start()
        copies.append(copy)
    own = pltpu.make_async_copy(x_ref, o_ref.at[me], local_sem)
    own.start()
    own.wait()
    for copy in copies:
        copy.wait()


def plane_swap_kernel(count, x_ref, o_ref, send_sem, recv_sem, local_sem):
    me = greet_blk(count)
    copies = []
    for step in range(1, count):
        peer = lax.rem(me + step, count)
        copy = pltpu.make_async_remote_copy(
            src_ref=x_ref.at[peer],
            dst_ref=o_ref.at[me],
            send_sem=send_sem.at[step - 1],
            recv_sem=recv_sem.at[step - 1],
            device_id={"blk": peer},
            device_id_type=MESH,
        )
        copy.start()
        copies.append(copy)
    own = pltpu.make_async_copy(x_ref.at[me], o_ref.at[me], local_sem)
    own.start()
    own.wait()
    for copy in copies:
        copy.wait()


def plane_call(kernel, x, out_shape, collective_id, name):
    count = lax.axis_size("blk")
    return pl.pallas_call(
        functools.partial(kernel, count),
        out_shape=jax.ShapeDtypeStruct(out_shape, x.dtype),
        in_specs=[ANY],
        out_specs=ANY,
        scratch_shapes=[
            pltpu.SemaphoreType.DMA((count - 1,)),
            pltpu.SemaphoreType.DMA((count - 1,)),
            pltpu.SemaphoreType.DMA,
        ],
        compiler_params=pltpu.CompilerParams(collective_id=collective_id, has_side_effects=True),
        cost_estimate=pl.CostEstimate(flops=0, bytes_accessed=20_000_000, transcendentals=0),
        name=name,
    )(x)


def plane_gather(x, collective_id, name):
    return plane_call(
        plane_gather_kernel, x, (lax.axis_size("blk"),) + x.shape, collective_id, name
    )


def plane_swap(x, collective_id, name):
    return plane_call(plane_swap_kernel, x, x.shape, collective_id, name)


def launch(body, name, inputs, outputs, scratch, collective_id, flops=0):
    names = list(inputs) + list(outputs)
    flat = []
    for value in scratch.values():
        flat.extend(value if isinstance(value, list) else [value])

    def kernel(*refs):
        named = dict(zip(names, refs))
        rest = list(refs[len(names) :])
        for name, value in scratch.items():
            if isinstance(value, list):
                named[name], rest = rest[: len(value)], rest[len(value) :]
            else:
                named[name], rest = rest[0], rest[1:]
        body(types.SimpleNamespace(**named))

    results = pl.pallas_call(
        kernel,
        out_shape=[jax.ShapeDtypeStruct(shape, dtype) for shape, dtype, _ in outputs.values()],
        in_specs=[spec for _, spec in inputs.values()],
        out_specs=[spec for _, _, spec in outputs.values()],
        scratch_shapes=flat,
        compiler_params=pltpu.CompilerParams(
            collective_id=collective_id, has_side_effects=True, vmem_limit_bytes=60 << 20
        ),
        cost_estimate=pl.CostEstimate(
            flops=flops, bytes_accessed=200_000_000, transcendentals=0
        ),
        name=name,
    )(*[array for array, _ in inputs.values()])
    return dict(zip(outputs, results))


VMEM = pl.BlockSpec(memory_space=pltpu.VMEM)


def dma(*shape):
    return pltpu.SemaphoreType.DMA(shape)


def remote(src, dst, send_sem, recv_sem, **place):
    return pltpu.make_async_remote_copy(
        src_ref=src,
        dst_ref=dst,
        send_sem=send_sem,
        recv_sem=recv_sem,
        device_id=place,
        device_id_type=MESH,
    )


class Place:
    def __init__(self):
        self.peers = lax.axis_size("blk")
        self.planes = lax.axis_size("head")
        self.depth = self.planes // 2
        self.peer = lax.axis_index("blk")
        self.plane = lax.axis_index("head")
        self.z = lax.div(self.plane, 2)
        self.core = lax.rem(self.plane, 2)
        self.sibling = self.plane + 1 - 2 * self.core


    def moved(self, step, sign):
        half = self.peers // 2
        low, high = (step % 2, step // 2) if isinstance(step, int) else (lax.rem(step, 2), lax.div(step, 2))
        bit = lax.rem(lax.rem(self.peer, 2) + low, 2)
        return bit + 2 * lax.rem(lax.div(self.peer, 2) + sign * high + half, half)

    def peer_after(self, step):
        return self.moved(step, 1)

    def peer_before(self, step):
        return self.moved(step, -1)

    def steps_between(self, early, late):
        half = self.peers // 2
        bit = lax.rem(lax.rem(early, 2) + lax.rem(late, 2), 2)
        return bit + 2 * lax.rem(lax.div(late, 2) - lax.div(early, 2) + half, half)

    def z_after(self, step):
        return lax.rem(self.z + step, self.depth)

    def z_before(self, step):
        return lax.rem(self.z + self.depth - step, self.depth)

    def greet(self):
        barrier = pltpu.get_barrier_semaphore()
        for step in range(1, self.peers):
            pl.semaphore_signal(
                barrier, inc=1, device_id={"blk": self.peer_after(step)}, device_id_type=MESH
            )
        for step in range(1, self.depth):
            pl.semaphore_signal(
                barrier,
                inc=1,
                device_id={"head": 2 * self.z_after(step) + self.core},
                device_id_type=MESH,
            )
        pl.semaphore_signal(barrier, inc=1, device_id={"head": self.sibling}, device_id_type=MESH)
        pl.semaphore_wait(barrier, self.peers - 1 + self.depth - 1 + 1)


class PlaneGather:
    def __init__(self, place, flat, send, recv):
        self.place, self.flat, self.send, self.recv = place, flat, send, recv
        self.rows = flat.shape[0] // place.peers

    def slot(self, peer):
        return self.flat.at[pl.ds(pl.multiple_of(peer * self.rows, self.rows), self.rows)]

    def copy(self, step):
        own = self.slot(self.place.peer)
        return remote(
            own,
            own,
            self.send.at[step - 1],
            self.recv.at[step - 1],
            blk=self.place.peer_after(step),
        )

    def start(self):
        for step in range(1, self.place.peers):
            self.copy(step).start()

    def await_step(self, step):
        if step:
            source = self.place.peer_before(step)
            remote(
                self.slot(source),
                self.slot(source),
                self.send.at[step - 1],
                self.recv.at[step - 1],
                blk=source,
            ).wait_recv()

    def finish(self):
        for step in range(1, self.place.peers):
            self.copy(step).wait_send()


def peer_groups(peers):
    return [(0,), (1, 2)] + [(step,) for step in range(3, peers)] if peers > 2 else [(0,), (1,)]


class PlaneSum:
    def __init__(self, place, src, dst, send, recv):
        self.place, self.src, self.dst, self.send, self.recv = place, src, dst, send, recv

    def copy_to(self, peer):
        index = jnp.maximum(self.place.steps_between(peer, self.place.peer) - 1, 0)
        return remote(
            self.src.at[peer],
            self.dst.at[self.place.peer],
            self.send.at[index],
            self.recv.at[index],
            blk=peer,
        )

    def send_to(self, peer):
        @pl.when(peer != self.place.peer)
        def _():
            self.copy_to(peer).start()

    def total(self):
        total = self.src[self.place.peer].astype(F32)
        for step in range(1, self.place.peers):
            source = self.place.peer_after(step)
            remote(
                self.src.at[source],
                self.dst.at[source],
                self.send.at[step - 1],
                self.recv.at[step - 1],
                blk=source,
            ).wait_recv()
            total = total + self.dst[source].astype(F32)
        return total

    def finish(self):
        for step in range(1, self.place.peers):
            self.copy_to(self.place.peer_before(step)).wait_send()


class HeadGather:
    def __init__(self, place, src, full, sems):
        self.place, self.src, self.full = place, src, full
        self.z_send, self.z_recv, self.s_send, self.s_recv, self.local, self.r_send = sems
        self.line = place.depth == 4

    @staticmethod
    def sems(depth):
        return [dma(depth - 1), dma(depth - 1), dma(depth), dma(depth), dma(), dma()]

    def slot(self, z, core):
        rows = self.src.shape[0]
        return self.full.at[pl.ds(pl.multiple_of((2 * z + core) * rows, rows), rows)]

    def z_copy(self, step):
        return remote(
            self.src,
            self.slot(self.place.z, self.place.core),
            self.z_send.at[step - 1],
            self.z_recv.at[step - 1],
            head=2 * self.place.z_after(step) + self.place.core,
        )

    def near(self, step):
        z = self.place.z
        if not self.line or step == 2:
            return z >= 0
        return z < 3 if step == 1 else z > 0

    def relays(self, which):
        return self.place.z == (2 if which == 3 else 1)

    def relay_copy(self, which):
        where = self.slot(self.place.z_before(2), self.place.core)
        return remote(
            where,
            where,
            self.r_send,
            self.z_recv.at[which - 1],
            head=2 * (3 if which == 3 else 0) + self.place.core,
        )

    def s_copy(self, step, core):
        z = self.place.z_before(step)
        where = self.slot(z, core)
        return remote(
            self.src if step == 0 else where,
            where,
            self.s_send.at[step],
            self.s_recv.at[step],
            head=self.place.sibling,
        )

    def own_copy(self):
        return pltpu.make_async_copy(
            self.src, self.slot(self.place.z, self.place.core), self.local
        )

    def start(self):
        for step in sorted(range(1, self.place.depth), key=lambda k: k != 2):

            @pl.when(self.near(step))
            def _(step=step):
                self.z_copy(step).start()

        self.s_copy(0, self.place.core).start()
        self.own_copy().start()

    def await_z(self, step):
        where = self.slot(self.place.z_before(step), self.place.core)
        remote(
            self.src,
            where,
            self.z_send.at[step - 1],
            self.z_recv.at[step - 1],
            head=self.place.sibling,
        ).wait_recv()

    def relay(self):
        if self.line:
            self.await_z(2)
            for which in (1, 3):

                @pl.when(self.relays(which))
                def _(which=which):
                    self.relay_copy(which).start()

            self.s_copy(2, self.place.core).start()

    def forward(self):
        for step in range(1, self.place.depth):
            if not (self.line and step == 2):
                self.await_z(step)
                self.s_copy(step, self.place.core).start()

    def arrive(self):
        self.own_copy().wait()
        for step in range(self.place.depth):
            self.s_copy(step, 1 - self.place.core).wait_recv()

    def finish(self):
        for step in range(1, self.place.depth):

            @pl.when(self.near(step))
            def _(step=step):
                self.z_copy(step).wait_send()

        if self.line:
            for which in (1, 3):

                @pl.when(self.relays(which))
                def _(which=which):
                    self.relay_copy(which).wait_send()

        for step in range(self.place.depth):
            self.s_copy(step, self.place.core).wait_send()


class OutGather:
    def __init__(self, place, src, mine, full, sems):
        self.place, self.src, self.mine, self.full = place, src, mine, full
        (
            self.p_send,
            self.p_recv,
            self.z_send,
            self.z_recv,
            self.s_send,
            self.s_recv,
            self.local,
        ) = sems

    @staticmethod
    def sems(peers, depth):
        return [dma(peers - 1), dma(peers - 1), dma(depth - 1), dma(), dma(), dma(), dma()]

    def piece(self, peer):
        rows = self.src.shape[0]
        return self.mine.at[pl.ds(pl.multiple_of(peer * rows, rows), rows)]

    def half(self, core):
        rows = self.mine.shape[0]
        return self.full.at[pl.ds(pl.multiple_of(core * rows, rows), rows)]

    def home(self):
        return self.place.peer == self.place.z

    def step_to_home(self):
        return self.place.steps_between(self.place.peer, self.place.z)

    def p_copy(self):
        index = jnp.maximum(self.step_to_home() - 1, 0)
        return remote(
            self.src,
            self.piece(self.place.peer),
            self.p_send.at[index],
            self.p_recv.at[index],
            blk=self.place.z,
        )

    def own_copy(self):
        return pltpu.make_async_copy(self.src, self.piece(self.place.peer), self.local)

    def start(self):
        @pl.when(self.home())
        def _():
            self.own_copy().start()

        @pl.when(jnp.logical_not(self.home()))
        def _():
            self.p_copy().start()

    def z_copy(self, step):
        return remote(
            self.mine,
            self.half(self.place.core),
            self.z_send.at[step - 1],
            self.z_recv,
            head=2 * self.place.z_after(step) + self.place.core,
        )

    def s_copy(self, core):
        return remote(
            self.half(core), self.half(core), self.s_send, self.s_recv, head=self.place.sibling
        )

    def spread(self):
        @pl.when(self.home())
        def _():
            self.own_copy().wait()
            for step in range(1, self.place.peers):
                source = self.place.peer_before(step)
                remote(
                    self.src,
                    self.piece(source),
                    self.p_send.at[step - 1],
                    self.p_recv.at[step - 1],
                    blk=source,
                ).wait_recv()
            for step in range(1, self.place.depth):
                self.z_copy(step).start()
            pltpu.make_async_copy(self.mine, self.half(self.place.core), self.local).start()

    def forward(self):
        @pl.when(self.home())
        def _():
            pltpu.make_async_copy(self.mine, self.half(self.place.core), self.local).wait()

        @pl.when(jnp.logical_not(self.home()))
        def _():
            remote(
                self.mine,
                self.half(self.place.core),
                self.z_send.at[0],
                self.z_recv,
                head=self.place.sibling,
            ).wait_recv()

        self.s_copy(self.place.core).start()

    def arrive(self):
        self.s_copy(1 - self.place.core).wait_recv()

    def finish(self):
        @pl.when(self.home())
        def _():
            for step in range(1, self.place.depth):
                self.z_copy(step).wait_send()

        @pl.when(jnp.logical_not(self.home()))
        def _():
            self.p_copy().wait_send()

        self.s_copy(self.place.core).wait_send()


class WeightSwap:
    def __init__(self, place, src, layer, mine, sems):
        self.place, self.src, self.layer, self.mine = place, src, layer, mine
        self.send, self.recv, self.local = sems

    @staticmethod
    def sems(peers):
        return [dma(peers - 1), dma(peers - 1), dma()]

    def piece(self, peer):
        rows = self.src.shape[2]
        return self.mine.at[pl.ds(pl.multiple_of(peer * rows, rows), rows)]

    def copy(self, step):
        target = self.place.peer_after(step)
        return remote(
            self.src.at[target, self.layer],
            self.piece(self.place.peer),
            self.send.at[step - 1],
            self.recv.at[step - 1],
            blk=target,
        )

    def own_copy(self):
        return pltpu.make_async_copy(
            self.src.at[self.place.peer, self.layer], self.piece(self.place.peer), self.local
        )

    def start(self):
        for step in range(1, self.place.peers):
            self.copy(step).start()
        self.own_copy().start()

    def arrive(self):
        self.own_copy().wait()
        for step in range(1, self.place.peers):
            source = self.place.peer_before(step)
            remote(
                self.src.at[source, self.layer],
                self.piece(source),
                self.send.at[step - 1],
                self.recv.at[step - 1],
                blk=source,
            ).wait_recv()

    def finish(self):
        for step in range(1, self.place.peers):
            self.copy(step).wait_send()


class Halo:
    def __init__(self, place, keys, reach, sems):
        self.place, self.keys, self.reach = place, keys, reach
        self.rows = keys.shape[0] // (reach + 1)
        self.z_send, self.z_recv, self.s_send, self.s_recv = sems

    def block(self, offset):
        return self.keys.at[pl.ds((self.reach - offset) * self.rows, self.rows)]

    @staticmethod
    def sems(reach):
        return [dma(reach // 2), dma(reach // 2), dma(reach // 2), dma(reach // 2)]

    def z_copy(self, hop):
        return remote(
            self.block(0),
            self.block(2 * hop),
            self.z_send.at[hop - 1],
            self.z_recv.at[hop - 1],
            head=self.place.plane + 2 * hop,
        )

    def sends(self, hop):
        return self.place.z + hop < self.place.depth

    def receives(self, hop):
        return self.place.z - hop >= 0

    def start(self):
        for hop in range(1, self.reach // 2 + 1):

            @pl.when(self.sends(hop))
            def _(hop=hop):
                self.z_copy(hop).start()


    def hand(self, i):
        def copy(offset):
            return remote(
                self.block(offset),
                self.block(2 * i - 1),
                self.s_send.at[i - 1],
                self.s_recv.at[i - 1],
                head=self.place.sibling,
            )

        return copy

    def hand_ready(self, i):
        return (
            (self.place.core == 1) & self.receives(i),
            (self.place.core == 0) & self.receives(i - 1),
        )

    def relay(self):
        for i in range(1, self.reach // 2 + 1):
            from_one, from_zero = self.hand_ready(i)
            if i == 1:

                @pl.when(from_zero)
                def _(i=i):
                    self.hand(i)(2 * i - 2).start()

            @pl.when(self.receives(i))
            def _(i=i):
                remote(
                    self.block(0),
                    self.block(2 * i),
                    self.z_send.at[i - 1],
                    self.z_recv.at[i - 1],
                    head=self.place.sibling,
                ).wait_recv()

            @pl.when(from_one)
            def _(i=i):
                self.hand(i)(2 * i).start()

            if i < self.reach // 2:

                @pl.when(self.hand_ready(i + 1)[1])
                def _(i=i):
                    self.hand(i + 1)(2 * i).start()

    def arrive(self):
        for i in range(1, self.reach // 2 + 1):

            @pl.when(self.place.z - i + self.place.core >= 0)
            def _(i=i):
                self.hand(i)(0).wait_recv()

    def finish(self):
        for hop in range(1, self.reach // 2 + 1):

            @pl.when(self.sends(hop))
            def _(hop=hop):
                self.z_copy(hop).wait_send()

            from_one, from_zero = self.hand_ready(hop)

            @pl.when(from_one)
            def _(hop=hop):
                self.hand(hop)(2 * hop).wait_send()

            @pl.when(from_zero)
            def _(hop=hop):
                self.hand(hop)(2 * hop - 2).wait_send()


def columns(total, most=256):
    width = math.gcd(total, most)
    return total // width, width


def by_columns(total, step, most=256):
    count, width = columns(total, most)

    def body(index, carry):
        step(pl.ds(pl.multiple_of(index * width, width), width))
        return carry

    lax.fori_loop(0, count, body, 0)


def attend_tile(sizes, place, tile_index, q_ref, keys_ref, first_ref, mixed_ref, attended_ref, log_ref):
    tile, chunk, cols, group, lead = sizes.tile, sizes.chunk, sizes.cols, sizes.group, sizes.lead
    row = pl.multiple_of(tile_index * tile, tile)
    rows = pl.ds(row, tile)
    first = first_ref[:, rows]
    last = lead + row + lax.broadcasted_iota(jnp.int32, (1, tile), 1)
    lane = lax.broadcasted_iota(jnp.int32, (tile, 2 * HD), 1)
    lowest = jnp.maximum(lead + row - (sizes.doc_max - 1), lead - place.plane * group)
    begin = lax.div(jnp.maximum(lowest, 0), chunk)
    end = lax.div(lead + row + tile + chunk - 1, chunk)
    for pair in range(cols // (2 * HD)):
        lanes = slice(pair * 2 * HD, (pair + 1) * 2 * HD)
        value_lanes = slice(cols + pair * 2 * HD, cols + (pair + 1) * 2 * HD)
        queries = q_ref[rows, lanes] * jnp.asarray(HD ** (-0.5), BF16)
        zero = jnp.zeros_like(queries)
        halves = [jnp.where(lane < HD, queries, zero), jnp.where(lane >= HD, queries, zero)]

        def step(block, state, lanes=lanes, value_lanes=value_lanes, halves=halves):
            offset = pl.multiple_of(block * chunk, chunk)
            keys = keys_ref[pl.ds(offset, chunk), lanes]
            values = keys_ref[pl.ds(offset, chunk), value_lanes]
            spot = offset + lax.broadcasted_iota(jnp.int32, (chunk, tile), 0)
            allowed = (spot >= first) & (spot <= last)
            out = []
            for half, (top, total, accum) in zip(halves, state):
                scores = jnp.where(allowed, dot_nt(keys, half), MASKED)
                new_top = jnp.maximum(top, jnp.max(scores, axis=0, keepdims=True))
                factor = jnp.exp(top - new_top)
                weights = jnp.exp(scores - new_top)
                total = total * factor + jnp.sum(weights, axis=0, keepdims=True)
                accum = accum * factor + dot_tn(values, weights.astype(BF16))
                out.append((new_top, total, accum))
            return tuple(out)

        start = (
            jnp.full((1, tile), MASKED, F32),
            jnp.zeros((1, tile), F32),
            jnp.zeros((2 * HD, tile), F32),
        )
        state = lax.fori_loop(begin, end, step, (start, start))
        parts = []
        for which, (top, total, accum) in enumerate(state):
            log_ref[2 * pair + which : 2 * pair + which + 1, rows] = top + jnp.log(total)
            parts.append(accum[which * HD : (which + 1) * HD] / total)
        attended = jnp.transpose(jnp.concatenate(parts, axis=0))
        attended_ref[rows, lanes] = attended
        mixed_ref[rows, lanes] = attended.astype(BF16)


def forward_body(sizes, layer, refs):
    place = Place()
    tok, cols, group, hidden = sizes.tok, sizes.cols, sizes.group, sizes.hidden
    tile = sizes.tile
    place.greet()
    loads = refs.load_sem
    gathers = []
    swaps = []
    if layer == 0:
        swap_q = [
            WeightSwap(place, refs.pack_q, l, refs.mine_q.at[l], getattr(refs, f"swap_q{l}"))
            for l in range(LAYERS)
        ]
        swap_g = [
            WeightSwap(place, refs.pack_g, l, refs.mine_g.at[l], getattr(refs, f"swap_g{l}"))
            for l in range(LAYERS)
        ]
        out_w = [
            OutGather(
                place,
                refs.w_out.at[l],
                refs.mine_o.at[l],
                getattr(refs, f"out_full{l}"),
                getattr(refs, f"out_sem{l}"),
            )
            for l in range(LAYERS)
        ]
        gather_q = [
            HeadGather(
                place, refs.mine_q.at[l], getattr(refs, f"q_full{l}"), getattr(refs, f"gq_sem{l}")
            )
            for l in range(LAYERS)
        ]
        gather_g = HeadGather(place, refs.mine_g.at[0], refs.g_full, refs.gg_sem)
        swap_q[0].start()
    else:
        gather_g = HeadGather(place, refs.mine_g.at[layer], refs.g_full, refs.gg_sem)
    gather_d = HeadGather(place, refs.w_down.at[layer], refs.d_full, refs.gd_sem)

    stream = refs.stream[...]
    scaled = (stream * inverse_rms(stream)).astype(BF16)
    own_rows = pl.ds(pl.multiple_of(place.peer * tok, tok), tok)
    refs.scaled[own_rows, :] = scaled
    ag1 = PlaneGather(place, refs.scaled, refs.ag1_s, refs.ag1_r)
    ag1.start()
    if layer == 0:
        out_w[0].start()
        swap_g[0].start()
        swap_q[0].arrive()
        gather_q[0].start()
        out_w[0].spread()
        gather_d.start()
        gather_q[0].relay()
        gather_q[0].forward()
        gather_q[0].arrive()
    else:
        gather_d.start()
    q_load = pltpu.make_async_copy(refs.q_full0 if layer == 0 else refs.q_full, refs.wq, loads.at[0])
    q_load.start()
    q_load.wait()

    for steps in peer_groups(place.peers):
        peers = [place.peer_before(step) for step in steps]
        rows = [pl.ds(pl.multiple_of(peer * tok, tok), tok) for peer in peers]
        for step in steps:
            ag1.await_step(step)
        x = jnp.concatenate([refs.scaled[where, :] for where in rows], axis=0)
        for part in range(3):

            def block(where, part=part, x=x, peers=peers, rows=rows):
                weight = refs.wq[
                    :, pl.ds(pl.multiple_of(part * cols + where.start, where.size), where.size)
                ]
                value = dot_nn(x, weight).astype(BF16)
                there = pl.ds(
                    pl.multiple_of(max(part - 1, 0) * cols + where.start, where.size), where.size
                )
                for index, peer in enumerate(peers):
                    piece = value[index * tok : (index + 1) * tok]
                    if part == 0:
                        refs.queries[rows[index], there] = piece
                    else:
                        spot = pl.multiple_of(sizes.lead + peer * tok, tok)
                        refs.keys[pl.ds(spot, tok), there] = piece

            by_columns(cols, block)
    halo = Halo(place, refs.keys, sizes.reach, refs.halo_sem)
    gather_d.relay()
    halo.start()
    if layer == 0:
        swap_g[0].arrive()
        gather_g.start()
        swap_q[1].start()
        out_w[1].start()
        swap_g[1].start()
    else:
        gather_g.start()
    halo.relay()
    halo.arrive()

    if layer == 0:
        out_w[0].forward()
        out_w[0].arrive()
    o_load = pltpu.make_async_copy(
        refs.out_full0 if layer == 0 else refs.o_full, refs.wo, loads.at[1]
    )
    o_load.start()
    o_load.wait()

    sum1 = PlaneSum(place, refs.part1, refs.sum1, refs.rs1_s, refs.rs1_r)

    def attend_step(index, carry):
        attend_tile(
            sizes,
            place,
            index,
            refs.queries,
            refs.keys,
            refs.first,
            refs.mixed,
            refs.attended,
            refs.logs,
        )
        for k in range(tile // tok):
            peer = index * (tile // tok) + k
            x = refs.mixed[pl.ds(pl.multiple_of(peer * tok, tok), tok), :]

            def block(where, x=x, peer=peer):
                refs.part1[peer, :, where] = dot_nn(x, refs.wo[:, where]).astype(BF16)

            by_columns(D, block)
            sum1.send_to(peer)
        return carry

    lax.fori_loop(0, group // tile, attend_step, 0)

    gather_g.relay()
    gather_d.forward()
    gather_g.forward()
    gather_g.arrive()
    gather_d.arrive()
    g_load = pltpu.make_async_copy(refs.g_full, refs.wg, loads.at[2])
    d_load = pltpu.make_async_copy(refs.d_full, refs.wd, loads.at[3])
    g_load.start()
    d_load.start()
    if layer == 0:
        swap_q[1].arrive()
        gather_q[1].start()
        out_w[1].spread()
        swap_g[1].arrive()

    middle = stream + sum1.total()
    refs.middle[...] = middle
    refs.scaled_ffn[own_rows, :] = (middle * inverse_rms(middle)).astype(BF16)
    ag2 = PlaneGather(place, refs.scaled_ffn, refs.ag2_s, refs.ag2_r)
    ag2.start()
    g_load.wait()
    d_load.wait()
    sum2 = PlaneSum(place, refs.part2, refs.sum2, refs.rs2_s, refs.rs2_r)

    stores = []
    for steps in peer_groups(place.peers):
        peers = [place.peer_before(step) for step in steps]
        rows = [pl.ds(pl.multiple_of(peer * tok, tok), tok) for peer in peers]
        for step in steps:
            ag2.await_step(step)
        x = jnp.concatenate([refs.scaled_ffn[where, :] for where in rows], axis=0)

        def block(where, x=x, rows=rows):
            there = pl.ds(pl.multiple_of(hidden + where.start, where.size), where.size)
            gate = dot_nn(x, refs.wg[:, where])
            up = dot_nn(x, refs.wg[:, there])
            low = (gate / (1.0 + jnp.exp(-gate)) * up).astype(BF16)
            for index, row in enumerate(rows):
                piece = slice(index * tok, (index + 1) * tok)
                refs.gate_up[row, where] = gate[piece]
                refs.gate_up[row, there] = up[piece]
                refs.hidden[row, where] = low[piece]

        by_columns(hidden, block)
        low = jnp.concatenate([refs.hidden[where, :] for where in rows], axis=0)

        def down(where, low=low, peers=peers):
            value = dot_nn(low, refs.wd[:, where]).astype(BF16)
            for index, peer in enumerate(peers):
                refs.part2[peer, :, where] = value[index * tok : (index + 1) * tok]

        by_columns(D, down)
        for step, peer, row in zip(steps, peers, rows):
            sum2.send_to(peer)
            store = pltpu.make_async_copy(
                refs.gate_up.at[row], refs.gate_up_out.at[row], refs.store_sem.at[step]
            )
            store.start()
            stores.append(store)
    if layer == 0:
        gather_q[1].relay()
        gather_q[1].forward()
        out_w[1].forward()
    refs.next[...] = middle + sum2.total()
    if layer == 0:
        gather_q[1].arrive()
        out_w[1].arrive()
        for item in swap_q + swap_g + gather_q + out_w:
            item.finish()
    for store in stores:
        store.wait()
    for item in (ag1, ag2, sum1, sum2, gather_g, gather_d, halo):
        item.finish()


def forward_layer(sizes, layer, stream, first_row, weights, collective_id):
    peers, planes, depth = sizes.peers, sizes.planes, sizes.planes // 2
    tok, cols, group, hidden, reach = sizes.tok, sizes.cols, sizes.group, sizes.hidden, sizes.reach
    inputs = {"stream": (stream, VMEM), "first": (first_row, VMEM), "w_down": (weights["w_down"], VMEM)}
    outputs = {
        "next": ((tok, D), F32, VMEM),
        "middle": ((tok, D), F32, VMEM),
        "scaled": ((group, D), BF16, VMEM),
        "scaled_ffn": ((group, D), BF16, VMEM),
        "queries": ((group, cols), BF16, VMEM),
        "keys": (((reach + 1) * group, 2 * cols), BF16, VMEM),
        "mixed": ((group, cols), BF16, VMEM),
        "attended": ((group, cols), F32, VMEM),
        "logs": ((cols // HD, group), F32, VMEM),
        "gate_up_out": ((group, 2 * hidden), F32, ANY),
        "hidden": ((group, hidden), BF16, VMEM),
        "g_full": ((D, 2 * hidden), BF16, ANY),
        "d_full": ((hidden, D), BF16, ANY),
    }
    scratch = {
        "wq": pltpu.VMEM((D, 3 * cols), BF16),
        "wo": pltpu.VMEM((cols, D), BF16),
        "wg": pltpu.VMEM((D, 2 * hidden), BF16),
        "wd": pltpu.VMEM((hidden, D), BF16),
        "gate_up": pltpu.VMEM((group, 2 * hidden), F32),
        "store_sem": dma(peers),
        "part1": pltpu.VMEM((peers, tok, D), BF16),
        "sum1": pltpu.VMEM((peers, tok, D), BF16),
        "part2": pltpu.VMEM((peers, tok, D), BF16),
        "sum2": pltpu.VMEM((peers, tok, D), BF16),
        "load_sem": dma(4),
        "halo_sem": Halo.sems(reach),
        "gg_sem": HeadGather.sems(depth),
        "gd_sem": HeadGather.sems(depth),
    }
    for name in ("ag1_s", "ag1_r", "ag2_s", "ag2_r", "rs1_s", "rs1_r", "rs2_s", "rs2_r"):
        scratch[name] = dma(peers - 1)
    if layer == 0:
        rows = peers * sizes.own_rows
        inputs["pack_q"] = (weights["pack_q"], ANY)
        inputs["pack_g"] = (weights["pack_g"], ANY)
        inputs["w_out"] = (weights["w_out"], ANY)
        outputs["mine_q"] = ((LAYERS, rows, 3 * cols), BF16, VMEM)
        outputs["mine_g"] = ((LAYERS, rows, 2 * hidden), BF16, VMEM)
        outputs["mine_o"] = ((LAYERS, rows, D), BF16, VMEM)
        for l in range(LAYERS):
            outputs[f"q_full{l}"] = ((D, 3 * cols), BF16, ANY)
            outputs[f"out_full{l}"] = ((cols, D), BF16, ANY)
            scratch[f"swap_q{l}"] = WeightSwap.sems(peers)
            scratch[f"swap_g{l}"] = WeightSwap.sems(peers)
            scratch[f"out_sem{l}"] = OutGather.sems(peers, depth)
            scratch[f"gq_sem{l}"] = HeadGather.sems(depth)
    else:
        inputs["mine_g"] = (weights["mine_g"], VMEM)
        inputs["q_full"] = (weights["q_full"], ANY)
        inputs["o_full"] = (weights["o_full"], ANY)
    return launch(
        functools.partial(forward_body, sizes, layer),
        f"forward{layer}",
        inputs,
        outputs,
        scratch,
        collective_id,
        flops=group * D * (4 * cols + 3 * hidden) * 2,
    )


def dot_nt(left, right):
    return lax.dot_general(left, right, (((1,), (1,)), ((), ())), preferred_element_type=F32)


def dot_nn(left, right):
    return lax.dot_general(left, right, (((1,), (0,)), ((), ())), preferred_element_type=F32)


def dot_tn(left, right):
    return lax.dot_general(left, right, (((0,), (0,)), ((), ())), preferred_element_type=F32)


class HaloBack:
    def __init__(self, place, total, give, land, s_land, reach, sems):
        self.place, self.total, self.give, self.land, self.s_land = place, total, give, land, s_land
        self.reach = reach
        self.rows, self.width = land.shape[1:]
        self.z_send, self.z_recv, self.s_send, self.s_recv = sems

    def block(self, ref, offset):
        return ref.at[self.reach - offset]

    def lanes(self, offset):
        return slice((self.reach - offset) * self.width, (self.reach - offset + 1) * self.width)

    def hand_copy(self, i):
        return remote(
            self.block(self.give, 2 * i - 1),
            self.s_land.at[i - 1],
            self.s_send.at[i - 1],
            self.s_recv.at[i - 1],
            head=self.place.sibling,
        )

    def hands(self, i):
        return self.place.z - i + self.place.core >= 0

    def handed(self, i):
        return self.place.z - i + 1 - self.place.core >= 0

    def low(self, offset):
        self.give[self.reach - offset] = self.total[:, self.lanes(offset)].astype(BF16)

    def hand(self):
        for i in range(1, self.reach // 2 + 1):

            @pl.when(self.hands(i))
            def _(i=i):
                self.low(2 * i - 1)
                self.hand_copy(i).start()

    def add(self, i, offset):
        where = self.lanes(offset)
        self.total[:, where] = self.total[:, where] + self.s_land[i - 1].astype(F32)

    def z_copy(self, i):
        return remote(
            self.block(self.give, 2 * i),
            self.land.at[i - 1],
            self.z_send.at[i - 1],
            self.z_recv.at[i - 1],
            head=self.place.plane - 2 * i,
        )

    def sends(self, i):
        return self.place.z - i >= 0

    def receives(self, i):
        return self.place.z + i < self.place.depth

    def send(self):
        for i in range(1, self.reach // 2 + 1):

            @pl.when((self.place.core == 1) & self.handed(i))
            def _(i=i):
                self.hand_copy(i).wait_recv()
                self.add(i, 2 * i)

            if i > 1:

                @pl.when((self.place.core == 0) & self.handed(i))
                def _(i=i):
                    self.hand_copy(i).wait_recv()
                    self.add(i, 2 * i - 2)

        for i in range(1, self.reach // 2 + 1):

            @pl.when(self.sends(i))
            def _(i=i):
                self.low(2 * i)
                self.z_copy(i).start()

    def collect(self):
        @pl.when((self.place.core == 0) & self.handed(1))
        def _():
            self.hand_copy(1).wait_recv()
            self.add(1, 0)

        where = self.lanes(0)
        for i in range(1, self.reach // 2 + 1):

            @pl.when(self.receives(i))
            def _(i=i):
                self.z_copy(i).wait_recv()
                self.total[:, where] = self.total[:, where] + self.land[i - 1].astype(F32)

    def finish(self):
        for i in range(1, self.reach // 2 + 1):

            @pl.when(self.hands(i))
            def _(i=i):
                self.hand_copy(i).wait_send()

            @pl.when(self.sends(i))
            def _(i=i):
                self.z_copy(i).wait_send()


class GradJob:
    def __init__(self, place, left, right, bufs, flips, sems):
        self.place, self.left, self.right = place, left, right
        self.left_sib, self.right_sib, self.out, self.land, self.far = bufs
        self.flipped, self.flipped_sib = flips
        self.s_send, self.s_recv, self.z_send, self.z_recv, self.f_send, self.f_recv = sems
        self.outer = (place.z == 0) | (place.z == place.depth - 1)
        self.width = self.out.shape[1]

    @staticmethod
    def sems(depth):
        return [dma(depth + 1), dma(depth + 1), dma(depth - 1), dma(depth - 1), dma(), dma()]

    @staticmethod
    def bufs(group, depth, width, cols):
        return [
            pltpu.VMEM((group, depth * width), BF16),
            pltpu.VMEM((group, cols), BF16),
            pltpu.VMEM((depth, width, cols), BF16),
            pltpu.VMEM((depth - 1, width, cols), BF16),
            pltpu.VMEM((width, cols), BF16),
        ]

    def lanes(self, z, core):
        return pl.ds(pl.multiple_of((2 * z + core) * self.width, self.width), self.width)

    def right_copy(self):
        return remote(
            self.right,
            self.right_sib,
            self.s_send.at[0],
            self.s_recv.at[0],
            head=self.place.sibling,
        )

    def left_copy(self, z):
        return remote(
            self.left.at[:, self.lanes(z, 1 - self.place.core)],
            self.left_sib.at[:, pl.ds(z * self.width, self.width)],
            self.s_send.at[z + 1],
            self.s_recv.at[z + 1],
            head=self.place.sibling,
        )

    def exchange(self):
        self.right_copy().start()
        for z in range(self.place.depth):
            self.left_copy(z).start()

    def z_copy(self, step):
        z = self.place.z_after(step)
        return remote(
            self.out.at[z],
            self.land.at[step - 1],
            self.z_send.at[step - 1],
            self.z_recv.at[step - 1],
            head=2 * z + self.place.core,
        )

    def send(self, step):
        self.z_copy(step).start()

    def far_copy(self):
        z = self.place.z
        return remote(
            self.out.at[self.place.depth - 1 - z],
            self.far,
            self.f_send,
            self.f_recv,
            head=2 * (1 + lax.div(z, 2)) + self.place.core,
        )

    def sends(self, step):
        z = self.place.z
        return z >= 0 if step == 2 else (z < 3 if step == 1 else z > 0)

    def receives(self, step):
        z = self.place.z
        return z >= 0 if step == 2 else (z > 0 if step == 1 else z < 3)

    def compute(self):
        for z in range(self.place.depth):
            mine = jnp.transpose(self.left[:, self.lanes(z, self.place.core)].astype(F32))
            self.flipped[z * self.width : (z + 1) * self.width, :] = mine.astype(BF16)
        for z in range(self.place.depth):
            self.left_copy(z).wait_recv()
            here = slice(z * self.width, (z + 1) * self.width)
            theirs = jnp.transpose(self.left_sib[:, here].astype(F32))
            self.flipped_sib[here, :] = theirs.astype(BF16)
        self.right_copy().wait_recv()

        def tile(where):
            value = dot_nn(self.flipped[...], self.right[:, where])
            value = value + dot_nn(self.flipped_sib[...], self.right_sib[:, where])
            value = value.astype(BF16)
            for z in range(self.place.depth):
                self.out[z, :, where] = value[z * self.width : (z + 1) * self.width]

        by_columns(self.out.shape[2], tile)

        @pl.when(self.outer)
        def _():
            self.far_copy().start()
            self.z_copy(2).start()

        for step in (1, 3):

            @pl.when(self.sends(step))
            def _(step=step):
                self.z_copy(step).start()

    def relay(self):
        @pl.when(jnp.logical_not(self.outer))
        def _():
            self.far_copy().wait_recv()
            z = self.place.z_after(2)
            self.out[z] = (self.out[z].astype(F32) + self.far[...].astype(F32)).astype(BF16)
            self.z_copy(2).start()

    def total(self):
        total = self.out[self.place.z].astype(F32)
        for step in range(1, self.place.depth):

            @pl.when(self.receives(step))
            def _(step=step):
                self.z_copy(step).wait_recv()

            piece = self.land[step - 1].astype(F32)
            total = total + jnp.where(self.receives(step), piece, 0.0)
        return total

    def finish(self):
        self.right_copy().wait_send()
        for z in range(self.place.depth):
            self.left_copy(z).wait_send()

        @pl.when(self.outer)
        def _():
            self.far_copy().wait_send()

        for step in range(1, self.place.depth):

            @pl.when(self.sends(step))
            def _(step=step):
                self.z_copy(step).wait_send()


class OutGradJob:
    def __init__(self, place, left, right, bufs, sems):
        self.place, self.left, self.right = place, left, right
        self.left_sib, self.right_sib, self.out, self.land = bufs
        self.s_send, self.s_recv, self.z_send, self.z_recv = sems
        self.width = self.out.shape[0]

    @staticmethod
    def sems(depth):
        return [dma(2), dma(2), dma(), dma(depth - 1)]

    @staticmethod
    def bufs(group, depth, width, cols):
        return [
            pltpu.VMEM((group, width), BF16),
            pltpu.VMEM((group, cols), BF16),
            pltpu.VMEM((width, cols), BF16),
            pltpu.VMEM((depth - 1, width, cols), BF16),
        ]

    def lanes(self, core):
        return pl.ds(pl.multiple_of(core * self.width, self.width), self.width)

    def copies(self):
        return (
            remote(
                self.right,
                self.right_sib,
                self.s_send.at[0],
                self.s_recv.at[0],
                head=self.place.sibling,
            ),
            remote(
                self.left.at[:, self.lanes(1 - self.place.core)],
                self.left_sib,
                self.s_send.at[1],
                self.s_recv.at[1],
                head=self.place.sibling,
            ),
        )

    def exchange(self):
        for copy in self.copies():
            copy.start()

    def home(self):
        return self.place.peer == self.place.z

    def z_copy(self):
        step = lax.rem(self.place.peer + self.place.depth - self.place.z, self.place.depth)
        index = jnp.maximum(step - 1, 0)
        return remote(
            self.out,
            self.land.at[index],
            self.z_send,
            self.z_recv.at[index],
            head=2 * self.place.peer + self.place.core,
        )

    def compute(self):
        for copy in self.copies():
            copy.wait_recv()
        mine = jnp.transpose(self.left[:, self.lanes(self.place.core)].astype(F32)).astype(BF16)
        theirs = jnp.transpose(self.left_sib[...].astype(F32)).astype(BF16)

        def tile(where):
            value = dot_nn(mine, self.right[:, where]) + dot_nn(theirs, self.right_sib[:, where])
            self.out[:, where] = value.astype(BF16)

        by_columns(self.out.shape[1], tile)

        @pl.when(jnp.logical_not(self.home()))
        def _():
            self.z_copy().start()

    def store(self, ref):
        @pl.when(self.home())
        def _():
            total = self.out[...].astype(F32)
            for step in range(1, self.place.depth):
                remote(
                    self.out,
                    self.land.at[step - 1],
                    self.z_send,
                    self.z_recv.at[step - 1],
                    head=self.place.sibling,
                ).wait_recv()
                total = total + self.land[step - 1].astype(F32)
            ref[...] = total.astype(BF16)

        @pl.when(jnp.logical_not(self.home()))
        def _():
            ref[...] = jnp.zeros_like(ref)

    def finish(self):
        for copy in self.copies():
            copy.wait_send()

        @pl.when(jnp.logical_not(self.home()))
        def _():
            self.z_copy().wait_send()


def rms_back_of(values, upstream):
    inverse = inverse_rms(values)
    inner_mean = jnp.mean(upstream * values, axis=-1, keepdims=True)
    return inverse * upstream - values * (inverse * inverse * inverse) * inner_mean


def attend_back_chunk(sizes, place, block_offset, index, refs):
    tile, chunk, cols, group, lead = sizes.tile, sizes.chunk, sizes.cols, sizes.group, sizes.lead
    block = sizes.reach - block_offset
    offset = pl.multiple_of(block * group + index * chunk, chunk)
    there = pl.ds(offset, chunk)
    here = pl.ds(pl.multiple_of(index * chunk, chunk), chunk)
    spot = offset + lax.broadcasted_iota(jnp.int32, (chunk, 1), 0)
    lane = lax.broadcasted_iota(jnp.int32, (tile, 2 * HD), 1)
    begin = lax.div(jnp.maximum(offset - lead, 0), tile)
    end = jnp.minimum(
        lax.div(jnp.maximum(offset + chunk + sizes.doc_max - 2 - lead + tile, 0), tile), group // tile
    )
    for pair in range(cols // (2 * HD)):
        lanes = slice(pair * 2 * HD, (pair + 1) * 2 * HD)
        value_lanes = slice(cols + pair * 2 * HD, cols + (pair + 1) * 2 * HD)
        keys = refs.keys[there, lanes]
        values = refs.keys[there, value_lanes]

        def step(index, state, pair=pair, lanes=lanes, keys=keys, values=values):
            key_sum, value_sum = state
            row = pl.multiple_of(index * tile, tile)
            rows = pl.ds(row, tile)
            last = lead + row + lax.broadcasted_iota(jnp.int32, (1, tile), 1)
            allowed = (spot >= refs.first[:, rows]) & (spot <= last)
            queries = refs.queries[rows, lanes] * jnp.asarray(HD ** (-0.5), BF16)
            grads = refs.mixed_grad[rows, lanes]
            zero = jnp.zeros_like(queries)
            back = []
            for which in range(2):
                mask = lane < HD if which == 0 else lane >= HD
                half = jnp.where(mask, queries, zero)
                grad = jnp.where(mask, grads, zero)
                head = slice(2 * pair + which, 2 * pair + which + 1)
                scores = dot_nt(keys, half)
                probs = jnp.where(allowed, jnp.exp(scores - refs.logs[head, rows]), 0.0)
                change = (probs * (dot_nt(values, grad) - refs.delta[head, rows])).astype(BF16)
                key_sum = key_sum + dot_nn(change, half)
                value_sum = value_sum + dot_nn(probs.astype(BF16), grad)
                back.append(dot_tn(change, keys))
            refs.dq[rows, lanes] += jnp.where(lane < HD, back[0], back[1])
            return key_sum, value_sum

        empty = jnp.zeros((chunk, 2 * HD), F32)
        key_sum, value_sum = lax.fori_loop(begin, end, step, (empty, empty))
        base = block * 2 * cols
        refs.dkv[here, base + lanes.start : base + lanes.stop] = key_sum
        refs.dkv[here, base + value_lanes.start : base + value_lanes.stop] = value_sum


def backward_body(sizes, layer, fused, refs):
    place = Place()
    tok, cols, group, hidden = sizes.tok, sizes.cols, sizes.group, sizes.hidden
    tile, chunk, lead, reach = sizes.tile, sizes.chunk, sizes.lead, sizes.reach
    refs.gate_up = refs.dkv.at[:, pl.ds(0, 2 * hidden)]
    place.greet()
    grad = refs.grad[...]
    own_rows = pl.ds(pl.multiple_of(place.peer * tok, tok), tok)
    refs.down_in[own_rows, :] = grad.astype(BF16)
    ag1 = PlaneGather(place, refs.down_in, refs.ag1_s, refs.ag1_r)
    ag1.start()
    loads = {
        name: pltpu.make_async_copy(src, dst, refs.load_sem.at[index])
        for index, (name, src, dst) in enumerate(
            (
                ("d", refs.d_full, refs.wd),
                ("gate_up", refs.gate_up_in, refs.gate_up),
                ("g", refs.g_full, refs.wg),
                ("o", refs.o_full, refs.wo),
                ("q", refs.q_full, refs.wq),
                ("hidden", refs.hidden_in, refs.hidden),
                ("scaled_ffn", refs.scaled_ffn_in, refs.scaled_ffn),
            )
        )
    }
    for copy in loads.values():
        copy.start()
    jobs = []
    if fused:
        job_d = GradJob(place, refs.hidden, refs.down_in, refs.jd_buf, refs.flips, refs.jd_sem)
        job_g = GradJob(place, refs.scaled_ffn, refs.gate_up_grad, refs.jg_buf, refs.flips, refs.jg_sem)
        job_o = OutGradJob(place, refs.mixed, refs.proj_in, refs.jo_buf, refs.jo_sem)
        jobs = [job_d, job_o]
        if layer == 0:
            job_q = GradJob(
                place, refs.old_scaled, refs.old_qkv, refs.jq_buf, refs.flips, refs.jq_sem
            )
            jobs.append(job_q)
            job_q.exchange()
        loads["hidden"].wait()
        loads["scaled_ffn"].wait()
    loads["d"].wait()
    loads["gate_up"].wait()
    loads["g"].wait()
    if fused and layer == 0:
        job_q.compute()
        job_q.relay()

    sum1 = PlaneSum(place, refs.part1, refs.sum1, refs.rs1_s, refs.rs1_r)

    for steps in peer_groups(place.peers):
        peers = [place.peer_before(step) for step in steps]
        rows = [pl.ds(pl.multiple_of(peer * tok, tok), tok) for peer in peers]
        for step in steps:
            ag1.await_step(step)
        if fused and steps[-1] == place.peers - 1:
            job_d.exchange()
        x = jnp.concatenate([refs.down_in[where, :] for where in rows], axis=0)

        def block(where, x=x, rows=rows):
            there = pl.ds(pl.multiple_of(hidden + where.start, where.size), where.size)
            grad_hidden = dot_nt(x, refs.wd[where, :])
            for index, row in enumerate(rows):
                piece = grad_hidden[index * tok : (index + 1) * tok]
                gate = refs.gate_up[row, where]
                up = refs.gate_up[row, there]
                sigmoid = 1.0 / (1.0 + jnp.exp(-gate))
                gate_grad = piece * up * (sigmoid * (1.0 + gate * (1.0 - sigmoid)))
                refs.gate_up_grad[row, where] = gate_grad.astype(BF16)
                refs.gate_up_grad[row, there] = (piece * (gate * sigmoid)).astype(BF16)

        by_columns(hidden, block)
        low = jnp.concatenate([refs.gate_up_grad[where, :] for where in rows], axis=0)

        def back(where, low=low, peers=peers):
            value = dot_nt(low, refs.wg[where, :]).astype(BF16)
            for index, peer in enumerate(peers):
                refs.part1[peer, :, where] = value[index * tok : (index + 1) * tok]

        by_columns(D, back)
        for peer in peers:
            sum1.send_to(peer)

    if fused:
        job_g.exchange()
        job_d.compute()
        if layer == 0:
            own_scaled = refs.wd.at[pl.ds(0, group)]
            scaled_load = pltpu.make_async_copy(refs.scaled_in, own_scaled, refs.load_sem.at[0])
            scaled_load.start()
    middle = refs.middle[...]
    grad_middle = grad + rms_back_of(middle, sum1.total())
    refs.proj_in[own_rows, :] = grad_middle.astype(BF16)
    ag2 = PlaneGather(place, refs.proj_in, refs.ag2_s, refs.ag2_r)
    ag2.start()
    if fused:
        job_g.compute()
        job_d.relay()
    refs.dq[...] = jnp.zeros_like(refs.dq)
    loads["o"].wait()
    loads["q"].wait()

    for steps in peer_groups(place.peers):
        rows = [
            pl.ds(pl.multiple_of(place.peer_before(step) * tok, tok), tok) for step in steps
        ]
        for step in steps:
            ag2.await_step(step)
        x = jnp.concatenate([refs.proj_in[where, :] for where in rows], axis=0)

        def block(where, x=x, rows=rows):
            value = dot_nt(x, refs.wo[where, :]).astype(BF16)
            for index, row in enumerate(rows):
                refs.mixed_grad[row, where] = value[index * tok : (index + 1) * tok]

        by_columns(cols, block)
    if fused:
        job_o.exchange()

    def deltas(index, carry):
        rows = pl.ds(pl.multiple_of(index * tile, tile), tile)
        for pair in range(cols // (2 * HD)):
            lanes = slice(pair * 2 * HD, (pair + 1) * 2 * HD)
            product = jnp.transpose(
                refs.mixed_grad[rows, lanes].astype(F32) * refs.attended[rows, lanes]
            )
            for which in range(2):
                refs.delta[2 * pair + which : 2 * pair + which + 1, rows] = jnp.sum(
                    product[which * HD : (which + 1) * HD], axis=0, keepdims=True
                )
        return carry

    lax.fori_loop(0, group // tile, deltas, 0)

    halo = HaloBack(place, refs.dkv, refs.give, refs.land, refs.s_land, reach, refs.halo_sem)
    per_block = group // chunk

    def key_blocks(offset):
        @pl.when(place.plane >= offset)
        def _():
            def body(index, carry):
                attend_back_chunk(sizes, place, offset, index, refs)
                return carry

            lax.fori_loop(0, per_block, body, 0)

    for offset in range(1, reach + 1, 2):
        key_blocks(offset)
    halo.hand()
    for offset in range(2, reach + 1, 2):
        key_blocks(offset)
    halo.send()
    if fused:
        job_g.relay()
    key_blocks(0)
    swaps = []

    def hand_out(name, value):
        pack = getattr(refs, f"pack_{name}")
        for peer in range(sizes.peers):
            pack[peer, 0] = value[peer * sizes.own_rows : (peer + 1) * sizes.own_rows]
        swap = WeightSwap(
            place, pack, 0, getattr(refs, f"rows_{name}"), getattr(refs, f"swap_{name}")
        )
        swap.start()
        swaps.append(swap)

    if fused:
        job_o.compute()
        if layer == 0:
            hand_out("q1", job_q.total().astype(BF16))
            hand_out("g1", refs.raw_g1[...])
    refs.qkv_grad[:, 0:cols] = (refs.dq[...] * (HD ** (-0.5))).astype(BF16)
    halo.collect()
    refs.qkv_grad[:, cols:] = refs.dkv[:, reach * 2 * cols : (reach + 1) * 2 * cols].astype(BF16)
    if fused and layer == 0:
        scaled_load.wait()
        job_p = GradJob(place, own_scaled, refs.qkv_grad, refs.jp_buf, refs.flips, refs.jp_sem)
        job_p.exchange()

    sum1.finish()
    sum2 = PlaneSum(place, refs.part1, refs.sum2, refs.rs2_s, refs.rs2_r)

    for steps in [g for g in peer_groups(place.peers)[1:]] + [(0,)]:
        peers = [place.peer_before(step) for step in steps]
        low = jnp.concatenate(
            [refs.qkv_grad[pl.ds(pl.multiple_of(peer * tok, tok), tok), :] for peer in peers], axis=0
        )

        def back(where, low=low, peers=peers):
            value = dot_nt(low, refs.wq[where, :]).astype(BF16)
            for index, peer in enumerate(peers):
                refs.part1[peer, :, where] = value[index * tok : (index + 1) * tok]

        by_columns(D, back)
        for peer in peers:
            sum2.send_to(peer)

    if fused and layer == 0:
        job_p.compute()
    refs.next[...] = grad_middle + rms_back_of(refs.stream[...], sum2.total())
    if fused and layer == 0:
        job_p.relay()
    for item in [ag1, ag2, sum2, halo]:
        item.finish()
    if not fused:
        loads["hidden"].wait()
        loads["scaled_ffn"].wait()
        return
    refs.raw_down[...] = job_d.total()
    job_o.store(refs.raw_o)
    if layer > 0:
        refs.raw_g[...] = job_g.total().astype(BF16)
        job_g.finish()
    else:
        rows = sizes.own_rows
        home = place.peer == place.z
        raw_o = (refs.raw_o, refs.raw_o1)
        rows_o = (refs.rows_o0, refs.rows_o1)

        def out_copy(l, peer, step):
            return remote(
                raw_o[l].at[pl.ds(pl.multiple_of(peer * rows, rows), rows)],
                rows_o[l],
                refs.out_send.at[l, step - 1],
                refs.out_recv.at[l],
                blk=peer,
            )

        def own_out(l):
            return pltpu.make_async_copy(
                raw_o[l].at[pl.ds(pl.multiple_of(place.peer * rows, rows), rows)],
                rows_o[l],
                refs.out_recv.at[l],
            )

        @pl.when(home)
        def _():
            for l in range(LAYERS):
                for step in range(1, place.peers):
                    out_copy(l, place.peer_after(step), step).start()
                own_out(l).start()

        hand_out("g0", job_g.total().astype(BF16))
        hand_out("q0", job_p.total().astype(BF16))
        job_g.finish()
        job_p.finish()

        @pl.when(home)
        def _():
            for l in range(LAYERS):
                own_out(l).wait()
                for step in range(1, place.peers):
                    out_copy(l, place.peer_after(step), step).wait_send()

        @pl.when(jnp.logical_not(home))
        def _():
            for l in range(LAYERS):
                out_copy(l, place.z, 1).wait_recv()

        for swap in swaps:
            swap.arrive()
            swap.finish()
    for item in jobs:
        item.finish()


def backward_layer(sizes, layer, fused, grad, first_row, kept, full, old, collective_id):
    peers, planes, depth = sizes.peers, sizes.planes, sizes.planes // 2
    tok, cols, group, hidden, reach = sizes.tok, sizes.cols, sizes.group, sizes.hidden, sizes.reach
    q_full, o_full, g_full, d_full = full
    inputs = {
        "grad": (grad, VMEM),
        "first": (first_row, VMEM),
        "middle": (kept["middle"], VMEM),
        "stream": (kept["stream"], VMEM),
        "queries": (kept["queries"], VMEM),
        "keys": (kept["keys"], VMEM),
        "attended": (kept["attended"], VMEM),
        "logs": (kept["logs"], VMEM),
        "mixed": (kept["mixed"], VMEM),
        "gate_up_in": (kept["gate_up_out"], ANY),
        "hidden_in": (kept["hidden"], ANY),
        "scaled_ffn_in": (kept["scaled_ffn"], ANY),
        "q_full": (q_full, ANY),
        "o_full": (o_full, ANY),
        "g_full": (g_full, ANY),
        "d_full": (d_full, ANY),
    }
    outputs = {
        "next": ((tok, D), F32, VMEM),
        "qkv_grad": ((group, 3 * cols), BF16, VMEM),
    }
    scratch = {
        "wq": pltpu.VMEM((D, 3 * cols), BF16),
        "wo": pltpu.VMEM((cols, D), BF16),
        "wg": pltpu.VMEM((D, 2 * hidden), BF16),
        "wd": pltpu.VMEM((hidden, D), BF16),
        "dkv": pltpu.VMEM((group, max(2 * hidden, (reach + 1) * 2 * cols)), F32),
        "hidden": pltpu.VMEM((group, hidden), BF16),
        "scaled_ffn": pltpu.VMEM((group, D), BF16),
        "mixed_grad": pltpu.VMEM((group, cols), BF16),
        "delta": pltpu.VMEM((cols // HD, group), F32),
        "dq": pltpu.VMEM((group, cols), F32),
        "give": pltpu.VMEM((reach, group, 2 * cols), BF16),
        "land": pltpu.VMEM((reach // 2, group, 2 * cols), BF16),
        "s_land": pltpu.VMEM((reach // 2, group, 2 * cols), BF16),
        "load_sem": dma(7),
        "halo_sem": Halo.sems(reach),
    }
    for name in ("part1", "sum1", "sum2"):
        scratch[name] = pltpu.VMEM((peers, tok, D), BF16)
    for name in ("ag1_s", "ag1_r", "ag2_s", "ag2_r", "rs1_s", "rs1_r", "rs2_s", "rs2_r"):
        scratch[name] = dma(peers - 1)
    space = pltpu.VMEM
    if fused:
        scratch["down_in"] = space((group, D), BF16)
        scratch["proj_in"] = space((group, D), BF16)
        scratch["gate_up_grad"] = space((group, 2 * hidden), BF16)
        width = D // planes
        strip = hidden // planes
        scratch["flips"] = [pltpu.VMEM((depth * width, group), BF16)] * 2
        scratch["jd_buf"] = GradJob.bufs(group, depth, strip, D)
        scratch["jg_buf"] = GradJob.bufs(group, depth, width, 2 * hidden)
        scratch["jo_buf"] = OutGradJob.bufs(group, depth, cols // 2, D)
        scratch["jd_sem"] = GradJob.sems(depth)
        scratch["jg_sem"] = GradJob.sems(depth)
        scratch["jo_sem"] = OutGradJob.sems(depth)
        outputs["raw_down"] = ((strip, D), F32, VMEM)
        outputs["raw_o"] = ((cols // 2, D), BF16, VMEM)
        if layer > 0:
            outputs["raw_g"] = ((width, 2 * hidden), BF16, VMEM)
        else:
            rows = sizes.own_rows
            inputs["old_scaled"] = (old["scaled"], VMEM)
            inputs["old_qkv"] = (old["qkv_grad"], VMEM)
            inputs["raw_g1"] = (old["raw_g"], VMEM)
            inputs["raw_o1"] = (old["raw_o"], VMEM)
            inputs["scaled_in"] = (kept["scaled"], ANY)
            for name in ("jq", "jp"):
                scratch[f"{name}_buf"] = GradJob.bufs(group, depth, width, 3 * cols)
                scratch[f"{name}_sem"] = GradJob.sems(depth)
            scratch["out_send"] = dma(LAYERS, peers - 1)
            scratch["out_recv"] = dma(LAYERS)
            for l in range(LAYERS):
                outputs[f"rows_o{l}"] = ((rows, D), BF16, VMEM)
                for kind, width_of in (("g", 2 * hidden), ("q", 3 * cols)):
                    outputs[f"rows_{kind}{l}"] = ((peers * rows, width_of), BF16, VMEM)
                    scratch[f"pack_{kind}{l}"] = pltpu.VMEM((peers, 1, rows, width_of), BF16)
                    scratch[f"swap_{kind}{l}"] = WeightSwap.sems(peers)
    else:
        outputs["down_in"] = ((group, D), BF16, VMEM)
        outputs["proj_in"] = ((group, D), BF16, VMEM)
        outputs["gate_up_grad"] = ((group, 2 * hidden), BF16, VMEM)
    return launch(
        functools.partial(backward_body, sizes, layer, fused),
        f"backward{layer}",
        inputs,
        outputs,
        scratch,
        collective_id,
        flops=group * D * (4 * cols + 3 * hidden) * 4,
    )


def inverse_rms(values):
    return lax.rsqrt(jnp.mean(values * values, axis=-1, keepdims=True) + EPSILON)


def matmul(left, right):
    return jnp.dot(left, right, preferred_element_type=F32)


def contract_rows(left, right):
    return jnp.einsum("td,te->de", left, right, preferred_element_type=F32)


def contract_cols(left, right):
    return jnp.einsum("te,de->td", left, right, preferred_element_type=F32)


def local(
    tokens,
    gain_attn,
    w_query,
    w_key,
    w_value,
    w_out,
    gain_ffn,
    w_gate,
    w_up,
    w_down,
    doc_ids,
    cotangent,
):
    planes = lax.axis_size("head")
    peers = lax.axis_size("blk")
    plane = lax.axis_index("head")
    tok = tokens.shape[0]
    group = tok * peers
    stream_rows = group * planes
    doc_max = stream_rows // 4
    reach = (doc_max - 1 + group - 1) // group
    reach = reach + reach % 2
    own_rows = w_query.shape[1]
    cols = D // peers
    strip = w_down.shape[1]
    hidden_cols = strip * planes
    tile = 256
    chunk = 256
    lead = reach * group

    places = jnp.arange(stream_rows, dtype=jnp.int32)
    opens = jnp.concatenate([jnp.ones((1,), jnp.bool_), doc_ids[1:] != doc_ids[:-1]])
    starts = lax.cummax(jnp.where(opens, places, 0))
    first_place = lax.dynamic_slice_in_dim(starts, plane * group, group, 0) - (
        plane * group - lead
    )
    low = first_place[::tile] // chunk
    first_place = first_place[:, None]

    attn_rows = gain_attn.astype(F32)[:, :, None]
    ffn_rows = gain_ffn.astype(F32)[:, :, None]

    def for_peers(weight, gain):
        scaled = (weight.astype(F32) * gain).astype(BF16)
        return scaled.reshape(LAYERS, own_rows, peers, cols).transpose(2, 0, 1, 3)

    def for_peers_ffn(weight, gain):
        scaled = (weight.astype(F32) * gain).astype(BF16)
        scaled = scaled.reshape(LAYERS, own_rows, planes, peers, strip).transpose(3, 0, 1, 2, 4)
        return scaled.reshape(peers, LAYERS, own_rows, hidden_cols)

    weights = {
        "pack_q": jnp.concatenate(
            [for_peers(w, attn_rows) for w in (w_query, w_key, w_value)], axis=3
        ),
        "pack_g": jnp.concatenate([for_peers_ffn(w, ffn_rows) for w in (w_gate, w_up)], axis=3),
        "w_out": w_out,
        "w_down": w_down,
    }
    sizes = types.SimpleNamespace(
        peers=peers,
        planes=planes,
        tok=tok,
        cols=cols,
        group=group,
        hidden=hidden_cols,
        reach=reach,
        own_rows=own_rows,
        tile=tile,
        chunk=chunk,
        lead=lead,
        doc_max=doc_max,
    )
    first_row = first_place.reshape(1, group)
    stream = tokens.astype(F32)
    saved = []
    full = []
    for layer in range(LAYERS):
        kept = forward_layer(sizes, layer, stream, first_row, weights, 10 + layer)
        if layer == 0:
            weights = weights | {
                "mine_g": kept["mine_g"],
                "q_full": kept["q_full1"],
                "o_full": kept["out_full1"],
            }
            full.append((kept["q_full0"], kept["out_full0"], kept["g_full"], kept["d_full"]))
        else:
            full.append((weights["q_full"], weights["o_full"], kept["g_full"], kept["d_full"]))
        saved.append(kept | {"stream": stream})
        stream = kept["next"]
    output = stream.astype(BF16)

    grad = cotangent.astype(F32)
    fused = planes == 8 and strip % 128 == 0
    backs = [None] * LAYERS
    old = None
    for layer in reversed(range(LAYERS)):
        kept = saved[layer]
        back = backward_layer(
            sizes, layer, fused, grad, first_row, kept, full[layer], old, 12 + layer
        )
        grad = back["next"]
        old = back | {"scaled": kept["scaled"]}
        backs[layer] = back
    if fused:
        rows = backs[0]
        raw = jnp.stack(
            [jnp.concatenate([rows[f"rows_q{l}"], rows[f"rows_g{l}"]], axis=1) for l in range(LAYERS)]
        )
        raw = raw.reshape(LAYERS, peers, own_rows, 3 * cols + 2 * hidden_cols)
        raw = raw.transpose(1, 0, 2, 3).astype(F32)
        grad_out = jnp.stack([rows[f"rows_o{l}"] for l in range(LAYERS)]).astype(F32)
        grad_down = jnp.stack([back["raw_down"] for back in backs])
    else:
        raw, grad_out, grad_down = [], [], []
        for kept, back in zip(saved, backs):
            down_in = back["down_in"]
            proj_in = back["proj_in"]
            scatter = functools.partial(lax.psum_scatter, scatter_dimension=0, tiled=True)
            grad_down.append(
                scatter(contract_rows(kept["hidden"], down_in).astype(BF16), "head").astype(F32)
            )
            padded = lax.dynamic_update_slice(
                jnp.zeros((D, D), BF16),
                contract_rows(kept["mixed"], proj_in).astype(BF16),
                (lax.axis_index("blk") * cols, 0),
            )
            grad_out.append(scatter(padded, ("head", "blk")).astype(F32))
            pieces = [
                scatter(contract_rows(kept[name], right).astype(BF16), "head")
                for name, right in (
                    ("scaled", back["qkv_grad"]),
                    ("scaled_ffn", back["gate_up_grad"]),
                )
            ]
            raw.append(jnp.concatenate(pieces, axis=1))
        raw = jnp.stack(raw).reshape(LAYERS, peers, own_rows, 3 * cols + 2 * hidden_cols)
        raw = plane_swap(raw.transpose(1, 0, 2, 3), 1, "rows_swap").astype(F32)
        grad_out, grad_down = jnp.stack(grad_out), jnp.stack(grad_down)

    def attn_rows_of(which):
        piece = raw[:, :, :, which * cols : (which + 1) * cols]
        return piece.transpose(1, 2, 0, 3).reshape(LAYERS, own_rows, D)

    def ffn_rows_of(which):
        begin = 3 * cols + which * hidden_cols
        piece = raw[:, :, :, begin : begin + hidden_cols]
        piece = piece.reshape(peers, LAYERS, own_rows, planes, strip).transpose(1, 2, 3, 0, 4)
        return piece.reshape(LAYERS, own_rows, peers * hidden_cols)

    raw_query, raw_key, raw_value = (attn_rows_of(which) for which in range(3))
    raw_gate, raw_up = (ffn_rows_of(which) for which in range(2))

    def gain_grad(*pairs):
        return sum(jnp.sum(weight.astype(F32) * raw_part, axis=2) for weight, raw_part in pairs)

    grad_gain_attn = gain_grad((w_query, raw_query), (w_key, raw_key), (w_value, raw_value))
    grad_gain_ffn = gain_grad((w_gate, raw_gate), (w_up, raw_up))
    return (
        output,
        grad,
        grad_gain_attn,
        raw_query * attn_rows,
        raw_key * attn_rows,
        raw_value * attn_rows,
        grad_out,
        grad_gain_ffn,
        raw_gate * ffn_rows,
        raw_up * ffn_rows,
        grad_down,
    )


def solution(mesh):
    rows = P(("head", "blk"), None)
    vector = P(None, ("head", "blk"))
    matrix = P(None, ("head", "blk"), None)
    return jax.shard_map(
        local,
        mesh=mesh,
        in_specs=(
            rows,
            vector,
            matrix,
            matrix,
            matrix,
            matrix,
            vector,
            matrix,
            matrix,
            matrix,
            P(),
            rows,
        ),
        out_specs=(
            rows,
            rows,
            vector,
            matrix,
            matrix,
            matrix,
            matrix,
            vector,
            matrix,
            matrix,
            matrix,
        ),
        check_vma=False,
    )
```

```python
import functools
import math
import types

import jax
import jax.numpy as jnp
from jax import lax
from jax.experimental import pallas as pl
from jax.experimental.pallas import tpu as pltpu
from jax.sharding import PartitionSpec as P

D = 1024
HD = 64
HEADS = D // HD
LAYERS = 2
EPSILON = 1e-05
MASKED = -1e30
MESH = pl.DeviceIdType.MESH
F32 = jnp.float32
BF16 = jnp.bfloat16
ANY = pl.BlockSpec(memory_space=pl.ANY)


def greet_blk(count):
    me = lax.axis_index("blk")
    barrier = pltpu.get_barrier_semaphore()
    for step in range(1, count):
        pl.semaphore_signal(
            barrier,
            inc=1,
            device_id={"blk": lax.rem(me + step, count)},
            device_id_type=MESH,
        )
    pl.semaphore_wait(barrier, count - 1)
    return me


def plane_gather_kernel(count, x_ref, o_ref, send_sem, recv_sem, local_sem):
    me = greet_blk(count)
    copies = []
    for step in range(1, count):
        copy = pltpu.make_async_remote_copy(
            src_ref=x_ref,
            dst_ref=o_ref.at[me],
            send_sem=send_sem.at[step - 1],
            recv_sem=recv_sem.at[step - 1],
            device_id={"blk": lax.rem(me + step, count)},
            device_id_type=MESH,
        )
        copy.start()
        copies.append(copy)
    own = pltpu.make_async_copy(x_ref, o_ref.at[me], local_sem)
    own.start()
    own.wait()
    for copy in copies:
        copy.wait()


def plane_swap_kernel(count, x_ref, o_ref, send_sem, recv_sem, local_sem):
    me = greet_blk(count)
    copies = []
    for step in range(1, count):
        peer = lax.rem(me + step, count)
        copy = pltpu.make_async_remote_copy(
            src_ref=x_ref.at[peer],
            dst_ref=o_ref.at[me],
            send_sem=send_sem.at[step - 1],
            recv_sem=recv_sem.at[step - 1],
            device_id={"blk": peer},
            device_id_type=MESH,
        )
        copy.start()
        copies.append(copy)
    own = pltpu.make_async_copy(x_ref.at[me], o_ref.at[me], local_sem)
    own.start()
    own.wait()
    for copy in copies:
        copy.wait()


def plane_call(kernel, x, out_shape, collective_id, name):
    count = lax.axis_size("blk")
    return pl.pallas_call(
        functools.partial(kernel, count),
        out_shape=jax.ShapeDtypeStruct(out_shape, x.dtype),
        in_specs=[ANY],
        out_specs=ANY,
        scratch_shapes=[
            pltpu.SemaphoreType.DMA((count - 1,)),
            pltpu.SemaphoreType.DMA((count - 1,)),
            pltpu.SemaphoreType.DMA,
        ],
        compiler_params=pltpu.CompilerParams(collective_id=collective_id, has_side_effects=True),
        cost_estimate=pl.CostEstimate(flops=0, bytes_accessed=20_000_000, transcendentals=0),
        name=name,
    )(x)


def plane_gather(x, collective_id, name):
    return plane_call(
        plane_gather_kernel, x, (lax.axis_size("blk"),) + x.shape, collective_id, name
    )


def plane_swap(x, collective_id, name):
    return plane_call(plane_swap_kernel, x, x.shape, collective_id, name)


def launch(body, name, inputs, outputs, scratch, collective_id, flops=0):
    names = list(inputs) + list(outputs)
    flat = []
    for value in scratch.values():
        flat.extend(value if isinstance(value, list) else [value])

    def kernel(*refs):
        named = dict(zip(names, refs))
        rest = list(refs[len(names) :])
        for name, value in scratch.items():
            if isinstance(value, list):
                named[name], rest = rest[: len(value)], rest[len(value) :]
            else:
                named[name], rest = rest[0], rest[1:]
        body(types.SimpleNamespace(**named))

    results = pl.pallas_call(
        kernel,
        out_shape=[jax.ShapeDtypeStruct(shape, dtype) for shape, dtype, _ in outputs.values()],
        in_specs=[spec for _, spec in inputs.values()],
        out_specs=[spec for _, _, spec in outputs.values()],
        scratch_shapes=flat,
        compiler_params=pltpu.CompilerParams(
            collective_id=collective_id, has_side_effects=True, vmem_limit_bytes=60 << 20
        ),
        cost_estimate=pl.CostEstimate(
            flops=flops, bytes_accessed=200_000_000, transcendentals=0
        ),
        name=name,
    )(*[array for array, _ in inputs.values()])
    return dict(zip(outputs, results))


VMEM = pl.BlockSpec(memory_space=pltpu.VMEM)


def dma(*shape):
    return pltpu.SemaphoreType.DMA(shape)


def remote(src, dst, send_sem, recv_sem, **place):
    return pltpu.make_async_remote_copy(
        src_ref=src,
        dst_ref=dst,
        send_sem=send_sem,
        recv_sem=recv_sem,
        device_id=place,
        device_id_type=MESH,
    )


class Place:
    def __init__(self):
        self.peers = lax.axis_size("blk")
        self.planes = lax.axis_size("head")
        self.depth = self.planes // 2
        self.peer = lax.axis_index("blk")
        self.plane = lax.axis_index("head")
        self.z = lax.div(self.plane, 2)
        self.core = lax.rem(self.plane, 2)
        self.sibling = self.plane + 1 - 2 * self.core


    def moved(self, step, sign):
        half = self.peers // 2
        low, high = (step % 2, step // 2) if isinstance(step, int) else (lax.rem(step, 2), lax.div(step, 2))
        bit = lax.rem(lax.rem(self.peer, 2) + low, 2)
        return bit + 2 * lax.rem(lax.div(self.peer, 2) + sign * high + half, half)

    def peer_after(self, step):
        return self.moved(step, 1)

    def peer_before(self, step):
        return self.moved(step, -1)

    def steps_between(self, early, late):
        half = self.peers // 2
        bit = lax.rem(lax.rem(early, 2) + lax.rem(late, 2), 2)
        return bit + 2 * lax.rem(lax.div(late, 2) - lax.div(early, 2) + half, half)

    def z_after(self, step):
        return lax.rem(self.z + step, self.depth)

    def z_before(self, step):
        return lax.rem(self.z + self.depth - step, self.depth)

    def greet(self):
        barrier = pltpu.get_barrier_semaphore()
        for step in range(1, self.peers):
            pl.semaphore_signal(
                barrier, inc=1, device_id={"blk": self.peer_after(step)}, device_id_type=MESH
            )
        for step in range(1, self.depth):
            pl.semaphore_signal(
                barrier,
                inc=1,
                device_id={"head": 2 * self.z_after(step) + self.core},
                device_id_type=MESH,
            )
        pl.semaphore_signal(barrier, inc=1, device_id={"head": self.sibling}, device_id_type=MESH)
        pl.semaphore_wait(barrier, self.peers - 1 + self.depth - 1 + 1)


class PlaneGather:
    def __init__(self, place, flat, send, recv):
        self.place, self.flat, self.send, self.recv = place, flat, send, recv
        self.rows = flat.shape[0] // place.peers

    def slot(self, peer):
        return self.flat.at[pl.ds(pl.multiple_of(peer * self.rows, self.rows), self.rows)]

    def copy(self, step):
        own = self.slot(self.place.peer)
        return remote(
            own,
            own,
            self.send.at[step - 1],
            self.recv.at[step - 1],
            blk=self.place.peer_after(step),
        )

    def start(self):
        for step in range(1, self.place.peers):
            self.copy(step).start()

    def await_step(self, step):
        if step:
            source = self.place.peer_before(step)
            remote(
                self.slot(source),
                self.slot(source),
                self.send.at[step - 1],
                self.recv.at[step - 1],
                blk=source,
            ).wait_recv()

    def finish(self):
        for step in range(1, self.place.peers):
            self.copy(step).wait_send()


def peer_groups(peers):
    return [(0,), (1, 2)] + [(step,) for step in range(3, peers)] if peers > 2 else [(0,), (1,)]


class PlaneSum:
    def __init__(self, place, src, dst, send, recv):
        self.place, self.src, self.dst, self.send, self.recv = place, src, dst, send, recv

    def copy_to(self, peer):
        index = jnp.maximum(self.place.steps_between(peer, self.place.peer) - 1, 0)
        return remote(
            self.src.at[peer],
            self.dst.at[self.place.peer],
            self.send.at[index],
            self.recv.at[index],
            blk=peer,
        )

    def send_to(self, peer):
        @pl.when(peer != self.place.peer)
        def _():
            self.copy_to(peer).start()

    def total(self):
        total = self.src[self.place.peer].astype(F32)
        for step in range(1, self.place.peers):
            source = self.place.peer_after(step)
            remote(
                self.src.at[source],
                self.dst.at[source],
                self.send.at[step - 1],
                self.recv.at[step - 1],
                blk=source,
            ).wait_recv()
            total = total + self.dst[source].astype(F32)
        return total

    def finish(self):
        for step in range(1, self.place.peers):
            self.copy_to(self.place.peer_before(step)).wait_send()


class HeadGather:
    def __init__(self, place, src, full, sems):
        self.place, self.src, self.full = place, src, full
        self.z_send, self.z_recv, self.s_send, self.s_recv, self.local, self.r_send = sems
        self.line = place.depth == 4

    @staticmethod
    def sems(depth):
        return [dma(depth - 1), dma(depth - 1), dma(depth), dma(depth), dma(), dma()]

    def slot(self, z, core):
        rows = self.src.shape[0]
        return self.full.at[pl.ds(pl.multiple_of((2 * z + core) * rows, rows), rows)]

    def z_copy(self, step):
        return remote(
            self.src,
            self.slot(self.place.z, self.place.core),
            self.z_send.at[step - 1],
            self.z_recv.at[step - 1],
            head=2 * self.place.z_after(step) + self.place.core,
        )

    def near(self, step):
        z = self.place.z
        if not self.line or step == 2:
            return z >= 0
        return z < 3 if step == 1 else z > 0

    def relays(self, which):
        return self.place.z == (2 if which == 3 else 1)

    def relay_copy(self, which):
        where = self.slot(self.place.z_before(2), self.place.core)
        return remote(
            where,
            where,
            self.r_send,
            self.z_recv.at[which - 1],
            head=2 * (3 if which == 3 else 0) + self.place.core,
        )

    def s_copy(self, step, core):
        z = self.place.z_before(step)
        where = self.slot(z, core)
        return remote(
            self.src if step == 0 else where,
            where,
            self.s_send.at[step],
            self.s_recv.at[step],
            head=self.place.sibling,
        )

    def own_copy(self):
        return pltpu.make_async_copy(
            self.src, self.slot(self.place.z, self.place.core), self.local
        )

    def start(self):
        for step in sorted(range(1, self.place.depth), key=lambda k: k != 2):

            @pl.when(self.near(step))
            def _(step=step):
                self.z_copy(step).start()

        self.s_copy(0, self.place.core).start()
        self.own_copy().start()

    def await_z(self, step):
        where = self.slot(self.place.z_before(step), self.place.core)
        remote(
            self.src,
            where,
            self.z_send.at[step - 1],
            self.z_recv.at[step - 1],
            head=self.place.sibling,
        ).wait_recv()

    def relay(self):
        if self.line:
            self.await_z(2)
            for which in (1, 3):

                @pl.when(self.relays(which))
                def _(which=which):
                    self.relay_copy(which).start()

            self.s_copy(2, self.place.core).start()

    def forward(self):
        for step in range(1, self.place.depth):
            if not (self.line and step == 2):
                self.await_z(step)
                self.s_copy(step, self.place.core).start()

    def arrive(self):
        self.own_copy().wait()
        for step in range(self.place.depth):
            self.s_copy(step, 1 - self.place.core).wait_recv()

    def finish(self):
        for step in range(1, self.place.depth):

            @pl.when(self.near(step))
            def _(step=step):
                self.z_copy(step).wait_send()

        if self.line:
            for which in (1, 3):

                @pl.when(self.relays(which))
                def _(which=which):
                    self.relay_copy(which).wait_send()

        for step in range(self.place.depth):
            self.s_copy(step, self.place.core).wait_send()


class OutGather:
    def __init__(self, place, src, mid, full, sems):
        self.place, self.mid, self.full = place, mid, full
        self.rows = src.shape[0]
        self.over_head = HeadGather(place, src, mid, sems[:6])
        self.send, self.recv, self.local = sems[6:]

    @staticmethod
    def sems(peers, depth):
        return HeadGather.sems(depth) + [dma(2, peers - 1), dma(2, peers - 1), dma(2)]

    def piece(self, peer, core):
        return self.mid.at[pl.ds(pl.multiple_of((2 * peer + core) * self.rows, self.rows), self.rows)]

    def slot(self, peer, core):
        where = (core * self.place.peers + peer) * self.rows
        return self.full.at[pl.ds(pl.multiple_of(where, self.rows), self.rows)]

    def copy(self, step, core):
        target = self.place.peer_after(step)
        return remote(
            self.piece(target, core),
            self.slot(self.place.peer, core),
            self.send.at[core, step - 1],
            self.recv.at[core, step - 1],
            blk=target,
        )

    def own_copy(self, core):
        return pltpu.make_async_copy(
            self.piece(self.place.peer, core),
            self.slot(self.place.peer, core),
            self.local.at[core],
        )

    def start(self):
        self.over_head.start()

    def spread(self):
        self.over_head.relay()
        self.over_head.forward()
        self.over_head.arrive()
        for core in range(2):
            for step in range(1, self.place.peers):
                self.copy(step, core).start()
            self.own_copy(core).start()

    def arrive(self):
        for core in range(2):
            self.own_copy(core).wait()
            for step in range(1, self.place.peers):
                source = self.place.peer_before(step)
                remote(
                    self.piece(source, core),
                    self.slot(source, core),
                    self.send.at[core, step - 1],
                    self.recv.at[core, step - 1],
                    blk=source,
                ).wait_recv()

    def finish(self):
        self.over_head.finish()
        for core in range(2):
            for step in range(1, self.place.peers):
                self.copy(step, core).wait_send()


class WeightSwap:
    def __init__(self, place, src, layer, mine, sems):
        self.place, self.src, self.layer, self.mine = place, src, layer, mine
        self.send, self.recv, self.local = sems

    @staticmethod
    def sems(peers):
        return [dma(peers - 1), dma(peers - 1), dma()]

    def piece(self, peer):
        rows = self.src.shape[2]
        return self.mine.at[pl.ds(pl.multiple_of(peer * rows, rows), rows)]

    def copy(self, step):
        target = self.place.peer_after(step)
        return remote(
            self.src.at[target, self.layer],
            self.piece(self.place.peer),
            self.send.at[step - 1],
            self.recv.at[step - 1],
            blk=target,
        )

    def own_copy(self):
        return pltpu.make_async_copy(
            self.src.at[self.place.peer, self.layer], self.piece(self.place.peer), self.local
        )

    def start(self):
        for step in range(1, self.place.peers):
            self.copy(step).start()
        self.own_copy().start()

    def arrive(self):
        self.own_copy().wait()
        for step in range(1, self.place.peers):
            source = self.place.peer_before(step)
            remote(
                self.src.at[source, self.layer],
                self.piece(source),
                self.send.at[step - 1],
                self.recv.at[step - 1],
                blk=source,
            ).wait_recv()

    def finish(self):
        for step in range(1, self.place.peers):
            self.copy(step).wait_send()


class Halo:
    def __init__(self, place, keys, reach, sems):
        self.place, self.keys, self.reach = place, keys, reach
        self.rows = keys.shape[0] // (reach + 1)
        self.z_send, self.z_recv, self.s_send, self.s_recv = sems

    def block(self, offset):
        return self.keys.at[pl.ds((self.reach - offset) * self.rows, self.rows)]

    @staticmethod
    def sems(reach):
        return [dma(reach // 2), dma(reach // 2), dma(reach // 2), dma(reach // 2)]

    def z_copy(self, hop):
        return remote(
            self.block(0),
            self.block(2 * hop),
            self.z_send.at[hop - 1],
            self.z_recv.at[hop - 1],
            head=self.place.plane + 2 * hop,
        )

    def sends(self, hop):
        return self.place.z + hop < self.place.depth

    def receives(self, hop):
        return self.place.z - hop >= 0

    def start(self):
        for hop in range(1, self.reach // 2 + 1):

            @pl.when(self.sends(hop))
            def _(hop=hop):
                self.z_copy(hop).start()


    def hand(self, i):
        def copy(offset):
            return remote(
                self.block(offset),
                self.block(2 * i - 1),
                self.s_send.at[i - 1],
                self.s_recv.at[i - 1],
                head=self.place.sibling,
            )

        return copy

    def hand_ready(self, i):
        return (
            (self.place.core == 1) & self.receives(i),
            (self.place.core == 0) & self.receives(i - 1),
        )

    def relay(self):
        for i in range(1, self.reach // 2 + 1):
            from_one, from_zero = self.hand_ready(i)
            if i == 1:

                @pl.when(from_zero)
                def _(i=i):
                    self.hand(i)(2 * i - 2).start()

            @pl.when(self.receives(i))
            def _(i=i):
                remote(
                    self.block(0),
                    self.block(2 * i),
                    self.z_send.at[i - 1],
                    self.z_recv.at[i - 1],
                    head=self.place.sibling,
                ).wait_recv()

            @pl.when(from_one)
            def _(i=i):
                self.hand(i)(2 * i).start()

            if i < self.reach // 2:

                @pl.when(self.hand_ready(i + 1)[1])
                def _(i=i):
                    self.hand(i + 1)(2 * i).start()

    def arrive(self):
        for i in range(1, self.reach // 2 + 1):

            @pl.when(self.place.z - i + self.place.core >= 0)
            def _(i=i):
                self.hand(i)(0).wait_recv()

    def finish(self):
        for hop in range(1, self.reach // 2 + 1):

            @pl.when(self.sends(hop))
            def _(hop=hop):
                self.z_copy(hop).wait_send()

            from_one, from_zero = self.hand_ready(hop)

            @pl.when(from_one)
            def _(hop=hop):
                self.hand(hop)(2 * hop).wait_send()

            @pl.when(from_zero)
            def _(hop=hop):
                self.hand(hop)(2 * hop - 2).wait_send()


def columns(total, most=256):
    width = math.gcd(total, most)
    return total // width, width


def by_columns(total, step, most=256):
    count, width = columns(total, most)

    def body(index, carry):
        step(pl.ds(pl.multiple_of(index * width, width), width))
        return carry

    lax.fori_loop(0, count, body, 0)


def attend_tile(sizes, place, tile_index, q_ref, keys_ref, first_ref, mixed_ref, attended_ref, log_ref):
    tile, chunk, cols, group, lead = sizes.tile, sizes.chunk, sizes.cols, sizes.group, sizes.lead
    row = pl.multiple_of(tile_index * tile, tile)
    rows = pl.ds(row, tile)
    first = first_ref[:, rows]
    last = lead + row + lax.broadcasted_iota(jnp.int32, (1, tile), 1)
    lane = lax.broadcasted_iota(jnp.int32, (tile, 2 * HD), 1)
    lowest = jnp.maximum(lead + row - (sizes.doc_max - 1), lead - place.plane * group)
    begin = lax.div(jnp.maximum(lowest, 0), chunk)
    end = lax.div(lead + row + tile + chunk - 1, chunk)
    pairs = range(cols // (2 * HD))
    halves = []
    for pair in pairs:
        queries = q_ref[rows, pair * 2 * HD : (pair + 1) * 2 * HD] * jnp.asarray(HD ** (-0.5), BF16)
        zero = jnp.zeros_like(queries)
        halves.append(jnp.where(lane < HD, queries, zero))
        halves.append(jnp.where(lane >= HD, queries, zero))

    def step(block, state):
        offset = pl.multiple_of(block * chunk, chunk)
        there = pl.ds(offset, chunk)
        spot = offset + lax.broadcasted_iota(jnp.int32, (chunk, tile), 0)
        allowed = (spot >= first) & (spot <= last)
        scores = []
        for index, half in enumerate(halves):
            lanes = slice(index // 2 * 2 * HD, (index // 2 + 1) * 2 * HD)
            scores.append(dot_nt(keys_ref[there, lanes], half))
        out = []
        for index, (top, total, accum) in enumerate(state):
            lanes = slice(cols + index // 2 * 2 * HD, cols + (index // 2 + 1) * 2 * HD)
            score = jnp.where(allowed, scores[index], MASKED)
            new_top = jnp.maximum(top, jnp.max(score, axis=0, keepdims=True))
            factor = jnp.exp(top - new_top)
            weights = jnp.exp(score - new_top)
            total = total * factor + jnp.sum(weights, axis=0, keepdims=True)
            accum = accum * factor + dot_tn(keys_ref[there, lanes], weights.astype(BF16))
            out.append((new_top, total, accum))
        return tuple(out)

    start = (
        jnp.full((1, tile), MASKED, F32),
        jnp.zeros((1, tile), F32),
        jnp.zeros((2 * HD, tile), F32),
    )
    state = lax.fori_loop(begin, end, step, tuple(start for _ in halves))
    for pair in pairs:
        lanes = slice(pair * 2 * HD, (pair + 1) * 2 * HD)
        parts = []
        for which in range(2):
            head = 2 * pair + which
            top, total, accum = state[head]
            log_ref[head : head + 1, rows] = top + jnp.log(total)
            parts.append(accum[which * HD : (which + 1) * HD] / total)
        attended = jnp.transpose(jnp.concatenate(parts, axis=0))
        attended_ref[rows, lanes] = attended
        mixed_ref[rows, lanes] = attended.astype(BF16)


def pack_query(sizes, l, refs):
    cols = sizes.cols
    gain = refs.attn_gain[l]
    for part, weight in enumerate((refs.w_query, refs.w_key, refs.w_value)):
        for peer in range(sizes.peers):
            piece = weight[l, :, peer * cols : (peer + 1) * cols].astype(F32) * gain
            refs.pack_q[peer, l, :, part * cols : (part + 1) * cols] = piece.astype(BF16)


def pack_ffn(sizes, l, refs):
    strip, hidden = sizes.hidden // sizes.planes, sizes.hidden
    gain = refs.ffn_gain[l]
    for part, weight in enumerate((refs.w_gate, refs.w_up)):
        for peer in range(sizes.peers):
            for plane in range(sizes.planes):
                source = (plane * sizes.peers + peer) * strip
                piece = weight[l, :, source : source + strip].astype(F32) * gain
                target = part * hidden + plane * strip
                refs.pack_g[peer, l, :, target : target + strip] = piece.astype(BF16)


def document_starts(sizes, place, documents):
    group = sizes.group
    here = pl.ds(pl.multiple_of(place.plane * group, group), group)
    own = documents[:, here]
    every = documents[...]
    starts = jnp.zeros_like(own)
    for document in range(sizes.documents - 1):
        count = jnp.sum((every == document).astype(jnp.int32), axis=1, keepdims=True)
        starts = starts + jnp.where(own > document, count, 0)
    return starts - (place.plane * group - sizes.lead)


def forward_body(sizes, layer, refs):
    place = Place()
    tok, cols, group, hidden = sizes.tok, sizes.cols, sizes.group, sizes.hidden
    tile = sizes.tile
    loads = refs.load_sem
    if layer == 0:
        if sizes.aligned:
            pack_query(sizes, 0, refs)
        place.greet()
        swap_q = [
            WeightSwap(place, refs.pack_q, l, refs.mine_q.at[l], getattr(refs, f"swap_q{l}"))
            for l in range(LAYERS)
        ]
        swap_g = [
            WeightSwap(place, refs.pack_g, l, refs.mine_g.at[l], getattr(refs, f"swap_g{l}"))
            for l in range(LAYERS)
        ]
        out_w = [
            OutGather(
                place,
                refs.w_out.at[l],
                refs.mid_o.at[l],
                getattr(refs, f"out_full{l}"),
                getattr(refs, f"out_sem{l}"),
            )
            for l in range(LAYERS)
        ]
        gather_q = [
            HeadGather(
                place, refs.mine_q.at[l], getattr(refs, f"q_full{l}"), getattr(refs, f"gq_sem{l}")
            )
            for l in range(LAYERS)
        ]
        gather_g = HeadGather(place, refs.mine_g.at[0], refs.g_full, refs.gg_sem)
        swap_q[0].start()
    else:
        place.greet()
        gather_g = HeadGather(place, refs.mine_g.at[layer], refs.g_full, refs.gg_sem)
    gather_d = HeadGather(place, refs.w_down.at[layer], refs.d_full, refs.gd_sem)

    stream = refs.stream[...].astype(F32)
    scaled = (stream * inverse_rms(stream)).astype(BF16)
    own_rows = pl.ds(pl.multiple_of(place.peer * tok, tok), tok)
    refs.scaled[own_rows, :] = scaled
    ag1 = PlaneGather(place, refs.scaled, refs.ag1_s, refs.ag1_r)
    ag1.start()
    if layer == 0:
        if sizes.aligned:
            pack_ffn(sizes, 0, refs)
        swap_g[0].start()
        swap_q[0].arrive()
        gather_q[0].start()
        out_w[0].start()
        gather_d.start()
        gather_q[0].relay()
        gather_q[0].forward()
        gather_q[0].arrive()
    else:
        gather_d.start()
    q_load = pltpu.make_async_copy(refs.q_full0 if layer == 0 else refs.q_full, refs.wq, loads.at[0])
    q_load.start()
    if layer == 0:
        refs.first[...] = document_starts(sizes, place, refs.documents)
        if sizes.aligned:
            pack_query(sizes, 1, refs)
            pack_ffn(sizes, 1, refs)
    q_load.wait()

    for steps in peer_groups(place.peers):
        peers = [place.peer_before(step) for step in steps]
        rows = [pl.ds(pl.multiple_of(peer * tok, tok), tok) for peer in peers]
        for step in steps:
            ag1.await_step(step)
        x = jnp.concatenate([refs.scaled[where, :] for where in rows], axis=0)
        for part in range(3):

            def block(where, part=part, x=x, peers=peers, rows=rows):
                weight = refs.wq[
                    :, pl.ds(pl.multiple_of(part * cols + where.start, where.size), where.size)
                ]
                value = dot_nn(x, weight).astype(BF16)
                there = pl.ds(
                    pl.multiple_of(max(part - 1, 0) * cols + where.start, where.size), where.size
                )
                for index, peer in enumerate(peers):
                    piece = value[index * tok : (index + 1) * tok]
                    if part == 0:
                        refs.queries[rows[index], there] = piece
                    else:
                        spot = pl.multiple_of(sizes.lead + peer * tok, tok)
                        refs.keys[pl.ds(spot, tok), there] = piece

            by_columns(cols, block)
    halo = Halo(place, refs.keys, sizes.reach, refs.halo_sem)
    halo.start()
    if layer == 0:
        swap_g[0].arrive()
        gather_g.start()
        out_w[0].spread()
        swap_q[1].start()
        swap_g[1].start()
    else:
        gather_g.start()
    gather_d.relay()
    halo.relay()
    halo.arrive()
    if layer == 0:
        out_w[0].arrive()
    wo = refs.out_full0 if layer == 0 else refs.o_full

    sum1 = PlaneSum(place, refs.part1, refs.sum1, refs.rs1_s, refs.rs1_r)

    def attend_step(index, carry):
        attend_tile(
            sizes,
            place,
            index,
            refs.queries,
            refs.keys,
            refs.first,
            refs.mixed,
            refs.attended,
            refs.logs,
        )
        for k in range(tile // tok):
            peer = index * (tile // tok) + k
            x = refs.mixed[pl.ds(pl.multiple_of(peer * tok, tok), tok), :]

            def block(where, x=x, peer=peer):
                refs.part1[peer, :, where] = dot_nn(x, wo[:, where]).astype(BF16)

            by_columns(D, block)
            sum1.send_to(peer)
        return carry

    lax.fori_loop(0, group // tile, attend_step, 0)

    gather_g.relay()
    gather_d.forward()
    gather_g.forward()
    gather_g.arrive()
    gather_d.arrive()
    g_load = pltpu.make_async_copy(refs.g_full, refs.wg, loads.at[2])
    d_load = pltpu.make_async_copy(refs.d_full, refs.wd, loads.at[3])
    g_load.start()
    d_load.start()
    if layer == 0:
        swap_q[1].arrive()
        gather_q[1].start()
        out_w[1].start()
        swap_g[1].arrive()

    middle = stream + sum1.total()
    refs.middle[...] = middle
    refs.scaled_ffn[own_rows, :] = (middle * inverse_rms(middle)).astype(BF16)
    ag2 = PlaneGather(place, refs.scaled_ffn, refs.ag2_s, refs.ag2_r)
    ag2.start()
    g_load.wait()
    d_load.wait()
    sum2 = PlaneSum(place, refs.part2, refs.sum2, refs.rs2_s, refs.rs2_r)

    stores = []
    for steps in peer_groups(place.peers):
        peers = [place.peer_before(step) for step in steps]
        rows = [pl.ds(pl.multiple_of(peer * tok, tok), tok) for peer in peers]
        for step in steps:
            ag2.await_step(step)
        x = jnp.concatenate([refs.scaled_ffn[where, :] for where in rows], axis=0)

        def block(where, x=x, rows=rows):
            there = pl.ds(pl.multiple_of(hidden + where.start, where.size), where.size)
            gate = dot_nn(x, refs.wg[:, where])
            up = dot_nn(x, refs.wg[:, there])
            low = (gate / (1.0 + jnp.exp(-gate)) * up).astype(BF16)
            for index, row in enumerate(rows):
                piece = slice(index * tok, (index + 1) * tok)
                refs.gate_up[row, where] = gate[piece]
                refs.gate_up[row, there] = up[piece]
                refs.hidden[row, where] = low[piece]

        by_columns(hidden, block)
        low = jnp.concatenate([refs.hidden[where, :] for where in rows], axis=0)

        def down(where, low=low, peers=peers):
            value = dot_nn(low, refs.wd[:, where]).astype(BF16)
            for index, peer in enumerate(peers):
                refs.part2[peer, :, where] = value[index * tok : (index + 1) * tok]

        by_columns(D, down)
        for step, peer, row in zip(steps, peers, rows):
            sum2.send_to(peer)
            store = pltpu.make_async_copy(
                refs.gate_up.at[row], refs.gate_up_out.at[row], refs.store_sem.at[step]
            )
            store.start()
            stores.append(store)
    if layer == 0:
        gather_q[1].relay()
        gather_q[1].forward()
        out_w[1].spread()
    after = middle + sum2.total()
    refs.next[...] = after if layer < LAYERS - 1 else after.astype(BF16)
    if layer == 0:
        gather_q[1].arrive()
        out_w[1].arrive()
        for item in swap_q + swap_g + gather_q + out_w:
            item.finish()
    for store in stores:
        store.wait()
    for item in (ag1, ag2, sum1, sum2, gather_g, gather_d, halo):
        item.finish()


def forward_layer(sizes, layer, stream, first_row, weights, collective_id):
    peers, planes, depth = sizes.peers, sizes.planes, sizes.planes // 2
    tok, cols, group, hidden, reach = sizes.tok, sizes.cols, sizes.group, sizes.hidden, sizes.reach
    inputs = {"stream": (stream, VMEM), "w_down": (weights["w_down"], VMEM)}
    outputs = {
        "next": ((tok, D), F32 if layer < LAYERS - 1 else BF16, VMEM),
        "middle": ((tok, D), F32, VMEM),
        "scaled": ((group, D), BF16, VMEM),
        "scaled_ffn": ((group, D), BF16, VMEM),
        "queries": ((group, cols), BF16, VMEM),
        "keys": (((reach + 1) * group, 2 * cols), BF16, VMEM),
        "mixed": ((group, cols), BF16, VMEM),
        "attended": ((group, cols), F32, VMEM),
        "logs": ((cols // HD, group), F32, VMEM),
        "gate_up_out": ((group, 2 * hidden), F32, ANY),
        "hidden": ((group, hidden), BF16, VMEM),
        "g_full": ((D, 2 * hidden), BF16, ANY),
        "d_full": ((hidden, D), BF16, ANY),
    }
    scratch = {
        "wq": pltpu.VMEM((D, 3 * cols), BF16),
        "wg": pltpu.VMEM((D, 2 * hidden), BF16),
        "wd": pltpu.VMEM((hidden, D), BF16),
        "gate_up": pltpu.VMEM((group, 2 * hidden), F32),
        "store_sem": dma(peers),
        "part1": pltpu.VMEM((peers, tok, D), BF16),
        "sum1": pltpu.VMEM((peers, tok, D), BF16),
        "part2": pltpu.VMEM((peers, tok, D), BF16),
        "sum2": pltpu.VMEM((peers, tok, D), BF16),
        "load_sem": dma(4),
        "halo_sem": Halo.sems(reach),
        "gg_sem": HeadGather.sems(depth),
        "gd_sem": HeadGather.sems(depth),
    }
    for name in ("ag1_s", "ag1_r", "ag2_s", "ag2_r", "rs1_s", "rs1_r", "rs2_s", "rs2_r"):
        scratch[name] = dma(peers - 1)
    if layer == 0:
        rows = peers * sizes.own_rows
        inputs["documents"] = (first_row, VMEM)
        outputs["first"] = ((1, group), jnp.int32, VMEM)
        if sizes.aligned:
            for name in ("w_query", "w_key", "w_value", "w_gate", "w_up", "attn_gain", "ffn_gain"):
                inputs[name] = (weights[name], VMEM)
            scratch["pack_q"] = pltpu.VMEM((peers, LAYERS, sizes.own_rows, 3 * cols), BF16)
            scratch["pack_g"] = pltpu.VMEM((peers, LAYERS, sizes.own_rows, 2 * hidden), BF16)
        else:
            inputs["pack_q"] = (weights["pack_q"], ANY)
            inputs["pack_g"] = (weights["pack_g"], ANY)
        inputs["w_out"] = (weights["w_out"], VMEM)
        outputs["mine_q"] = ((LAYERS, rows, 3 * cols), BF16, VMEM)
        outputs["mine_g"] = ((LAYERS, rows, 2 * hidden), BF16, VMEM)
        scratch["mid_o"] = pltpu.VMEM((LAYERS, planes * sizes.own_rows, D), BF16)
        for l in range(LAYERS):
            outputs[f"q_full{l}"] = ((D, 3 * cols), BF16, ANY)
            outputs[f"out_full{l}"] = ((cols, D), BF16, VMEM)
            scratch[f"swap_q{l}"] = WeightSwap.sems(peers)
            scratch[f"swap_g{l}"] = WeightSwap.sems(peers)
            scratch[f"out_sem{l}"] = OutGather.sems(peers, depth)
            scratch[f"gq_sem{l}"] = HeadGather.sems(depth)
    else:
        inputs["mine_g"] = (weights["mine_g"], VMEM)
        inputs["q_full"] = (weights["q_full"], ANY)
        inputs["o_full"] = (weights["o_full"], VMEM)
        inputs["first"] = (first_row, VMEM)
    return launch(
        functools.partial(forward_body, sizes, layer),
        f"forward{layer}",
        inputs,
        outputs,
        scratch,
        collective_id,
        flops=group * D * (4 * cols + 3 * hidden) * 2,
    )


def dot_nt(left, right):
    return lax.dot_general(left, right, (((1,), (1,)), ((), ())), preferred_element_type=F32)


def dot_nn(left, right):
    return lax.dot_general(left, right, (((1,), (0,)), ((), ())), preferred_element_type=F32)


def dot_tn(left, right):
    return lax.dot_general(left, right, (((0,), (0,)), ((), ())), preferred_element_type=F32)


class HaloBack:
    def __init__(self, place, total, give, land, s_land, reach, sems):
        self.place, self.total, self.give, self.land, self.s_land = place, total, give, land, s_land
        self.reach = reach
        self.rows, self.width = land.shape[1:]
        self.z_send, self.z_recv, self.s_send, self.s_recv = sems

    def block(self, ref, offset):
        return ref.at[self.reach - offset]

    def lanes(self, offset):
        return slice((self.reach - offset) * self.width, (self.reach - offset + 1) * self.width)

    def hand_copy(self, i):
        return remote(
            self.block(self.give, 2 * i - 1),
            self.s_land.at[i - 1],
            self.s_send.at[i - 1],
            self.s_recv.at[i - 1],
            head=self.place.sibling,
        )

    def hands(self, i):
        return self.place.z - i + self.place.core >= 0

    def handed(self, i):
        return self.place.z - i + 1 - self.place.core >= 0

    def low(self, offset):
        self.give[self.reach - offset] = self.total[:, self.lanes(offset)].astype(BF16)

    def hand(self):
        for i in range(1, self.reach // 2 + 1):

            @pl.when(self.hands(i))
            def _(i=i):
                self.low(2 * i - 1)
                self.hand_copy(i).start()

    def add(self, i, offset):
        where = self.lanes(offset)
        self.total[:, where] = self.total[:, where] + self.s_land[i - 1].astype(F32)

    def z_copy(self, i):
        return remote(
            self.block(self.give, 2 * i),
            self.land.at[i - 1],
            self.z_send.at[i - 1],
            self.z_recv.at[i - 1],
            head=self.place.plane - 2 * i,
        )

    def sends(self, i):
        return self.place.z - i >= 0

    def receives(self, i):
        return self.place.z + i < self.place.depth

    def send(self):
        for i in range(1, self.reach // 2 + 1):

            @pl.when((self.place.core == 1) & self.handed(i))
            def _(i=i):
                self.hand_copy(i).wait_recv()
                self.add(i, 2 * i)

            if i > 1:

                @pl.when((self.place.core == 0) & self.handed(i))
                def _(i=i):
                    self.hand_copy(i).wait_recv()
                    self.add(i, 2 * i - 2)

        for i in range(1, self.reach // 2 + 1):

            @pl.when(self.sends(i))
            def _(i=i):
                self.low(2 * i)
                self.z_copy(i).start()

    def collect(self):
        @pl.when((self.place.core == 0) & self.handed(1))
        def _():
            self.hand_copy(1).wait_recv()
            self.add(1, 0)

        where = self.lanes(0)
        for i in range(1, self.reach // 2 + 1):

            @pl.when(self.receives(i))
            def _(i=i):
                self.z_copy(i).wait_recv()
                self.total[:, where] = self.total[:, where] + self.land[i - 1].astype(F32)

    def finish(self):
        for i in range(1, self.reach // 2 + 1):

            @pl.when(self.hands(i))
            def _(i=i):
                self.hand_copy(i).wait_send()

            @pl.when(self.sends(i))
            def _(i=i):
                self.z_copy(i).wait_send()


class GradJob:
    def __init__(self, place, left, right, bufs, flips, sems):
        self.place, self.left, self.right = place, left, right
        self.left_sib, self.right_sib, self.out, self.land, self.far = bufs
        self.flipped, self.flipped_sib = flips
        self.s_send, self.s_recv, self.z_send, self.z_recv, self.f_send, self.f_recv = sems
        self.outer = (place.z == 0) | (place.z == place.depth - 1)
        self.width = self.out.shape[1]

    @staticmethod
    def sems(depth):
        return [dma(depth + 1), dma(depth + 1), dma(depth - 1), dma(depth - 1), dma(), dma()]

    @staticmethod
    def bufs(group, depth, width, cols):
        return [
            pltpu.VMEM((group, depth * width), BF16),
            pltpu.VMEM((group, cols), BF16),
            pltpu.VMEM((depth, width, cols), BF16),
            pltpu.VMEM((depth - 1, width, cols), BF16),
            pltpu.VMEM((width, cols), BF16),
        ]

    def lanes(self, z, core):
        return pl.ds(pl.multiple_of((2 * z + core) * self.width, self.width), self.width)

    def right_copy(self):
        return remote(
            self.right,
            self.right_sib,
            self.s_send.at[0],
            self.s_recv.at[0],
            head=self.place.sibling,
        )

    def left_copy(self, z):
        return remote(
            self.left.at[:, self.lanes(z, 1 - self.place.core)],
            self.left_sib.at[:, pl.ds(z * self.width, self.width)],
            self.s_send.at[z + 1],
            self.s_recv.at[z + 1],
            head=self.place.sibling,
        )

    def exchange(self):
        self.right_copy().start()
        for z in range(self.place.depth):
            self.left_copy(z).start()

    def z_copy(self, step):
        z = self.place.z_after(step)
        return remote(
            self.out.at[z],
            self.land.at[step - 1],
            self.z_send.at[step - 1],
            self.z_recv.at[step - 1],
            head=2 * z + self.place.core,
        )

    def send(self, step):
        self.z_copy(step).start()

    def far_copy(self):
        z = self.place.z
        return remote(
            self.out.at[self.place.depth - 1 - z],
            self.far,
            self.f_send,
            self.f_recv,
            head=2 * (1 + lax.div(z, 2)) + self.place.core,
        )

    def sends(self, step):
        z = self.place.z
        return z >= 0 if step == 2 else (z < 3 if step == 1 else z > 0)

    def receives(self, step):
        z = self.place.z
        return z >= 0 if step == 2 else (z > 0 if step == 1 else z < 3)

    def compute(self):
        for z in range(self.place.depth):
            mine = jnp.transpose(self.left[:, self.lanes(z, self.place.core)].astype(F32))
            self.flipped[z * self.width : (z + 1) * self.width, :] = mine.astype(BF16)
        for z in range(self.place.depth):
            self.left_copy(z).wait_recv()
            here = slice(z * self.width, (z + 1) * self.width)
            theirs = jnp.transpose(self.left_sib[:, here].astype(F32))
            self.flipped_sib[here, :] = theirs.astype(BF16)
        self.right_copy().wait_recv()

        def tile(where):
            value = dot_nn(self.flipped[...], self.right[:, where])
            value = value + dot_nn(self.flipped_sib[...], self.right_sib[:, where])
            value = value.astype(BF16)
            for z in range(self.place.depth):
                self.out[z, :, where] = value[z * self.width : (z + 1) * self.width]

        by_columns(self.out.shape[2], tile)

        @pl.when(self.outer)
        def _():
            self.far_copy().start()
            self.z_copy(2).start()

        for step in (1, 3):

            @pl.when(self.sends(step))
            def _(step=step):
                self.z_copy(step).start()

    def relay(self):
        @pl.when(jnp.logical_not(self.outer))
        def _():
            self.far_copy().wait_recv()
            z = self.place.z_after(2)
            self.out[z] = (self.out[z].astype(F32) + self.far[...].astype(F32)).astype(BF16)
            self.z_copy(2).start()

    def total(self):
        total = self.out[self.place.z].astype(F32)
        for step in range(1, self.place.depth):

            @pl.when(self.receives(step))
            def _(step=step):
                self.z_copy(step).wait_recv()

            piece = self.land[step - 1].astype(F32)
            total = total + jnp.where(self.receives(step), piece, 0.0)
        return total

    def finish(self):
        self.right_copy().wait_send()
        for z in range(self.place.depth):
            self.left_copy(z).wait_send()

        @pl.when(self.outer)
        def _():
            self.far_copy().wait_send()

        for step in range(1, self.place.depth):

            @pl.when(self.sends(step))
            def _(step=step):
                self.z_copy(step).wait_send()


class OutGradJob:
    def __init__(self, place, left, right, bufs, sems):
        self.place, self.left, self.right = place, left, right
        self.left_sib, self.right_sib, self.out, self.mid, self.land = bufs
        self.s_send, self.s_recv, self.p_send, self.p_recv, self.z_send, self.z_recv, self.local = sems
        self.width = self.out.shape[0]
        self.rows = self.mid.shape[1]

    @staticmethod
    def sems(peers, depth):
        return [
            dma(2),
            dma(2),
            dma(peers - 1),
            dma(peers - 1),
            dma(depth - 1),
            dma(depth - 1),
            dma(),
        ]

    @staticmethod
    def bufs(group, peers, depth, width, cols):
        return [
            pltpu.VMEM((group, width), BF16),
            pltpu.VMEM((group, cols), BF16),
            pltpu.VMEM((width, cols), BF16),
            pltpu.VMEM((peers, width // peers, cols), BF16),
            pltpu.VMEM((depth - 1, width // peers, cols), BF16),
        ]

    def lanes(self, core):
        return pl.ds(pl.multiple_of(core * self.width, self.width), self.width)

    def copies(self):
        return (
            remote(
                self.right,
                self.right_sib,
                self.s_send.at[0],
                self.s_recv.at[0],
                head=self.place.sibling,
            ),
            remote(
                self.left.at[:, self.lanes(1 - self.place.core)],
                self.left_sib,
                self.s_send.at[1],
                self.s_recv.at[1],
                head=self.place.sibling,
            ),
        )

    def exchange(self):
        for copy in self.copies():
            copy.start()

    def piece(self, peer):
        return self.out.at[pl.ds(pl.multiple_of(peer * self.rows, self.rows), self.rows)]

    def p_copy(self, step):
        target = self.place.peer_after(step)
        return remote(
            self.piece(target),
            self.mid.at[self.place.peer],
            self.p_send.at[step - 1],
            self.p_recv.at[step - 1],
            blk=target,
        )

    def own_copy(self):
        return pltpu.make_async_copy(
            self.piece(self.place.peer), self.mid.at[self.place.peer], self.local
        )

    def z_copy(self, step):
        z = self.place.z_after(step)
        return remote(
            self.mid.at[z],
            self.land.at[step - 1],
            self.z_send.at[step - 1],
            self.z_recv.at[step - 1],
            head=2 * z + self.place.core,
        )

    def compute(self):
        for copy in self.copies():
            copy.wait_recv()
        mine = jnp.transpose(self.left[:, self.lanes(self.place.core)].astype(F32)).astype(BF16)
        theirs = jnp.transpose(self.left_sib[...].astype(F32)).astype(BF16)

        def tile(where):
            value = dot_nn(mine, self.right[:, where]) + dot_nn(theirs, self.right_sib[:, where])
            self.out[:, where] = value.astype(BF16)

        by_columns(self.out.shape[1], tile)
        for step in range(1, self.place.peers):
            self.p_copy(step).start()
        self.own_copy().start()

    def spread(self):
        self.own_copy().wait()
        for step in range(1, self.place.peers):
            source = self.place.peer_before(step)
            remote(
                self.piece(source),
                self.mid.at[source],
                self.p_send.at[step - 1],
                self.p_recv.at[step - 1],
                blk=source,
            ).wait_recv()
        for step in range(1, self.place.depth):
            self.z_copy(step).start()

    def total(self):
        total = self.mid[self.place.z].astype(F32)
        for step in range(1, self.place.depth):
            self.z_copy(step).wait_recv()
            total = total + self.land[step - 1].astype(F32)
        return total

    def finish(self):
        for copy in self.copies():
            copy.wait_send()
        for step in range(1, self.place.peers):
            self.p_copy(step).wait_send()
        for step in range(1, self.place.depth):
            self.z_copy(step).wait_send()


def rms_back_of(values, upstream):
    inverse = inverse_rms(values)
    inner_mean = jnp.mean(upstream * values, axis=-1, keepdims=True)
    return inverse * upstream - values * (inverse * inverse * inverse) * inner_mean


def attend_back_chunk(sizes, place, block_offset, index, refs):
    tile, chunk, cols, group, lead = sizes.tile, sizes.chunk, sizes.cols, sizes.group, sizes.lead
    block = sizes.reach - block_offset
    offset = pl.multiple_of(block * group + index * chunk, chunk)
    there = pl.ds(offset, chunk)
    here = pl.ds(pl.multiple_of(index * chunk, chunk), chunk)
    spot = offset + lax.broadcasted_iota(jnp.int32, (chunk, 1), 0)
    lane = lax.broadcasted_iota(jnp.int32, (tile, 2 * HD), 1)
    begin = lax.div(jnp.maximum(offset - lead, 0), tile)
    end = jnp.minimum(
        lax.div(jnp.maximum(offset + chunk + sizes.doc_max - 2 - lead + tile, 0), tile), group // tile
    )
    pairs = range(cols // (2 * HD))
    lanes = [slice(pair * 2 * HD, (pair + 1) * 2 * HD) for pair in pairs]
    value_lanes = [slice(cols + part.start, cols + part.stop) for part in lanes]

    def step(index, sums):
        row = pl.multiple_of(index * tile, tile)
        rows = pl.ds(row, tile)
        last = lead + row + lax.broadcasted_iota(jnp.int32, (1, tile), 1)
        allowed = (spot >= refs.first[:, rows]) & (spot <= last)
        masks = (lane < HD, lane >= HD)
        halves, grads, scores, changes = [], [], [], []
        for pair in pairs:
            queries = refs.queries[rows, lanes[pair]] * jnp.asarray(HD ** (-0.5), BF16)
            upstream = refs.mixed_grad[rows, lanes[pair]]
            for mask in masks:
                halves.append(jnp.where(mask, queries, jnp.zeros_like(queries)))
                grads.append(jnp.where(mask, upstream, jnp.zeros_like(upstream)))
                scores.append(dot_nt(refs.keys[there, lanes[pair]], halves[-1]))
                changes.append(dot_nt(refs.keys[there, value_lanes[pair]], grads[-1]))
        out = list(sums)
        for pair in pairs:
            back = []
            for which in range(2):
                head = 2 * pair + which
                line = slice(head, head + 1)
                probs = jnp.where(allowed, jnp.exp(scores[head] - refs.logs[line, rows]), 0.0)
                change = (probs * (changes[head] - refs.delta[line, rows])).astype(BF16)
                out[2 * pair] = out[2 * pair] + dot_nn(change, halves[head])
                out[2 * pair + 1] = out[2 * pair + 1] + dot_nn(probs.astype(BF16), grads[head])
                back.append(dot_tn(change, refs.keys[there, lanes[pair]]))
            refs.dq[rows, lanes[pair]] += jnp.where(masks[0], back[0], back[1])
        return tuple(out)

    empty = jnp.zeros((chunk, 2 * HD), F32)
    sums = lax.fori_loop(begin, end, step, tuple(empty for _ in pairs for _ in range(2)))
    base = block * 2 * cols
    for pair in pairs:
        for part, value in ((lanes[pair], sums[2 * pair]), (value_lanes[pair], sums[2 * pair + 1])):
            refs.dkv[here, base + part.start : base + part.stop] = value


def backward_body(sizes, layer, fused, refs):
    place = Place()
    tok, cols, group, hidden = sizes.tok, sizes.cols, sizes.group, sizes.hidden
    tile, chunk, lead, reach = sizes.tile, sizes.chunk, sizes.lead, sizes.reach
    refs.gate_up = refs.dkv.at[:, pl.ds(0, 2 * hidden)]
    place.greet()
    grad = refs.grad[...].astype(F32)
    own_rows = pl.ds(pl.multiple_of(place.peer * tok, tok), tok)
    refs.down_in[own_rows, :] = grad.astype(BF16)
    ag1 = PlaneGather(place, refs.down_in, refs.ag1_s, refs.ag1_r)
    ag1.start()
    loads = {
        name: pltpu.make_async_copy(src, dst, refs.load_sem.at[index])
        for index, (name, src, dst) in enumerate(
            (
                ("d", refs.d_full, refs.wd),
                ("gate_up", refs.gate_up_in, refs.gate_up),
                ("g", refs.g_full, refs.wg),
                ("o", refs.o_full, refs.wo),
                ("q", refs.q_full, refs.wq),
                ("hidden", refs.hidden_in, refs.hidden),
                ("scaled_ffn", refs.scaled_ffn_in, refs.scaled_ffn),
            )
        )
    }
    for copy in loads.values():
        copy.start()
    jobs = []
    if fused:
        job_d = GradJob(place, refs.hidden, refs.down_in, refs.jd_buf, refs.flips, refs.jd_sem)
        job_g = GradJob(place, refs.scaled_ffn, refs.gate_up_grad, refs.jg_buf, refs.flips, refs.jg_sem)
        job_o = OutGradJob(place, refs.mixed, refs.proj_in, refs.jo_buf, refs.jo_sem)
        jobs = [job_d, job_o]
        if layer == 0:
            job_q = GradJob(
                place, refs.old_scaled, refs.old_qkv, refs.jq_buf, refs.flips, refs.jq_sem
            )
            jobs.append(job_q)
            job_q.exchange()
        loads["hidden"].wait()
        loads["scaled_ffn"].wait()
    loads["d"].wait()
    loads["gate_up"].wait()
    loads["g"].wait()
    if fused and layer == 0:
        job_q.compute()
        job_q.relay()

    sum1 = PlaneSum(place, refs.part1, refs.sum1, refs.rs1_s, refs.rs1_r)

    for steps in peer_groups(place.peers):
        peers = [place.peer_before(step) for step in steps]
        rows = [pl.ds(pl.multiple_of(peer * tok, tok), tok) for peer in peers]
        for step in steps:
            ag1.await_step(step)
        if fused and steps[-1] == place.peers - 1:
            job_d.exchange()
        x = jnp.concatenate([refs.down_in[where, :] for where in rows], axis=0)

        def block(where, x=x, rows=rows):
            there = pl.ds(pl.multiple_of(hidden + where.start, where.size), where.size)
            grad_hidden = dot_nt(x, refs.wd[where, :])
            for index, row in enumerate(rows):
                piece = grad_hidden[index * tok : (index + 1) * tok]
                gate = refs.gate_up[row, where]
                up = refs.gate_up[row, there]
                sigmoid = 1.0 / (1.0 + jnp.exp(-gate))
                gate_grad = piece * up * (sigmoid * (1.0 + gate * (1.0 - sigmoid)))
                refs.gate_up_grad[row, where] = gate_grad.astype(BF16)
                refs.gate_up_grad[row, there] = (piece * (gate * sigmoid)).astype(BF16)

        by_columns(hidden, block)
        low = jnp.concatenate([refs.gate_up_grad[where, :] for where in rows], axis=0)

        def back(where, low=low, peers=peers):
            value = dot_nt(low, refs.wg[where, :]).astype(BF16)
            for index, peer in enumerate(peers):
                refs.part1[peer, :, where] = value[index * tok : (index + 1) * tok]

        by_columns(D, back)
        for peer in peers:
            sum1.send_to(peer)

    if fused:
        job_g.exchange()
        job_d.compute()
        if layer == 0:
            own_scaled = refs.wd.at[pl.ds(0, group)]
            scaled_load = pltpu.make_async_copy(refs.scaled_in, own_scaled, refs.load_sem.at[0])
            scaled_load.start()
    middle = refs.middle[...]
    grad_middle = grad + rms_back_of(middle, sum1.total())
    refs.proj_in[own_rows, :] = grad_middle.astype(BF16)
    ag2 = PlaneGather(place, refs.proj_in, refs.ag2_s, refs.ag2_r)
    ag2.start()
    if fused:
        job_g.compute()
        job_d.relay()
    refs.dq[...] = jnp.zeros_like(refs.dq)
    loads["o"].wait()
    loads["q"].wait()

    for steps in peer_groups(place.peers):
        rows = [
            pl.ds(pl.multiple_of(place.peer_before(step) * tok, tok), tok) for step in steps
        ]
        for step in steps:
            ag2.await_step(step)
        x = jnp.concatenate([refs.proj_in[where, :] for where in rows], axis=0)

        def block(where, x=x, rows=rows):
            value = dot_nt(x, refs.wo[where, :]).astype(BF16)
            for index, row in enumerate(rows):
                refs.mixed_grad[row, where] = value[index * tok : (index + 1) * tok]

        by_columns(cols, block)
    if fused:
        job_o.exchange()

    def deltas(index, carry):
        rows = pl.ds(pl.multiple_of(index * tile, tile), tile)
        for pair in range(cols // (2 * HD)):
            lanes = slice(pair * 2 * HD, (pair + 1) * 2 * HD)
            product = jnp.transpose(
                refs.mixed_grad[rows, lanes].astype(F32) * refs.attended[rows, lanes]
            )
            for which in range(2):
                refs.delta[2 * pair + which : 2 * pair + which + 1, rows] = jnp.sum(
                    product[which * HD : (which + 1) * HD], axis=0, keepdims=True
                )
        return carry

    lax.fori_loop(0, group // tile, deltas, 0)

    halo = HaloBack(place, refs.dkv, refs.give, refs.land, refs.s_land, reach, refs.halo_sem)
    per_block = group // chunk

    def key_blocks(offset):
        @pl.when(place.plane >= offset)
        def _():
            def body(index, carry):
                attend_back_chunk(sizes, place, offset, index, refs)
                return carry

            lax.fori_loop(0, per_block, body, 0)

    for offset in range(1, reach + 1, 2):
        key_blocks(offset)
    halo.hand()
    for offset in range(2, reach + 1, 2):
        key_blocks(offset)
    halo.send()
    if fused:
        job_g.relay()
    key_blocks(0)
    swaps = []

    def hand_out(name, value):
        pack = getattr(refs, f"pack_{name}")
        for peer in range(sizes.peers):
            pack[peer, 0] = value[peer * sizes.own_rows : (peer + 1) * sizes.own_rows]
        swap = WeightSwap(
            place, pack, 0, getattr(refs, f"rows_{name}"), getattr(refs, f"swap_{name}")
        )
        swap.start()
        swaps.append(swap)

    if fused:
        job_o.compute()
        if layer == 0:
            hand_out("q1", job_q.total().astype(BF16))
            hand_out("g1", refs.raw_g1[...])
    refs.qkv_grad[:, 0:cols] = (refs.dq[...] * (HD ** (-0.5))).astype(BF16)
    if fused:
        job_o.spread()
    halo.collect()
    refs.qkv_grad[:, cols:] = refs.dkv[:, reach * 2 * cols : (reach + 1) * 2 * cols].astype(BF16)
    if fused and layer == 0:
        scaled_load.wait()
        job_p = GradJob(place, own_scaled, refs.qkv_grad, refs.jp_buf, refs.flips, refs.jp_sem)
        job_p.exchange()

    sum1.finish()
    sum2 = PlaneSum(place, refs.part1, refs.sum2, refs.rs2_s, refs.rs2_r)

    for steps in [g for g in peer_groups(place.peers)[1:]] + [(0,)]:
        peers = [place.peer_before(step) for step in steps]
        low = jnp.concatenate(
            [refs.qkv_grad[pl.ds(pl.multiple_of(peer * tok, tok), tok), :] for peer in peers], axis=0
        )

        def back(where, low=low, peers=peers):
            value = dot_nt(low, refs.wq[where, :]).astype(BF16)
            for index, peer in enumerate(peers):
                refs.part1[peer, :, where] = value[index * tok : (index + 1) * tok]

        by_columns(D, back)
        for peer in peers:
            sum2.send_to(peer)

    if fused and layer == 0:
        job_p.compute()
    refs.next[...] = grad_middle + rms_back_of(refs.stream[...].astype(F32), sum2.total())
    if fused and layer == 0:
        job_p.relay()
    for item in [ag1, ag2, sum2, halo]:
        item.finish()
    if not fused:
        loads["hidden"].wait()
        loads["scaled_ffn"].wait()
        return
    refs.raw_down[...] = job_d.total()
    refs.raw_o[...] = job_o.total()
    if layer > 0:
        refs.raw_g[...] = job_g.total().astype(BF16)
        job_g.finish()
    else:
        hand_out("g0", job_g.total().astype(BF16))
        hand_out("q0", job_p.total().astype(BF16))
        job_g.finish()
        job_p.finish()

        for swap in swaps:
            swap.arrive()
            swap.finish()
    for item in jobs:
        item.finish()


def backward_layer(sizes, layer, fused, grad, first_row, kept, full, old, collective_id):
    peers, planes, depth = sizes.peers, sizes.planes, sizes.planes // 2
    tok, cols, group, hidden, reach = sizes.tok, sizes.cols, sizes.group, sizes.hidden, sizes.reach
    q_full, o_full, g_full, d_full = full
    inputs = {
        "grad": (grad, VMEM),
        "first": (first_row, VMEM),
        "middle": (kept["middle"], VMEM),
        "stream": (kept["stream"], VMEM),
        "queries": (kept["queries"], VMEM),
        "keys": (kept["keys"], VMEM),
        "attended": (kept["attended"], VMEM),
        "logs": (kept["logs"], VMEM),
        "mixed": (kept["mixed"], VMEM),
        "gate_up_in": (kept["gate_up_out"], ANY),
        "hidden_in": (kept["hidden"], ANY),
        "scaled_ffn_in": (kept["scaled_ffn"], ANY),
        "q_full": (q_full, ANY),
        "o_full": (o_full, ANY),
        "g_full": (g_full, ANY),
        "d_full": (d_full, ANY),
    }
    outputs = {
        "next": ((tok, D), F32, VMEM),
        "qkv_grad": ((group, 3 * cols), BF16, VMEM),
    }
    scratch = {
        "wq": pltpu.VMEM((D, 3 * cols), BF16),
        "wo": pltpu.VMEM((cols, D), BF16),
        "wg": pltpu.VMEM((D, 2 * hidden), BF16),
        "wd": pltpu.VMEM((hidden, D), BF16),
        "dkv": pltpu.VMEM((group, max(2 * hidden, (reach + 1) * 2 * cols)), F32),
        "hidden": pltpu.VMEM((group, hidden), BF16),
        "scaled_ffn": pltpu.VMEM((group, D), BF16),
        "mixed_grad": pltpu.VMEM((group, cols), BF16),
        "delta": pltpu.VMEM((cols // HD, group), F32),
        "dq": pltpu.VMEM((group, cols), F32),
        "give": pltpu.VMEM((reach, group, 2 * cols), BF16),
        "land": pltpu.VMEM((reach // 2, group, 2 * cols), BF16),
        "s_land": pltpu.VMEM((reach // 2, group, 2 * cols), BF16),
        "load_sem": dma(7),
        "halo_sem": Halo.sems(reach),
    }
    for name in ("part1", "sum1", "sum2"):
        scratch[name] = pltpu.VMEM((peers, tok, D), BF16)
    for name in ("ag1_s", "ag1_r", "ag2_s", "ag2_r", "rs1_s", "rs1_r", "rs2_s", "rs2_r"):
        scratch[name] = dma(peers - 1)
    space = pltpu.VMEM
    if fused:
        scratch["down_in"] = space((group, D), BF16)
        scratch["proj_in"] = space((group, D), BF16)
        scratch["gate_up_grad"] = space((group, 2 * hidden), BF16)
        width = D // planes
        strip = hidden // planes
        scratch["flips"] = [pltpu.VMEM((depth * width, group), BF16)] * 2
        scratch["jd_buf"] = GradJob.bufs(group, depth, strip, D)
        scratch["jg_buf"] = GradJob.bufs(group, depth, width, 2 * hidden)
        scratch["jo_buf"] = OutGradJob.bufs(group, peers, depth, cols // 2, D)
        scratch["jd_sem"] = GradJob.sems(depth)
        scratch["jg_sem"] = GradJob.sems(depth)
        scratch["jo_sem"] = OutGradJob.sems(peers, depth)
        outputs["raw_down"] = ((strip, D), F32, VMEM)
        outputs["raw_o"] = ((sizes.own_rows, D), F32, VMEM)
        if layer > 0:
            outputs["raw_g"] = ((width, 2 * hidden), BF16, VMEM)
        else:
            rows = sizes.own_rows
            inputs["old_scaled"] = (old["scaled"], VMEM)
            inputs["old_qkv"] = (old["qkv_grad"], VMEM)
            inputs["raw_g1"] = (old["raw_g"], VMEM)
            inputs["scaled_in"] = (kept["scaled"], ANY)
            for name in ("jq", "jp"):
                scratch[f"{name}_buf"] = GradJob.bufs(group, depth, width, 3 * cols)
                scratch[f"{name}_sem"] = GradJob.sems(depth)
            for l in range(LAYERS):
                for kind, width_of in (("g", 2 * hidden), ("q", 3 * cols)):
                    outputs[f"rows_{kind}{l}"] = ((peers * rows, width_of), BF16, VMEM)
                    scratch[f"pack_{kind}{l}"] = pltpu.VMEM((peers, 1, rows, width_of), BF16)
                    scratch[f"swap_{kind}{l}"] = WeightSwap.sems(peers)
    else:
        outputs["down_in"] = ((group, D), BF16, VMEM)
        outputs["proj_in"] = ((group, D), BF16, VMEM)
        outputs["gate_up_grad"] = ((group, 2 * hidden), BF16, VMEM)
    return launch(
        functools.partial(backward_body, sizes, layer, fused),
        f"backward{layer}",
        inputs,
        outputs,
        scratch,
        collective_id,
        flops=group * D * (4 * cols + 3 * hidden) * 4,
    )


def inverse_rms(values):
    return lax.rsqrt(jnp.mean(values * values, axis=-1, keepdims=True) + EPSILON)


def matmul(left, right):
    return jnp.dot(left, right, preferred_element_type=F32)


def contract_rows(left, right):
    return jnp.einsum("td,te->de", left, right, preferred_element_type=F32)


def contract_cols(left, right):
    return jnp.einsum("te,de->td", left, right, preferred_element_type=F32)


def local(
    tokens,
    gain_attn,
    w_query,
    w_key,
    w_value,
    w_out,
    gain_ffn,
    w_gate,
    w_up,
    w_down,
    doc_ids,
    cotangent,
):
    planes = lax.axis_size("head")
    peers = lax.axis_size("blk")
    plane = lax.axis_index("head")
    tok = tokens.shape[0]
    group = tok * peers
    stream_rows = group * planes
    doc_max = stream_rows // 4
    reach = (doc_max - 1 + group - 1) // group
    reach = reach + reach % 2
    own_rows = w_query.shape[1]
    cols = D // peers
    strip = w_down.shape[1]
    hidden_cols = strip * planes
    tile = 256
    chunk = 256
    lead = reach * group

    attn_rows = gain_attn.astype(F32)[:, :, None]
    ffn_rows = gain_ffn.astype(F32)[:, :, None]

    def for_peers(weight, gain):
        scaled = (weight.astype(F32) * gain).astype(BF16)
        return scaled.reshape(LAYERS, own_rows, peers, cols).transpose(2, 0, 1, 3)

    def for_peers_ffn(weight, gain):
        scaled = (weight.astype(F32) * gain).astype(BF16)
        scaled = scaled.reshape(LAYERS, own_rows, planes, peers, strip).transpose(3, 0, 1, 2, 4)
        return scaled.reshape(peers, LAYERS, own_rows, hidden_cols)

    aligned = strip % 128 == 0
    weights = {"w_out": w_out, "w_down": w_down}
    if aligned:
        weights |= {
            "w_query": w_query,
            "w_key": w_key,
            "w_value": w_value,
            "w_gate": w_gate,
            "w_up": w_up,
            "attn_gain": attn_rows,
            "ffn_gain": ffn_rows,
        }
    else:
        weights |= {
            "pack_q": jnp.concatenate(
                [for_peers(w, attn_rows) for w in (w_query, w_key, w_value)], axis=3
            ),
            "pack_g": jnp.concatenate([for_peers_ffn(w, ffn_rows) for w in (w_gate, w_up)], axis=3),
        }
    sizes = types.SimpleNamespace(
        peers=peers,
        planes=planes,
        tok=tok,
        cols=cols,
        group=group,
        hidden=hidden_cols,
        reach=reach,
        own_rows=own_rows,
        tile=tile,
        chunk=chunk,
        lead=lead,
        doc_max=doc_max,
        documents=stream_rows // 256,
        aligned=aligned,
    )
    first_row = doc_ids.reshape(1, stream_rows)
    stream = tokens
    saved = []
    full = []
    for layer in range(LAYERS):
        kept = forward_layer(sizes, layer, stream, first_row, weights, 10 + layer)
        if layer == 0:
            first_row = kept["first"]
            weights = weights | {
                "mine_g": kept["mine_g"],
                "q_full": kept["q_full1"],
                "o_full": kept["out_full1"],
            }
            full.append((kept["q_full0"], kept["out_full0"], kept["g_full"], kept["d_full"]))
        else:
            full.append((weights["q_full"], weights["o_full"], kept["g_full"], kept["d_full"]))
        saved.append(kept | {"stream": stream})
        stream = kept["next"]
    output = stream

    grad = cotangent
    fused = planes == 8 and aligned
    backs = [None] * LAYERS
    old = None
    for layer in reversed(range(LAYERS)):
        kept = saved[layer]
        back = backward_layer(
            sizes, layer, fused, grad, first_row, kept, full[layer], old, 12 + layer
        )
        grad = back["next"]
        old = back | {"scaled": kept["scaled"]}
        backs[layer] = back
    if fused:
        rows = backs[0]
        grad_out = jnp.stack([back["raw_o"] for back in backs])
        grad_down = jnp.stack([back["raw_down"] for back in backs])
    else:
        raw, grad_out, grad_down = [], [], []
        for kept, back in zip(saved, backs):
            down_in = back["down_in"]
            proj_in = back["proj_in"]
            scatter = functools.partial(lax.psum_scatter, scatter_dimension=0, tiled=True)
            grad_down.append(
                scatter(contract_rows(kept["hidden"], down_in).astype(BF16), "head").astype(F32)
            )
            padded = lax.dynamic_update_slice(
                jnp.zeros((D, D), BF16),
                contract_rows(kept["mixed"], proj_in).astype(BF16),
                (lax.axis_index("blk") * cols, 0),
            )
            grad_out.append(scatter(padded, ("head", "blk")).astype(F32))
            pieces = [
                scatter(contract_rows(kept[name], right).astype(BF16), "head")
                for name, right in (
                    ("scaled", back["qkv_grad"]),
                    ("scaled_ffn", back["gate_up_grad"]),
                )
            ]
            raw.append(jnp.concatenate(pieces, axis=1))
        raw = jnp.stack(raw).reshape(LAYERS, peers, own_rows, 3 * cols + 2 * hidden_cols)
        raw = plane_swap(raw.transpose(1, 0, 2, 3), 1, "rows_swap")
        rows = {}
        for layer in range(LAYERS):
            flat = raw[:, layer].reshape(peers * own_rows, 3 * cols + 2 * hidden_cols)
            rows[f"rows_q{layer}"] = flat[:, : 3 * cols]
            rows[f"rows_g{layer}"] = flat[:, 3 * cols :]
        grad_out, grad_down = jnp.stack(grad_out), jnp.stack(grad_down)

    def attn_rows_of(which):
        pieces = [
            rows[f"rows_q{layer}"].reshape(peers, own_rows, 3, cols)[:, :, which].transpose(1, 0, 2)
            for layer in range(LAYERS)
        ]
        return jnp.stack([p.reshape(own_rows, D).astype(F32) for p in pieces])

    def ffn_rows_of(which):
        pieces = [
            rows[f"rows_g{layer}"]
            .reshape(peers, own_rows, 2, planes, strip)[:, :, which]
            .transpose(1, 2, 0, 3)
            for layer in range(LAYERS)
        ]
        return jnp.stack([p.reshape(own_rows, peers * hidden_cols).astype(F32) for p in pieces])

    raw_query, raw_key, raw_value = (attn_rows_of(which) for which in range(3))
    raw_gate, raw_up = (ffn_rows_of(which) for which in range(2))

    def gain_grad(*pairs):
        return sum(jnp.sum(weight.astype(F32) * raw_part, axis=2) for weight, raw_part in pairs)

    grad_gain_attn = gain_grad((w_query, raw_query), (w_key, raw_key), (w_value, raw_value))
    grad_gain_ffn = gain_grad((w_gate, raw_gate), (w_up, raw_up))
    return (
        output,
        grad,
        grad_gain_attn,
        raw_query * attn_rows,
        raw_key * attn_rows,
        raw_value * attn_rows,
        grad_out,
        grad_gain_ffn,
        raw_gate * ffn_rows,
        raw_up * ffn_rows,
        grad_down,
    )


def solution(mesh):
    rows = P(("head", "blk"), None)
    vector = P(None, ("head", "blk"))
    matrix = P(None, ("head", "blk"), None)
    return jax.shard_map(
        local,
        mesh=mesh,
        in_specs=(
            rows,
            vector,
            matrix,
            matrix,
            matrix,
            matrix,
            vector,
            matrix,
            matrix,
            matrix,
            P(),
            rows,
        ),
        out_specs=(
            rows,
            rows,
            vector,
            matrix,
            matrix,
            matrix,
            matrix,
            vector,
            matrix,
            matrix,
            matrix,
        ),
        check_vma=False,
    )
```

```python
import functools
import math
import types

import jax
import jax.numpy as jnp
from jax import lax
from jax.experimental import pallas as pl
from jax.experimental.pallas import tpu as pltpu
from jax.sharding import PartitionSpec as P

D = 1024
HD = 64
HEADS = D // HD
LAYERS = 2
EPSILON = 1e-05
MASKED = -1e30
MESH = pl.DeviceIdType.MESH
F32 = jnp.float32
BF16 = jnp.bfloat16
ANY = pl.BlockSpec(memory_space=pl.ANY)


def greet_blk(count):
    me = lax.axis_index("blk")
    barrier = pltpu.get_barrier_semaphore()
    for step in range(1, count):
        pl.semaphore_signal(
            barrier,
            inc=1,
            device_id={"blk": lax.rem(me + step, count)},
            device_id_type=MESH,
        )
    pl.semaphore_wait(barrier, count - 1)
    return me


def plane_gather_kernel(count, x_ref, o_ref, send_sem, recv_sem, local_sem):
    me = greet_blk(count)
    copies = []
    for step in range(1, count):
        copy = pltpu.make_async_remote_copy(
            src_ref=x_ref,
            dst_ref=o_ref.at[me],
            send_sem=send_sem.at[step - 1],
            recv_sem=recv_sem.at[step - 1],
            device_id={"blk": lax.rem(me + step, count)},
            device_id_type=MESH,
        )
        copy.start()
        copies.append(copy)
    own = pltpu.make_async_copy(x_ref, o_ref.at[me], local_sem)
    own.start()
    own.wait()
    for copy in copies:
        copy.wait()


def plane_swap_kernel(count, x_ref, o_ref, send_sem, recv_sem, local_sem):
    me = greet_blk(count)
    copies = []
    for step in range(1, count):
        peer = lax.rem(me + step, count)
        copy = pltpu.make_async_remote_copy(
            src_ref=x_ref.at[peer],
            dst_ref=o_ref.at[me],
            send_sem=send_sem.at[step - 1],
            recv_sem=recv_sem.at[step - 1],
            device_id={"blk": peer},
            device_id_type=MESH,
        )
        copy.start()
        copies.append(copy)
    own = pltpu.make_async_copy(x_ref.at[me], o_ref.at[me], local_sem)
    own.start()
    own.wait()
    for copy in copies:
        copy.wait()


def plane_call(kernel, x, out_shape, collective_id, name):
    count = lax.axis_size("blk")
    return pl.pallas_call(
        functools.partial(kernel, count),
        out_shape=jax.ShapeDtypeStruct(out_shape, x.dtype),
        in_specs=[ANY],
        out_specs=ANY,
        scratch_shapes=[
            pltpu.SemaphoreType.DMA((count - 1,)),
            pltpu.SemaphoreType.DMA((count - 1,)),
            pltpu.SemaphoreType.DMA,
        ],
        compiler_params=pltpu.CompilerParams(collective_id=collective_id, has_side_effects=True),
        cost_estimate=pl.CostEstimate(flops=0, bytes_accessed=20_000_000, transcendentals=0),
        name=name,
    )(x)


def plane_gather(x, collective_id, name):
    return plane_call(
        plane_gather_kernel, x, (lax.axis_size("blk"),) + x.shape, collective_id, name
    )


def plane_swap(x, collective_id, name):
    return plane_call(plane_swap_kernel, x, x.shape, collective_id, name)


def launch(body, name, inputs, outputs, scratch, collective_id, flops=0):
    names = list(inputs) + list(outputs)
    flat = []
    for value in scratch.values():
        flat.extend(value if isinstance(value, list) else [value])

    def kernel(*refs):
        named = dict(zip(names, refs))
        rest = list(refs[len(names) :])
        for name, value in scratch.items():
            if isinstance(value, list):
                named[name], rest = rest[: len(value)], rest[len(value) :]
            else:
                named[name], rest = rest[0], rest[1:]
        body(types.SimpleNamespace(**named))

    results = pl.pallas_call(
        kernel,
        out_shape=[jax.ShapeDtypeStruct(shape, dtype) for shape, dtype, _ in outputs.values()],
        in_specs=[spec for _, spec in inputs.values()],
        out_specs=[spec for _, _, spec in outputs.values()],
        scratch_shapes=flat,
        compiler_params=pltpu.CompilerParams(
            collective_id=collective_id, has_side_effects=True, vmem_limit_bytes=60 << 20
        ),
        cost_estimate=pl.CostEstimate(
            flops=flops, bytes_accessed=200_000_000, transcendentals=0
        ),
        name=name,
    )(*[array for array, _ in inputs.values()])
    return dict(zip(outputs, results))


VMEM = pl.BlockSpec(memory_space=pltpu.VMEM)


def dma(*shape):
    return pltpu.SemaphoreType.DMA(shape)


def remote(src, dst, send_sem, recv_sem, **place):
    return pltpu.make_async_remote_copy(
        src_ref=src,
        dst_ref=dst,
        send_sem=send_sem,
        recv_sem=recv_sem,
        device_id=place,
        device_id_type=MESH,
    )


class Place:
    def __init__(self):
        self.peers = lax.axis_size("blk")
        self.planes = lax.axis_size("head")
        self.depth = self.planes // 2
        self.peer = lax.axis_index("blk")
        self.plane = lax.axis_index("head")
        self.z = lax.div(self.plane, 2)
        self.core = lax.rem(self.plane, 2)
        self.sibling = self.plane + 1 - 2 * self.core


    def moved(self, step, sign):
        half = self.peers // 2
        low, high = (step % 2, step // 2) if isinstance(step, int) else (lax.rem(step, 2), lax.div(step, 2))
        bit = lax.rem(lax.rem(self.peer, 2) + low, 2)
        return bit + 2 * lax.rem(lax.div(self.peer, 2) + sign * high + half, half)

    def peer_after(self, step):
        return self.moved(step, 1)

    def peer_before(self, step):
        return self.moved(step, -1)

    def steps_between(self, early, late):
        half = self.peers // 2
        bit = lax.rem(lax.rem(early, 2) + lax.rem(late, 2), 2)
        return bit + 2 * lax.rem(lax.div(late, 2) - lax.div(early, 2) + half, half)

    def z_after(self, step):
        return lax.rem(self.z + step, self.depth)

    def z_before(self, step):
        return lax.rem(self.z + self.depth - step, self.depth)

    def greet(self):
        barrier = pltpu.get_barrier_semaphore()
        for step in range(1, self.peers):
            pl.semaphore_signal(
                barrier, inc=1, device_id={"blk": self.peer_after(step)}, device_id_type=MESH
            )
        for step in range(1, self.depth):
            pl.semaphore_signal(
                barrier,
                inc=1,
                device_id={"head": 2 * self.z_after(step) + self.core},
                device_id_type=MESH,
            )
        pl.semaphore_signal(barrier, inc=1, device_id={"head": self.sibling}, device_id_type=MESH)
        pl.semaphore_wait(barrier, self.peers - 1 + self.depth - 1 + 1)


class PlaneGather:
    def __init__(self, place, flat, send, recv):
        self.place, self.flat, self.send, self.recv = place, flat, send, recv
        self.rows = flat.shape[0] // place.peers
        self.square = place.peers == 4
        self.direct = range(1, 3) if self.square else range(1, place.peers)

    @staticmethod
    def sems(peers):
        return dma(peers)

    def slot(self, peer, half=None):
        start = pl.multiple_of(peer * self.rows, self.rows)
        if half is None:
            return self.flat.at[pl.ds(start, self.rows)]
        middle = self.rows // 2
        return self.flat.at[pl.ds(pl.multiple_of(start + half * middle, middle), middle)]

    def copy(self, step):
        own = self.slot(self.place.peer)
        return remote(
            own,
            own,
            self.send.at[step - 1],
            self.recv.at[step - 1],
            blk=self.place.peer_after(step),
        )

    def relay(self, step):
        where = self.slot(self.place.peer_before(step), step - 1)
        return remote(
            where,
            where,
            self.send.at[step + 1],
            self.recv.at[step + 1],
            blk=self.place.peer_after(3 - step),
        )

    def start(self):
        for step in self.direct:
            self.copy(step).start()

    def await_step(self, step):
        if not step:
            return
        source = self.place.peer_before(step)
        if step in self.direct:
            where = self.slot(source)
            remote(
                where, where, self.send.at[step - 1], self.recv.at[step - 1], blk=source
            ).wait_recv()
            if self.square:
                self.relay(step).start()
        else:
            for half in range(2):
                where = self.slot(source, half)
                remote(
                    where, where, self.send.at[half + 2], self.recv.at[half + 2], blk=source
                ).wait_recv()

    def finish(self):
        for step in self.direct:
            self.copy(step).wait_send()
            if self.square:
                self.relay(step).wait_send()


def peer_groups(peers):
    return [(0,), (1, 2)] + [(step,) for step in range(3, peers)] if peers > 2 else [(0,), (1,)]


class PlaneSum:
    def __init__(self, place, src, dst, send, recv):
        self.place, self.src, self.dst, self.send, self.recv = place, src, dst, send, recv

    def copy_to(self, peer):
        index = jnp.maximum(self.place.steps_between(peer, self.place.peer) - 1, 0)
        return remote(
            self.src.at[peer],
            self.dst.at[self.place.peer],
            self.send.at[index],
            self.recv.at[index],
            blk=peer,
        )

    def send_to(self, peer):
        @pl.when(peer != self.place.peer)
        def _():
            self.copy_to(peer).start()

    def total(self):
        total = self.src[self.place.peer].astype(F32)
        for step in range(1, self.place.peers):
            source = self.place.peer_after(step)
            remote(
                self.src.at[source],
                self.dst.at[source],
                self.send.at[step - 1],
                self.recv.at[step - 1],
                blk=source,
            ).wait_recv()
            total = total + self.dst[source].astype(F32)
        return total

    def finish(self):
        for step in range(1, self.place.peers):
            self.copy_to(self.place.peer_before(step)).wait_send()


class HeadGather:
    def __init__(self, place, src, full, sems):
        self.place, self.src, self.full = place, src, full
        self.z_send, self.z_recv, self.s_send, self.s_recv, self.local, self.r_send = sems
        self.line = place.depth == 4

    @staticmethod
    def sems(depth):
        return [dma(depth - 1), dma(depth - 1), dma(depth), dma(depth), dma(), dma()]

    def slot(self, z, core):
        rows = self.src.shape[0]
        return self.full.at[pl.ds(pl.multiple_of((2 * z + core) * rows, rows), rows)]

    def z_copy(self, step):
        return remote(
            self.src,
            self.slot(self.place.z, self.place.core),
            self.z_send.at[step - 1],
            self.z_recv.at[step - 1],
            head=2 * self.place.z_after(step) + self.place.core,
        )

    def near(self, step):
        z = self.place.z
        if not self.line or step == 2:
            return z >= 0
        return z < 3 if step == 1 else z > 0

    def relays(self, which):
        return self.place.z == (2 if which == 3 else 1)

    def relay_copy(self, which):
        where = self.slot(self.place.z_before(2), self.place.core)
        return remote(
            where,
            where,
            self.r_send,
            self.z_recv.at[which - 1],
            head=2 * (3 if which == 3 else 0) + self.place.core,
        )

    def s_copy(self, step, core):
        z = self.place.z_before(step)
        where = self.slot(z, core)
        return remote(
            self.src if step == 0 else where,
            where,
            self.s_send.at[step],
            self.s_recv.at[step],
            head=self.place.sibling,
        )

    def own_copy(self):
        return pltpu.make_async_copy(
            self.src, self.slot(self.place.z, self.place.core), self.local
        )

    def start(self):
        for step in sorted(range(1, self.place.depth), key=lambda k: k != 2):

            @pl.when(self.near(step))
            def _(step=step):
                self.z_copy(step).start()

        self.s_copy(0, self.place.core).start()
        self.own_copy().start()

    def await_z(self, step):
        where = self.slot(self.place.z_before(step), self.place.core)
        remote(
            self.src,
            where,
            self.z_send.at[step - 1],
            self.z_recv.at[step - 1],
            head=self.place.sibling,
        ).wait_recv()

    def relay(self):
        if self.line:
            self.await_z(2)
            for which in (1, 3):

                @pl.when(self.relays(which))
                def _(which=which):
                    self.relay_copy(which).start()

            self.s_copy(2, self.place.core).start()

    def forward(self):
        for step in range(1, self.place.depth):
            if not (self.line and step == 2):
                self.await_z(step)
                self.s_copy(step, self.place.core).start()

    def arrive(self):
        self.own_copy().wait()
        for step in range(self.place.depth):
            self.s_copy(step, 1 - self.place.core).wait_recv()

    def finish(self):
        for step in range(1, self.place.depth):

            @pl.when(self.near(step))
            def _(step=step):
                self.z_copy(step).wait_send()

        if self.line:
            for which in (1, 3):

                @pl.when(self.relays(which))
                def _(which=which):
                    self.relay_copy(which).wait_send()

        for step in range(self.place.depth):
            self.s_copy(step, self.place.core).wait_send()


class OutGather:
    def __init__(self, place, src, mid, full, sems):
        self.place, self.mid, self.full = place, mid, full
        self.rows = src.shape[0]
        self.over_head = HeadGather(place, src, mid, sems[:6])
        self.send, self.recv, self.local = sems[6:]

    @staticmethod
    def sems(peers, depth):
        return HeadGather.sems(depth) + [dma(2, peers - 1), dma(2, peers - 1), dma(2)]

    def piece(self, peer, core):
        return self.mid.at[pl.ds(pl.multiple_of((2 * peer + core) * self.rows, self.rows), self.rows)]

    def slot(self, peer, core):
        where = (core * self.place.peers + peer) * self.rows
        return self.full.at[pl.ds(pl.multiple_of(where, self.rows), self.rows)]

    def copy(self, step, core):
        target = self.place.peer_after(step)
        return remote(
            self.piece(target, core),
            self.slot(self.place.peer, core),
            self.send.at[core, step - 1],
            self.recv.at[core, step - 1],
            blk=target,
        )

    def own_copy(self, core):
        return pltpu.make_async_copy(
            self.piece(self.place.peer, core),
            self.slot(self.place.peer, core),
            self.local.at[core],
        )

    def start(self):
        self.over_head.start()

    def spread(self):
        self.over_head.relay()
        self.over_head.forward()
        self.over_head.arrive()
        for core in range(2):
            for step in range(1, self.place.peers):
                self.copy(step, core).start()
            self.own_copy(core).start()

    def arrive(self):
        for core in range(2):
            self.own_copy(core).wait()
            for step in range(1, self.place.peers):
                source = self.place.peer_before(step)
                remote(
                    self.piece(source, core),
                    self.slot(source, core),
                    self.send.at[core, step - 1],
                    self.recv.at[core, step - 1],
                    blk=source,
                ).wait_recv()

    def finish(self):
        self.over_head.finish()
        for core in range(2):
            for step in range(1, self.place.peers):
                self.copy(step, core).wait_send()


class WeightSwap:
    def __init__(self, place, src, layer, mine, sems):
        self.place, self.src, self.layer, self.mine = place, src, layer, mine
        self.send, self.recv, self.local = sems

    @staticmethod
    def sems(peers):
        return [dma(peers - 1), dma(peers - 1), dma()]

    def piece(self, peer):
        rows = self.src.shape[2]
        return self.mine.at[pl.ds(pl.multiple_of(peer * rows, rows), rows)]

    def copy(self, step):
        target = self.place.peer_after(step)
        return remote(
            self.src.at[target, self.layer],
            self.piece(self.place.peer),
            self.send.at[step - 1],
            self.recv.at[step - 1],
            blk=target,
        )

    def own_copy(self):
        return pltpu.make_async_copy(
            self.src.at[self.place.peer, self.layer], self.piece(self.place.peer), self.local
        )

    def start(self):
        for step in range(1, self.place.peers):
            self.copy(step).start()
        self.own_copy().start()

    def arrive(self):
        self.own_copy().wait()
        for step in range(1, self.place.peers):
            source = self.place.peer_before(step)
            remote(
                self.src.at[source, self.layer],
                self.piece(source),
                self.send.at[step - 1],
                self.recv.at[step - 1],
                blk=source,
            ).wait_recv()

    def finish(self):
        for step in range(1, self.place.peers):
            self.copy(step).wait_send()


class Halo:
    def __init__(self, place, keys, reach, sems):
        self.place, self.keys, self.reach = place, keys, reach
        self.rows = keys.shape[0] // (reach + 1)
        self.z_send, self.z_recv, self.s_send, self.s_recv = sems

    def block(self, offset):
        return self.keys.at[pl.ds((self.reach - offset) * self.rows, self.rows)]

    @staticmethod
    def sems(reach):
        return [dma(reach // 2), dma(reach // 2), dma(reach // 2), dma(reach // 2)]

    def z_copy(self, hop):
        return remote(
            self.block(0),
            self.block(2 * hop),
            self.z_send.at[hop - 1],
            self.z_recv.at[hop - 1],
            head=self.place.plane + 2 * hop,
        )

    def sends(self, hop):
        return self.place.z + hop < self.place.depth

    def receives(self, hop):
        return self.place.z - hop >= 0

    def start(self):
        for hop in range(1, self.reach // 2 + 1):

            @pl.when(self.sends(hop))
            def _(hop=hop):
                self.z_copy(hop).start()


    def hand(self, i):
        def copy(offset):
            return remote(
                self.block(offset),
                self.block(2 * i - 1),
                self.s_send.at[i - 1],
                self.s_recv.at[i - 1],
                head=self.place.sibling,
            )

        return copy

    def hand_ready(self, i):
        return (
            (self.place.core == 1) & self.receives(i),
            (self.place.core == 0) & self.receives(i - 1),
        )

    def relay(self):
        for i in range(1, self.reach // 2 + 1):
            from_one, from_zero = self.hand_ready(i)
            if i == 1:

                @pl.when(from_zero)
                def _(i=i):
                    self.hand(i)(2 * i - 2).start()

            @pl.when(self.receives(i))
            def _(i=i):
                remote(
                    self.block(0),
                    self.block(2 * i),
                    self.z_send.at[i - 1],
                    self.z_recv.at[i - 1],
                    head=self.place.sibling,
                ).wait_recv()

            @pl.when(from_one)
            def _(i=i):
                self.hand(i)(2 * i).start()

            if i < self.reach // 2:

                @pl.when(self.hand_ready(i + 1)[1])
                def _(i=i):
                    self.hand(i + 1)(2 * i).start()

    def arrive(self):
        for i in range(1, self.reach // 2 + 1):

            @pl.when(self.place.z - i + self.place.core >= 0)
            def _(i=i):
                self.hand(i)(0).wait_recv()

    def finish(self):
        for hop in range(1, self.reach // 2 + 1):

            @pl.when(self.sends(hop))
            def _(hop=hop):
                self.z_copy(hop).wait_send()

            from_one, from_zero = self.hand_ready(hop)

            @pl.when(from_one)
            def _(hop=hop):
                self.hand(hop)(2 * hop).wait_send()

            @pl.when(from_zero)
            def _(hop=hop):
                self.hand(hop)(2 * hop - 2).wait_send()


def columns(total, most=256):
    width = math.gcd(total, most)
    return total // width, width


def by_columns(total, step, most=256):
    count, width = columns(total, most)

    def body(index, carry):
        step(pl.ds(pl.multiple_of(index * width, width), width))
        return carry

    lax.fori_loop(0, count, body, 0)


def attend_tile(sizes, place, tile_index, q_ref, keys_ref, first_ref, mixed_ref, attended_ref, log_ref):
    tile, chunk, cols, group, lead = sizes.tile, sizes.chunk, sizes.cols, sizes.group, sizes.lead
    row = pl.multiple_of(tile_index * tile, tile)
    rows = pl.ds(row, tile)
    first = first_ref[:, rows]
    last = lead + row + lax.broadcasted_iota(jnp.int32, (1, tile), 1)
    lane = lax.broadcasted_iota(jnp.int32, (tile, 2 * HD), 1)
    lowest = jnp.maximum(lead + row - (sizes.doc_max - 1), lead - place.plane * group)
    begin = lax.div(jnp.maximum(lowest, 0), chunk)
    end = lax.div(lead + row + tile + chunk - 1, chunk)
    pairs = range(cols // (2 * HD))
    halves = []
    for pair in pairs:
        queries = q_ref[rows, pair * 2 * HD : (pair + 1) * 2 * HD] * jnp.asarray(HD ** (-0.5), BF16)
        zero = jnp.zeros_like(queries)
        halves.append(jnp.where(lane < HD, queries, zero))
        halves.append(jnp.where(lane >= HD, queries, zero))

    def step(block, state):
        offset = pl.multiple_of(block * chunk, chunk)
        there = pl.ds(offset, chunk)
        spot = offset + lax.broadcasted_iota(jnp.int32, (chunk, tile), 0)
        allowed = (spot >= first) & (spot <= last)
        scores = []
        for index, half in enumerate(halves):
            lanes = slice(index // 2 * 2 * HD, (index // 2 + 1) * 2 * HD)
            scores.append(dot_nt(keys_ref[there, lanes], half))
        out = []
        for index, (top, total, accum) in enumerate(state):
            lanes = slice(cols + index // 2 * 2 * HD, cols + (index // 2 + 1) * 2 * HD)
            score = jnp.where(allowed, scores[index], MASKED)
            new_top = jnp.maximum(top, jnp.max(score, axis=0, keepdims=True))
            factor = jnp.exp(top - new_top)
            weights = jnp.exp(score - new_top)
            total = total * factor + jnp.sum(weights, axis=0, keepdims=True)
            accum = accum * factor + dot_tn(keys_ref[there, lanes], weights.astype(BF16))
            out.append((new_top, total, accum))
        return tuple(out)

    start = (
        jnp.full((1, tile), MASKED, F32),
        jnp.zeros((1, tile), F32),
        jnp.zeros((2 * HD, tile), F32),
    )
    state = lax.fori_loop(begin, end, step, tuple(start for _ in halves))
    for pair in pairs:
        lanes = slice(pair * 2 * HD, (pair + 1) * 2 * HD)
        parts = []
        for which in range(2):
            head = 2 * pair + which
            top, total, accum = state[head]
            log_ref[head : head + 1, rows] = top + jnp.log(total)
            parts.append(accum[which * HD : (which + 1) * HD] / total)
        attended = jnp.transpose(jnp.concatenate(parts, axis=0))
        attended_ref[rows, lanes] = attended
        mixed_ref[rows, lanes] = attended.astype(BF16)


def pack_query(sizes, l, refs):
    cols = sizes.cols
    gain = refs.attn_gain[l]
    for part, weight in enumerate((refs.w_query, refs.w_key, refs.w_value)):
        for peer in range(sizes.peers):
            piece = weight[l, :, peer * cols : (peer + 1) * cols].astype(F32) * gain
            refs.pack_q[peer, l, :, part * cols : (part + 1) * cols] = piece.astype(BF16)


def pack_ffn(sizes, l, refs):
    strip, hidden = sizes.hidden // sizes.planes, sizes.hidden
    gain = refs.ffn_gain[l]
    for part, weight in enumerate((refs.w_gate, refs.w_up)):
        for peer in range(sizes.peers):
            for plane in range(sizes.planes):
                source = (plane * sizes.peers + peer) * strip
                piece = weight[l, :, source : source + strip].astype(F32) * gain
                target = part * hidden + plane * strip
                refs.pack_g[peer, l, :, target : target + strip] = piece.astype(BF16)


def document_starts(sizes, place, documents):
    group = sizes.group
    here = pl.ds(pl.multiple_of(place.plane * group, group), group)
    own = documents[:, here]
    every = documents[...]
    starts = jnp.zeros_like(own)
    for document in range(sizes.documents - 1):
        count = jnp.sum((every == document).astype(jnp.int32), axis=1, keepdims=True)
        starts = starts + jnp.where(own > document, count, 0)
    return starts - (place.plane * group - sizes.lead)


def forward_body(sizes, layer, refs):
    place = Place()
    tok, cols, group, hidden = sizes.tok, sizes.cols, sizes.group, sizes.hidden
    tile = sizes.tile
    loads = refs.load_sem
    if layer == 0:
        if sizes.aligned:
            pack_query(sizes, 0, refs)
        place.greet()
        swap_q = [
            WeightSwap(place, refs.pack_q, l, refs.mine_q.at[l], getattr(refs, f"swap_q{l}"))
            for l in range(LAYERS)
        ]
        swap_g = [
            WeightSwap(place, refs.pack_g, l, refs.mine_g.at[l], getattr(refs, f"swap_g{l}"))
            for l in range(LAYERS)
        ]
        out_w = [
            OutGather(
                place,
                refs.w_out.at[l],
                refs.mid_o.at[l],
                getattr(refs, f"out_full{l}"),
                getattr(refs, f"out_sem{l}"),
            )
            for l in range(LAYERS)
        ]
        gather_q = [
            HeadGather(
                place,
                refs.mine_q.at[l],
                refs.q_full1 if l else refs.wq,
                getattr(refs, f"gq_sem{l}"),
            )
            for l in range(LAYERS)
        ]
        gather_g = HeadGather(place, refs.mine_g.at[0], refs.wg, refs.gg_sem)
        swap_q[0].start()
    else:
        place.greet()
        gather_g = HeadGather(place, refs.mine_g.at[layer], refs.wg, refs.gg_sem)
    gather_d = HeadGather(place, refs.w_down.at[layer], refs.wd, refs.gd_sem)

    stream = refs.stream[...].astype(F32)
    scaled = (stream * inverse_rms(stream)).astype(BF16)
    own_rows = pl.ds(pl.multiple_of(place.peer * tok, tok), tok)
    refs.scaled[own_rows, :] = scaled
    ag1 = PlaneGather(place, refs.scaled, refs.ag1_s, refs.ag1_r)
    ag1.start()
    if layer == 0:
        if sizes.aligned:
            pack_ffn(sizes, 0, refs)
        swap_g[0].start()
        swap_q[0].arrive()
        gather_q[0].start()
        out_w[0].start()
        gather_d.start()
        gather_q[0].relay()
        gather_q[0].forward()
        gather_q[0].arrive()
        q_copy = pltpu.make_async_copy(refs.wq, refs.q_full0, loads.at[0])
        q_copy.start()
        refs.first[...] = document_starts(sizes, place, refs.documents)
        if sizes.aligned:
            pack_query(sizes, 1, refs)
            pack_ffn(sizes, 1, refs)
    else:
        q_copy = pltpu.make_async_copy(refs.q_full, refs.wq, loads.at[0])
        q_copy.start()
        gather_d.start()
        q_copy.wait()

    for steps in peer_groups(place.peers):
        peers = [place.peer_before(step) for step in steps]
        rows = [pl.ds(pl.multiple_of(peer * tok, tok), tok) for peer in peers]
        for step in steps:
            ag1.await_step(step)
        x = jnp.concatenate([refs.scaled[where, :] for where in rows], axis=0)
        for part in range(3):

            def block(where, part=part, x=x, peers=peers, rows=rows):
                weight = refs.wq[
                    :, pl.ds(pl.multiple_of(part * cols + where.start, where.size), where.size)
                ]
                value = dot_nn(x, weight).astype(BF16)
                there = pl.ds(
                    pl.multiple_of(max(part - 1, 0) * cols + where.start, where.size), where.size
                )
                for index, peer in enumerate(peers):
                    piece = value[index * tok : (index + 1) * tok]
                    if part == 0:
                        refs.queries[rows[index], there] = piece
                    else:
                        spot = pl.multiple_of(sizes.lead + peer * tok, tok)
                        refs.keys[pl.ds(spot, tok), there] = piece

            by_columns(cols, block)
    halo = Halo(place, refs.keys, sizes.reach, refs.halo_sem)
    halo.start()
    if layer == 0:
        swap_g[0].arrive()
        gather_g.start()
        out_w[0].spread()
        swap_q[1].start()
        swap_g[1].start()
    else:
        gather_g.start()
    gather_d.relay()
    halo.relay()
    halo.arrive()
    if layer == 0:
        out_w[0].arrive()
    wo = refs.out_full0 if layer == 0 else refs.o_full

    sum1 = PlaneSum(place, refs.part1, refs.sum1, refs.rs1_s, refs.rs1_r)

    def attend_step(index, carry):
        attend_tile(
            sizes,
            place,
            index,
            refs.queries,
            refs.keys,
            refs.first,
            refs.mixed,
            refs.attended,
            refs.logs,
        )
        for k in range(tile // tok):
            peer = index * (tile // tok) + k
            x = refs.mixed[pl.ds(pl.multiple_of(peer * tok, tok), tok), :]

            def block(where, x=x, peer=peer):
                refs.part1[peer, :, where] = dot_nn(x, wo[:, where]).astype(BF16)

            by_columns(D, block)
            sum1.send_to(peer)
        return carry

    lax.fori_loop(0, group // tile, attend_step, 0)

    gather_g.relay()
    gather_d.forward()
    gather_g.forward()
    if layer == 0:
        swap_q[1].arrive()
        gather_q[1].start()
        out_w[1].start()
        swap_g[1].arrive()

    middle = stream + sum1.total()
    refs.middle[...] = middle
    refs.scaled_ffn[own_rows, :] = (middle * inverse_rms(middle)).astype(BF16)
    ag2 = PlaneGather(place, refs.scaled_ffn, refs.ag2_s, refs.ag2_r)
    ag2.start()
    gather_g.arrive()
    gather_d.arrive()
    d_copy = pltpu.make_async_copy(refs.wd, refs.d_full, loads.at[3])
    d_copy.start()
    g_copy = pltpu.make_async_copy(refs.wg, refs.g_full, loads.at[2])
    g_copy.start()
    sum2 = PlaneSum(place, refs.part2, refs.sum2, refs.rs2_s, refs.rs2_r)

    stores = []
    for steps in peer_groups(place.peers):
        peers = [place.peer_before(step) for step in steps]
        rows = [pl.ds(pl.multiple_of(peer * tok, tok), tok) for peer in peers]
        for step in steps:
            ag2.await_step(step)
        x = jnp.concatenate([refs.scaled_ffn[where, :] for where in rows], axis=0)

        def block(where, x=x, rows=rows):
            there = pl.ds(pl.multiple_of(hidden + where.start, where.size), where.size)
            gate = dot_nn(x, refs.wg[:, where])
            up = dot_nn(x, refs.wg[:, there])
            low = (gate / (1.0 + jnp.exp(-gate)) * up).astype(BF16)
            for index, row in enumerate(rows):
                piece = slice(index * tok, (index + 1) * tok)
                refs.gate_up[row, where] = gate[piece]
                refs.gate_up[row, there] = up[piece]
                refs.hidden[row, where] = low[piece]

        by_columns(hidden, block)
        low = jnp.concatenate([refs.hidden[where, :] for where in rows], axis=0)

        def down(where, low=low, peers=peers):
            value = dot_nn(low, refs.wd[:, where]).astype(BF16)
            for index, peer in enumerate(peers):
                refs.part2[peer, :, where] = value[index * tok : (index + 1) * tok]

        by_columns(D, down)
        for step, peer, row in zip(steps, peers, rows):
            sum2.send_to(peer)
            store = pltpu.make_async_copy(
                refs.gate_up.at[row], refs.gate_up_out.at[row], refs.store_sem.at[step]
            )
            store.start()
            stores.append(store)
    if layer == 0:
        gather_q[1].relay()
        gather_q[1].forward()
        out_w[1].spread()
    after = middle + sum2.total()
    refs.next[...] = after if layer < LAYERS - 1 else after.astype(BF16)
    if layer == 0:
        gather_q[1].arrive()
        out_w[1].arrive()
        q_copy.wait()
        for item in swap_q + swap_g + gather_q + out_w:
            item.finish()
    g_copy.wait()
    d_copy.wait()
    for store in stores:
        store.wait()
    for item in (ag1, ag2, sum1, sum2, gather_g, gather_d, halo):
        item.finish()


def forward_layer(sizes, layer, stream, first_row, weights, collective_id):
    peers, planes, depth = sizes.peers, sizes.planes, sizes.planes // 2
    tok, cols, group, hidden, reach = sizes.tok, sizes.cols, sizes.group, sizes.hidden, sizes.reach
    inputs = {"stream": (stream, VMEM), "w_down": (weights["w_down"], VMEM)}
    outputs = {
        "d_full": ((hidden, D), BF16, ANY),
        "next": ((tok, D), F32 if layer < LAYERS - 1 else BF16, VMEM),
        "middle": ((tok, D), F32, VMEM),
        "scaled": ((group, D), BF16, VMEM),
        "scaled_ffn": ((group, D), BF16, VMEM),
        "queries": ((group, cols), BF16, VMEM),
        "keys": (((reach + 1) * group, 2 * cols), BF16, VMEM),
        "mixed": ((group, cols), BF16, VMEM),
        "attended": ((group, cols), F32, VMEM),
        "logs": ((cols // HD, group), F32, VMEM),
        "gate_up_out": ((group, 2 * hidden), F32, ANY),
        "hidden": ((group, hidden), BF16, VMEM),
        "g_full": ((D, 2 * hidden), BF16, ANY),
    }
    scratch = {
        "wq": pltpu.VMEM((D, 3 * cols), BF16),
        "wg": pltpu.VMEM((D, 2 * hidden), BF16),
        "wd": pltpu.VMEM((hidden, D), BF16),
        "gate_up": pltpu.VMEM((group, 2 * hidden), F32),
        "store_sem": dma(peers),
        "part1": pltpu.VMEM((peers, tok, D), BF16),
        "sum1": pltpu.VMEM((peers, tok, D), BF16),
        "part2": pltpu.VMEM((peers, tok, D), BF16),
        "sum2": pltpu.VMEM((peers, tok, D), BF16),
        "load_sem": dma(4),
        "halo_sem": Halo.sems(reach),
        "gg_sem": HeadGather.sems(depth),
        "gd_sem": HeadGather.sems(depth),
    }
    for name in ("rs1_s", "rs1_r", "rs2_s", "rs2_r"):
        scratch[name] = dma(peers - 1)
    for name in ("ag1_s", "ag1_r", "ag2_s", "ag2_r"):
        scratch[name] = PlaneGather.sems(peers)
    if layer == 0:
        rows = peers * sizes.own_rows
        inputs["documents"] = (first_row, VMEM)
        outputs["first"] = ((1, group), jnp.int32, VMEM)
        if sizes.aligned:
            for name in ("w_query", "w_key", "w_value", "w_gate", "w_up", "attn_gain", "ffn_gain"):
                inputs[name] = (weights[name], VMEM)
            scratch["pack_q"] = pltpu.VMEM((peers, LAYERS, sizes.own_rows, 3 * cols), BF16)
            scratch["pack_g"] = pltpu.VMEM((peers, LAYERS, sizes.own_rows, 2 * hidden), BF16)
        else:
            inputs["pack_q"] = (weights["pack_q"], ANY)
            inputs["pack_g"] = (weights["pack_g"], ANY)
        inputs["w_out"] = (weights["w_out"], VMEM)
        outputs["mine_q"] = ((LAYERS, rows, 3 * cols), BF16, VMEM)
        outputs["mine_g"] = ((LAYERS, rows, 2 * hidden), BF16, VMEM)
        scratch["mid_o"] = pltpu.VMEM((LAYERS, planes * sizes.own_rows, D), BF16)
        for l in range(LAYERS):
            outputs[f"q_full{l}"] = ((D, 3 * cols), BF16, ANY)
            outputs[f"out_full{l}"] = ((cols, D), BF16, VMEM)
            scratch[f"swap_q{l}"] = WeightSwap.sems(peers)
            scratch[f"swap_g{l}"] = WeightSwap.sems(peers)
            scratch[f"out_sem{l}"] = OutGather.sems(peers, depth)
            scratch[f"gq_sem{l}"] = HeadGather.sems(depth)
    else:
        inputs["mine_g"] = (weights["mine_g"], VMEM)
        inputs["q_full"] = (weights["q_full"], ANY)
        inputs["o_full"] = (weights["o_full"], VMEM)
        inputs["first"] = (first_row, VMEM)
    return launch(
        functools.partial(forward_body, sizes, layer),
        f"forward{layer}",
        inputs,
        outputs,
        scratch,
        collective_id,
        flops=group * D * (4 * cols + 3 * hidden) * 2,
    )


def dot_nt(left, right):
    return lax.dot_general(left, right, (((1,), (1,)), ((), ())), preferred_element_type=F32)


def dot_nn(left, right):
    return lax.dot_general(left, right, (((1,), (0,)), ((), ())), preferred_element_type=F32)


def dot_tn(left, right):
    return lax.dot_general(left, right, (((0,), (0,)), ((), ())), preferred_element_type=F32)


class HaloBack:
    def __init__(self, place, total, give, land, s_land, reach, sems):
        self.place, self.total, self.give, self.land, self.s_land = place, total, give, land, s_land
        self.reach = reach
        self.rows, self.width = land.shape[1:]
        self.z_send, self.z_recv, self.s_send, self.s_recv = sems

    def block(self, ref, offset):
        return ref.at[self.reach - offset]

    def lanes(self, offset):
        return slice((self.reach - offset) * self.width, (self.reach - offset + 1) * self.width)

    def hand_copy(self, i):
        return remote(
            self.block(self.give, 2 * i - 1),
            self.s_land.at[i - 1],
            self.s_send.at[i - 1],
            self.s_recv.at[i - 1],
            head=self.place.sibling,
        )

    def hands(self, i):
        return self.place.z - i + self.place.core >= 0

    def handed(self, i):
        return self.place.z - i + 1 - self.place.core >= 0

    def low(self, offset):
        self.give[self.reach - offset] = self.total[:, self.lanes(offset)].astype(BF16)

    def hand(self):
        for i in range(1, self.reach // 2 + 1):

            @pl.when(self.hands(i))
            def _(i=i):
                self.low(2 * i - 1)
                self.hand_copy(i).start()

    def add(self, i, offset):
        where = self.lanes(offset)
        self.total[:, where] = self.total[:, where] + self.s_land[i - 1].astype(F32)

    def z_copy(self, i):
        return remote(
            self.block(self.give, 2 * i),
            self.land.at[i - 1],
            self.z_send.at[i - 1],
            self.z_recv.at[i - 1],
            head=self.place.plane - 2 * i,
        )

    def sends(self, i):
        return self.place.z - i >= 0

    def receives(self, i):
        return self.place.z + i < self.place.depth

    def send(self):
        for i in range(1, self.reach // 2 + 1):

            @pl.when((self.place.core == 1) & self.handed(i))
            def _(i=i):
                self.hand_copy(i).wait_recv()
                self.add(i, 2 * i)

            if i > 1:

                @pl.when((self.place.core == 0) & self.handed(i))
                def _(i=i):
                    self.hand_copy(i).wait_recv()
                    self.add(i, 2 * i - 2)

        for i in range(1, self.reach // 2 + 1):

            @pl.when(self.sends(i))
            def _(i=i):
                self.low(2 * i)
                self.z_copy(i).start()

    def collect(self):
        @pl.when((self.place.core == 0) & self.handed(1))
        def _():
            self.hand_copy(1).wait_recv()
            self.add(1, 0)

        where = self.lanes(0)
        for i in range(1, self.reach // 2 + 1):

            @pl.when(self.receives(i))
            def _(i=i):
                self.z_copy(i).wait_recv()
                self.total[:, where] = self.total[:, where] + self.land[i - 1].astype(F32)

    def finish(self):
        for i in range(1, self.reach // 2 + 1):

            @pl.when(self.hands(i))
            def _(i=i):
                self.hand_copy(i).wait_send()

            @pl.when(self.sends(i))
            def _(i=i):
                self.z_copy(i).wait_send()


class GradJob:
    def __init__(self, place, left, right, bufs, flips, sems):
        self.place, self.left, self.right = place, left, right
        self.left_sib, self.right_sib, self.out, self.land, self.far = bufs
        self.flipped, self.flipped_sib = flips
        self.s_send, self.s_recv, self.z_send, self.z_recv, self.f_send, self.f_recv = sems
        self.outer = (place.z == 0) | (place.z == place.depth - 1)
        self.width = self.out.shape[1]

    @staticmethod
    def sems(depth):
        return [dma(depth + 1), dma(depth + 1), dma(depth - 1), dma(depth - 1), dma(), dma()]

    @staticmethod
    def bufs(group, depth, width, cols):
        return [
            pltpu.VMEM((group, depth * width), BF16),
            pltpu.VMEM((group, cols), BF16),
            pltpu.VMEM((depth, width, cols), BF16),
            pltpu.VMEM((depth - 1, width, cols), BF16),
            pltpu.VMEM((width, cols), BF16),
        ]

    def lanes(self, z, core):
        return pl.ds(pl.multiple_of((2 * z + core) * self.width, self.width), self.width)

    def right_copy(self):
        return remote(
            self.right,
            self.right_sib,
            self.s_send.at[0],
            self.s_recv.at[0],
            head=self.place.sibling,
        )

    def left_copy(self, z):
        return remote(
            self.left.at[:, self.lanes(z, 1 - self.place.core)],
            self.left_sib.at[:, pl.ds(z * self.width, self.width)],
            self.s_send.at[z + 1],
            self.s_recv.at[z + 1],
            head=self.place.sibling,
        )

    def exchange(self):
        self.right_copy().start()
        for z in range(self.place.depth):
            self.left_copy(z).start()

    def z_copy(self, step):
        z = self.place.z_after(step)
        return remote(
            self.out.at[z],
            self.land.at[step - 1],
            self.z_send.at[step - 1],
            self.z_recv.at[step - 1],
            head=2 * z + self.place.core,
        )

    def send(self, step):
        self.z_copy(step).start()

    def far_copy(self):
        z = self.place.z
        return remote(
            self.out.at[self.place.depth - 1 - z],
            self.far,
            self.f_send,
            self.f_recv,
            head=2 * (1 + lax.div(z, 2)) + self.place.core,
        )

    def sends(self, step):
        z = self.place.z
        return z >= 0 if step == 2 else (z < 3 if step == 1 else z > 0)

    def receives(self, step):
        z = self.place.z
        return z >= 0 if step == 2 else (z > 0 if step == 1 else z < 3)

    def compute(self, hold=False):
        for z in range(self.place.depth):
            mine = jnp.transpose(self.left[:, self.lanes(z, self.place.core)].astype(F32))
            self.flipped[z * self.width : (z + 1) * self.width, :] = mine.astype(BF16)
        for z in range(self.place.depth):
            self.left_copy(z).wait_recv()
            here = slice(z * self.width, (z + 1) * self.width)
            theirs = jnp.transpose(self.left_sib[:, here].astype(F32))
            self.flipped_sib[here, :] = theirs.astype(BF16)
        self.right_copy().wait_recv()

        def tile(where):
            value = dot_nn(self.flipped[...], self.right[:, where])
            value = value + dot_nn(self.flipped_sib[...], self.right_sib[:, where])
            value = value.astype(BF16)
            for z in range(self.place.depth):
                self.out[z, :, where] = value[z * self.width : (z + 1) * self.width]

        by_columns(self.out.shape[2], tile)

        @pl.when(self.outer)
        def _():
            self.far_copy().start()

        @pl.when(self.place.z == 0)
        def _():
            self.z_copy(2).start()

        @pl.when(self.sends(1))
        def _():
            self.z_copy(1).start()

        if not hold:
            self.rest()

    def rest(self):
        @pl.when(self.place.z == self.place.depth - 1)
        def _():
            self.z_copy(2).start()

        @pl.when(self.sends(3))
        def _():
            self.z_copy(3).start()

    def relay(self):
        @pl.when(jnp.logical_not(self.outer))
        def _():
            self.far_copy().wait_recv()
            z = self.place.z_after(2)
            self.out[z] = (self.out[z].astype(F32) + self.far[...].astype(F32)).astype(BF16)
            self.z_copy(2).start()

    def total(self):
        total = self.out[self.place.z].astype(F32)
        for step in range(1, self.place.depth):

            @pl.when(self.receives(step))
            def _(step=step):
                self.z_copy(step).wait_recv()

            piece = self.land[step - 1].astype(F32)
            total = total + jnp.where(self.receives(step), piece, 0.0)
        return total

    def finish(self):
        self.right_copy().wait_send()
        for z in range(self.place.depth):
            self.left_copy(z).wait_send()

        @pl.when(self.outer)
        def _():
            self.far_copy().wait_send()

        for step in range(1, self.place.depth):

            @pl.when(self.sends(step))
            def _(step=step):
                self.z_copy(step).wait_send()


class OutGradJob:
    def __init__(self, place, left, right, bufs, sems):
        self.place, self.left, self.right = place, left, right
        self.left_sib, self.right_sib, self.out, self.mid, self.land = bufs
        self.s_send, self.s_recv, self.p_send, self.p_recv, self.z_send, self.z_recv, self.local = sems
        self.width = self.out.shape[0]
        self.rows = self.mid.shape[1]

    @staticmethod
    def sems(peers, depth):
        return [
            dma(2),
            dma(2),
            dma(peers - 1),
            dma(peers - 1),
            dma(depth - 1),
            dma(depth - 1),
            dma(),
        ]

    @staticmethod
    def bufs(group, peers, depth, width, cols):
        return [
            pltpu.VMEM((group, width), BF16),
            pltpu.VMEM((group, cols), BF16),
            pltpu.VMEM((width, cols), BF16),
            pltpu.VMEM((peers, width // peers, cols), BF16),
            pltpu.VMEM((depth - 1, width // peers, cols), BF16),
        ]

    def lanes(self, core):
        return pl.ds(pl.multiple_of(core * self.width, self.width), self.width)

    def copies(self):
        return (
            remote(
                self.right,
                self.right_sib,
                self.s_send.at[0],
                self.s_recv.at[0],
                head=self.place.sibling,
            ),
            remote(
                self.left.at[:, self.lanes(1 - self.place.core)],
                self.left_sib,
                self.s_send.at[1],
                self.s_recv.at[1],
                head=self.place.sibling,
            ),
        )

    def exchange(self):
        for copy in self.copies():
            copy.start()

    def piece(self, peer):
        return self.out.at[pl.ds(pl.multiple_of(peer * self.rows, self.rows), self.rows)]

    def p_copy(self, step):
        target = self.place.peer_after(step)
        return remote(
            self.piece(target),
            self.mid.at[self.place.peer],
            self.p_send.at[step - 1],
            self.p_recv.at[step - 1],
            blk=target,
        )

    def own_copy(self):
        return pltpu.make_async_copy(
            self.piece(self.place.peer), self.mid.at[self.place.peer], self.local
        )

    def z_copy(self, step):
        z = self.place.z_after(step)
        return remote(
            self.mid.at[z],
            self.land.at[step - 1],
            self.z_send.at[step - 1],
            self.z_recv.at[step - 1],
            head=2 * z + self.place.core,
        )

    def compute(self):
        for copy in self.copies():
            copy.wait_recv()
        mine = jnp.transpose(self.left[:, self.lanes(self.place.core)].astype(F32)).astype(BF16)
        theirs = jnp.transpose(self.left_sib[...].astype(F32)).astype(BF16)

        def tile(where):
            value = dot_nn(mine, self.right[:, where]) + dot_nn(theirs, self.right_sib[:, where])
            self.out[:, where] = value.astype(BF16)

        by_columns(self.out.shape[1], tile)
        for step in range(1, self.place.peers):
            self.p_copy(step).start()
        self.own_copy().start()

    def spread(self):
        self.own_copy().wait()
        for step in range(1, self.place.peers):
            source = self.place.peer_before(step)
            remote(
                self.piece(source),
                self.mid.at[source],
                self.p_send.at[step - 1],
                self.p_recv.at[step - 1],
                blk=source,
            ).wait_recv()
        for step in range(1, self.place.depth):
            self.z_copy(step).start()

    def total(self):
        total = self.mid[self.place.z].astype(F32)
        for step in range(1, self.place.depth):
            self.z_copy(step).wait_recv()
            total = total + self.land[step - 1].astype(F32)
        return total

    def finish(self):
        for copy in self.copies():
            copy.wait_send()
        for step in range(1, self.place.peers):
            self.p_copy(step).wait_send()
        for step in range(1, self.place.depth):
            self.z_copy(step).wait_send()


def rms_back_of(values, upstream):
    inverse = inverse_rms(values)
    inner_mean = jnp.mean(upstream * values, axis=-1, keepdims=True)
    return inverse * upstream - values * (inverse * inverse * inverse) * inner_mean


def attend_back_chunk(sizes, place, block_offset, index, refs):
    tile, chunk, cols, group, lead = sizes.tile, sizes.chunk, sizes.cols, sizes.group, sizes.lead
    block = sizes.reach - block_offset
    offset = pl.multiple_of(block * group + index * chunk, chunk)
    there = pl.ds(offset, chunk)
    here = pl.ds(pl.multiple_of(index * chunk, chunk), chunk)
    spot = offset + lax.broadcasted_iota(jnp.int32, (chunk, 1), 0)
    lane = lax.broadcasted_iota(jnp.int32, (tile, 2 * HD), 1)
    begin = lax.div(jnp.maximum(offset - lead, 0), tile)
    end = jnp.minimum(
        lax.div(jnp.maximum(offset + chunk + sizes.doc_max - 2 - lead + tile, 0), tile), group // tile
    )
    pairs = range(cols // (2 * HD))
    lanes = [slice(pair * 2 * HD, (pair + 1) * 2 * HD) for pair in pairs]
    value_lanes = [slice(cols + part.start, cols + part.stop) for part in lanes]

    def step(index, sums):
        row = pl.multiple_of(index * tile, tile)
        rows = pl.ds(row, tile)
        last = lead + row + lax.broadcasted_iota(jnp.int32, (1, tile), 1)
        allowed = (spot >= refs.first[:, rows]) & (spot <= last)
        masks = (lane < HD, lane >= HD)
        halves, grads, scores, changes = [], [], [], []
        for pair in pairs:
            queries = refs.queries[rows, lanes[pair]] * jnp.asarray(HD ** (-0.5), BF16)
            upstream = refs.mixed_grad[rows, lanes[pair]]
            for mask in masks:
                halves.append(jnp.where(mask, queries, jnp.zeros_like(queries)))
                grads.append(jnp.where(mask, upstream, jnp.zeros_like(upstream)))
                scores.append(dot_nt(refs.keys[there, lanes[pair]], halves[-1]))
                changes.append(dot_nt(refs.keys[there, value_lanes[pair]], grads[-1]))
        out = list(sums)
        for pair in pairs:
            back = []
            for which in range(2):
                head = 2 * pair + which
                line = slice(head, head + 1)
                probs = jnp.where(allowed, jnp.exp(scores[head] - refs.logs[line, rows]), 0.0)
                change = (probs * (changes[head] - refs.delta[line, rows])).astype(BF16)
                out[2 * pair] = out[2 * pair] + dot_nn(change, halves[head])
                out[2 * pair + 1] = out[2 * pair + 1] + dot_nn(probs.astype(BF16), grads[head])
                back.append(dot_tn(change, refs.keys[there, lanes[pair]]))
            refs.dq[rows, lanes[pair]] += jnp.where(masks[0], back[0], back[1])
        return tuple(out)

    empty = jnp.zeros((chunk, 2 * HD), F32)
    sums = lax.fori_loop(begin, end, step, tuple(empty for _ in pairs for _ in range(2)))
    base = block * 2 * cols
    for pair in pairs:
        for part, value in ((lanes[pair], sums[2 * pair]), (value_lanes[pair], sums[2 * pair + 1])):
            refs.dkv[here, base + part.start : base + part.stop] = value


def backward_body(sizes, layer, fused, refs):
    place = Place()
    tok, cols, group, hidden = sizes.tok, sizes.cols, sizes.group, sizes.hidden
    tile, chunk, lead, reach = sizes.tile, sizes.chunk, sizes.lead, sizes.reach
    refs.gate_up = refs.dkv.at[:, pl.ds(0, 2 * hidden)]
    place.greet()
    grad = refs.grad[...].astype(F32)
    own_rows = pl.ds(pl.multiple_of(place.peer * tok, tok), tok)
    refs.down_in[own_rows, :] = grad.astype(BF16)
    ag1 = PlaneGather(place, refs.down_in, refs.ag1_s, refs.ag1_r)
    ag1.start()
    loads = {
        name: pltpu.make_async_copy(src, dst, refs.load_sem.at[index])
        for index, (name, src, dst) in enumerate(
            (
                ("d", refs.d_full, refs.wd),
                ("gate_up", refs.gate_up_in, refs.gate_up),
                ("g", refs.g_full, refs.wg),
                ("o", refs.o_full, refs.wo),
                ("q", refs.q_full, refs.wq),
                ("hidden", refs.hidden_in, refs.hidden),
                ("scaled_ffn", refs.scaled_ffn_in, refs.scaled_ffn),
            )
        )
    }
    for copy in loads.values():
        copy.start()
    jobs = []
    if fused:
        job_d = GradJob(place, refs.hidden, refs.down_in, refs.jd_buf, refs.flips, refs.jd_sem)
        job_g = GradJob(place, refs.scaled_ffn, refs.gate_up_grad, refs.jg_buf, refs.flips, refs.jg_sem)
        job_o = OutGradJob(place, refs.mixed, refs.proj_in, refs.jo_buf, refs.jo_sem)
        jobs = [job_d, job_o]
        if layer == 0:
            job_q = GradJob(
                place, refs.old_scaled, refs.old_qkv, refs.jq_buf, refs.flips, refs.jq_sem
            )
            jobs.append(job_q)
            job_q.exchange()
        loads["hidden"].wait()
        loads["scaled_ffn"].wait()
    loads["d"].wait()
    loads["gate_up"].wait()
    loads["g"].wait()
    if fused and layer == 0:
        job_q.compute()
        job_q.relay()

    sum1 = PlaneSum(place, refs.part1, refs.sum1, refs.rs1_s, refs.rs1_r)

    for steps in peer_groups(place.peers):
        peers = [place.peer_before(step) for step in steps]
        rows = [pl.ds(pl.multiple_of(peer * tok, tok), tok) for peer in peers]
        for step in steps:
            ag1.await_step(step)
        if fused and steps[-1] == place.peers - 1:
            job_d.exchange()
        x = jnp.concatenate([refs.down_in[where, :] for where in rows], axis=0)

        def block(where, x=x, rows=rows):
            there = pl.ds(pl.multiple_of(hidden + where.start, where.size), where.size)
            grad_hidden = dot_nt(x, refs.wd[where, :])
            for index, row in enumerate(rows):
                piece = grad_hidden[index * tok : (index + 1) * tok]
                gate = refs.gate_up[row, where]
                up = refs.gate_up[row, there]
                sigmoid = 1.0 / (1.0 + jnp.exp(-gate))
                gate_grad = piece * up * (sigmoid * (1.0 + gate * (1.0 - sigmoid)))
                refs.gate_up_grad[row, where] = gate_grad.astype(BF16)
                refs.gate_up_grad[row, there] = (piece * (gate * sigmoid)).astype(BF16)

        by_columns(hidden, block)
        low = jnp.concatenate([refs.gate_up_grad[where, :] for where in rows], axis=0)

        def back(where, low=low, peers=peers):
            value = dot_nt(low, refs.wg[where, :]).astype(BF16)
            for index, peer in enumerate(peers):
                refs.part1[peer, :, where] = value[index * tok : (index + 1) * tok]

        by_columns(D, back)
        for peer in peers:
            sum1.send_to(peer)

    if fused:
        job_g.exchange()
        job_d.compute()
        if layer == 0:
            own_scaled = refs.wd.at[pl.ds(0, group)]
            scaled_load = pltpu.make_async_copy(refs.scaled_in, own_scaled, refs.load_sem.at[0])
            scaled_load.start()
    middle = refs.middle[...]
    grad_middle = grad + rms_back_of(middle, sum1.total())
    refs.proj_in[own_rows, :] = grad_middle.astype(BF16)
    ag2 = PlaneGather(place, refs.proj_in, refs.ag2_s, refs.ag2_r)
    ag2.start()
    if fused:
        job_g.compute()
        job_d.relay()
    refs.dq[...] = jnp.zeros_like(refs.dq)
    loads["o"].wait()
    loads["q"].wait()

    for steps in peer_groups(place.peers):
        rows = [
            pl.ds(pl.multiple_of(place.peer_before(step) * tok, tok), tok) for step in steps
        ]
        for step in steps:
            ag2.await_step(step)
        x = jnp.concatenate([refs.proj_in[where, :] for where in rows], axis=0)

        def block(where, x=x, rows=rows):
            value = dot_nt(x, refs.wo[where, :]).astype(BF16)
            for index, row in enumerate(rows):
                refs.mixed_grad[row, where] = value[index * tok : (index + 1) * tok]

        by_columns(cols, block)
    if fused:
        job_o.exchange()

    def deltas(index, carry):
        rows = pl.ds(pl.multiple_of(index * tile, tile), tile)
        for pair in range(cols // (2 * HD)):
            lanes = slice(pair * 2 * HD, (pair + 1) * 2 * HD)
            product = jnp.transpose(
                refs.mixed_grad[rows, lanes].astype(F32) * refs.attended[rows, lanes]
            )
            for which in range(2):
                refs.delta[2 * pair + which : 2 * pair + which + 1, rows] = jnp.sum(
                    product[which * HD : (which + 1) * HD], axis=0, keepdims=True
                )
        return carry

    lax.fori_loop(0, group // tile, deltas, 0)

    halo = HaloBack(place, refs.dkv, refs.give, refs.land, refs.s_land, reach, refs.halo_sem)
    per_block = group // chunk

    def key_blocks(offset):
        @pl.when(place.plane >= offset)
        def _():
            def body(index, carry):
                attend_back_chunk(sizes, place, offset, index, refs)
                return carry

            lax.fori_loop(0, per_block, body, 0)

    for offset in range(1, reach + 1, 2):
        key_blocks(offset)
    halo.hand()
    for offset in range(2, reach + 1, 2):
        key_blocks(offset)
    halo.send()
    if fused:
        job_g.relay()
    key_blocks(0)
    swaps = []

    def hand_out(name, value):
        pack = getattr(refs, f"pack_{name}")
        for peer in range(sizes.peers):
            pack[peer, 0] = value[peer * sizes.own_rows : (peer + 1) * sizes.own_rows]
        swap = WeightSwap(
            place, pack, 0, getattr(refs, f"rows_{name}"), getattr(refs, f"swap_{name}")
        )
        swap.start()
        swaps.append(swap)

    if fused:
        job_o.compute()
        if layer == 0:
            hand_out("q1", job_q.total().astype(BF16))
            hand_out("g1", refs.raw_g1[...])
    refs.qkv_grad[:, 0:cols] = (refs.dq[...] * (HD ** (-0.5))).astype(BF16)
    if fused:
        job_o.spread()
    halo.collect()
    refs.qkv_grad[:, cols:] = refs.dkv[:, reach * 2 * cols : (reach + 1) * 2 * cols].astype(BF16)
    if fused and layer == 0:
        scaled_load.wait()
        job_p = GradJob(place, own_scaled, refs.qkv_grad, refs.jp_buf, refs.flips, refs.jp_sem)
        job_p.exchange()

    sum1.finish()
    sum2 = PlaneSum(place, refs.part1, refs.sum2, refs.rs2_s, refs.rs2_r)

    for steps in [g for g in peer_groups(place.peers)[1:]] + [(0,)]:
        peers = [place.peer_before(step) for step in steps]
        low = jnp.concatenate(
            [refs.qkv_grad[pl.ds(pl.multiple_of(peer * tok, tok), tok), :] for peer in peers], axis=0
        )

        def back(where, low=low, peers=peers):
            value = dot_nt(low, refs.wq[where, :]).astype(BF16)
            for index, peer in enumerate(peers):
                refs.part1[peer, :, where] = value[index * tok : (index + 1) * tok]

        by_columns(D, back)
        for peer in peers:
            sum2.send_to(peer)

    if fused and layer == 0:
        job_p.compute()
    refs.next[...] = grad_middle + rms_back_of(refs.stream[...].astype(F32), sum2.total())
    if fused and layer == 0:
        job_p.relay()
    for item in [ag1, ag2, sum2, halo]:
        item.finish()
    if not fused:
        loads["hidden"].wait()
        loads["scaled_ffn"].wait()
        return
    refs.raw_down[...] = job_d.total()
    refs.raw_o[...] = job_o.total()
    if layer > 0:
        refs.raw_g[...] = job_g.total().astype(BF16)
        job_g.finish()
    else:
        hand_out("g0", job_g.total().astype(BF16))
        hand_out("q0", job_p.total().astype(BF16))
        job_g.finish()
        job_p.finish()

        for swap in swaps:
            swap.arrive()
            swap.finish()
    for item in jobs:
        item.finish()


def backward_layer(sizes, layer, fused, grad, first_row, kept, full, old, collective_id):
    peers, planes, depth = sizes.peers, sizes.planes, sizes.planes // 2
    tok, cols, group, hidden, reach = sizes.tok, sizes.cols, sizes.group, sizes.hidden, sizes.reach
    q_full, o_full, g_full, d_full = full
    inputs = {
        "grad": (grad, VMEM),
        "first": (first_row, VMEM),
        "middle": (kept["middle"], VMEM),
        "stream": (kept["stream"], VMEM),
        "queries": (kept["queries"], VMEM),
        "keys": (kept["keys"], VMEM),
        "attended": (kept["attended"], VMEM),
        "logs": (kept["logs"], VMEM),
        "mixed": (kept["mixed"], VMEM),
        "gate_up_in": (kept["gate_up_out"], ANY),
        "hidden_in": (kept["hidden"], ANY),
        "scaled_ffn_in": (kept["scaled_ffn"], ANY),
        "q_full": (q_full, ANY),
        "o_full": (o_full, ANY),
        "g_full": (g_full, ANY),
        "d_full": (d_full, ANY),
    }
    outputs = {
        "next": ((tok, D), F32, VMEM),
        "qkv_grad": ((group, 3 * cols), BF16, VMEM),
    }
    scratch = {
        "wq": pltpu.VMEM((D, 3 * cols), BF16),
        "wo": pltpu.VMEM((cols, D), BF16),
        "wg": pltpu.VMEM((D, 2 * hidden), BF16),
        "wd": pltpu.VMEM((hidden, D), BF16),
        "dkv": pltpu.VMEM((group, max(2 * hidden, (reach + 1) * 2 * cols)), F32),
        "hidden": pltpu.VMEM((group, hidden), BF16),
        "scaled_ffn": pltpu.VMEM((group, D), BF16),
        "mixed_grad": pltpu.VMEM((group, cols), BF16),
        "delta": pltpu.VMEM((cols // HD, group), F32),
        "dq": pltpu.VMEM((group, cols), F32),
        "give": pltpu.VMEM((reach, group, 2 * cols), BF16),
        "land": pltpu.VMEM((reach // 2, group, 2 * cols), BF16),
        "s_land": pltpu.VMEM((reach // 2, group, 2 * cols), BF16),
        "load_sem": dma(7),
        "halo_sem": Halo.sems(reach),
    }
    for name in ("part1", "sum1", "sum2"):
        scratch[name] = pltpu.VMEM((peers, tok, D), BF16)
    for name in ("rs1_s", "rs1_r", "rs2_s", "rs2_r"):
        scratch[name] = dma(peers - 1)
    for name in ("ag1_s", "ag1_r", "ag2_s", "ag2_r"):
        scratch[name] = PlaneGather.sems(peers)
    space = pltpu.VMEM
    if fused:
        scratch["down_in"] = space((group, D), BF16)
        scratch["proj_in"] = space((group, D), BF16)
        scratch["gate_up_grad"] = space((group, 2 * hidden), BF16)
        width = D // planes
        strip = hidden // planes
        scratch["flips"] = [pltpu.VMEM((depth * width, group), BF16)] * 2
        scratch["jd_buf"] = GradJob.bufs(group, depth, strip, D)
        scratch["jg_buf"] = GradJob.bufs(group, depth, width, 2 * hidden)
        scratch["jo_buf"] = OutGradJob.bufs(group, peers, depth, cols // 2, D)
        scratch["jd_sem"] = GradJob.sems(depth)
        scratch["jg_sem"] = GradJob.sems(depth)
        scratch["jo_sem"] = OutGradJob.sems(peers, depth)
        outputs["raw_down"] = ((strip, D), F32, VMEM)
        outputs["raw_o"] = ((sizes.own_rows, D), F32, VMEM)
        if layer > 0:
            outputs["raw_g"] = ((width, 2 * hidden), BF16, VMEM)
        else:
            rows = sizes.own_rows
            inputs["old_scaled"] = (old["scaled"], VMEM)
            inputs["old_qkv"] = (old["qkv_grad"], VMEM)
            inputs["raw_g1"] = (old["raw_g"], VMEM)
            inputs["scaled_in"] = (kept["scaled"], ANY)
            for name in ("jq", "jp"):
                scratch[f"{name}_buf"] = GradJob.bufs(group, depth, width, 3 * cols)
                scratch[f"{name}_sem"] = GradJob.sems(depth)
            for l in range(LAYERS):
                for kind, width_of in (("g", 2 * hidden), ("q", 3 * cols)):
                    outputs[f"rows_{kind}{l}"] = ((peers * rows, width_of), BF16, VMEM)
                    scratch[f"pack_{kind}{l}"] = pltpu.VMEM((peers, 1, rows, width_of), BF16)
                    scratch[f"swap_{kind}{l}"] = WeightSwap.sems(peers)
    else:
        outputs["down_in"] = ((group, D), BF16, VMEM)
        outputs["proj_in"] = ((group, D), BF16, VMEM)
        outputs["gate_up_grad"] = ((group, 2 * hidden), BF16, VMEM)
    return launch(
        functools.partial(backward_body, sizes, layer, fused),
        f"backward{layer}",
        inputs,
        outputs,
        scratch,
        collective_id,
        flops=group * D * (4 * cols + 3 * hidden) * 4,
    )


def inverse_rms(values):
    return lax.rsqrt(jnp.mean(values * values, axis=-1, keepdims=True) + EPSILON)


def matmul(left, right):
    return jnp.dot(left, right, preferred_element_type=F32)


def contract_rows(left, right):
    return jnp.einsum("td,te->de", left, right, preferred_element_type=F32)


def contract_cols(left, right):
    return jnp.einsum("te,de->td", left, right, preferred_element_type=F32)


def local(
    tokens,
    gain_attn,
    w_query,
    w_key,
    w_value,
    w_out,
    gain_ffn,
    w_gate,
    w_up,
    w_down,
    doc_ids,
    cotangent,
):
    planes = lax.axis_size("head")
    peers = lax.axis_size("blk")
    plane = lax.axis_index("head")
    tok = tokens.shape[0]
    group = tok * peers
    stream_rows = group * planes
    doc_max = stream_rows // 4
    reach = (doc_max - 1 + group - 1) // group
    reach = reach + reach % 2
    own_rows = w_query.shape[1]
    cols = D // peers
    strip = w_down.shape[1]
    hidden_cols = strip * planes
    tile = 256
    chunk = 256
    lead = reach * group

    attn_rows = gain_attn.astype(F32)[:, :, None]
    ffn_rows = gain_ffn.astype(F32)[:, :, None]

    def for_peers(weight, gain):
        scaled = (weight.astype(F32) * gain).astype(BF16)
        return scaled.reshape(LAYERS, own_rows, peers, cols).transpose(2, 0, 1, 3)

    def for_peers_ffn(weight, gain):
        scaled = (weight.astype(F32) * gain).astype(BF16)
        scaled = scaled.reshape(LAYERS, own_rows, planes, peers, strip).transpose(3, 0, 1, 2, 4)
        return scaled.reshape(peers, LAYERS, own_rows, hidden_cols)

    aligned = strip % 128 == 0
    weights = {"w_out": w_out, "w_down": w_down}
    if aligned:
        weights |= {
            "w_query": w_query,
            "w_key": w_key,
            "w_value": w_value,
            "w_gate": w_gate,
            "w_up": w_up,
            "attn_gain": attn_rows,
            "ffn_gain": ffn_rows,
        }
    else:
        weights |= {
            "pack_q": jnp.concatenate(
                [for_peers(w, attn_rows) for w in (w_query, w_key, w_value)], axis=3
            ),
            "pack_g": jnp.concatenate([for_peers_ffn(w, ffn_rows) for w in (w_gate, w_up)], axis=3),
        }
    sizes = types.SimpleNamespace(
        peers=peers,
        planes=planes,
        tok=tok,
        cols=cols,
        group=group,
        hidden=hidden_cols,
        reach=reach,
        own_rows=own_rows,
        tile=tile,
        chunk=chunk,
        lead=lead,
        doc_max=doc_max,
        documents=stream_rows // 256,
        aligned=aligned,
    )
    first_row = doc_ids.reshape(1, stream_rows)
    stream = tokens
    saved = []
    full = []
    for layer in range(LAYERS):
        kept = forward_layer(sizes, layer, stream, first_row, weights, 10 + layer)
        if layer == 0:
            first_row = kept["first"]
            weights = weights | {
                "mine_g": kept["mine_g"],
                "q_full": kept["q_full1"],
                "o_full": kept["out_full1"],
            }
            full.append((kept["q_full0"], kept["out_full0"], kept["g_full"], kept["d_full"]))
        else:
            full.append((weights["q_full"], weights["o_full"], kept["g_full"], kept["d_full"]))
        saved.append(kept | {"stream": stream})
        stream = kept["next"]
    output = stream

    grad = cotangent
    fused = planes == 8 and aligned
    backs = [None] * LAYERS
    old = None
    for layer in reversed(range(LAYERS)):
        kept = saved[layer]
        back = backward_layer(
            sizes, layer, fused, grad, first_row, kept, full[layer], old, 12 + layer
        )
        grad = back["next"]
        old = back | {"scaled": kept["scaled"]}
        backs[layer] = back
    if fused:
        rows = backs[0]
        grad_out = jnp.stack([back["raw_o"] for back in backs])
        grad_down = jnp.stack([back["raw_down"] for back in backs])
    else:
        raw, grad_out, grad_down = [], [], []
        for kept, back in zip(saved, backs):
            down_in = back["down_in"]
            proj_in = back["proj_in"]
            scatter = functools.partial(lax.psum_scatter, scatter_dimension=0, tiled=True)
            grad_down.append(
                scatter(contract_rows(kept["hidden"], down_in).astype(BF16), "head").astype(F32)
            )
            padded = lax.dynamic_update_slice(
                jnp.zeros((D, D), BF16),
                contract_rows(kept["mixed"], proj_in).astype(BF16),
                (lax.axis_index("blk") * cols, 0),
            )
            grad_out.append(scatter(padded, ("head", "blk")).astype(F32))
            pieces = [
                scatter(contract_rows(kept[name], right).astype(BF16), "head")
                for name, right in (
                    ("scaled", back["qkv_grad"]),
                    ("scaled_ffn", back["gate_up_grad"]),
                )
            ]
            raw.append(jnp.concatenate(pieces, axis=1))
        raw = jnp.stack(raw).reshape(LAYERS, peers, own_rows, 3 * cols + 2 * hidden_cols)
        raw = plane_swap(raw.transpose(1, 0, 2, 3), 1, "rows_swap")
        rows = {}
        for layer in range(LAYERS):
            flat = raw[:, layer].reshape(peers * own_rows, 3 * cols + 2 * hidden_cols)
            rows[f"rows_q{layer}"] = flat[:, : 3 * cols]
            rows[f"rows_g{layer}"] = flat[:, 3 * cols :]
        grad_out, grad_down = jnp.stack(grad_out), jnp.stack(grad_down)

    def attn_rows_of(which):
        pieces = [
            rows[f"rows_q{layer}"].reshape(peers, own_rows, 3, cols)[:, :, which].transpose(1, 0, 2)
            for layer in range(LAYERS)
        ]
        return jnp.stack([p.reshape(own_rows, D).astype(F32) for p in pieces])

    def ffn_rows_of(which):
        pieces = [
            rows[f"rows_g{layer}"]
            .reshape(peers, own_rows, 2, planes, strip)[:, :, which]
            .transpose(1, 2, 0, 3)
            for layer in range(LAYERS)
        ]
        return jnp.stack([p.reshape(own_rows, peers * hidden_cols).astype(F32) for p in pieces])

    raw_query, raw_key, raw_value = (attn_rows_of(which) for which in range(3))
    raw_gate, raw_up = (ffn_rows_of(which) for which in range(2))

    def gain_grad(*pairs):
        return sum(jnp.sum(weight.astype(F32) * raw_part, axis=2) for weight, raw_part in pairs)

    grad_gain_attn = gain_grad((w_query, raw_query), (w_key, raw_key), (w_value, raw_value))
    grad_gain_ffn = gain_grad((w_gate, raw_gate), (w_up, raw_up))
    return (
        output,
        grad,
        grad_gain_attn,
        raw_query * attn_rows,
        raw_key * attn_rows,
        raw_value * attn_rows,
        grad_out,
        grad_gain_ffn,
        raw_gate * ffn_rows,
        raw_up * ffn_rows,
        grad_down,
    )


def solution(mesh):
    rows = P(("head", "blk"), None)
    vector = P(None, ("head", "blk"))
    matrix = P(None, ("head", "blk"), None)
    return jax.shard_map(
        local,
        mesh=mesh,
        in_specs=(
            rows,
            vector,
            matrix,
            matrix,
            matrix,
            matrix,
            vector,
            matrix,
            matrix,
            matrix,
            P(),
            rows,
        ),
        out_specs=(
            rows,
            rows,
            vector,
            matrix,
            matrix,
            matrix,
            matrix,
            vector,
            matrix,
            matrix,
            matrix,
        ),
        check_vma=False,
    )
```

```python
import functools
import math
import types

import jax
import jax.numpy as jnp
from jax import lax
from jax.experimental import pallas as pl
from jax.experimental.pallas import tpu as pltpu
from jax.sharding import PartitionSpec as P

D = 1024
HD = 64
HEADS = D // HD
LAYERS = 2
EPSILON = 1e-05
MASKED = -1e30
MESH = pl.DeviceIdType.MESH
F32 = jnp.float32
BF16 = jnp.bfloat16
ANY = pl.BlockSpec(memory_space=pl.ANY)


def greet_blk(count):
    me = lax.axis_index("blk")
    barrier = pltpu.get_barrier_semaphore()
    for step in range(1, count):
        pl.semaphore_signal(
            barrier,
            inc=1,
            device_id={"blk": lax.rem(me + step, count)},
            device_id_type=MESH,
        )
    pl.semaphore_wait(barrier, count - 1)
    return me


def plane_gather_kernel(count, x_ref, o_ref, send_sem, recv_sem, local_sem):
    me = greet_blk(count)
    copies = []
    for step in range(1, count):
        copy = pltpu.make_async_remote_copy(
            src_ref=x_ref,
            dst_ref=o_ref.at[me],
            send_sem=send_sem.at[step - 1],
            recv_sem=recv_sem.at[step - 1],
            device_id={"blk": lax.rem(me + step, count)},
            device_id_type=MESH,
        )
        copy.start()
        copies.append(copy)
    own = pltpu.make_async_copy(x_ref, o_ref.at[me], local_sem)
    own.start()
    own.wait()
    for copy in copies:
        copy.wait()


def plane_swap_kernel(count, x_ref, o_ref, send_sem, recv_sem, local_sem):
    me = greet_blk(count)
    copies = []
    for step in range(1, count):
        peer = lax.rem(me + step, count)
        copy = pltpu.make_async_remote_copy(
            src_ref=x_ref.at[peer],
            dst_ref=o_ref.at[me],
            send_sem=send_sem.at[step - 1],
            recv_sem=recv_sem.at[step - 1],
            device_id={"blk": peer},
            device_id_type=MESH,
        )
        copy.start()
        copies.append(copy)
    own = pltpu.make_async_copy(x_ref.at[me], o_ref.at[me], local_sem)
    own.start()
    own.wait()
    for copy in copies:
        copy.wait()


def plane_call(kernel, x, out_shape, collective_id, name):
    count = lax.axis_size("blk")
    return pl.pallas_call(
        functools.partial(kernel, count),
        out_shape=jax.ShapeDtypeStruct(out_shape, x.dtype),
        in_specs=[ANY],
        out_specs=ANY,
        scratch_shapes=[
            pltpu.SemaphoreType.DMA((count - 1,)),
            pltpu.SemaphoreType.DMA((count - 1,)),
            pltpu.SemaphoreType.DMA,
        ],
        compiler_params=pltpu.CompilerParams(collective_id=collective_id, has_side_effects=True),
        cost_estimate=pl.CostEstimate(flops=0, bytes_accessed=20_000_000, transcendentals=0),
        name=name,
    )(x)


def plane_gather(x, collective_id, name):
    return plane_call(
        plane_gather_kernel, x, (lax.axis_size("blk"),) + x.shape, collective_id, name
    )


def plane_swap(x, collective_id, name):
    return plane_call(plane_swap_kernel, x, x.shape, collective_id, name)


def launch(body, name, inputs, outputs, scratch, collective_id, flops=0):
    names = list(inputs) + list(outputs)
    flat = []
    for value in scratch.values():
        flat.extend(value if isinstance(value, list) else [value])

    def kernel(*refs):
        named = dict(zip(names, refs))
        rest = list(refs[len(names) :])
        for name, value in scratch.items():
            if isinstance(value, list):
                named[name], rest = rest[: len(value)], rest[len(value) :]
            else:
                named[name], rest = rest[0], rest[1:]
        body(types.SimpleNamespace(**named))

    results = pl.pallas_call(
        kernel,
        out_shape=[jax.ShapeDtypeStruct(shape, dtype) for shape, dtype, _ in outputs.values()],
        in_specs=[spec for _, spec in inputs.values()],
        out_specs=[spec for _, _, spec in outputs.values()],
        scratch_shapes=flat,
        compiler_params=pltpu.CompilerParams(
            collective_id=collective_id, has_side_effects=True, vmem_limit_bytes=60 << 20
        ),
        cost_estimate=pl.CostEstimate(
            flops=flops, bytes_accessed=200_000_000, transcendentals=0
        ),
        name=name,
    )(*[array for array, _ in inputs.values()])
    return dict(zip(outputs, results))


VMEM = pl.BlockSpec(memory_space=pltpu.VMEM)


def dma(*shape):
    return pltpu.SemaphoreType.DMA(shape)


def remote(src, dst, send_sem, recv_sem, **place):
    return pltpu.make_async_remote_copy(
        src_ref=src,
        dst_ref=dst,
        send_sem=send_sem,
        recv_sem=recv_sem,
        device_id=place,
        device_id_type=MESH,
    )


class Place:
    def __init__(self):
        self.peers = lax.axis_size("blk")
        self.planes = lax.axis_size("head")
        self.depth = self.planes // 2
        self.peer = lax.axis_index("blk")
        self.plane = lax.axis_index("head")
        self.z = lax.div(self.plane, 2)
        self.core = lax.rem(self.plane, 2)
        self.sibling = self.plane + 1 - 2 * self.core


    def moved(self, step, sign):
        half = self.peers // 2
        low, high = (step % 2, step // 2) if isinstance(step, int) else (lax.rem(step, 2), lax.div(step, 2))
        bit = lax.rem(lax.rem(self.peer, 2) + low, 2)
        return bit + 2 * lax.rem(lax.div(self.peer, 2) + sign * high + half, half)

    def peer_after(self, step):
        return self.moved(step, 1)

    def peer_before(self, step):
        return self.moved(step, -1)

    def steps_between(self, early, late):
        half = self.peers // 2
        bit = lax.rem(lax.rem(early, 2) + lax.rem(late, 2), 2)
        return bit + 2 * lax.rem(lax.div(late, 2) - lax.div(early, 2) + half, half)

    def z_after(self, step):
        return lax.rem(self.z + step, self.depth)

    def z_before(self, step):
        return lax.rem(self.z + self.depth - step, self.depth)

    def greet(self):
        barrier = pltpu.get_barrier_semaphore()
        for step in range(1, self.peers):
            pl.semaphore_signal(
                barrier, inc=1, device_id={"blk": self.peer_after(step)}, device_id_type=MESH
            )
        for step in range(1, self.depth):
            pl.semaphore_signal(
                barrier,
                inc=1,
                device_id={"head": 2 * self.z_after(step) + self.core},
                device_id_type=MESH,
            )
        pl.semaphore_signal(barrier, inc=1, device_id={"head": self.sibling}, device_id_type=MESH)
        pl.semaphore_wait(barrier, self.peers - 1 + self.depth - 1 + 1)


class PlaneGather:
    def __init__(self, place, flat, send, recv):
        self.place, self.flat, self.send, self.recv = place, flat, send, recv
        self.rows = flat.shape[0] // place.peers
        self.square = place.peers == 4
        self.direct = range(1, 3) if self.square else range(1, place.peers)

    @staticmethod
    def sems(peers):
        return dma(peers)

    def slot(self, peer, half=None):
        start = pl.multiple_of(peer * self.rows, self.rows)
        if half is None:
            return self.flat.at[pl.ds(start, self.rows)]
        middle = self.rows // 2
        return self.flat.at[pl.ds(pl.multiple_of(start + half * middle, middle), middle)]

    def copy(self, step):
        own = self.slot(self.place.peer)
        return remote(
            own,
            own,
            self.send.at[step - 1],
            self.recv.at[step - 1],
            blk=self.place.peer_after(step),
        )

    def relay(self, step):
        where = self.slot(self.place.peer_before(step), step - 1)
        return remote(
            where,
            where,
            self.send.at[step + 1],
            self.recv.at[step + 1],
            blk=self.place.peer_after(3 - step),
        )

    def start(self):
        for step in self.direct:
            self.copy(step).start()

    def await_step(self, step):
        if not step:
            return
        source = self.place.peer_before(step)
        if step in self.direct:
            where = self.slot(source)
            remote(
                where, where, self.send.at[step - 1], self.recv.at[step - 1], blk=source
            ).wait_recv()
            if self.square:
                self.relay(step).start()
        else:
            for half in range(2):
                where = self.slot(source, half)
                remote(
                    where, where, self.send.at[half + 2], self.recv.at[half + 2], blk=source
                ).wait_recv()

    def finish(self):
        for step in self.direct:
            self.copy(step).wait_send()
            if self.square:
                self.relay(step).wait_send()


def peer_groups(peers):
    return [(0,), (1, 2)] + [(step,) for step in range(3, peers)] if peers > 2 else [(0,), (1,)]


class PlaneSum:
    def __init__(self, place, src, dst, send, recv):
        self.place, self.src, self.dst, self.send, self.recv = place, src, dst, send, recv

    def copy_to(self, peer):
        index = jnp.maximum(self.place.steps_between(peer, self.place.peer) - 1, 0)
        return remote(
            self.src.at[peer],
            self.dst.at[self.place.peer],
            self.send.at[index],
            self.recv.at[index],
            blk=peer,
        )

    def send_to(self, peer):
        @pl.when(peer != self.place.peer)
        def _():
            self.copy_to(peer).start()

    def total(self):
        total = self.src[self.place.peer].astype(F32)
        for step in range(1, self.place.peers):
            source = self.place.peer_after(step)
            remote(
                self.src.at[source],
                self.dst.at[source],
                self.send.at[step - 1],
                self.recv.at[step - 1],
                blk=source,
            ).wait_recv()
            total = total + self.dst[source].astype(F32)
        return total

    def finish(self):
        for step in range(1, self.place.peers):
            self.copy_to(self.place.peer_before(step)).wait_send()


class HeadGather:
    def __init__(self, place, src, full, sems):
        self.place, self.src, self.full = place, src, full
        self.z_send, self.z_recv, self.s_send, self.s_recv, self.local, self.r_send = sems
        self.line = place.depth == 4

    @staticmethod
    def sems(depth):
        return [dma(depth - 1), dma(depth - 1), dma(depth), dma(depth), dma(), dma()]

    def slot(self, z, core):
        rows = self.src.shape[0]
        return self.full.at[pl.ds(pl.multiple_of((2 * z + core) * rows, rows), rows)]

    def z_copy(self, step):
        return remote(
            self.src,
            self.slot(self.place.z, self.place.core),
            self.z_send.at[step - 1],
            self.z_recv.at[step - 1],
            head=2 * self.place.z_after(step) + self.place.core,
        )

    def near(self, step):
        z = self.place.z
        if not self.line or step == 2:
            return z >= 0
        return z < 3 if step == 1 else z > 0

    def relays(self, which):
        return self.place.z == (2 if which == 3 else 1)

    def relay_copy(self, which):
        where = self.slot(self.place.z_before(2), self.place.core)
        return remote(
            where,
            where,
            self.r_send,
            self.z_recv.at[which - 1],
            head=2 * (3 if which == 3 else 0) + self.place.core,
        )

    def s_copy(self, step, core):
        z = self.place.z_before(step)
        where = self.slot(z, core)
        return remote(
            self.src if step == 0 else where,
            where,
            self.s_send.at[step],
            self.s_recv.at[step],
            head=self.place.sibling,
        )

    def own_copy(self):
        return pltpu.make_async_copy(
            self.src, self.slot(self.place.z, self.place.core), self.local
        )

    def start(self):
        for step in sorted(range(1, self.place.depth), key=lambda k: k != 2):

            @pl.when(self.near(step))
            def _(step=step):
                self.z_copy(step).start()

        self.s_copy(0, self.place.core).start()
        self.own_copy().start()

    def await_z(self, step):
        where = self.slot(self.place.z_before(step), self.place.core)
        remote(
            self.src,
            where,
            self.z_send.at[step - 1],
            self.z_recv.at[step - 1],
            head=self.place.sibling,
        ).wait_recv()

    def relay(self):
        if self.line:
            self.await_z(2)
            for which in (1, 3):

                @pl.when(self.relays(which))
                def _(which=which):
                    self.relay_copy(which).start()

            self.s_copy(2, self.place.core).start()

    def forward(self):
        for step in range(1, self.place.depth):
            if not (self.line and step == 2):
                self.await_z(step)
                self.s_copy(step, self.place.core).start()

    def arrive(self):
        self.own_copy().wait()
        for step in range(self.place.depth):
            self.s_copy(step, 1 - self.place.core).wait_recv()

    def finish(self):
        for step in range(1, self.place.depth):

            @pl.when(self.near(step))
            def _(step=step):
                self.z_copy(step).wait_send()

        if self.line:
            for which in (1, 3):

                @pl.when(self.relays(which))
                def _(which=which):
                    self.relay_copy(which).wait_send()

        for step in range(self.place.depth):
            self.s_copy(step, self.place.core).wait_send()


class OutGather:
    def __init__(self, place, src, mid, full, sems):
        self.place, self.mid, self.full = place, mid, full
        self.rows = src.shape[0]
        self.over_head = HeadGather(place, src, mid, sems[:6])
        self.send, self.recv, self.local = sems[6:]

    @staticmethod
    def sems(peers, depth):
        return HeadGather.sems(depth) + [dma(2, peers - 1), dma(2, peers - 1), dma(2)]

    def piece(self, peer, core):
        return self.mid.at[pl.ds(pl.multiple_of((2 * peer + core) * self.rows, self.rows), self.rows)]

    def slot(self, peer, core):
        where = (core * self.place.peers + peer) * self.rows
        return self.full.at[pl.ds(pl.multiple_of(where, self.rows), self.rows)]

    def copy(self, step, core):
        target = self.place.peer_after(step)
        return remote(
            self.piece(target, core),
            self.slot(self.place.peer, core),
            self.send.at[core, step - 1],
            self.recv.at[core, step - 1],
            blk=target,
        )

    def own_copy(self, core):
        return pltpu.make_async_copy(
            self.piece(self.place.peer, core),
            self.slot(self.place.peer, core),
            self.local.at[core],
        )

    def start(self):
        self.over_head.start()

    def spread(self):
        self.over_head.relay()
        self.over_head.forward()
        self.over_head.arrive()
        for core in range(2):
            for step in range(1, self.place.peers):
                self.copy(step, core).start()
            self.own_copy(core).start()

    def arrive(self):
        for core in range(2):
            self.own_copy(core).wait()
            for step in range(1, self.place.peers):
                source = self.place.peer_before(step)
                remote(
                    self.piece(source, core),
                    self.slot(source, core),
                    self.send.at[core, step - 1],
                    self.recv.at[core, step - 1],
                    blk=source,
                ).wait_recv()

    def finish(self):
        self.over_head.finish()
        for core in range(2):
            for step in range(1, self.place.peers):
                self.copy(step, core).wait_send()


class WeightSwap:
    def __init__(self, place, src, layer, mine, sems):
        self.place, self.src, self.layer, self.mine = place, src, layer, mine
        self.send, self.recv, self.local = sems

    @staticmethod
    def sems(peers):
        return [dma(peers - 1), dma(peers - 1), dma()]

    def piece(self, peer):
        rows = self.src.shape[2]
        return self.mine.at[pl.ds(pl.multiple_of(peer * rows, rows), rows)]

    def copy(self, step):
        target = self.place.peer_after(step)
        return remote(
            self.src.at[target, self.layer],
            self.piece(self.place.peer),
            self.send.at[step - 1],
            self.recv.at[step - 1],
            blk=target,
        )

    def own_copy(self):
        return pltpu.make_async_copy(
            self.src.at[self.place.peer, self.layer], self.piece(self.place.peer), self.local
        )

    def start(self):
        for step in range(1, self.place.peers):
            self.copy(step).start()
        self.own_copy().start()

    def arrive(self):
        self.own_copy().wait()
        for step in range(1, self.place.peers):
            source = self.place.peer_before(step)
            remote(
                self.src.at[source, self.layer],
                self.piece(source),
                self.send.at[step - 1],
                self.recv.at[step - 1],
                blk=source,
            ).wait_recv()

    def finish(self):
        for step in range(1, self.place.peers):
            self.copy(step).wait_send()


class Halo:
    def __init__(self, place, keys, reach, sems):
        self.place, self.keys, self.reach = place, keys, reach
        self.rows = keys.shape[0] // (reach + 1)
        self.z_send, self.z_recv, self.s_send, self.s_recv = sems

    def block(self, offset):
        return self.keys.at[pl.ds((self.reach - offset) * self.rows, self.rows)]

    @staticmethod
    def sems(reach):
        return [dma(reach // 2), dma(reach // 2), dma(reach // 2), dma(reach // 2)]

    def z_copy(self, hop):
        return remote(
            self.block(0),
            self.block(2 * hop),
            self.z_send.at[hop - 1],
            self.z_recv.at[hop - 1],
            head=self.place.plane + 2 * hop,
        )

    def sends(self, hop):
        return self.place.z + hop < self.place.depth

    def receives(self, hop):
        return self.place.z - hop >= 0

    def start(self):
        for hop in range(1, self.reach // 2 + 1):

            @pl.when(self.sends(hop))
            def _(hop=hop):
                self.z_copy(hop).start()


    def hand(self, i):
        def copy(offset):
            return remote(
                self.block(offset),
                self.block(2 * i - 1),
                self.s_send.at[i - 1],
                self.s_recv.at[i - 1],
                head=self.place.sibling,
            )

        return copy

    def hand_ready(self, i):
        return (
            (self.place.core == 1) & self.receives(i),
            (self.place.core == 0) & self.receives(i - 1),
        )

    def relay(self):
        for i in range(1, self.reach // 2 + 1):
            from_one, from_zero = self.hand_ready(i)
            if i == 1:

                @pl.when(from_zero)
                def _(i=i):
                    self.hand(i)(2 * i - 2).start()

            @pl.when(self.receives(i))
            def _(i=i):
                remote(
                    self.block(0),
                    self.block(2 * i),
                    self.z_send.at[i - 1],
                    self.z_recv.at[i - 1],
                    head=self.place.sibling,
                ).wait_recv()

            @pl.when(from_one)
            def _(i=i):
                self.hand(i)(2 * i).start()

            if i < self.reach // 2:

                @pl.when(self.hand_ready(i + 1)[1])
                def _(i=i):
                    self.hand(i + 1)(2 * i).start()

    def arrive(self):
        for i in range(1, self.reach // 2 + 1):

            @pl.when(self.place.z - i + self.place.core >= 0)
            def _(i=i):
                self.hand(i)(0).wait_recv()

    def finish(self):
        for hop in range(1, self.reach // 2 + 1):

            @pl.when(self.sends(hop))
            def _(hop=hop):
                self.z_copy(hop).wait_send()

            from_one, from_zero = self.hand_ready(hop)

            @pl.when(from_one)
            def _(hop=hop):
                self.hand(hop)(2 * hop).wait_send()

            @pl.when(from_zero)
            def _(hop=hop):
                self.hand(hop)(2 * hop - 2).wait_send()


def columns(total, most=256):
    width = math.gcd(total, most)
    return total // width, width


def by_columns(total, step, most=256):
    count, width = columns(total, most)

    def body(index, carry):
        step(pl.ds(pl.multiple_of(index * width, width), width))
        return carry

    lax.fori_loop(0, count, body, 0)


def attend_tile(sizes, place, tile_index, q_ref, keys_ref, first_ref, mixed_ref, attended_ref, log_ref):
    tile, chunk, cols, group, lead = sizes.tile, sizes.chunk, sizes.cols, sizes.group, sizes.lead
    row = pl.multiple_of(tile_index * tile, tile)
    rows = pl.ds(row, tile)
    first = first_ref[:, rows]
    last = lead + row + lax.broadcasted_iota(jnp.int32, (1, tile), 1)
    lane = lax.broadcasted_iota(jnp.int32, (tile, 2 * HD), 1)
    lowest = jnp.maximum(lead + row - (sizes.doc_max - 1), lead - place.plane * group)
    begin = lax.div(jnp.maximum(lowest, 0), chunk)
    end = lax.div(lead + row + tile + chunk - 1, chunk)
    pairs = range(cols // (2 * HD))
    halves = []
    for pair in pairs:
        queries = q_ref[rows, pair * 2 * HD : (pair + 1) * 2 * HD] * jnp.asarray(HD ** (-0.5), BF16)
        zero = jnp.zeros_like(queries)
        halves.append(jnp.where(lane < HD, queries, zero))
        halves.append(jnp.where(lane >= HD, queries, zero))

    def step(block, state):
        offset = pl.multiple_of(block * chunk, chunk)
        there = pl.ds(offset, chunk)
        spot = offset + lax.broadcasted_iota(jnp.int32, (chunk, tile), 0)
        allowed = (spot >= first) & (spot <= last)
        scores = []
        for index, half in enumerate(halves):
            lanes = slice(index // 2 * 2 * HD, (index // 2 + 1) * 2 * HD)
            scores.append(dot_nt(keys_ref[there, lanes], half))
        out = []
        for index, (top, total, accum) in enumerate(state):
            lanes = slice(cols + index // 2 * 2 * HD, cols + (index // 2 + 1) * 2 * HD)
            score = jnp.where(allowed, scores[index], MASKED)
            new_top = jnp.maximum(top, jnp.max(score, axis=0, keepdims=True))
            factor = jnp.exp(top - new_top)
            weights = jnp.exp(score - new_top)
            total = total * factor + jnp.sum(weights, axis=0, keepdims=True)
            accum = accum * factor + dot_tn(keys_ref[there, lanes], weights.astype(BF16))
            out.append((new_top, total, accum))
        return tuple(out)

    start = (
        jnp.full((1, tile), MASKED, F32),
        jnp.zeros((1, tile), F32),
        jnp.zeros((2 * HD, tile), F32),
    )
    state = lax.fori_loop(begin, end, step, tuple(start for _ in halves))
    for pair in pairs:
        lanes = slice(pair * 2 * HD, (pair + 1) * 2 * HD)
        parts = []
        for which in range(2):
            head = 2 * pair + which
            top, total, accum = state[head]
            log_ref[head : head + 1, rows] = top + jnp.log(total)
            parts.append(accum[which * HD : (which + 1) * HD] / total)
        attended = jnp.transpose(jnp.concatenate(parts, axis=0))
        attended_ref[rows, lanes] = attended
        mixed_ref[rows, lanes] = attended.astype(BF16)


def pack_query(sizes, l, refs):
    cols = sizes.cols
    gain = refs.attn_gain[l]
    for part, weight in enumerate((refs.w_query, refs.w_key, refs.w_value)):
        for peer in range(sizes.peers):
            piece = weight[l, :, peer * cols : (peer + 1) * cols].astype(F32) * gain
            refs.pack_q[peer, l, :, part * cols : (part + 1) * cols] = piece.astype(BF16)


def pack_ffn(sizes, l, refs):
    strip, hidden = sizes.hidden // sizes.planes, sizes.hidden
    gain = refs.ffn_gain[l]
    for part, weight in enumerate((refs.w_gate, refs.w_up)):
        for peer in range(sizes.peers):
            for plane in range(sizes.planes):
                source = (plane * sizes.peers + peer) * strip
                piece = weight[l, :, source : source + strip].astype(F32) * gain
                target = part * hidden + plane * strip
                refs.pack_g[peer, l, :, target : target + strip] = piece.astype(BF16)


def document_starts(sizes, place, documents):
    group = sizes.group
    here = pl.ds(pl.multiple_of(place.plane * group, group), group)
    own = documents[:, here]
    every = documents[...]
    starts = jnp.zeros_like(own)
    for document in range(sizes.documents - 1):
        count = jnp.sum((every == document).astype(jnp.int32), axis=1, keepdims=True)
        starts = starts + jnp.where(own > document, count, 0)
    return starts - (place.plane * group - sizes.lead)


def forward_body(sizes, layer, refs):
    place = Place()
    tok, cols, group, hidden = sizes.tok, sizes.cols, sizes.group, sizes.hidden
    tile = sizes.tile
    loads = refs.load_sem
    if layer == 0:
        if sizes.aligned:
            pack_query(sizes, 0, refs)
        place.greet()
        swap_q = [
            WeightSwap(place, refs.pack_q, l, refs.mine_q.at[l], getattr(refs, f"swap_q{l}"))
            for l in range(LAYERS)
        ]
        swap_g = [
            WeightSwap(place, refs.pack_g, l, refs.mine_g.at[l], getattr(refs, f"swap_g{l}"))
            for l in range(LAYERS)
        ]
        out_w = [
            OutGather(
                place,
                refs.w_out.at[l],
                refs.mid_o.at[l],
                getattr(refs, f"out_full{l}"),
                getattr(refs, f"out_sem{l}"),
            )
            for l in range(LAYERS)
        ]
        gather_q = [
            HeadGather(
                place,
                refs.mine_q.at[l],
                refs.q_full1 if l else refs.wq,
                getattr(refs, f"gq_sem{l}"),
            )
            for l in range(LAYERS)
        ]
        gather_g = HeadGather(place, refs.mine_g.at[0], refs.wg, refs.gg_sem)
        swap_q[0].start()
    else:
        place.greet()
        gather_g = HeadGather(place, refs.mine_g.at[layer], refs.wg, refs.gg_sem)
    gather_d = HeadGather(place, refs.w_down.at[layer], refs.wd, refs.gd_sem)

    stream = refs.stream[...].astype(F32)
    scaled = (stream * inverse_rms(stream)).astype(BF16)
    own_rows = pl.ds(pl.multiple_of(place.peer * tok, tok), tok)
    refs.scaled[own_rows, :] = scaled
    ag1 = PlaneGather(place, refs.scaled, refs.ag1_s, refs.ag1_r)
    ag1.start()
    if layer == 0:
        if sizes.aligned:
            pack_ffn(sizes, 0, refs)
        swap_g[0].start()
        swap_q[0].arrive()
        gather_q[0].start()
        out_w[0].start()
        gather_d.start()
        gather_q[0].relay()
        gather_q[0].forward()
        gather_q[0].arrive()
        q_copy = pltpu.make_async_copy(refs.wq, refs.q_full0, loads.at[0])
        q_copy.start()
        refs.first[...] = document_starts(sizes, place, refs.documents)
        if sizes.aligned:
            pack_query(sizes, 1, refs)
            pack_ffn(sizes, 1, refs)
    else:
        q_copy = pltpu.make_async_copy(refs.q_full, refs.wq, loads.at[0])
        q_copy.start()
        gather_d.start()
        q_copy.wait()

    for steps in peer_groups(place.peers):
        peers = [place.peer_before(step) for step in steps]
        rows = [pl.ds(pl.multiple_of(peer * tok, tok), tok) for peer in peers]
        for step in steps:
            ag1.await_step(step)
        x = jnp.concatenate([refs.scaled[where, :] for where in rows], axis=0)
        for part in range(3):

            def block(where, part=part, x=x, peers=peers, rows=rows):
                weight = refs.wq[
                    :, pl.ds(pl.multiple_of(part * cols + where.start, where.size), where.size)
                ]
                value = dot_nn(x, weight).astype(BF16)
                there = pl.ds(
                    pl.multiple_of(max(part - 1, 0) * cols + where.start, where.size), where.size
                )
                for index, peer in enumerate(peers):
                    piece = value[index * tok : (index + 1) * tok]
                    if part == 0:
                        refs.queries[rows[index], there] = piece
                    else:
                        spot = pl.multiple_of(sizes.lead + peer * tok, tok)
                        refs.keys[pl.ds(spot, tok), there] = piece

            by_columns(cols, block)
    halo = Halo(place, refs.keys, sizes.reach, refs.halo_sem)
    halo.start()
    if layer == 0:
        swap_g[0].arrive()
        gather_g.start()
        out_w[0].spread()
        swap_q[1].start()
        swap_g[1].start()
    else:
        gather_g.start()
    gather_d.relay()
    halo.relay()
    halo.arrive()
    if layer == 0:
        out_w[0].arrive()
    wo = refs.out_full0 if layer == 0 else refs.o_full

    sum1 = PlaneSum(place, refs.part1, refs.sum1, refs.rs1_s, refs.rs1_r)

    def attend_step(index, carry):
        attend_tile(
            sizes,
            place,
            index,
            refs.queries,
            refs.keys,
            refs.first,
            refs.mixed,
            refs.attended,
            refs.logs,
        )
        for k in range(tile // tok):
            peer = index * (tile // tok) + k
            x = refs.mixed[pl.ds(pl.multiple_of(peer * tok, tok), tok), :]

            def block(where, x=x, peer=peer):
                refs.part1[peer, :, where] = dot_nn(x, wo[:, where]).astype(BF16)

            by_columns(D, block)
            sum1.send_to(peer)
        return carry

    lax.fori_loop(0, group // tile, attend_step, 0)

    gather_g.relay()
    gather_d.forward()
    gather_g.forward()
    if layer == 0:
        swap_q[1].arrive()
        gather_q[1].start()
        out_w[1].start()
        swap_g[1].arrive()

    middle = stream + sum1.total()
    refs.middle[...] = middle
    refs.scaled_ffn[own_rows, :] = (middle * inverse_rms(middle)).astype(BF16)
    ag2 = PlaneGather(place, refs.scaled_ffn, refs.ag2_s, refs.ag2_r)
    ag2.start()
    gather_g.arrive()
    gather_d.arrive()
    d_copy = pltpu.make_async_copy(refs.wd, refs.d_full, loads.at[3])
    d_copy.start()
    g_copy = pltpu.make_async_copy(refs.wg, refs.g_full, loads.at[2])
    g_copy.start()
    sum2 = PlaneSum(place, refs.part2, refs.sum2, refs.rs2_s, refs.rs2_r)

    stores = []
    for steps in peer_groups(place.peers):
        peers = [place.peer_before(step) for step in steps]
        rows = [pl.ds(pl.multiple_of(peer * tok, tok), tok) for peer in peers]
        for step in steps:
            ag2.await_step(step)
        x = jnp.concatenate([refs.scaled_ffn[where, :] for where in rows], axis=0)

        def block(where, x=x, rows=rows):
            there = pl.ds(pl.multiple_of(hidden + where.start, where.size), where.size)
            gate = dot_nn(x, refs.wg[:, where])
            up = dot_nn(x, refs.wg[:, there])
            low = (gate / (1.0 + jnp.exp(-gate)) * up).astype(BF16)
            for index, row in enumerate(rows):
                piece = slice(index * tok, (index + 1) * tok)
                refs.gate_up[row, where] = gate[piece]
                refs.gate_up[row, there] = up[piece]
                refs.hidden[row, where] = low[piece]

        by_columns(hidden, block)
        low = jnp.concatenate([refs.hidden[where, :] for where in rows], axis=0)

        def down(where, low=low, peers=peers):
            value = dot_nn(low, refs.wd[:, where]).astype(BF16)
            for index, peer in enumerate(peers):
                refs.part2[peer, :, where] = value[index * tok : (index + 1) * tok]

        by_columns(D, down)
        for step, peer, row in zip(steps, peers, rows):
            sum2.send_to(peer)
            store = pltpu.make_async_copy(
                refs.gate_up.at[row], refs.gate_up_out.at[row], refs.store_sem.at[step]
            )
            store.start()
            stores.append(store)
    if layer == 0:
        gather_q[1].relay()
        gather_q[1].forward()
        out_w[1].spread()
    after = middle + sum2.total()
    refs.next[...] = after if layer < LAYERS - 1 else after.astype(BF16)
    if layer == 0:
        gather_q[1].arrive()
        out_w[1].arrive()
        q_copy.wait()
        for item in swap_q + swap_g + gather_q + out_w:
            item.finish()
    g_copy.wait()
    d_copy.wait()
    for store in stores:
        store.wait()
    for item in (ag1, ag2, sum1, sum2, gather_g, gather_d, halo):
        item.finish()


def forward_layer(sizes, layer, stream, first_row, weights, collective_id):
    peers, planes, depth = sizes.peers, sizes.planes, sizes.planes // 2
    tok, cols, group, hidden, reach = sizes.tok, sizes.cols, sizes.group, sizes.hidden, sizes.reach
    inputs = {"stream": (stream, VMEM), "w_down": (weights["w_down"], VMEM)}
    outputs = {
        "d_full": ((hidden, D), BF16, ANY),
        "next": ((tok, D), F32 if layer < LAYERS - 1 else BF16, VMEM),
        "middle": ((tok, D), F32, VMEM),
        "scaled": ((group, D), BF16, VMEM),
        "scaled_ffn": ((group, D), BF16, VMEM),
        "queries": ((group, cols), BF16, VMEM),
        "keys": (((reach + 1) * group, 2 * cols), BF16, VMEM),
        "mixed": ((group, cols), BF16, VMEM),
        "attended": ((group, cols), F32, VMEM),
        "logs": ((cols // HD, group), F32, VMEM),
        "gate_up_out": ((group, 2 * hidden), F32, ANY),
        "hidden": ((group, hidden), BF16, VMEM),
        "g_full": ((D, 2 * hidden), BF16, ANY),
    }
    scratch = {
        "wq": pltpu.VMEM((D, 3 * cols), BF16),
        "wg": pltpu.VMEM((D, 2 * hidden), BF16),
        "wd": pltpu.VMEM((hidden, D), BF16),
        "gate_up": pltpu.VMEM((group, 2 * hidden), F32),
        "store_sem": dma(peers),
        "part1": pltpu.VMEM((peers, tok, D), BF16),
        "sum1": pltpu.VMEM((peers, tok, D), BF16),
        "part2": pltpu.VMEM((peers, tok, D), BF16),
        "sum2": pltpu.VMEM((peers, tok, D), BF16),
        "load_sem": dma(4),
        "halo_sem": Halo.sems(reach),
        "gg_sem": HeadGather.sems(depth),
        "gd_sem": HeadGather.sems(depth),
    }
    for name in ("rs1_s", "rs1_r", "rs2_s", "rs2_r"):
        scratch[name] = dma(peers - 1)
    for name in ("ag1_s", "ag1_r", "ag2_s", "ag2_r"):
        scratch[name] = PlaneGather.sems(peers)
    if layer == 0:
        rows = peers * sizes.own_rows
        inputs["documents"] = (first_row, VMEM)
        outputs["first"] = ((1, group), jnp.int32, VMEM)
        if sizes.aligned:
            for name in ("w_query", "w_key", "w_value", "w_gate", "w_up", "attn_gain", "ffn_gain"):
                inputs[name] = (weights[name], VMEM)
            scratch["pack_q"] = pltpu.VMEM((peers, LAYERS, sizes.own_rows, 3 * cols), BF16)
            scratch["pack_g"] = pltpu.VMEM((peers, LAYERS, sizes.own_rows, 2 * hidden), BF16)
        else:
            inputs["pack_q"] = (weights["pack_q"], ANY)
            inputs["pack_g"] = (weights["pack_g"], ANY)
        inputs["w_out"] = (weights["w_out"], VMEM)
        outputs["mine_q"] = ((LAYERS, rows, 3 * cols), BF16, VMEM)
        outputs["mine_g"] = ((LAYERS, rows, 2 * hidden), BF16, VMEM)
        scratch["mid_o"] = pltpu.VMEM((LAYERS, planes * sizes.own_rows, D), BF16)
        for l in range(LAYERS):
            outputs[f"q_full{l}"] = ((D, 3 * cols), BF16, ANY)
            outputs[f"out_full{l}"] = ((cols, D), BF16, VMEM)
            scratch[f"swap_q{l}"] = WeightSwap.sems(peers)
            scratch[f"swap_g{l}"] = WeightSwap.sems(peers)
            scratch[f"out_sem{l}"] = OutGather.sems(peers, depth)
            scratch[f"gq_sem{l}"] = HeadGather.sems(depth)
    else:
        inputs["mine_g"] = (weights["mine_g"], VMEM)
        inputs["q_full"] = (weights["q_full"], ANY)
        inputs["o_full"] = (weights["o_full"], VMEM)
        inputs["first"] = (first_row, VMEM)
    return launch(
        functools.partial(forward_body, sizes, layer),
        f"forward{layer}",
        inputs,
        outputs,
        scratch,
        collective_id,
        flops=group * D * (4 * cols + 3 * hidden) * 2,
    )


def dot_nt(left, right):
    return lax.dot_general(left, right, (((1,), (1,)), ((), ())), preferred_element_type=F32)


def dot_nn(left, right):
    return lax.dot_general(left, right, (((1,), (0,)), ((), ())), preferred_element_type=F32)


def dot_tn(left, right):
    return lax.dot_general(left, right, (((0,), (0,)), ((), ())), preferred_element_type=F32)


class HaloBack:
    def __init__(self, place, total, give, land, s_land, reach, sems):
        self.place, self.total, self.give, self.land, self.s_land = place, total, give, land, s_land
        self.reach = reach
        self.rows, self.width = land.shape[1:]
        self.z_send, self.z_recv, self.s_send, self.s_recv = sems

    def block(self, ref, offset):
        return ref.at[self.reach - offset]

    def lanes(self, offset):
        return slice((self.reach - offset) * self.width, (self.reach - offset + 1) * self.width)

    def hand_copy(self, i):
        return remote(
            self.block(self.give, 2 * i - 1),
            self.s_land.at[i - 1],
            self.s_send.at[i - 1],
            self.s_recv.at[i - 1],
            head=self.place.sibling,
        )

    def hands(self, i):
        return self.place.z - i + self.place.core >= 0

    def handed(self, i):
        return self.place.z - i + 1 - self.place.core >= 0

    def low(self, offset):
        self.give[self.reach - offset] = self.total[:, self.lanes(offset)].astype(BF16)

    def hand(self):
        for i in range(1, self.reach // 2 + 1):

            @pl.when(self.hands(i))
            def _(i=i):
                self.low(2 * i - 1)
                self.hand_copy(i).start()

    def add(self, i, offset):
        where = self.lanes(offset)
        self.total[:, where] = self.total[:, where] + self.s_land[i - 1].astype(F32)

    def z_copy(self, i):
        return remote(
            self.block(self.give, 2 * i),
            self.land.at[i - 1],
            self.z_send.at[i - 1],
            self.z_recv.at[i - 1],
            head=self.place.plane - 2 * i,
        )

    def sends(self, i):
        return self.place.z - i >= 0

    def receives(self, i):
        return self.place.z + i < self.place.depth

    def send(self):
        for i in range(1, self.reach // 2 + 1):

            @pl.when((self.place.core == 1) & self.handed(i))
            def _(i=i):
                self.hand_copy(i).wait_recv()
                self.add(i, 2 * i)

            if i > 1:

                @pl.when((self.place.core == 0) & self.handed(i))
                def _(i=i):
                    self.hand_copy(i).wait_recv()
                    self.add(i, 2 * i - 2)

        for i in range(1, self.reach // 2 + 1):

            @pl.when(self.sends(i))
            def _(i=i):
                self.low(2 * i)
                self.z_copy(i).start()

    def collect(self):
        @pl.when((self.place.core == 0) & self.handed(1))
        def _():
            self.hand_copy(1).wait_recv()
            self.add(1, 0)

        where = self.lanes(0)
        for i in range(1, self.reach // 2 + 1):

            @pl.when(self.receives(i))
            def _(i=i):
                self.z_copy(i).wait_recv()
                self.total[:, where] = self.total[:, where] + self.land[i - 1].astype(F32)

    def finish(self):
        for i in range(1, self.reach // 2 + 1):

            @pl.when(self.hands(i))
            def _(i=i):
                self.hand_copy(i).wait_send()

            @pl.when(self.sends(i))
            def _(i=i):
                self.z_copy(i).wait_send()


class GradJob:
    def __init__(self, place, left, right, bufs, flips, sems):
        self.place, self.left, self.right = place, left, right
        self.left_sib, self.right_sib, self.out, self.land, self.far = bufs
        self.flipped, self.flipped_sib = flips
        self.s_send, self.s_recv, self.z_send, self.z_recv, self.f_send, self.f_recv = sems
        self.outer = (place.z == 0) | (place.z == place.depth - 1)
        self.width = self.out.shape[1]

    @staticmethod
    def sems(depth):
        return [dma(depth + 1), dma(depth + 1), dma(depth - 1), dma(depth - 1), dma(), dma()]

    @staticmethod
    def bufs(group, depth, width, cols):
        return [
            pltpu.VMEM((group, depth * width), BF16),
            pltpu.VMEM((group, cols), BF16),
            pltpu.VMEM((depth, width, cols), BF16),
            pltpu.VMEM((depth - 1, width, cols), BF16),
            pltpu.VMEM((width, cols), BF16),
        ]

    def lanes(self, z, core):
        return pl.ds(pl.multiple_of((2 * z + core) * self.width, self.width), self.width)

    def right_copy(self):
        return remote(
            self.right,
            self.right_sib,
            self.s_send.at[0],
            self.s_recv.at[0],
            head=self.place.sibling,
        )

    def left_copy(self, z):
        return remote(
            self.left.at[:, self.lanes(z, 1 - self.place.core)],
            self.left_sib.at[:, pl.ds(z * self.width, self.width)],
            self.s_send.at[z + 1],
            self.s_recv.at[z + 1],
            head=self.place.sibling,
        )

    def exchange(self):
        self.right_copy().start()
        for z in range(self.place.depth):
            self.left_copy(z).start()

    def z_copy(self, step):
        z = self.place.z_after(step)
        return remote(
            self.out.at[z],
            self.land.at[step - 1],
            self.z_send.at[step - 1],
            self.z_recv.at[step - 1],
            head=2 * z + self.place.core,
        )

    def send(self, step):
        self.z_copy(step).start()

    def far_copy(self):
        z = self.place.z
        return remote(
            self.out.at[self.place.depth - 1 - z],
            self.far,
            self.f_send,
            self.f_recv,
            head=2 * (1 + lax.div(z, 2)) + self.place.core,
        )

    def sends(self, step):
        z = self.place.z
        return z >= 0 if step == 2 else (z < 3 if step == 1 else z > 0)

    def receives(self, step):
        z = self.place.z
        return z >= 0 if step == 2 else (z > 0 if step == 1 else z < 3)

    def compute(self, hold=False):
        for z in range(self.place.depth):
            mine = jnp.transpose(self.left[:, self.lanes(z, self.place.core)].astype(F32))
            self.flipped[z * self.width : (z + 1) * self.width, :] = mine.astype(BF16)
        for z in range(self.place.depth):
            self.left_copy(z).wait_recv()
            here = slice(z * self.width, (z + 1) * self.width)
            theirs = jnp.transpose(self.left_sib[:, here].astype(F32))
            self.flipped_sib[here, :] = theirs.astype(BF16)
        self.right_copy().wait_recv()

        def tile(where):
            value = dot_nn(self.flipped[...], self.right[:, where])
            value = value + dot_nn(self.flipped_sib[...], self.right_sib[:, where])
            value = value.astype(BF16)
            for z in range(self.place.depth):
                self.out[z, :, where] = value[z * self.width : (z + 1) * self.width]

        by_columns(self.out.shape[2], tile)

        @pl.when(self.outer)
        def _():
            self.far_copy().start()

        @pl.when(self.place.z == 0)
        def _():
            self.z_copy(2).start()

        @pl.when(self.sends(1))
        def _():
            self.z_copy(1).start()

        if not hold:
            self.rest()

    def rest(self):
        @pl.when(self.place.z == self.place.depth - 1)
        def _():
            self.z_copy(2).start()

        @pl.when(self.sends(3))
        def _():
            self.z_copy(3).start()

    def relay(self):
        @pl.when(jnp.logical_not(self.outer))
        def _():
            self.far_copy().wait_recv()
            z = self.place.z_after(2)
            self.out[z] = (self.out[z].astype(F32) + self.far[...].astype(F32)).astype(BF16)
            self.z_copy(2).start()

    def total(self):
        total = self.out[self.place.z].astype(F32)
        for step in range(1, self.place.depth):

            @pl.when(self.receives(step))
            def _(step=step):
                self.z_copy(step).wait_recv()

            piece = self.land[step - 1].astype(F32)
            total = total + jnp.where(self.receives(step), piece, 0.0)
        return total

    def finish(self):
        self.right_copy().wait_send()
        for z in range(self.place.depth):
            self.left_copy(z).wait_send()

        @pl.when(self.outer)
        def _():
            self.far_copy().wait_send()

        for step in range(1, self.place.depth):

            @pl.when(self.sends(step))
            def _(step=step):
                self.z_copy(step).wait_send()


class OutGradJob:
    def __init__(self, place, left, right, bufs, sems):
        self.place, self.left, self.right = place, left, right
        self.left_sib, self.right_sib, self.out, self.mid, self.land = bufs
        self.s_send, self.s_recv, self.p_send, self.p_recv, self.z_send, self.z_recv, self.local = sems
        self.width = self.out.shape[0]
        self.rows = self.mid.shape[1]

    @staticmethod
    def sems(peers, depth):
        return [
            dma(2),
            dma(2),
            dma(peers - 1),
            dma(peers - 1),
            dma(depth - 1),
            dma(depth - 1),
            dma(),
        ]

    @staticmethod
    def bufs(group, peers, depth, width, cols):
        return [
            pltpu.VMEM((group, width), BF16),
            pltpu.VMEM((group, cols), BF16),
            pltpu.VMEM((width, cols), BF16),
            pltpu.VMEM((peers, width // peers, cols), BF16),
            pltpu.VMEM((depth - 1, width // peers, cols), BF16),
        ]

    def lanes(self, core):
        return pl.ds(pl.multiple_of(core * self.width, self.width), self.width)

    def copies(self):
        return (
            remote(
                self.right,
                self.right_sib,
                self.s_send.at[0],
                self.s_recv.at[0],
                head=self.place.sibling,
            ),
            remote(
                self.left.at[:, self.lanes(1 - self.place.core)],
                self.left_sib,
                self.s_send.at[1],
                self.s_recv.at[1],
                head=self.place.sibling,
            ),
        )

    def exchange(self):
        for copy in self.copies():
            copy.start()

    def piece(self, peer):
        return self.out.at[pl.ds(pl.multiple_of(peer * self.rows, self.rows), self.rows)]

    def p_copy(self, step):
        target = self.place.peer_after(step)
        return remote(
            self.piece(target),
            self.mid.at[self.place.peer],
            self.p_send.at[step - 1],
            self.p_recv.at[step - 1],
            blk=target,
        )

    def own_copy(self):
        return pltpu.make_async_copy(
            self.piece(self.place.peer), self.mid.at[self.place.peer], self.local
        )

    def z_copy(self, step):
        z = self.place.z_after(step)
        return remote(
            self.mid.at[z],
            self.land.at[step - 1],
            self.z_send.at[step - 1],
            self.z_recv.at[step - 1],
            head=2 * z + self.place.core,
        )

    def compute(self):
        for copy in self.copies():
            copy.wait_recv()
        mine = jnp.transpose(self.left[:, self.lanes(self.place.core)].astype(F32)).astype(BF16)
        theirs = jnp.transpose(self.left_sib[...].astype(F32)).astype(BF16)

        def tile(where):
            value = dot_nn(mine, self.right[:, where]) + dot_nn(theirs, self.right_sib[:, where])
            self.out[:, where] = value.astype(BF16)

        by_columns(self.out.shape[1], tile)
        for step in range(1, self.place.peers):
            self.p_copy(step).start()
        self.own_copy().start()

    def spread(self):
        self.own_copy().wait()
        for step in range(1, self.place.peers):
            source = self.place.peer_before(step)
            remote(
                self.piece(source),
                self.mid.at[source],
                self.p_send.at[step - 1],
                self.p_recv.at[step - 1],
                blk=source,
            ).wait_recv()
        for step in range(1, self.place.depth):
            self.z_copy(step).start()

    def total(self):
        total = self.mid[self.place.z].astype(F32)
        for step in range(1, self.place.depth):
            self.z_copy(step).wait_recv()
            total = total + self.land[step - 1].astype(F32)
        return total

    def finish(self):
        for copy in self.copies():
            copy.wait_send()
        for step in range(1, self.place.peers):
            self.p_copy(step).wait_send()
        for step in range(1, self.place.depth):
            self.z_copy(step).wait_send()


def rms_back_of(values, upstream):
    inverse = inverse_rms(values)
    inner_mean = jnp.mean(upstream * values, axis=-1, keepdims=True)
    return inverse * upstream - values * (inverse * inverse * inverse) * inner_mean


def attend_back_chunk(sizes, place, block_offset, index, refs):
    tile, chunk, cols, group, lead = sizes.tile, sizes.chunk, sizes.cols, sizes.group, sizes.lead
    block = sizes.reach - block_offset
    offset = pl.multiple_of(block * group + index * chunk, chunk)
    there = pl.ds(offset, chunk)
    here = pl.ds(pl.multiple_of(index * chunk, chunk), chunk)
    spot = offset + lax.broadcasted_iota(jnp.int32, (chunk, 1), 0)
    lane = lax.broadcasted_iota(jnp.int32, (tile, 2 * HD), 1)
    begin = lax.div(jnp.maximum(offset - lead, 0), tile)
    end = jnp.minimum(
        lax.div(jnp.maximum(offset + chunk + sizes.doc_max - 2 - lead + tile, 0), tile), group // tile
    )
    pairs = range(cols // (2 * HD))
    lanes = [slice(pair * 2 * HD, (pair + 1) * 2 * HD) for pair in pairs]
    value_lanes = [slice(cols + part.start, cols + part.stop) for part in lanes]

    def step(index, sums):
        row = pl.multiple_of(index * tile, tile)
        rows = pl.ds(row, tile)
        last = lead + row + lax.broadcasted_iota(jnp.int32, (1, tile), 1)
        allowed = (spot >= refs.first[:, rows]) & (spot <= last)
        masks = (lane < HD, lane >= HD)
        halves, grads, scores, changes = [], [], [], []
        for pair in pairs:
            queries = refs.queries[rows, lanes[pair]] * jnp.asarray(HD ** (-0.5), BF16)
            upstream = refs.mixed_grad[rows, lanes[pair]]
            for mask in masks:
                halves.append(jnp.where(mask, queries, jnp.zeros_like(queries)))
                grads.append(jnp.where(mask, upstream, jnp.zeros_like(upstream)))
                scores.append(dot_nt(refs.keys[there, lanes[pair]], halves[-1]))
                changes.append(dot_nt(refs.keys[there, value_lanes[pair]], grads[-1]))
        out = list(sums)
        for pair in pairs:
            back = []
            for which in range(2):
                head = 2 * pair + which
                line = slice(head, head + 1)
                probs = jnp.where(allowed, jnp.exp(scores[head] - refs.logs[line, rows]), 0.0)
                change = (probs * (changes[head] - refs.delta[line, rows])).astype(BF16)
                out[2 * pair] = out[2 * pair] + dot_nn(change, halves[head])
                out[2 * pair + 1] = out[2 * pair + 1] + dot_nn(probs.astype(BF16), grads[head])
                back.append(dot_tn(change, refs.keys[there, lanes[pair]]))
            refs.dq[rows, lanes[pair]] += jnp.where(masks[0], back[0], back[1])
        return tuple(out)

    empty = jnp.zeros((chunk, 2 * HD), F32)
    sums = lax.fori_loop(begin, end, step, tuple(empty for _ in pairs for _ in range(2)))
    base = block * 2 * cols
    for pair in pairs:
        for part, value in ((lanes[pair], sums[2 * pair]), (value_lanes[pair], sums[2 * pair + 1])):
            refs.dkv[here, base + part.start : base + part.stop] = value


def backward_body(sizes, layer, fused, refs):
    place = Place()
    tok, cols, group, hidden = sizes.tok, sizes.cols, sizes.group, sizes.hidden
    tile, chunk, lead, reach = sizes.tile, sizes.chunk, sizes.lead, sizes.reach
    refs.gate_up = refs.dkv.at[:, pl.ds(0, 2 * hidden)]
    place.greet()
    grad = refs.grad[...].astype(F32)
    own_rows = pl.ds(pl.multiple_of(place.peer * tok, tok), tok)
    refs.down_in[own_rows, :] = grad.astype(BF16)
    ag1 = PlaneGather(place, refs.down_in, refs.ag1_s, refs.ag1_r)
    ag1.start()
    loads = {
        name: pltpu.make_async_copy(src, dst, refs.load_sem.at[index])
        for index, (name, src, dst) in enumerate(
            (
                ("d", refs.d_full, refs.wd),
                ("gate_up", refs.gate_up_in, refs.gate_up),
                ("g", refs.g_full, refs.wg),
                ("o", refs.o_full, refs.wo),
                ("q", refs.q_full, refs.wq),
                ("hidden", refs.hidden_in, refs.hidden),
                ("scaled_ffn", refs.scaled_ffn_in, refs.scaled_ffn),
            )
        )
    }
    for copy in loads.values():
        copy.start()
    jobs = []
    if fused:
        job_d = GradJob(place, refs.hidden, refs.down_in, refs.jd_buf, refs.flips, refs.jd_sem)
        job_g = GradJob(place, refs.scaled_ffn, refs.gate_up_grad, refs.jg_buf, refs.flips, refs.jg_sem)
        job_o = OutGradJob(place, refs.mixed, refs.proj_in, refs.jo_buf, refs.jo_sem)
        jobs = [job_d, job_o]
        if layer == 0:
            job_q = GradJob(
                place, refs.old_scaled, refs.old_qkv, refs.jq_buf, refs.flips, refs.jq_sem
            )
            jobs.append(job_q)
            job_q.exchange()
        loads["hidden"].wait()
        loads["scaled_ffn"].wait()
    loads["d"].wait()
    loads["gate_up"].wait()
    loads["g"].wait()
    if fused and layer == 0:
        job_q.compute()

    sum1 = PlaneSum(place, refs.part1, refs.sum1, refs.rs1_s, refs.rs1_r)

    for steps in peer_groups(place.peers):
        peers = [place.peer_before(step) for step in steps]
        rows = [pl.ds(pl.multiple_of(peer * tok, tok), tok) for peer in peers]
        for step in steps:
            ag1.await_step(step)
        if fused and steps[-1] == place.peers - 1:
            job_d.exchange()
        x = jnp.concatenate([refs.down_in[where, :] for where in rows], axis=0)

        def block(where, x=x, rows=rows):
            there = pl.ds(pl.multiple_of(hidden + where.start, where.size), where.size)
            grad_hidden = dot_nt(x, refs.wd[where, :])
            for index, row in enumerate(rows):
                piece = grad_hidden[index * tok : (index + 1) * tok]
                gate = refs.gate_up[row, where]
                up = refs.gate_up[row, there]
                sigmoid = 1.0 / (1.0 + jnp.exp(-gate))
                gate_grad = piece * up * (sigmoid * (1.0 + gate * (1.0 - sigmoid)))
                refs.gate_up_grad[row, where] = gate_grad.astype(BF16)
                refs.gate_up_grad[row, there] = (piece * (gate * sigmoid)).astype(BF16)

        by_columns(hidden, block)
        low = jnp.concatenate([refs.gate_up_grad[where, :] for where in rows], axis=0)

        def back(where, low=low, peers=peers):
            value = dot_nt(low, refs.wg[where, :]).astype(BF16)
            for index, peer in enumerate(peers):
                refs.part1[peer, :, where] = value[index * tok : (index + 1) * tok]

        by_columns(D, back)
        for peer in peers:
            sum1.send_to(peer)

    if fused:
        if layer == 0:
            job_q.relay()
        job_g.exchange()
        job_d.compute()
        if layer == 0:
            own_scaled = refs.wd.at[pl.ds(0, group)]
            scaled_load = pltpu.make_async_copy(refs.scaled_in, own_scaled, refs.load_sem.at[0])
            scaled_load.start()
    middle = refs.middle[...]
    grad_middle = grad + rms_back_of(middle, sum1.total())
    refs.proj_in[own_rows, :] = grad_middle.astype(BF16)
    ag2 = PlaneGather(place, refs.proj_in, refs.ag2_s, refs.ag2_r)
    ag2.start()
    if fused:
        job_g.compute()
        job_d.relay()
    refs.dq[...] = jnp.zeros_like(refs.dq)
    loads["o"].wait()
    loads["q"].wait()

    for steps in peer_groups(place.peers):
        rows = [
            pl.ds(pl.multiple_of(place.peer_before(step) * tok, tok), tok) for step in steps
        ]
        for step in steps:
            ag2.await_step(step)
        x = jnp.concatenate([refs.proj_in[where, :] for where in rows], axis=0)

        def block(where, x=x, rows=rows):
            value = dot_nt(x, refs.wo[where, :]).astype(BF16)
            for index, row in enumerate(rows):
                refs.mixed_grad[row, where] = value[index * tok : (index + 1) * tok]

        by_columns(cols, block)
    if fused:
        job_o.exchange()

    def deltas(index, carry):
        rows = pl.ds(pl.multiple_of(index * tile, tile), tile)
        for pair in range(cols // (2 * HD)):
            lanes = slice(pair * 2 * HD, (pair + 1) * 2 * HD)
            product = jnp.transpose(
                refs.mixed_grad[rows, lanes].astype(F32) * refs.attended[rows, lanes]
            )
            for which in range(2):
                refs.delta[2 * pair + which : 2 * pair + which + 1, rows] = jnp.sum(
                    product[which * HD : (which + 1) * HD], axis=0, keepdims=True
                )
        return carry

    lax.fori_loop(0, group // tile, deltas, 0)

    halo = HaloBack(place, refs.dkv, refs.give, refs.land, refs.s_land, reach, refs.halo_sem)
    per_block = group // chunk

    def key_blocks(offset):
        @pl.when(place.plane >= offset)
        def _():
            def body(index, carry):
                attend_back_chunk(sizes, place, offset, index, refs)
                return carry

            lax.fori_loop(0, per_block, body, 0)

    for offset in range(1, reach + 1, 2):
        key_blocks(offset)
    halo.hand()
    for offset in range(2, reach + 1, 2):
        key_blocks(offset)
    halo.send()
    if fused:
        job_g.relay()
    key_blocks(0)
    swaps = []

    def hand_out(name, value):
        pack = getattr(refs, f"pack_{name}")
        for peer in range(sizes.peers):
            pack[peer, 0] = value[peer * sizes.own_rows : (peer + 1) * sizes.own_rows]
        swap = WeightSwap(
            place, pack, 0, getattr(refs, f"rows_{name}"), getattr(refs, f"swap_{name}")
        )
        swap.start()
        swaps.append(swap)

    if fused:
        job_o.compute()
        if layer == 0:
            hand_out("q1", job_q.total().astype(BF16))
            hand_out("g1", refs.raw_g1[...])
    refs.qkv_grad[:, 0:cols] = (refs.dq[...] * (HD ** (-0.5))).astype(BF16)
    if fused:
        job_o.spread()
    halo.collect()
    refs.qkv_grad[:, cols:] = refs.dkv[:, reach * 2 * cols : (reach + 1) * 2 * cols].astype(BF16)
    if fused and layer == 0:
        scaled_load.wait()
        job_p = GradJob(place, own_scaled, refs.qkv_grad, refs.jp_buf, refs.flips, refs.jp_sem)
        job_p.exchange()

    sum1.finish()
    sum2 = PlaneSum(place, refs.part1, refs.sum2, refs.rs2_s, refs.rs2_r)

    for steps in [g for g in peer_groups(place.peers)[1:]] + [(0,)]:
        peers = [place.peer_before(step) for step in steps]
        low = jnp.concatenate(
            [refs.qkv_grad[pl.ds(pl.multiple_of(peer * tok, tok), tok), :] for peer in peers], axis=0
        )

        def back(where, low=low, peers=peers):
            value = dot_nt(low, refs.wq[where, :]).astype(BF16)
            for index, peer in enumerate(peers):
                refs.part1[peer, :, where] = value[index * tok : (index + 1) * tok]

        by_columns(D, back)
        for peer in peers:
            sum2.send_to(peer)

    if fused and layer == 0:
        job_p.compute()
    refs.next[...] = grad_middle + rms_back_of(refs.stream[...].astype(F32), sum2.total())
    if fused and layer == 0:
        job_p.relay()
    for item in [ag1, ag2, sum2, halo]:
        item.finish()
    if not fused:
        loads["hidden"].wait()
        loads["scaled_ffn"].wait()
        return
    refs.raw_down[...] = job_d.total()
    refs.raw_o[...] = job_o.total()
    if layer > 0:
        refs.raw_g[...] = job_g.total().astype(BF16)
        job_g.finish()
    else:
        hand_out("g0", job_g.total().astype(BF16))
        hand_out("q0", job_p.total().astype(BF16))
        job_g.finish()
        job_p.finish()

        for swap in swaps:
            swap.arrive()
            swap.finish()
    for item in jobs:
        item.finish()


def backward_layer(sizes, layer, fused, grad, first_row, kept, full, old, collective_id):
    peers, planes, depth = sizes.peers, sizes.planes, sizes.planes // 2
    tok, cols, group, hidden, reach = sizes.tok, sizes.cols, sizes.group, sizes.hidden, sizes.reach
    q_full, o_full, g_full, d_full = full
    inputs = {
        "grad": (grad, VMEM),
        "first": (first_row, VMEM),
        "middle": (kept["middle"], VMEM),
        "stream": (kept["stream"], VMEM),
        "queries": (kept["queries"], VMEM),
        "keys": (kept["keys"], VMEM),
        "attended": (kept["attended"], VMEM),
        "logs": (kept["logs"], VMEM),
        "mixed": (kept["mixed"], VMEM),
        "gate_up_in": (kept["gate_up_out"], ANY),
        "hidden_in": (kept["hidden"], ANY),
        "scaled_ffn_in": (kept["scaled_ffn"], ANY),
        "q_full": (q_full, ANY),
        "o_full": (o_full, ANY),
        "g_full": (g_full, ANY),
        "d_full": (d_full, ANY),
    }
    outputs = {
        "next": ((tok, D), F32, VMEM),
        "qkv_grad": ((group, 3 * cols), BF16, VMEM),
    }
    scratch = {
        "wq": pltpu.VMEM((D, 3 * cols), BF16),
        "wo": pltpu.VMEM((cols, D), BF16),
        "wg": pltpu.VMEM((D, 2 * hidden), BF16),
        "wd": pltpu.VMEM((hidden, D), BF16),
        "dkv": pltpu.VMEM((group, max(2 * hidden, (reach + 1) * 2 * cols)), F32),
        "hidden": pltpu.VMEM((group, hidden), BF16),
        "scaled_ffn": pltpu.VMEM((group, D), BF16),
        "mixed_grad": pltpu.VMEM((group, cols), BF16),
        "delta": pltpu.VMEM((cols // HD, group), F32),
        "dq": pltpu.VMEM((group, cols), F32),
        "give": pltpu.VMEM((reach, group, 2 * cols), BF16),
        "land": pltpu.VMEM((reach // 2, group, 2 * cols), BF16),
        "s_land": pltpu.VMEM((reach // 2, group, 2 * cols), BF16),
        "load_sem": dma(7),
        "halo_sem": Halo.sems(reach),
    }
    for name in ("part1", "sum1", "sum2"):
        scratch[name] = pltpu.VMEM((peers, tok, D), BF16)
    for name in ("rs1_s", "rs1_r", "rs2_s", "rs2_r"):
        scratch[name] = dma(peers - 1)
    for name in ("ag1_s", "ag1_r", "ag2_s", "ag2_r"):
        scratch[name] = PlaneGather.sems(peers)
    space = pltpu.VMEM
    if fused:
        scratch["down_in"] = space((group, D), BF16)
        scratch["proj_in"] = space((group, D), BF16)
        scratch["gate_up_grad"] = space((group, 2 * hidden), BF16)
        width = D // planes
        strip = hidden // planes
        scratch["flips"] = [pltpu.VMEM((depth * width, group), BF16)] * 2
        scratch["jd_buf"] = GradJob.bufs(group, depth, strip, D)
        scratch["jg_buf"] = GradJob.bufs(group, depth, width, 2 * hidden)
        scratch["jo_buf"] = OutGradJob.bufs(group, peers, depth, cols // 2, D)
        scratch["jd_sem"] = GradJob.sems(depth)
        scratch["jg_sem"] = GradJob.sems(depth)
        scratch["jo_sem"] = OutGradJob.sems(peers, depth)
        outputs["raw_down"] = ((strip, D), F32, VMEM)
        outputs["raw_o"] = ((sizes.own_rows, D), F32, VMEM)
        if layer > 0:
            outputs["raw_g"] = ((width, 2 * hidden), BF16, VMEM)
        else:
            rows = sizes.own_rows
            inputs["old_scaled"] = (old["scaled"], VMEM)
            inputs["old_qkv"] = (old["qkv_grad"], VMEM)
            inputs["raw_g1"] = (old["raw_g"], VMEM)
            inputs["scaled_in"] = (kept["scaled"], ANY)
            for name in ("jq", "jp"):
                scratch[f"{name}_buf"] = GradJob.bufs(group, depth, width, 3 * cols)
                scratch[f"{name}_sem"] = GradJob.sems(depth)
            for l in range(LAYERS):
                for kind, width_of in (("g", 2 * hidden), ("q", 3 * cols)):
                    outputs[f"rows_{kind}{l}"] = ((peers * rows, width_of), BF16, VMEM)
                    scratch[f"pack_{kind}{l}"] = pltpu.VMEM((peers, 1, rows, width_of), BF16)
                    scratch[f"swap_{kind}{l}"] = WeightSwap.sems(peers)
    else:
        outputs["down_in"] = ((group, D), BF16, VMEM)
        outputs["proj_in"] = ((group, D), BF16, VMEM)
        outputs["gate_up_grad"] = ((group, 2 * hidden), BF16, VMEM)
    return launch(
        functools.partial(backward_body, sizes, layer, fused),
        f"backward{layer}",
        inputs,
        outputs,
        scratch,
        collective_id,
        flops=group * D * (4 * cols + 3 * hidden) * 4,
    )


def inverse_rms(values):
    return lax.rsqrt(jnp.mean(values * values, axis=-1, keepdims=True) + EPSILON)


def matmul(left, right):
    return jnp.dot(left, right, preferred_element_type=F32)


def contract_rows(left, right):
    return jnp.einsum("td,te->de", left, right, preferred_element_type=F32)


def contract_cols(left, right):
    return jnp.einsum("te,de->td", left, right, preferred_element_type=F32)


def local(
    tokens,
    gain_attn,
    w_query,
    w_key,
    w_value,
    w_out,
    gain_ffn,
    w_gate,
    w_up,
    w_down,
    doc_ids,
    cotangent,
):
    planes = lax.axis_size("head")
    peers = lax.axis_size("blk")
    plane = lax.axis_index("head")
    tok = tokens.shape[0]
    group = tok * peers
    stream_rows = group * planes
    doc_max = stream_rows // 4
    reach = (doc_max - 1 + group - 1) // group
    reach = reach + reach % 2
    own_rows = w_query.shape[1]
    cols = D // peers
    strip = w_down.shape[1]
    hidden_cols = strip * planes
    tile = 256
    chunk = 256
    lead = reach * group

    attn_rows = gain_attn.astype(F32)[:, :, None]
    ffn_rows = gain_ffn.astype(F32)[:, :, None]

    def for_peers(weight, gain):
        scaled = (weight.astype(F32) * gain).astype(BF16)
        return scaled.reshape(LAYERS, own_rows, peers, cols).transpose(2, 0, 1, 3)

    def for_peers_ffn(weight, gain):
        scaled = (weight.astype(F32) * gain).astype(BF16)
        scaled = scaled.reshape(LAYERS, own_rows, planes, peers, strip).transpose(3, 0, 1, 2, 4)
        return scaled.reshape(peers, LAYERS, own_rows, hidden_cols)

    aligned = strip % 128 == 0
    weights = {"w_out": w_out, "w_down": w_down}
    if aligned:
        weights |= {
            "w_query": w_query,
            "w_key": w_key,
            "w_value": w_value,
            "w_gate": w_gate,
            "w_up": w_up,
            "attn_gain": attn_rows,
            "ffn_gain": ffn_rows,
        }
    else:
        weights |= {
            "pack_q": jnp.concatenate(
                [for_peers(w, attn_rows) for w in (w_query, w_key, w_value)], axis=3
            ),
            "pack_g": jnp.concatenate([for_peers_ffn(w, ffn_rows) for w in (w_gate, w_up)], axis=3),
        }
    sizes = types.SimpleNamespace(
        peers=peers,
        planes=planes,
        tok=tok,
        cols=cols,
        group=group,
        hidden=hidden_cols,
        reach=reach,
        own_rows=own_rows,
        tile=tile,
        chunk=chunk,
        lead=lead,
        doc_max=doc_max,
        documents=stream_rows // 256,
        aligned=aligned,
    )
    first_row = doc_ids.reshape(1, stream_rows)
    stream = tokens
    saved = []
    full = []
    for layer in range(LAYERS):
        kept = forward_layer(sizes, layer, stream, first_row, weights, 10 + layer)
        if layer == 0:
            first_row = kept["first"]
            weights = weights | {
                "mine_g": kept["mine_g"],
                "q_full": kept["q_full1"],
                "o_full": kept["out_full1"],
            }
            full.append((kept["q_full0"], kept["out_full0"], kept["g_full"], kept["d_full"]))
        else:
            full.append((weights["q_full"], weights["o_full"], kept["g_full"], kept["d_full"]))
        saved.append(kept | {"stream": stream})
        stream = kept["next"]
    output = stream

    grad = cotangent
    fused = planes == 8 and aligned
    backs = [None] * LAYERS
    old = None
    for layer in reversed(range(LAYERS)):
        kept = saved[layer]
        back = backward_layer(
            sizes, layer, fused, grad, first_row, kept, full[layer], old, 12 + layer
        )
        grad = back["next"]
        old = back | {"scaled": kept["scaled"]}
        backs[layer] = back
    if fused:
        rows = backs[0]
        grad_out = jnp.stack([back["raw_o"] for back in backs])
        grad_down = jnp.stack([back["raw_down"] for back in backs])
    else:
        raw, grad_out, grad_down = [], [], []
        for kept, back in zip(saved, backs):
            down_in = back["down_in"]
            proj_in = back["proj_in"]
            scatter = functools.partial(lax.psum_scatter, scatter_dimension=0, tiled=True)
            grad_down.append(
                scatter(contract_rows(kept["hidden"], down_in).astype(BF16), "head").astype(F32)
            )
            padded = lax.dynamic_update_slice(
                jnp.zeros((D, D), BF16),
                contract_rows(kept["mixed"], proj_in).astype(BF16),
                (lax.axis_index("blk") * cols, 0),
            )
            grad_out.append(scatter(padded, ("head", "blk")).astype(F32))
            pieces = [
                scatter(contract_rows(kept[name], right).astype(BF16), "head")
                for name, right in (
                    ("scaled", back["qkv_grad"]),
                    ("scaled_ffn", back["gate_up_grad"]),
                )
            ]
            raw.append(jnp.concatenate(pieces, axis=1))
        raw = jnp.stack(raw).reshape(LAYERS, peers, own_rows, 3 * cols + 2 * hidden_cols)
        raw = plane_swap(raw.transpose(1, 0, 2, 3), 1, "rows_swap")
        rows = {}
        for layer in range(LAYERS):
            flat = raw[:, layer].reshape(peers * own_rows, 3 * cols + 2 * hidden_cols)
            rows[f"rows_q{layer}"] = flat[:, : 3 * cols]
            rows[f"rows_g{layer}"] = flat[:, 3 * cols :]
        grad_out, grad_down = jnp.stack(grad_out), jnp.stack(grad_down)

    def attn_rows_of(which):
        pieces = [
            rows[f"rows_q{layer}"].reshape(peers, own_rows, 3, cols)[:, :, which].transpose(1, 0, 2)
            for layer in range(LAYERS)
        ]
        return jnp.stack([p.reshape(own_rows, D).astype(F32) for p in pieces])

    def ffn_rows_of(which):
        pieces = [
            rows[f"rows_g{layer}"]
            .reshape(peers, own_rows, 2, planes, strip)[:, :, which]
            .transpose(1, 2, 0, 3)
            for layer in range(LAYERS)
        ]
        return jnp.stack([p.reshape(own_rows, peers * hidden_cols).astype(F32) for p in pieces])

    raw_query, raw_key, raw_value = (attn_rows_of(which) for which in range(3))
    raw_gate, raw_up = (ffn_rows_of(which) for which in range(2))

    def gain_grad(*pairs):
        return sum(jnp.sum(weight.astype(F32) * raw_part, axis=2) for weight, raw_part in pairs)

    grad_gain_attn = gain_grad((w_query, raw_query), (w_key, raw_key), (w_value, raw_value))
    grad_gain_ffn = gain_grad((w_gate, raw_gate), (w_up, raw_up))
    return (
        output,
        grad,
        grad_gain_attn,
        raw_query * attn_rows,
        raw_key * attn_rows,
        raw_value * attn_rows,
        grad_out,
        grad_gain_ffn,
        raw_gate * ffn_rows,
        raw_up * ffn_rows,
        grad_down,
    )


def solution(mesh):
    rows = P(("head", "blk"), None)
    vector = P(None, ("head", "blk"))
    matrix = P(None, ("head", "blk"), None)
    return jax.shard_map(
        local,
        mesh=mesh,
        in_specs=(
            rows,
            vector,
            matrix,
            matrix,
            matrix,
            matrix,
            vector,
            matrix,
            matrix,
            matrix,
            P(),
            rows,
        ),
        out_specs=(
            rows,
            rows,
            vector,
            matrix,
            matrix,
            matrix,
            matrix,
            vector,
            matrix,
            matrix,
            matrix,
        ),
        check_vma=False,
    )
```
